32 devices in a mesh: dp: 8 (over z, x), fsdp: 4 (over y, core).
Axes of the slice: x: 2, y: 2, z: 4, core: 2. Of those that a mesh axis runs over, the one named last changes fastest.
Arguments:
- tokens: bfloat16 [4096, 2048], P(('dp', 'fsdp')), may hold values from -4 to 4
- cotangent: bfloat16 [4096, 2048], P(('dp', 'fsdp')), may hold values from -4 to 4
- context: bfloat16 [64, 128, 4096], P(('dp', 'fsdp')), may hold values from -6 to 6
- lengths: int32 [32, 2], P(('dp', 'fsdp')), may hold values from 0 to 128, as said below
- keep: int32 [4096], P(('dp', 'fsdp')), may hold values 0 or 1
- owners: int32 [18], replicated, may hold values from 0 to 3, as said below
- master: float32 [24, 2048, 2048], P('fsdp', 'dp'), may hold values from -0.125 to 0.125
- moment_one: float32 [24, 2048, 2048], P('fsdp', 'dp'), may hold values from -14 to 14
- moment_two: float32 [24, 2048, 2048], P('fsdp', 'dp'), may hold values from 20.48 to 86.016
- gains: float32 [3, 2048], replicated, may hold values from 0.5 to 1.5
- gain_one: float32 [3, 2048], replicated, may hold values from -20 to 20
- gain_two: float32 [3, 2048], replicated, may hold values from 53.248 to 204.8
Outputs:
- layer_out: bfloat16 [4096, 2048], P(('dp', 'fsdp'))
- grad_tokens: bfloat16 [4096, 2048], P(('dp', 'fsdp'))
- new_master: float32 [24, 2048, 2048], P('fsdp', 'dp')
- new_one: float32 [24, 2048, 2048], P('fsdp', 'dp')
- new_two: float32 [24, 2048, 2048], P('fsdp', 'dp')
- new_gains: float32 [3, 2048], replicated
- new_gain_one: float32 [3, 2048], replicated
- new_gain_two: float32 [3, 2048], replicated
The draws below stay inside these ranges and needn't reach their ends.
Inputs may be any that keep to these rules, and one draw needn't show every extreme that they name: `lengths`: each device's row is either one item of 128 tokens followed by zeros, or 2 items of 64 tokens; both kinds occur in every draw. `owners`: every owner holds 1 to 6 tiles, and two hold exactly 6.
All inputs are finite; a program needn't handle non-finite values. No bound on the sum of `keep` on one device may be relied on, other than what follows from the above.
Results may differ from the reference program's by a relative error of at most 0.028.
Values may be sent and summed in bfloat16 or wider, within the bound.
No kernel may reach another device: no remote copies, remote signals or barrier semaphores. Data moves between devices by JAX's collectives and lax.ppermute only.
A program may use at most 576 MiB of HBM per device.

```python
import math
import jax
import jax.numpy as jnp
from jax import lax

D = 2048
HEADS = 16
HEAD_DIM = 128
CTX = 4096
CL = 128
TOK_DEV = 128
SLOTS = 2
TILES = 18
CAP = 6
NORMS = 3
STEP = 10
GROUPS = 32
TOKENS = 4096
ITEMS = 64
N_FSDP = 4


def activation_draw(key):
    values = jax.random.truncated_normal(key, -4.0, 4.0, (TOKENS, D), jnp.float32)
    return values.astype(jnp.bfloat16)


def draw_tokens(key, part):
    return activation_draw(jax.random.fold_in(key, 11))


def draw_cotangent(key, part):
    return activation_draw(jax.random.fold_in(key, 23))


def draw_lengths(key, part):
    first, second, third = jax.random.split(key, 3)
    coin = jax.random.randint(first, (GROUPS,), 0, 2)
    pick_long = jax.random.randint(second, (), 0, GROUPS)
    pick_short = (pick_long + jax.random.randint(third, (), 1, GROUPS)) % GROUPS
    places = jnp.arange(GROUPS)
    coin = jnp.where(places == pick_long, 1, jnp.where(places == pick_short, 0, coin))
    short_row = jnp.full((SLOTS,), TOK_DEV // SLOTS, jnp.int32)
    long_row = jnp.zeros((SLOTS,), jnp.int32).at[0].set(TOK_DEV)
    return jnp.where(coin[:, None] == 1, long_row[None, :], short_row[None, :]).astype(jnp.int32)


def draw_owners(key, part):
    first, second, third = jax.random.split(key, 3)
    tile_order = jax.random.permutation(first, TILES)
    owner_order = jax.random.permutation(second, N_FSDP)
    extra = jax.random.randint(third, (), 1, CAP)
    places = jnp.arange(TILES)
    group = (places >= CAP).astype(jnp.int32) + (places >= 2 * CAP).astype(jnp.int32) + (places >= 2 * CAP + extra).astype(jnp.int32)
    owner_of_place = owner_order[group]
    return jnp.zeros((TILES,), jnp.int32).at[tile_order].set(owner_of_place).astype(jnp.int32)


def set_ends(entries, stream_key, smallest, high):
    shape = entries.shape
    place = [jax.random.randint(jax.random.fold_in(stream_key, axis), (), 0, shape[axis]) for axis in range(len(shape))]
    entries = entries.at[tuple(place)].set(smallest)
    longest = shape.index(max(shape))
    place[longest] = (place[longest] + 1) % shape[longest]
    return entries.at[tuple(place)].set(high)


def levels(own_key, dims, pieces, smallest, largest):
    level, own = 1.0, jax.random.fold_in(own_key, 6)
    for position, parts in pieces:
        draws = jnp.exp(jax.random.uniform(jax.random.fold_in(own, position), (parts,), jnp.float32, smallest / len(pieces), largest / len(pieces)))
        level = level * jnp.repeat(draws, dims[position] // parts).reshape([-1 if axis == position else 1 for axis in range(len(dims))])
    return level


def bell_draw(own_key, extent, scale, limit, shards=(), kind=jnp.bfloat16):
    entries = jax.random.normal(own_key, extent, jnp.float32) * scale
    if len(shards) > 0:
        entries = levels(own_key, extent, shards, -0.22, 0.18) * entries
    return jnp.clip(entries, min=-limit, max=limit).astype(kind)


def setup_inputs(seed: int = 0) -> dict:
    key_of = jax.random.split(jax.random.key(seed), 13)
    tokens = draw_tokens(jax.random.fold_in(key_of[12], 71), 0)
    cotangent = draw_cotangent(jax.random.fold_in(key_of[12], 71), 0)
    context = bell_draw(key_of[2], (ITEMS, CL, CTX), 1.0, 6.0, ((0, 32),))
    lengths = draw_lengths(jax.random.fold_in(key_of[12], 71), 0)
    keep = set_ends((jax.random.randint(key_of[4], (TOKENS,), 0, 8) < 7).astype(jnp.int32), jax.random.fold_in(key_of[4], 1), 0, 1)
    owners = draw_owners(jax.random.fold_in(key_of[12], 71), 0)
    master = bell_draw(key_of[6], (N_FSDP * CAP, D, D), D ** -0.5, 0.125, ((0, 4), (1, 8)), jnp.float32)
    moment_one = bell_draw(key_of[7], (N_FSDP * CAP, D, D), (0.035 * TOKENS ** 0.5), 14.0, ((0, 4), (1, 8)), jnp.float32)
    moment_two = jnp.clip(jnp.exp(math.log(86.016) - 1.43508453 * jax.random.uniform(key_of[8], (N_FSDP * CAP, D, D), jnp.float32) ** levels(key_of[8], (N_FSDP * CAP, D, D), ((0, 4), (1, 8)), -0.2, 0.2)), 20.48, 86.016)
    gains = jnp.clip(1.0 + 0.1 * jax.random.normal(key_of[9], (NORMS, D), jnp.float32), 0.5, 1.5)
    gain_one = bell_draw(key_of[10], (NORMS, D), (0.055 * TOKENS ** 0.5), 20.0, (), jnp.float32)
    gain_two = jnp.clip(jnp.exp(jax.random.uniform(key_of[11], (NORMS, D), jnp.float32, math.log(53.248), math.log(204.8))), 53.248, 204.8)
    return dict(tokens=tokens, cotangent=cotangent, context=context, lengths=lengths, keep=keep, owners=owners, master=master, moment_one=moment_one, moment_two=moment_two, gains=gains, gain_one=gain_one, gain_two=gain_two)


norm_eps = 1e-06
beta_one = 0.9
beta_two = 0.95
adam_eps = 1e-08
decay_rate = 0.1
rate_matrix = 0.1
rate_gain = 0.8

@jax.custom_vjp
def low(v):
    return lax.optimization_barrier(v.astype(jnp.bfloat16)).astype(jnp.float32)

@jax.custom_vjp
def low_back(v):
    return v

def low_keep(v):
    return (low(v), None)

def low_pass(kept, grad):
    return (grad,)

def back_keep(v):
    return (v, None)

def back_low(kept, grad):
    return (low(grad),)
low.defvjp(low_keep, low_pass)
low_back.defvjp(back_keep, back_low)

def normalize(h, gain):
    scale = lax.rsqrt(lax.optimization_barrier(jnp.mean(h * h, axis=-1, keepdims=True)) + norm_eps)
    return h * scale * gain

def gelu_tanh(u):
    return 0.5 * u * (1.0 + jnp.tanh(0.7978845608028654 * (u + 0.044715 * u * u * u)))

def softmax_rows(scores):
    shifted = scores - lax.optimization_barrier(jnp.max(scores, axis=-1, keepdims=True))
    expo = jnp.exp(shifted)
    return expo / lax.optimization_barrier(jnp.sum(expo, axis=-1, keepdims=True))

def product(left, right):
    return jnp.dot(left, right, precision=lax.Precision.HIGHEST)

def slot_table(owners, cap):
    order = jnp.arange(owners.shape[0])
    same = (owners[:, None] == owners[None, :]) & (order[None, :] < order[:, None])
    return (owners * cap + lax.optimization_barrier(jnp.sum(same.astype(jnp.int32), axis=1))).astype(jnp.int32)

def adam_update(weight, first, second, grad, rate, decay):
    first = beta_one * first + (1.0 - beta_one) * grad
    second = beta_two * second + (1.0 - beta_two) * grad * grad
    fix_one = 1.0 - beta_one ** STEP
    fix_two = 1.0 - beta_two ** STEP
    move = first / fix_one / (jnp.sqrt(second / fix_two) + adam_eps)
    return (weight - rate * (move + decay * weight), first, second)

def row_forward(h0, ctx, seg, live, tiles, gains):
    count = h0.shape[0]
    highest = lax.Precision.HIGHEST
    scale = HEAD_DIM ** (-0.5)
    places = jnp.arange(count)
    allowed = (seg[:, None] == seg[None, :]) & (live[None, :] | (places[:, None] == places[None, :]))
    a_in = low(normalize(h0, gains[0]))
    query = low_back(low(product(a_in, tiles[0]))).reshape(count, HEADS, HEAD_DIM)
    keys = low_back(low(product(a_in, tiles[1]))).reshape(count, HEADS, HEAD_DIM)
    values = low_back(low(product(a_in, tiles[2]))).reshape(count, HEADS, HEAD_DIM)
    scores = low_back(jnp.einsum('qhd,khd->hqk', query, keys, precision=highest) * scale)
    probs = softmax_rows(jnp.where(allowed[None], scores, -1e+30))
    attended = jnp.einsum('hqk,khd->qhd', low(probs), values, precision=highest).reshape(count, D)
    attended = low_back(low(attended))
    h1 = h0 + low_back(product(attended, tiles[3]))
    b_in = low(normalize(h1, gains[1]))
    ctx_flat = ctx.reshape(SLOTS * CL, CTX)
    w_ck = jnp.concatenate([tiles[5], tiles[6]], axis=0)
    w_cv = jnp.concatenate([tiles[7], tiles[8]], axis=0)
    cross_q = low_back(low(product(b_in, tiles[4]))).reshape(count, HEADS, HEAD_DIM)
    cross_k = low_back(low(product(ctx_flat, w_ck))).reshape(SLOTS * CL, HEADS, HEAD_DIM)
    cross_v = low_back(low(product(ctx_flat, w_cv))).reshape(SLOTS * CL, HEADS, HEAD_DIM)
    owner_slot = jnp.arange(SLOTS * CL) // CL
    mine = seg[:, None] == owner_slot[None, :]
    cross_s = low_back(jnp.einsum('qhd,khd->hqk', cross_q, cross_k, precision=highest) * scale)
    cross_p = softmax_rows(jnp.where(mine[None], cross_s, -1e+30))
    cross_o = jnp.einsum('hqk,khd->qhd', low(cross_p), cross_v, precision=highest).reshape(count, D)
    cross_o = low_back(low(cross_o))
    h2 = h1 + low_back(product(cross_o, tiles[9]))
    c_in = low(normalize(h2, gains[2]))
    w_in = jnp.concatenate([tiles[10], tiles[11], tiles[12], tiles[13]], axis=1)
    w_out = jnp.concatenate([tiles[14], tiles[15], tiles[16], tiles[17]], axis=0)
    hidden = low_back(product(c_in, w_in))
    activated = low(gelu_tanh(hidden))
    return h2 + low_back(product(activated, w_out))

def reference(tokens, cotangent, context, lengths, keep, owners, master, moment_one, moment_two, gains, gain_one, gain_two):
    slot_of = slot_table(owners, CAP)
    tiles = low(master[slot_of])
    ends = jnp.cumsum(lengths, axis=1).astype(jnp.int32)
    places = jnp.arange(TOK_DEV).astype(jnp.int32)
    segs = lax.optimization_barrier(jnp.sum((places[None, :, None] >= ends[:, None, :]).astype(jnp.int32), axis=2)).astype(jnp.int32)
    lives = (keep == 1).reshape(GROUPS, TOK_DEV)
    rows = tokens.astype(jnp.float32).reshape(GROUPS, TOK_DEV, D)
    ctxs = context.astype(jnp.float32).reshape(GROUPS, SLOTS, CL, CTX)
    weight_keep = (keep == 1).astype(jnp.float32)
    cots = (cotangent.astype(jnp.float32) * weight_keep[:, None]).reshape(GROUPS, TOK_DEV, D)

    def whole(rows, tiles, gains):

        def one(carry, item):
            h0, ctx, seg, live = item
            return (carry, row_forward(h0, ctx, seg, live, tiles, gains))
        _, outputs = lax.scan(jax.checkpoint(one), jnp.zeros((), jnp.float32), (rows, ctxs, segs, lives))
        return outputs
    outputs, pullback = jax.vjp(whole, rows, tiles, gains)
    d_rows, d_tiles, d_gains = pullback(cots)
    layer_out = outputs.reshape(TOKENS, D).astype(jnp.bfloat16)
    grad_tokens = d_rows.reshape(TOKENS, D).astype(jnp.bfloat16)
    grad_slots = jnp.zeros((N_FSDP * CAP, D, D), jnp.float32).at[slot_of].set(d_tiles)
    used = jnp.zeros((N_FSDP * CAP,), jnp.float32).at[slot_of].set(1.0) > 0.5
    new_w, new_m, new_v = adam_update(master, moment_one, moment_two, grad_slots, rate_matrix, decay_rate)
    zero = jnp.zeros_like(master)
    new_w = jnp.where(used[:, None, None], new_w, zero)
    new_m = jnp.where(used[:, None, None], new_m, zero)
    new_v = jnp.where(used[:, None, None], new_v, zero)
    new_g, new_gm, new_gv = adam_update(gains, gain_one, gain_two, d_gains, rate_gain, 0.0)
    return (layer_out, grad_tokens, new_w, new_m, new_v, new_g, new_gm, new_gv)
```

```python
import jax
import jax.numpy as jnp
import numpy as np
from jax import lax
from jax.experimental import pallas as pl
from jax.experimental.pallas import tpu as pltpu
from jax.sharding import Mesh
from jax.sharding import PartitionSpec as P

HEADS = 16
STEP = 10

norm_eps = 1e-06
beta_one = 0.9
beta_two = 0.95
adam_eps = 1e-08
decay_rate = 0.1
rate_matrix = 0.1
rate_gain = 0.8

f32 = jnp.float32
bf16 = jnp.bfloat16

SHIFT = (0, 0, 0, 0, 2, 2, 2, 2, 2, 2, 0, 1, 2, 3, 0, 1, 2, 3)
ROW_TILES = (3, 9, 14, 15, 16, 17)
VMEM_LIMIT = 48 << 20


def normalize(h, gain):
    scale = lax.rsqrt(jnp.mean(h * h, axis=-1, keepdims=True) + norm_eps)
    return h * scale * gain


def gelu_tanh(u):
    return 0.5 * u * (1.0 + jnp.tanh(0.7978845608028654 * (u + 0.044715 * u * u * u)))


def matmul(left, right):
    return jnp.dot(left, right, preferred_element_type=f32)


def matmul_left(left, right):
    return lax.dot_general(left, right, (((0,), (0,)), ((), ())), preferred_element_type=f32)


def matmul_right(left, right):
    return lax.dot_general(left, right, (((1,), (1,)), ((), ())), preferred_element_type=f32)


def ranks_of(owners):
    order = jnp.arange(owners.shape[0])
    same = (owners[:, None] == owners[None, :]) & (order[None, :] < order[:, None])
    return jnp.sum(same.astype(jnp.int32), axis=1)


def segments(lengths, count):
    places = jnp.arange(count)
    end = jnp.zeros((), jnp.int32)
    seg = jnp.zeros((count,), jnp.int32)
    for item in range(lengths.shape[0]):
        end = end + lengths[item]
        seg = seg + (places >= end).astype(jnp.int32)
    return seg


def adam_update(weight, first, second, grad, rate, decay):
    first = beta_one * first + (1.0 - beta_one) * grad
    second = beta_two * second + (1.0 - beta_two) * grad * grad
    fix_one = 1.0 - beta_one**STEP
    fix_two = 1.0 - beta_two**STEP
    move = first / fix_one / (jnp.sqrt(second / fix_two) + adam_eps)
    return (weight - rate * (move + decay * weight), first, second)


def pack_columns(master, table, first_slot, slots):
    _, rows, columns = master.shape
    width = columns // 8

    def kernel(table_ref, in_ref, out_ref):
        slot = pl.program_id(0)
        for rank in range(8):
            start = pl.multiple_of(table_ref[slot * 8 + rank] * width, width)
            out_ref[rank, 0] = in_ref[0, :, pl.ds(start, width)].astype(bf16)

    return pl.pallas_call(
        kernel,
        out_shape=jax.ShapeDtypeStruct((8, slots, rows, width), bf16),
        grid_spec=pltpu.PrefetchScalarGridSpec(
            num_scalar_prefetch=1,
            grid=(slots,),
            in_specs=[pl.BlockSpec((1, rows, columns), lambda k, t: (first_slot + k, 0, 0))],
            out_specs=pl.BlockSpec((8, 1, rows, width), lambda k, t: (0, k, 0, 0)),
        ),
        compiler_params=pltpu.CompilerParams(vmem_limit_bytes=VMEM_LIMIT),
        name="pack_columns",
    )(table, master)


def pick_blocks(sources, which, index, count):
    _, rows, width = sources[0].shape
    n_src = len(sources)

    def kernel(which_ref, index_ref, *refs):
        place = pl.program_id(0) * 2 + pl.program_id(1)
        out_ref = refs[n_src]
        for number in range(n_src):

            @pl.when(which_ref[place] == number)
            def _():
                out_ref[...] = refs[number][0]

    def spec(number):
        def at(n, half, which, index):
            place = n * 2 + half
            return (jnp.where(which[place] == number, index[place], 0), 0, 0)

        return pl.BlockSpec((1, rows, width), at)

    return pl.pallas_call(
        kernel,
        out_shape=jax.ShapeDtypeStruct((2 * rows, count * width), bf16),
        grid_spec=pltpu.PrefetchScalarGridSpec(
            num_scalar_prefetch=2,
            grid=(count, 2),
            in_specs=[spec(number) for number in range(n_src)],
            out_specs=pl.BlockSpec((rows, width), lambda n, half, which, index: (half, n)),
        ),
        compiler_params=pltpu.CompilerParams(vmem_limit_bytes=VMEM_LIMIT),
        name="pick_blocks",
    )(which, index, *sources)


def pack_gradients(groups, which, column, rows, width, slots):
    n_src = len(groups)

    def kernel(which_ref, column_ref, *refs):
        place = pl.program_id(0) * slots + pl.program_id(1)
        out_ref = refs[n_src]
        for number in range(n_src):

            @pl.when(which_ref[place] == number)
            def _():
                out_ref[0, 0] = refs[number][...]

    def spec(number):
        def at(rank, k, which, column):
            place = rank * slots + k
            return (rank // 4, jnp.where(which[place] == number, column[place], 0))

        return pl.BlockSpec((rows, width), at)

    return pl.pallas_call(
        kernel,
        out_shape=jax.ShapeDtypeStruct((8, slots, rows, width), bf16),
        grid_spec=pltpu.PrefetchScalarGridSpec(
            num_scalar_prefetch=2,
            grid=(8, slots),
            in_specs=[spec(number) for number in range(n_src)],
            out_specs=pl.BlockSpec((1, 1, rows, width), lambda rank, k, which, column: (rank, k, 0, 0)),
        ),
        compiler_params=pltpu.CompilerParams(vmem_limit_bytes=VMEM_LIMIT),
        name="pack_gradients",
    )(which, column, *groups)


def adam_tiles(master, one, two, col_grads, row_grads, used, is_row, col_source, row_source):
    cap, rows, columns = master.shape
    width = columns // 8

    def kernel(used_ref, is_row_ref, cs_ref, rs_ref, w_ref, m_ref, v_ref, cg_ref, rg_ref, nw_ref, nm_ref, nv_ref):
        slot = pl.program_id(0)

        @pl.when(used_ref[slot] == 0)
        def _():
            for ref in (nw_ref, nm_ref, nv_ref):
                ref[...] = jnp.zeros_like(ref)

        def update(grad):
            w, m, v = adam_update(w_ref[0], m_ref[0], v_ref[0], grad.astype(f32), rate_matrix, decay_rate)
            nw_ref[0] = w
            nm_ref[0] = m
            nv_ref[0] = v

        @pl.when((used_ref[slot] == 1) & (is_row_ref[slot] == 0))
        def _():
            update(cg_ref[0])

        @pl.when((used_ref[slot] == 1) & (is_row_ref[slot] == 1))
        def _():
            update(rg_ref[0])

    state = pl.BlockSpec((1, rows, width), lambda k, b, u, i, cs, rs: (k, 0, b))
    shape = jax.ShapeDtypeStruct(master.shape, f32)
    return pl.pallas_call(
        kernel,
        out_shape=(shape, shape, shape),
        grid_spec=pltpu.PrefetchScalarGridSpec(
            num_scalar_prefetch=4,
            grid=(cap, 8),
            in_specs=[
                state,
                state,
                state,
                pl.BlockSpec((1, rows, width), lambda k, b, u, i, cs, rs: (cs[k * 8 + b] * cap + k, 0, 0)),
                pl.BlockSpec((1, rows, width), lambda k, b, u, i, cs, rs: (rs[k], 0, b)),
            ],
            out_specs=(state, state, state),
        ),
        compiler_params=pltpu.CompilerParams(vmem_limit_bytes=VMEM_LIMIT),
        name="adam_tiles",
    )(used, is_row, col_source, row_source, master, one, two, col_grads, row_grads)


def swap(value, axis):
    return lax.ppermute(value, axis, [(0, 1), (1, 0)])


def gather_rows(value):
    half = value.shape[0] // 2
    over_x = swap(value, "x")
    over_y = swap(value, "y")
    far_low = swap(over_y[:half], "x")
    far_high = swap(over_x[half:], "y")
    four = jnp.concatenate([value, over_y, over_x, far_low, far_high], axis=0)
    return jnp.concatenate([four, swap(four, "c")], axis=0)


def scatter_rows(part):
    rows, width = part.shape[0] // 8, part.shape[1]
    half = width // 2
    part = part.reshape(2, 2, 2, rows, width)
    chip = part[0] + swap(part[1], "c")
    low, high = chip[..., :half], chip[..., half:]
    low_two = low[:, 0] + swap(low[:, 1].astype(bf16), "y").astype(f32)
    high_two = high[0] + swap(high[1].astype(bf16), "x").astype(f32)
    low_one = low_two[0] + swap(low_two[1].astype(bf16), "x").astype(f32)
    high_one = high_two[0] + swap(high_two[1].astype(bf16), "y").astype(f32)
    return jnp.concatenate([low_one, high_one], axis=1)


def flip_pairs(mask, keep=None):
    pairs = []
    for z in range(4):
        for place in range(8):
            target = place ^ mask
            if keep is None or keep(z, place, target):
                pairs.append((z * 8 + place, z * 8 + target))
    return pairs


ALL_AXES = ("z", "x", "y", "c")
PLANE = ("x", "y", "c")


def plane_body(
    tokens, cotangent, context, lengths, keep, owners, master, moment_one, moment_two, gains, gain_one, gain_two
):
    cap, rows, _ = master.shape
    count, width = tokens.shape
    heads_here = HEADS // 8
    head_dim = width // HEADS
    scale = head_dim ** (-0.5)
    block = width // 8
    z = lax.axis_index("z")
    x = lax.axis_index("x")
    f = lax.axis_index("y") * 2 + lax.axis_index("c")

    n_tiles = owners.shape[0]
    rank = ranks_of(owners)
    shift_of = np.array(SHIFT, np.int32)
    row_of = np.array([t in ROW_TILES for t in range(n_tiles)])
    all_slots = jnp.arange(4 * cap).reshape(4, cap)
    holds = (owners * cap + rank)[None, None, :] == all_slots[:, :, None]
    used_at = jnp.any(holds, axis=2)
    tile_at = jnp.sum(jnp.where(holds, np.arange(n_tiles, dtype=np.int32), 0), axis=2)
    shift_at = jnp.sum(jnp.where(holds, shift_of, 0), axis=2)
    row_at = jnp.any(holds & row_of, axis=2)
    mine = (jnp.arange(4) == f)[:, None]

    def my(value):
        return jnp.sum(jnp.where(mine, value.astype(jnp.int32), 0), axis=0)

    my_used, my_tile, my_shift, my_row = my(used_at), my(tile_at), my(shift_at), my(row_at)

    to_x = np.arange(8) // 4
    to_f = np.arange(8) % 4
    column_table = 2 * ((to_f[None, :] + my_shift[:, None]) % 4) + to_x[None, :]
    half_cap = cap // 2
    received = []
    for first in (0, half_cap):
        sent = pack_columns(master, column_table[first : first + half_cap].reshape(-1), first, half_cap)
        got = lax.all_to_all(sent, PLANE, 0, 0, tiled=True)
        received.append(got.reshape(8 * half_cap, rows, block))

    def source_of(tile):
        if isinstance(tile, int):
            owner, slot = owners[tile], rank[tile]
        else:
            chosen = jnp.arange(n_tiles) == tile
            owner = jnp.sum(jnp.where(chosen, owners, 0))
            slot = jnp.sum(jnp.where(chosen, rank, 0))
        part = slot // half_cap
        return part, owner * half_cap + slot % half_cap

    def gather_columns(tiles, parts):
        which, index = [], []
        for tile in tiles:
            part, place = source_of(tile)
            for side in range(2):
                which.append(part)
                index.append(side * 4 * half_cap + place)
        local = pick_blocks(received[:parts], jnp.stack(which), jnp.stack(index), len(tiles))
        return lax.all_gather(local, "z", axis=0, tiled=True)

    w_qkv = gather_columns([0, 1, 2], 1)

    def my_block(tile):
        chosen = jnp.arange(n_tiles) == tile
        slot = jnp.sum(jnp.where(chosen, rank, 0))
        return lax.dynamic_index_in_dim(master, slot, 0, keepdims=False).astype(bf16)

    def owner_of(tile):
        return jnp.sum(jnp.where(jnp.arange(n_tiles) == tile, owners, 0))

    def take_rows(tile_for, keep_pair):
        found = None
        source = owner_of(tile_for(f)) ^ f
        for mask in range(4):
            got = my_block(tile_for(f ^ mask))
            if mask:
                got = lax.ppermute(got, ALL_AXES, flip_pairs(mask, keep_pair))
            found = got if found is None else jnp.where(source == mask, got, found)
        return found

    def self_or_cross(place):
        return jnp.where(place == z, 3, 9)

    def needs_outer(zz, place, target):
        return target % 4 in (zz, (zz + 2) % 4)

    outer = take_rows(self_or_cross, needs_outer)
    half_rows = rows // 2
    odd = z % 2
    to_pair = lax.dynamic_slice_in_dim(outer, (1 - odd) * half_rows, half_rows, 0)
    own_half = lax.dynamic_slice_in_dim(outer, odd * half_rows, half_rows, 0)
    pair_swap = [
        (zz * 8 + place, (zz ^ 1) * 8 + place)
        for zz in range(4)
        for place in range(8)
        if place % 4 in (zz, (zz + 2) % 4)
    ]
    from_pair = lax.ppermute(to_pair, ALL_AXES, pair_swap)
    has_outer = (f == z) | (f == (z + 2) % 4)
    outer_all = lax.all_gather(jnp.where(has_outer, own_half, from_pair), "z", axis=0, tiled=True)
    low_y = lax.axis_index("y") == 0
    w_self_out = jnp.where(low_y, outer_all[:rows], outer_all[rows:])
    w_cross_out = jnp.where(low_y, outer_all[rows:], outer_all[:rows])

    w_cross = gather_columns([4, 5, 7, 6, 8], 2)
    w_in = gather_columns([10 + (place - f) % 4 for place in range(4)], 2)
    w_out = lax.all_gather(take_rows(lambda place: 14 + (z - place) % 4, None), "z", axis=0, tiled=True)

    seg = segments(lengths[0], count)
    live = keep == 1
    code = seg * 2 + live.astype(jnp.int32)
    for axis in ("y", "x", "c"):
        code = jnp.concatenate([code, swap(code, axis)])
    seg_all = (code // 2).reshape(8, count)
    live_all = (code % 2 == 1).reshape(8, count)

    h0 = tokens.astype(f32)
    a_all = gather_rows(normalize(h0, gains[0]).astype(bf16))
    slots, ctx_len, ctx_width = context.shape
    ctx_all = gather_rows(context.reshape(slots * ctx_len, ctx_width))
    grad_out = cotangent.astype(f32) * live.astype(f32)[:, None]
    d_ff = gather_rows(grad_out.astype(bf16))

    def split(value):
        return value.reshape(8, -1, heads_here, head_dim)

    qkv = matmul(a_all, w_qkv).astype(bf16)
    query, keys, values = (split(qkv[:, n * block : (n + 1) * block]) for n in range(3))
    places = jnp.arange(count)
    allowed = (seg_all[:, :, None] == seg_all[:, None, :]) & (
        live_all[:, None, :] | (places[:, None] == places[None, :])
    )

    def probabilities(left, right, mask):
        scores = jnp.einsum("bqhd,bkhd->bhqk", left, right, preferred_element_type=f32) * scale
        scores = jnp.where(mask[:, None], scores, -1e30)
        expo = jnp.exp(scores - jnp.max(scores, axis=-1, keepdims=True))
        return expo / jnp.sum(expo, axis=-1, keepdims=True)

    def weighted(probs, right):
        return jnp.einsum("bhqk,bkhd->bqhd", probs, right, preferred_element_type=f32)

    def joined(value):
        return value.astype(bf16).reshape(-1, block)

    probs = probabilities(query, keys, allowed)
    probs_low = probs.astype(bf16)
    attended = joined(weighted(probs_low, values))
    h1 = h0 + scatter_rows(matmul(attended, w_self_out))
    b_all = gather_rows(normalize(h1, gains[1]).astype(bf16))

    w_cross_q = w_cross[:, :block]
    w_low = w_cross[:, block : 3 * block]
    w_high = w_cross[:, 3 * block :]
    ctx_low, ctx_high = ctx_all[:, :width], ctx_all[:, width:]
    ctx_kv = (matmul(ctx_low, w_low) + matmul(ctx_high, w_high)).astype(bf16)
    cross_q = split(matmul(b_all, w_cross_q).astype(bf16))
    cross_k, cross_v = split(ctx_kv[:, :block]), split(ctx_kv[:, block:])
    item = jnp.arange(slots * ctx_len) // ctx_len
    own_item = seg_all[:, :, None] == item[None, None, :]
    cross_p = probabilities(cross_q, cross_k, own_item)
    cross_low = cross_p.astype(bf16)
    cross_o = joined(weighted(cross_low, cross_v))
    h2 = h1 + scatter_rows(matmul(cross_o, w_cross_out))
    c_all = gather_rows(normalize(h2, gains[2]).astype(bf16))

    hidden = matmul(c_all, w_in)
    activated = gelu_tanh(hidden).astype(bf16)
    layer_out = (h2 + scatter_rows(matmul(activated, w_out))).astype(bf16)

    def sum_rows(value):
        return lax.psum_scatter(value.astype(bf16), "z", scatter_dimension=0, tiled=True)

    g_out = sum_rows(matmul_left(activated, d_ff))
    d_act = matmul_right(d_ff, w_out)
    d_hidden = jax.vjp(gelu_tanh, hidden)[1](d_act)[0].astype(bf16)
    g_in = sum_rows(matmul_left(c_all, d_hidden))
    part_two, gain_grad_two = jax.vjp(normalize, h2, gains[2])[1](scatter_rows(matmul_right(d_hidden, w_in)))
    dh2 = grad_out + part_two
    d_cross_out = gather_rows(dh2.astype(bf16))
    g_cross_out = matmul_left(cross_o, d_cross_out)

    def through(weights, d_out, left, right, probs, probs_low, values):
        d_mixed = split(matmul_right(d_out, weights).astype(bf16))
        d_probs = jnp.einsum("bqhd,bkhd->bhqk", d_mixed, values, preferred_element_type=f32)
        d_scores = (probs * (d_probs - jnp.sum(probs * d_probs, axis=-1, keepdims=True))).astype(bf16)
        d_left = joined(weighted(d_scores, right) * scale)
        d_right = joined(jnp.einsum("bhqk,bqhd->bkhd", d_scores, left, preferred_element_type=f32) * scale)
        d_values = joined(jnp.einsum("bhqk,bqhd->bkhd", probs_low, d_mixed, preferred_element_type=f32))
        return d_left, d_right, d_values

    d_cq, d_ck, d_cv = through(w_cross_out, d_cross_out, cross_q, cross_k, cross_p, cross_low, cross_v)
    d_ckv = jnp.concatenate([d_ck, d_cv], axis=1)
    g_cross = sum_rows(
        jnp.concatenate(
            [
                value.astype(bf16)
                for value in (matmul_left(b_all, d_cq), matmul_left(ctx_low, d_ckv), matmul_left(ctx_high, d_ckv))
            ],
            axis=1,
        )
    )
    part_one, gain_grad_one = jax.vjp(normalize, h1, gains[1])[1](scatter_rows(matmul_right(d_cq, w_cross_q)))
    dh1 = dh2 + part_one
    d_self_out = gather_rows(dh1.astype(bf16))
    g_self_out = matmul_left(attended, d_self_out)
    d_q, d_k, d_v = through(w_self_out, d_self_out, query, keys, probs, probs_low, values)
    d_qkv = jnp.concatenate([d_q, d_k, d_v], axis=1)
    g_qkv = sum_rows(matmul_left(a_all, d_qkv))
    g_outer = sum_rows(
        jnp.concatenate(
            [
                jnp.where(low_y, g_self_out, g_cross_out).astype(bf16),
                jnp.where(low_y, g_cross_out, g_self_out).astype(bf16),
            ],
            axis=0,
        )
    )
    part_zero, gain_grad_zero = jax.vjp(normalize, h0, gains[0])[1](scatter_rows(matmul_right(d_qkv, w_qkv)))
    grad_tokens = (dh1 + part_zero).astype(bf16)

    back_swap = [(target, source) for source, target in pair_swap]
    other_half = lax.ppermute(g_outer, ALL_AXES, back_swap)
    outer_grad = jnp.where(
        odd == 0,
        jnp.concatenate([g_outer, other_half], axis=0),
        jnp.concatenate([other_half, g_outer], axis=0),
    )

    def from_outer(zz, place, target):
        return place % 4 in (zz, (zz + 2) % 4)

    row_grads = []
    for value, keep_pair in ((g_out, None), (outer_grad, from_outer)):
        for mask in range(4):
            row_grads.append(lax.ppermute(value, ALL_AXES, flip_pairs(mask, keep_pair)) if mask else value)
    row_grads = jnp.stack(row_grads)

    group_of = np.array([0, 0, 0, 0, 1, 1, 1, 1, 1, 1, 2, 2, 2, 2, 0, 0, 0, 0], np.int32)
    column_of = np.array([0, 1, 2, 0, 0, 1, 3, 2, 4, 0, 0, 1, 2, 3, 0, 0, 0, 0], np.int32)
    group_at = jnp.sum(jnp.where(holds, group_of, 0), axis=2)
    column_at = jnp.sum(jnp.where(holds, column_of, 0), axis=2)
    column_at = jnp.where(group_at == 2, (column_at + f) % 4, column_at)
    sent = pack_gradients(
        [g_qkv, g_cross, g_in],
        jnp.tile(group_at.reshape(-1), 2),
        jnp.tile(column_at.reshape(-1), 2),
        rows,
        block,
        cap,
    )
    col_grads = lax.all_to_all(sent, PLANE, 0, 0, tiled=True).reshape(8 * cap, rows, block)
    place = np.arange(8)
    col_source = (place % 2)[None, :] * 4 + ((place // 2)[None, :] - my_shift[:, None]) % 4
    from_f = (z - my_shift) % 4
    row_source = (from_f ^ f) + jnp.where(my_tile < 10, 4, 0)
    new_w, new_m, new_v = adam_tiles(
        master,
        moment_one,
        moment_two,
        col_grads,
        row_grads,
        my_used,
        my_row,
        col_source.reshape(-1),
        row_source,
    )
    gain_grads = jnp.stack([gain_grad_zero, gain_grad_one, gain_grad_two])
    gain_total = lax.psum(gain_grads, ALL_AXES)
    new_g, new_gm, new_gv = adam_update(gains, gain_one, gain_two, gain_total, rate_gain, 0.0)
    return (layer_out, grad_tokens, new_w, new_m, new_v, new_g, new_gm, new_gv)


def whole_body(
    tokens, cotangent, context, lengths, keep, owners, master, moment_one, moment_two, gains, gain_one, gain_two
):
    cap = master.shape[0]
    n_tiles = owners.shape[0]
    slot_of = owners * cap + ranks_of(owners)
    owner_rows = lax.all_gather(master.astype(bf16), "fsdp", axis=0, tiled=True)
    tiles = [
        lax.all_gather(
            lax.dynamic_index_in_dim(owner_rows, slot_of[tile], 0, keepdims=False), "dp", axis=0, tiled=True
        )
        for tile in range(n_tiles)
    ]
    w_in = jnp.concatenate(tiles[10:14], axis=1)
    w_out = jnp.concatenate(tiles[14:18], axis=0)
    count, width = tokens.shape
    head_dim = width // HEADS
    scale = head_dim ** (-0.5)
    seg = segments(lengths[0], count)
    live = keep == 1
    places = jnp.arange(count)

    def split(value):
        return value.astype(bf16).reshape(-1, HEADS, head_dim)

    def joined(value):
        return value.astype(bf16).reshape(-1, width)

    def probabilities(left, right, mask):
        scores = jnp.einsum("qhd,khd->hqk", left, right, preferred_element_type=f32) * scale
        scores = jnp.where(mask[None], scores, -1e30)
        expo = jnp.exp(scores - jnp.max(scores, axis=-1, keepdims=True))
        return expo / jnp.sum(expo, axis=-1, keepdims=True)

    def weighted(probs, right):
        return jnp.einsum("hqk,khd->qhd", probs, right, preferred_element_type=f32)

    def through(weights, d_out, left, right, probs, values):
        d_mixed = split(matmul_right(d_out, weights))
        d_probs = jnp.einsum("qhd,khd->hqk", d_mixed, values, preferred_element_type=f32)
        d_scores = (probs * (d_probs - jnp.sum(probs * d_probs, axis=-1, keepdims=True))).astype(bf16)
        d_left = joined(weighted(d_scores, right) * scale)
        d_right = joined(jnp.einsum("hqk,qhd->khd", d_scores, left, preferred_element_type=f32) * scale)
        d_values = joined(jnp.einsum("hqk,qhd->khd", probs.astype(bf16), d_mixed, preferred_element_type=f32))
        return d_left, d_right, d_values

    h0 = tokens.astype(f32)
    a_in = normalize(h0, gains[0]).astype(bf16)
    query, keys, values = (split(matmul(a_in, tiles[n])) for n in range(3))
    allowed = (seg[:, None] == seg[None, :]) & (live[None, :] | (places[:, None] == places[None, :]))
    probs = probabilities(query, keys, allowed)
    attended = joined(weighted(probs.astype(bf16), values))
    h1 = h0 + matmul(attended, tiles[3])
    b_in = normalize(h1, gains[1]).astype(bf16)
    slots, ctx_len, ctx_width = context.shape
    ctx = context.reshape(slots * ctx_len, ctx_width)
    ctx_low, ctx_high = ctx[:, :width], ctx[:, width:]
    cross_q = split(matmul(b_in, tiles[4]))
    cross_k = split(matmul(ctx_low, tiles[5]) + matmul(ctx_high, tiles[6]))
    cross_v = split(matmul(ctx_low, tiles[7]) + matmul(ctx_high, tiles[8]))
    item = jnp.arange(slots * ctx_len) // ctx_len
    cross_p = probabilities(cross_q, cross_k, seg[:, None] == item[None, :])
    cross_o = joined(weighted(cross_p.astype(bf16), cross_v))
    h2 = h1 + matmul(cross_o, tiles[9])
    c_in = normalize(h2, gains[2]).astype(bf16)
    hidden = matmul(c_in, w_in)
    activated = gelu_tanh(hidden).astype(bf16)
    layer_out = (h2 + matmul(activated, w_out)).astype(bf16)
    grad_out = cotangent.astype(f32) * live.astype(f32)[:, None]
    d_ff = grad_out.astype(bf16)
    d_hidden = jax.vjp(gelu_tanh, hidden)[1](matmul_right(d_ff, w_out))[0].astype(bf16)
    part_two, gain_grad_two = jax.vjp(normalize, h2, gains[2])[1](matmul_right(d_hidden, w_in))
    dh2 = grad_out + part_two
    d_cross_out = dh2.astype(bf16)
    d_cq, d_ck, d_cv = through(tiles[9], d_cross_out, cross_q, cross_k, cross_p, cross_v)
    part_one, gain_grad_one = jax.vjp(normalize, h1, gains[1])[1](matmul_right(d_cq, tiles[4]))
    dh1 = dh2 + part_one
    d_self_out = dh1.astype(bf16)
    d_q, d_k, d_v = through(tiles[3], d_self_out, query, keys, probs, values)
    d_a = matmul_right(d_q, tiles[0]) + matmul_right(d_k, tiles[1]) + matmul_right(d_v, tiles[2])
    part_zero, gain_grad_zero = jax.vjp(normalize, h0, gains[0])[1](d_a)
    grad_tokens = (dh1 + part_zero).astype(bf16)
    pairs = [
        (a_in, d_q),
        (a_in, d_k),
        (a_in, d_v),
        (attended, d_self_out),
        (b_in, d_cq),
        (ctx_low, d_ck),
        (ctx_high, d_ck),
        (ctx_low, d_cv),
        (ctx_high, d_cv),
        (cross_o, d_cross_out),
    ]
    for part in range(4):
        pairs.append((c_in, d_hidden[:, part * width : (part + 1) * width]))
    for part in range(4):
        pairs.append((activated[:, part * width : (part + 1) * width], d_ff))
    total_slots = lax.axis_size("fsdp") * cap
    placed = jnp.zeros((total_slots,) + master.shape[1:], bf16)
    for tile, (left, right) in enumerate(pairs):
        term = lax.psum_scatter(
            matmul_left(left, right).astype(bf16), "dp", scatter_dimension=0, tiled=True
        )
        placed = lax.dynamic_update_index_in_dim(placed, term, slot_of[tile], 0)
    owned = lax.psum_scatter(placed, "fsdp", scatter_dimension=0, tiled=True).astype(f32)
    my_slots = lax.axis_index("fsdp") * cap + jnp.arange(cap)
    used = jnp.any(slot_of[None, :] == my_slots[:, None], axis=1)[:, None, None]
    updated = adam_update(master, moment_one, moment_two, owned, rate_matrix, decay_rate)
    new_w, new_m, new_v = (jnp.where(used, value, 0.0) for value in updated)
    gain_grads = jnp.stack([gain_grad_zero, gain_grad_one, gain_grad_two])
    gain_total = lax.psum(gain_grads, ("dp", "fsdp"))
    new_g, new_gm, new_gv = adam_update(gains, gain_one, gain_two, gain_total, rate_gain, 0.0)
    return (layer_out, grad_tokens, new_w, new_m, new_v, new_g, new_gm, new_gv)


def solution(mesh):
    planes = mesh.shape["dp"] == 8 and mesh.shape["fsdp"] == 4
    if planes:
        used = Mesh(mesh.devices.reshape(4, 2, 2, 2), ALL_AXES)
        dp, fsdp, body = ("z", "x"), ("y", "c"), plane_body
    else:
        used, dp, fsdp, body = mesh, ("dp",), ("fsdp",), whole_body
    rows = P(dp + fsdp, None)
    tiles = P(fsdp, dp, None)
    return jax.shard_map(
        body,
        mesh=used,
        in_specs=(rows, rows, P(dp + fsdp, None, None), rows, P(dp + fsdp), P(), tiles, tiles, tiles, P(), P(), P()),
        out_specs=(rows, rows, tiles, tiles, tiles, P(), P(), P()),
        check_vma=False,
    )
```

```python
import jax
import jax.numpy as jnp
import numpy as np
from jax import lax
from jax.experimental import pallas as pl
from jax.experimental.pallas import tpu as pltpu
from jax.sharding import Mesh
from jax.sharding import PartitionSpec as P

HEADS = 16
STEP = 10

norm_eps = 1e-06
beta_one = 0.9
beta_two = 0.95
adam_eps = 1e-08
decay_rate = 0.1
rate_matrix = 0.1
rate_gain = 0.8

f32 = jnp.float32
bf16 = jnp.bfloat16

SHIFT = (0, 0, 0, 0, 2, 2, 2, 2, 2, 2, 0, 1, 2, 3, 0, 1, 2, 3)
ROW_TILES = (3, 9, 14, 15, 16, 17)
VMEM_LIMIT = 48 << 20


def normalize(h, gain):
    scale = lax.rsqrt(jnp.mean(h * h, axis=-1, keepdims=True) + norm_eps)
    return h * scale * gain


def gelu_tanh(u):
    return 0.5 * u * (1.0 + jnp.tanh(0.7978845608028654 * (u + 0.044715 * u * u * u)))


def matmul(left, right):
    return jnp.dot(left, right, preferred_element_type=f32)


def matmul_left(left, right):
    return lax.dot_general(left, right, (((0,), (0,)), ((), ())), preferred_element_type=f32)


def matmul_right(left, right):
    return lax.dot_general(left, right, (((1,), (1,)), ((), ())), preferred_element_type=f32)


def ranks_of(owners):
    order = jnp.arange(owners.shape[0])
    same = (owners[:, None] == owners[None, :]) & (order[None, :] < order[:, None])
    return jnp.sum(same.astype(jnp.int32), axis=1)


def segments(lengths, count):
    places = jnp.arange(count)
    end = jnp.zeros((), jnp.int32)
    seg = jnp.zeros((count,), jnp.int32)
    for item in range(lengths.shape[0]):
        end = end + lengths[item]
        seg = seg + (places >= end).astype(jnp.int32)
    return seg


def adam_update(weight, first, second, grad, rate, decay):
    first = beta_one * first + (1.0 - beta_one) * grad
    second = beta_two * second + (1.0 - beta_two) * grad * grad
    fix_one = 1.0 / (1.0 - beta_one**STEP)
    fix_two = 1.0 / (1.0 - beta_two**STEP)
    move = first * fix_one / (jnp.sqrt(second * fix_two) + adam_eps)
    return (weight - rate * (move + decay * weight), first, second)


def pack_columns(master, table, first_slot, slots):
    _, rows, columns = master.shape
    width = columns // 8

    def kernel(table_ref, in_ref, out_ref):
        slot = pl.program_id(0)
        for rank in range(8):
            start = pl.multiple_of(table_ref[slot * 8 + rank] * width, width)
            out_ref[rank, 0] = in_ref[0, :, pl.ds(start, width)].astype(bf16)

    return pl.pallas_call(
        kernel,
        out_shape=jax.ShapeDtypeStruct((8, slots, rows, width), bf16),
        grid_spec=pltpu.PrefetchScalarGridSpec(
            num_scalar_prefetch=1,
            grid=(slots,),
            in_specs=[pl.BlockSpec((1, rows, columns), lambda k, t: (first_slot + k, 0, 0))],
            out_specs=pl.BlockSpec((8, 1, rows, width), lambda k, t: (0, k, 0, 0)),
        ),
        compiler_params=pltpu.CompilerParams(vmem_limit_bytes=VMEM_LIMIT),
        name="pack_columns",
    )(table, master)


def pick_blocks(sources, which, index, count):
    _, rows, width = sources[0].shape
    n_src = len(sources)

    def kernel(which_ref, index_ref, *refs):
        place = pl.program_id(0) * 2 + pl.program_id(1)
        out_ref = refs[n_src]
        for number in range(n_src):

            @pl.when(which_ref[place] == number)
            def _():
                out_ref[...] = refs[number][0]

    def spec(number):
        def at(n, half, which, index):
            place = n * 2 + half
            return (jnp.where(which[place] == number, index[place], 0), 0, 0)

        return pl.BlockSpec((1, rows, width), at)

    return pl.pallas_call(
        kernel,
        out_shape=jax.ShapeDtypeStruct((2 * rows, count * width), bf16),
        grid_spec=pltpu.PrefetchScalarGridSpec(
            num_scalar_prefetch=2,
            grid=(count, 2),
            in_specs=[spec(number) for number in range(n_src)],
            out_specs=pl.BlockSpec((rows, width), lambda n, half, which, index: (half, n)),
        ),
        compiler_params=pltpu.CompilerParams(vmem_limit_bytes=VMEM_LIMIT),
        name="pick_blocks",
    )(which, index, *sources)


def pack_gradients(groups, which, column, rows, width, slots):
    n_src = len(groups)

    def kernel(which_ref, column_ref, *refs):
        place = pl.program_id(0) * slots + pl.program_id(1)
        out_ref = refs[n_src]
        for number in range(n_src):

            @pl.when(which_ref[place] == number)
            def _():
                out_ref[0, 0] = refs[number][...]

    def spec(number):
        def at(rank, k, which, column):
            place = rank * slots + k
            return (rank // 4, jnp.where(which[place] == number, column[place], 0))

        return pl.BlockSpec((rows, width), at)

    return pl.pallas_call(
        kernel,
        out_shape=jax.ShapeDtypeStruct((8, slots, rows, width), bf16),
        grid_spec=pltpu.PrefetchScalarGridSpec(
            num_scalar_prefetch=2,
            grid=(8, slots),
            in_specs=[spec(number) for number in range(n_src)],
            out_specs=pl.BlockSpec((1, 1, rows, width), lambda rank, k, which, column: (rank, k, 0, 0)),
        ),
        compiler_params=pltpu.CompilerParams(vmem_limit_bytes=VMEM_LIMIT),
        name="pack_gradients",
    )(which, column, *groups)


def adam_tiles(master, one, two, columns_from, rows_from, visit, mode, column_place, row_place, hold, previous=None):
    _, rows, columns = master.shape
    width = columns // 8
    n_visit = visit.shape[0]
    n_col, n_row = len(columns_from), len(rows_from)
    kept = () if previous is None else tuple(previous)

    def kernel(visit_ref, mode_ref, cp_ref, rp_ref, hold_ref, *refs):
        w_ref, m_ref, v_ref = refs[:3]
        grads = refs[3 : 3 + n_col + n_row]
        outs = refs[3 + n_col + n_row + len(kept) :]
        how = mode_ref[pl.program_id(0)]

        @pl.when(how == 1)
        def _():
            for ref in outs:
                ref[...] = jnp.zeros_like(ref)

        for number, grad_ref in enumerate(grads):

            @pl.when(how == number + 2)
            def _():
                grad = grad_ref[0].astype(f32)
                results = adam_update(w_ref[0], m_ref[0], v_ref[0], grad, rate_matrix, decay_rate)
                for ref, value in zip(outs, results, strict=True):
                    ref[0] = value

    def block_of(n, b, hold):
        return jnp.where(hold[n] == 1, 7, b)

    state = pl.BlockSpec((1, rows, width), lambda n, b, vi, mo, cp, rp, ho: (vi[n], 0, block_of(n, b, ho)))

    def column_spec(number):
        def at(n, b, vi, mo, cp, rp, ho):
            return (jnp.where(mo[n] == number + 2, cp[n * 8 + block_of(n, b, ho)], 0), 0, 0)

        return pl.BlockSpec((1, rows, width), at)

    def row_spec(number):
        def at(n, b, vi, mo, cp, rp, ho):
            taken = mo[n] == number + 2
            return (jnp.where(taken, rp[n], 0), 0, jnp.where(taken, block_of(n, b, ho), 0))

        return pl.BlockSpec((1, rows, width), at)

    shape = jax.ShapeDtypeStruct(master.shape, f32)
    n_before = 5 + 3 + n_col + n_row
    return pl.pallas_call(
        kernel,
        out_shape=(shape, shape, shape),
        grid_spec=pltpu.PrefetchScalarGridSpec(
            num_scalar_prefetch=5,
            grid=(n_visit, 8),
            in_specs=[
                state,
                state,
                state,
                *(column_spec(number) for number in range(n_col)),
                *(row_spec(n_col + number) for number in range(n_row)),
                *(pl.BlockSpec(memory_space=pl.ANY) for _ in kept),
            ],
            out_specs=(state, state, state),
        ),
        input_output_aliases={n_before + n: n for n in range(len(kept))},
        compiler_params=pltpu.CompilerParams(vmem_limit_bytes=VMEM_LIMIT),
        name="adam_tiles",
    )(visit, mode, column_place, row_place, hold, master, one, two, *columns_from, *rows_from, *kept)


def after(value, *others):
    return lax.optimization_barrier((value, *others))[0]


def swap(value, axis):
    return lax.ppermute(value, axis, [(0, 1), (1, 0)])


def gather_rows(value):
    half = value.shape[0] // 2
    over_x = swap(value, "x")
    over_y = swap(value, "y")
    far_low = swap(over_y[:half], "x")
    far_high = swap(over_x[half:], "y")
    four = jnp.concatenate([value, over_y, over_x, far_low, far_high], axis=0)
    return jnp.concatenate([four, swap(four, "c")], axis=0)


def scatter_rows(part):
    rows, width = part.shape[0] // 8, part.shape[1]
    half = width // 2
    part = part.reshape(2, 2, 2, rows, width)
    chip = part[0] + swap(part[1], "c")
    low, high = chip[..., :half], chip[..., half:]
    low_two = low[:, 0] + swap(low[:, 1].astype(bf16), "y").astype(f32)
    high_two = high[0] + swap(high[1].astype(bf16), "x").astype(f32)
    low_one = low_two[0] + swap(low_two[1].astype(bf16), "x").astype(f32)
    high_one = high_two[0] + swap(high_two[1].astype(bf16), "y").astype(f32)
    return jnp.concatenate([low_one, high_one], axis=1)


def flip_pairs(mask, keep=None):
    pairs = []
    for z in range(4):
        for place in range(8):
            target = place ^ mask
            if keep is None or keep(z, place, target):
                pairs.append((z * 8 + place, z * 8 + target))
    return pairs


ALL_AXES = ("z", "x", "y", "c")
PLANE = ("x", "y", "c")


def plane_body(
    tokens, cotangent, context, lengths, keep, owners, master, moment_one, moment_two, gains, gain_one, gain_two
):
    cap, rows, _ = master.shape
    count, width = tokens.shape
    heads_here = HEADS // 8
    head_dim = width // HEADS
    scale = head_dim ** (-0.5)
    block = width // 8
    z = lax.axis_index("z")
    x = lax.axis_index("x")
    f = lax.axis_index("y") * 2 + lax.axis_index("c")

    n_tiles = owners.shape[0]
    rank = ranks_of(owners)
    shift_of = np.array(SHIFT, np.int32)
    row_of = np.array([t in ROW_TILES for t in range(n_tiles)])
    all_slots = jnp.arange(4 * cap).reshape(4, cap)
    holds = (owners * cap + rank)[None, None, :] == all_slots[:, :, None]
    used_at = jnp.any(holds, axis=2)
    tile_at = jnp.sum(jnp.where(holds, np.arange(n_tiles, dtype=np.int32), 0), axis=2)
    shift_at = jnp.sum(jnp.where(holds, shift_of, 0), axis=2)
    row_at = jnp.any(holds & row_of, axis=2)
    mine = (jnp.arange(4) == f)[:, None]

    def my(value):
        return jnp.sum(jnp.where(mine, value.astype(jnp.int32), 0), axis=0)

    my_used, my_tile, my_shift, my_row = my(used_at), my(tile_at), my(shift_at), my(row_at)

    to_x = np.arange(8) // 4
    to_f = np.arange(8) % 4
    column_table = 2 * ((to_f[None, :] + my_shift[:, None]) % 4) + to_x[None, :]
    half_cap = cap // 2

    def exchange_columns(first, weights):
        table = column_table[first : first + half_cap].reshape(-1)
        got = lax.all_to_all(pack_columns(weights, table, first, half_cap), PLANE, 0, 0, tiled=True)
        return got.reshape(8 * half_cap, rows, block)

    received = [exchange_columns(0, master)]

    def source_of(tile):
        if isinstance(tile, int):
            owner, slot = owners[tile], rank[tile]
        else:
            chosen = jnp.arange(n_tiles) == tile
            owner = jnp.sum(jnp.where(chosen, owners, 0))
            slot = jnp.sum(jnp.where(chosen, rank, 0))
        part = slot // half_cap
        return part, owner * half_cap + slot % half_cap

    def gather_columns(tiles, parts):
        which, index = [], []
        for tile in tiles:
            part, place = source_of(tile)
            for side in range(2):
                which.append(part)
                index.append(side * 4 * half_cap + place)
        local = pick_blocks(received[:parts], jnp.stack(which), jnp.stack(index), len(tiles))
        return lax.all_gather(local, "z", axis=0, tiled=True)

    w_qkv = gather_columns([0, 1, 2], 1)

    def my_block(tile):
        chosen = jnp.arange(n_tiles) == tile
        slot = jnp.sum(jnp.where(chosen, rank, 0))
        return lax.dynamic_index_in_dim(master, slot, 0, keepdims=False).astype(bf16)

    h0 = tokens.astype(f32)
    a_all = gather_rows(after(normalize(h0, gains[0]).astype(bf16), received[0]))

    def owner_of(tile):
        return jnp.sum(jnp.where(jnp.arange(n_tiles) == tile, owners, 0))

    def take_rows(tile_for, keep_pair, *earlier):
        found = None
        source = owner_of(tile_for(f)) ^ f
        for mask in range(4):
            got = after(my_block(tile_for(f ^ mask)), *earlier)
            if mask:
                got = lax.ppermute(got, ALL_AXES, flip_pairs(mask, keep_pair))
            found = got if found is None else jnp.where(source == mask, got, found)
        return found

    def self_or_cross(place):
        return jnp.where(place == z, 3, 9)

    def needs_outer(zz, place, target):
        return target % 4 in (zz, (zz + 2) % 4)

    outer = take_rows(self_or_cross, needs_outer, received[0])
    half_rows = rows // 2
    odd = z % 2
    to_pair = lax.dynamic_slice_in_dim(outer, (1 - odd) * half_rows, half_rows, 0)
    own_half = lax.dynamic_slice_in_dim(outer, odd * half_rows, half_rows, 0)
    pair_swap = [
        (zz * 8 + place, (zz ^ 1) * 8 + place)
        for zz in range(4)
        for place in range(8)
        if place % 4 in (zz, (zz + 2) % 4)
    ]
    from_pair = lax.ppermute(to_pair, ALL_AXES, pair_swap)
    has_outer = (f == z) | (f == (z + 2) % 4)
    outer_all = lax.all_gather(jnp.where(has_outer, own_half, from_pair), "z", axis=0, tiled=True)
    low_y = lax.axis_index("y") == 0
    w_self_out = jnp.where(low_y, outer_all[:rows], outer_all[rows:])
    w_cross_out = jnp.where(low_y, outer_all[rows:], outer_all[:rows])

    received.append(exchange_columns(half_cap, after(master, a_all, from_pair)))
    w_cross = gather_columns([4, 5, 7, 6, 8], 2)
    w_in = gather_columns([10 + (place - f) % 4 for place in range(4)], 2)
    slots, ctx_len, ctx_width = context.shape
    ctx_all = gather_rows(after(context.reshape(slots * ctx_len, ctx_width), received[1]))
    out_rows = take_rows(lambda place: 14 + (z - place) % 4, None, ctx_all)
    w_out = lax.all_gather(out_rows, "z", axis=0, tiled=True)

    seg = segments(lengths[0], count)
    live = keep == 1
    code = seg * 2 + live.astype(jnp.int32)
    for axis in ("y", "x", "c"):
        code = jnp.concatenate([code, swap(code, axis)])
    seg_all = (code // 2).reshape(8, count)
    live_all = (code % 2 == 1).reshape(8, count)

    grad_out = cotangent.astype(f32) * live.astype(f32)[:, None]
    d_ff = gather_rows(after(grad_out.astype(bf16), out_rows))

    def split(value):
        return value.reshape(8, -1, heads_here, head_dim)

    qkv = matmul(a_all, w_qkv).astype(bf16)
    query, keys, values = (split(qkv[:, n * block : (n + 1) * block]) for n in range(3))
    places = jnp.arange(count)
    allowed = (seg_all[:, :, None] == seg_all[:, None, :]) & (
        live_all[:, None, :] | (places[:, None] == places[None, :])
    )

    def probabilities(left, right, mask):
        scores = jnp.einsum("bqhd,bkhd->bhqk", left, right, preferred_element_type=f32) * scale
        scores = jnp.where(mask[:, None], scores, -1e30)
        expo = jnp.exp(scores - jnp.max(scores, axis=-1, keepdims=True))
        return expo / jnp.sum(expo, axis=-1, keepdims=True)

    def weighted(probs, right):
        return jnp.einsum("bhqk,bkhd->bqhd", probs, right, preferred_element_type=f32)

    def joined(value):
        return value.astype(bf16).reshape(-1, block)

    probs = probabilities(query, keys, allowed)
    probs_low = probs.astype(bf16)
    attended = joined(weighted(probs_low, values))
    h1 = h0 + scatter_rows(matmul(attended, w_self_out))
    b_all = gather_rows(normalize(h1, gains[1]).astype(bf16))

    w_cross_q = w_cross[:, :block]
    w_low = w_cross[:, block : 3 * block]
    w_high = w_cross[:, 3 * block :]
    ctx_low, ctx_high = ctx_all[:, :width], ctx_all[:, width:]
    ctx_kv = (matmul(ctx_low, w_low) + matmul(ctx_high, w_high)).astype(bf16)
    cross_q = split(matmul(b_all, w_cross_q).astype(bf16))
    cross_k, cross_v = split(ctx_kv[:, :block]), split(ctx_kv[:, block:])
    item = jnp.arange(slots * ctx_len) // ctx_len
    own_item = seg_all[:, :, None] == item[None, None, :]
    cross_p = probabilities(cross_q, cross_k, own_item)
    cross_low = cross_p.astype(bf16)
    cross_o = joined(weighted(cross_low, cross_v))
    h2 = h1 + scatter_rows(matmul(cross_o, w_cross_out))
    c_all = gather_rows(normalize(h2, gains[2]).astype(bf16))

    hidden = matmul(c_all, w_in)
    activated = gelu_tanh(hidden).astype(bf16)

    def sum_rows(value):
        return lax.psum_scatter(value, "z", scatter_dimension=0, tiled=True)

    t_out = matmul_left(activated, d_ff).astype(bf16)
    g_out = sum_rows(t_out)
    d_act = matmul_right(d_ff, after(w_out, t_out))
    layer_out = (h2 + scatter_rows(matmul(activated, w_out))).astype(bf16)
    d_hidden = jax.vjp(gelu_tanh, hidden)[1](d_act)[0].astype(bf16)
    t_in = matmul_left(c_all, d_hidden).astype(bf16)
    g_in = sum_rows(t_in)
    part_two, gain_grad_two = jax.vjp(normalize, h2, gains[2])[1](scatter_rows(matmul_right(d_hidden, w_in)))
    dh2 = grad_out + part_two
    d_cross_out = gather_rows(after(dh2.astype(bf16), t_in))
    g_cross_out = matmul_left(cross_o, d_cross_out)

    def through(weights, d_out, left, right, probs, probs_low, values):
        d_mixed = split(matmul_right(d_out, weights).astype(bf16))
        d_probs = jnp.einsum("bqhd,bkhd->bhqk", d_mixed, values, preferred_element_type=f32)
        d_scores = (probs * (d_probs - jnp.sum(probs * d_probs, axis=-1, keepdims=True))).astype(bf16)
        d_left = joined(weighted(d_scores, right) * scale)
        d_right = joined(jnp.einsum("bhqk,bqhd->bkhd", d_scores, left, preferred_element_type=f32) * scale)
        d_values = joined(jnp.einsum("bhqk,bqhd->bkhd", probs_low, d_mixed, preferred_element_type=f32))
        return d_left, d_right, d_values

    d_cq, d_ck, d_cv = through(w_cross_out, d_cross_out, cross_q, cross_k, cross_p, cross_low, cross_v)
    d_ckv = jnp.concatenate([d_ck, d_cv], axis=1)
    t_cross = jnp.concatenate(
        [
            value.astype(bf16)
            for value in (matmul_left(b_all, d_cq), matmul_left(ctx_low, d_ckv), matmul_left(ctx_high, d_ckv))
        ],
        axis=1,
    )
    g_cross = sum_rows(t_cross)
    part_one, gain_grad_one = jax.vjp(normalize, h1, gains[1])[1](scatter_rows(matmul_right(d_cq, w_cross_q)))
    dh1 = dh2 + part_one
    d_self_out = gather_rows(after(dh1.astype(bf16), t_cross))
    g_self_out = matmul_left(attended, d_self_out)
    g_outer = sum_rows(
        jnp.concatenate(
            [
                jnp.where(low_y, g_self_out, g_cross_out).astype(bf16),
                jnp.where(low_y, g_cross_out, g_self_out).astype(bf16),
            ],
            axis=0,
        )
    )
    d_q, d_k, d_v = through(w_self_out, d_self_out, query, keys, probs, probs_low, values)
    d_qkv = jnp.concatenate([d_q, d_k, d_v], axis=1)
    g_qkv = sum_rows(matmul_left(a_all, d_qkv).astype(bf16))
    part_zero, gain_grad_zero = jax.vjp(normalize, h0, gains[0])[1](scatter_rows(matmul_right(d_qkv, w_qkv)))
    grad_tokens = (dh1 + part_zero).astype(bf16)

    def to_owners(value, keep_pair):
        moved = [lax.ppermute(value, ALL_AXES, flip_pairs(mask, keep_pair)) for mask in range(1, 4)]
        return jnp.stack([value, *moved])

    out_grads = to_owners(g_out, None)
    group_of = np.array([0, 0, 0, 0, 0, 0, 0, 0, 0, 0, 1, 1, 1, 1, 0, 0, 0, 0], np.int32)
    column_of = np.array([0, 0, 0, 0, 0, 1, 3, 2, 4, 0, 0, 1, 2, 3, 0, 0, 0, 0], np.int32)
    group_at = jnp.sum(jnp.where(holds, group_of, 0), axis=2)
    column_at = jnp.sum(jnp.where(holds, column_of, 0), axis=2)
    column_at = jnp.where(group_at == 1, (column_at + f) % 4, column_at)
    sent = pack_gradients(
        [g_cross, g_in],
        jnp.tile(group_at.reshape(-1), 2),
        jnp.tile(column_at.reshape(-1), 2),
        rows,
        block,
        cap,
    )
    early_grads = lax.all_to_all(sent, PLANE, 0, 0, tiled=True).reshape(8 * cap, rows, block)
    place = np.arange(8)
    source = (place % 2)[None, :] * 4 + ((place // 2)[None, :] - my_shift[:, None]) % 4
    row_source = ((z - my_shift) % 4) ^ f
    late = (my_used == 1) & ((my_tile < 4) | (my_tile == 9))
    early_mode = jnp.where(my_used == 0, 1, jnp.where(late, 0, jnp.where(my_row == 1, 3, 2)))
    states = (master, moment_one, moment_two)
    slot = np.arange(cap, dtype=np.int32)
    early = adam_tiles(
        *states,
        [early_grads],
        [out_grads],
        slot,
        early_mode,
        (source * cap + slot[:, None]).reshape(-1),
        row_source,
        np.zeros(cap, np.int32),
    )

    back_swap = [(target, source) for source, target in pair_swap]
    other_half = lax.ppermute(g_outer, ALL_AXES, back_swap)
    outer_grad = jnp.where(
        odd == 0,
        jnp.concatenate([g_outer, other_half], axis=0),
        jnp.concatenate([other_half, g_outer], axis=0),
    )
    outer_grads = to_owners(outer_grad, lambda zz, place, target: place % 4 in (zz, (zz + 2) % 4))
    by_tile = jnp.swapaxes(g_qkv.reshape(2, rows, 3, block), 1, 2)
    sent = jnp.broadcast_to(by_tile[:, None], (2, 4, 3, rows, block)).reshape(8, 3, rows, block)
    late_grads = lax.all_to_all(sent, PLANE, 0, 0, tiled=True).reshape(8 * 3, rows, block)

    n_late = 5
    order = jnp.sum(jnp.where(slot[None, :] < slot[:, None], late.astype(jnp.int32)[None, :], 0), axis=1)
    count_late = jnp.sum(late.astype(jnp.int32))
    step = np.arange(n_late)
    wanted = jnp.minimum(step, jnp.maximum(count_late - 1, 0))
    here = late[None, :] & (order[None, :] == wanted[:, None])

    def at_step(value):
        return jnp.sum(jnp.where(here, value.astype(jnp.int32)[None, :], 0), axis=1)

    hold = (step >= jnp.maximum(count_late, 1)).astype(jnp.int32)
    tile = at_step(my_tile)
    some = count_late > 0
    visit = jnp.where(some, at_step(slot), 0)
    first_mode = jnp.where(early_mode[0] == 3, 4, early_mode[0])
    late_mode = jnp.where(at_step(my_row) == 1, 5, 3)
    mode = jnp.where(hold == 1, 0, jnp.where(some, late_mode, first_mode))
    late_place = (place % 2)[None, :] * 4 + (place // 2)[None, :]
    column_place = jnp.where(some, late_place * 3 + tile[:, None], (source * cap + slot[:, None])[0][None, :])
    new_w, new_m, new_v = adam_tiles(
        *states,
        [early_grads, late_grads],
        [out_grads, outer_grads],
        visit,
        mode,
        column_place.reshape(-1),
        jnp.where(some, at_step(row_source), row_source[0]),
        hold,
        early,
    )
    gain_grads = jnp.stack([gain_grad_zero, gain_grad_one, gain_grad_two])
    gain_total = lax.psum(gain_grads, ALL_AXES)
    new_g, new_gm, new_gv = adam_update(gains, gain_one, gain_two, gain_total, rate_gain, 0.0)
    return (layer_out, grad_tokens, new_w, new_m, new_v, new_g, new_gm, new_gv)


def whole_body(
    tokens, cotangent, context, lengths, keep, owners, master, moment_one, moment_two, gains, gain_one, gain_two
):
    cap = master.shape[0]
    n_tiles = owners.shape[0]
    slot_of = owners * cap + ranks_of(owners)
    owner_rows = lax.all_gather(master.astype(bf16), "fsdp", axis=0, tiled=True)
    tiles = [
        lax.all_gather(
            lax.dynamic_index_in_dim(owner_rows, slot_of[tile], 0, keepdims=False), "dp", axis=0, tiled=True
        )
        for tile in range(n_tiles)
    ]
    w_in = jnp.concatenate(tiles[10:14], axis=1)
    w_out = jnp.concatenate(tiles[14:18], axis=0)
    count, width = tokens.shape
    head_dim = width // HEADS
    scale = head_dim ** (-0.5)
    seg = segments(lengths[0], count)
    live = keep == 1
    places = jnp.arange(count)

    def split(value):
        return value.astype(bf16).reshape(-1, HEADS, head_dim)

    def joined(value):
        return value.astype(bf16).reshape(-1, width)

    def probabilities(left, right, mask):
        scores = jnp.einsum("qhd,khd->hqk", left, right, preferred_element_type=f32) * scale
        scores = jnp.where(mask[None], scores, -1e30)
        expo = jnp.exp(scores - jnp.max(scores, axis=-1, keepdims=True))
        return expo / jnp.sum(expo, axis=-1, keepdims=True)

    def weighted(probs, right):
        return jnp.einsum("hqk,khd->qhd", probs, right, preferred_element_type=f32)

    def through(weights, d_out, left, right, probs, values):
        d_mixed = split(matmul_right(d_out, weights))
        d_probs = jnp.einsum("qhd,khd->hqk", d_mixed, values, preferred_element_type=f32)
        d_scores = (probs * (d_probs - jnp.sum(probs * d_probs, axis=-1, keepdims=True))).astype(bf16)
        d_left = joined(weighted(d_scores, right) * scale)
        d_right = joined(jnp.einsum("hqk,qhd->khd", d_scores, left, preferred_element_type=f32) * scale)
        d_values = joined(jnp.einsum("hqk,qhd->khd", probs.astype(bf16), d_mixed, preferred_element_type=f32))
        return d_left, d_right, d_values

    h0 = tokens.astype(f32)
    a_in = normalize(h0, gains[0]).astype(bf16)
    query, keys, values = (split(matmul(a_in, tiles[n])) for n in range(3))
    allowed = (seg[:, None] == seg[None, :]) & (live[None, :] | (places[:, None] == places[None, :]))
    probs = probabilities(query, keys, allowed)
    attended = joined(weighted(probs.astype(bf16), values))
    h1 = h0 + matmul(attended, tiles[3])
    b_in = normalize(h1, gains[1]).astype(bf16)
    slots, ctx_len, ctx_width = context.shape
    ctx = context.reshape(slots * ctx_len, ctx_width)
    ctx_low, ctx_high = ctx[:, :width], ctx[:, width:]
    cross_q = split(matmul(b_in, tiles[4]))
    cross_k = split(matmul(ctx_low, tiles[5]) + matmul(ctx_high, tiles[6]))
    cross_v = split(matmul(ctx_low, tiles[7]) + matmul(ctx_high, tiles[8]))
    item = jnp.arange(slots * ctx_len) // ctx_len
    cross_p = probabilities(cross_q, cross_k, seg[:, None] == item[None, :])
    cross_o = joined(weighted(cross_p.astype(bf16), cross_v))
    h2 = h1 + matmul(cross_o, tiles[9])
    c_in = normalize(h2, gains[2]).astype(bf16)
    hidden = matmul(c_in, w_in)
    activated = gelu_tanh(hidden).astype(bf16)
    layer_out = (h2 + matmul(activated, w_out)).astype(bf16)
    grad_out = cotangent.astype(f32) * live.astype(f32)[:, None]
    d_ff = grad_out.astype(bf16)
    d_hidden = jax.vjp(gelu_tanh, hidden)[1](matmul_right(d_ff, w_out))[0].astype(bf16)
    part_two, gain_grad_two = jax.vjp(normalize, h2, gains[2])[1](matmul_right(d_hidden, w_in))
    dh2 = grad_out + part_two
    d_cross_out = dh2.astype(bf16)
    d_cq, d_ck, d_cv = through(tiles[9], d_cross_out, cross_q, cross_k, cross_p, cross_v)
    part_one, gain_grad_one = jax.vjp(normalize, h1, gains[1])[1](matmul_right(d_cq, tiles[4]))
    dh1 = dh2 + part_one
    d_self_out = dh1.astype(bf16)
    d_q, d_k, d_v = through(tiles[3], d_self_out, query, keys, probs, values)
    d_a = matmul_right(d_q, tiles[0]) + matmul_right(d_k, tiles[1]) + matmul_right(d_v, tiles[2])
    part_zero, gain_grad_zero = jax.vjp(normalize, h0, gains[0])[1](d_a)
    grad_tokens = (dh1 + part_zero).astype(bf16)
    pairs = [
        (a_in, d_q),
        (a_in, d_k),
        (a_in, d_v),
        (attended, d_self_out),
        (b_in, d_cq),
        (ctx_low, d_ck),
        (ctx_high, d_ck),
        (ctx_low, d_cv),
        (ctx_high, d_cv),
        (cross_o, d_cross_out),
    ]
    for part in range(4):
        pairs.append((c_in, d_hidden[:, part * width : (part + 1) * width]))
    for part in range(4):
        pairs.append((activated[:, part * width : (part + 1) * width], d_ff))
    total_slots = lax.axis_size("fsdp") * cap
    placed = jnp.zeros((total_slots,) + master.shape[1:], bf16)
    for tile, (left, right) in enumerate(pairs):
        term = lax.psum_scatter(
            matmul_left(left, right).astype(bf16), "dp", scatter_dimension=0, tiled=True
        )
        placed = lax.dynamic_update_index_in_dim(placed, term, slot_of[tile], 0)
    owned = lax.psum_scatter(placed, "fsdp", scatter_dimension=0, tiled=True).astype(f32)
    my_slots = lax.axis_index("fsdp") * cap + jnp.arange(cap)
    used = jnp.any(slot_of[None, :] == my_slots[:, None], axis=1)[:, None, None]
    updated = adam_update(master, moment_one, moment_two, owned, rate_matrix, decay_rate)
    new_w, new_m, new_v = (jnp.where(used, value, 0.0) for value in updated)
    gain_grads = jnp.stack([gain_grad_zero, gain_grad_one, gain_grad_two])
    gain_total = lax.psum(gain_grads, ("dp", "fsdp"))
    new_g, new_gm, new_gv = adam_update(gains, gain_one, gain_two, gain_total, rate_gain, 0.0)
    return (layer_out, grad_tokens, new_w, new_m, new_v, new_g, new_gm, new_gv)


def solution(mesh):
    planes = mesh.shape["dp"] == 8 and mesh.shape["fsdp"] == 4
    if planes:
        used = Mesh(mesh.devices.reshape(4, 2, 2, 2), ALL_AXES)
        dp, fsdp, body = ("z", "x"), ("y", "c"), plane_body
    else:
        used, dp, fsdp, body = mesh, ("dp",), ("fsdp",), whole_body
    rows = P(dp + fsdp, None)
    tiles = P(fsdp, dp, None)
    return jax.shard_map(
        body,
        mesh=used,
        in_specs=(rows, rows, P(dp + fsdp, None, None), rows, P(dp + fsdp), P(), tiles, tiles, tiles, P(), P(), P()),
        out_specs=(rows, rows, tiles, tiles, tiles, P(), P(), P()),
        check_vma=False,
    )
```

```python
import jax
import jax.numpy as jnp
import numpy as np
from jax import lax
from jax.experimental import pallas as pl
from jax.experimental.pallas import tpu as pltpu
from jax.sharding import Mesh
from jax.sharding import PartitionSpec as P

HEADS = 16
STEP = 10

norm_eps = 1e-06
beta_one = 0.9
beta_two = 0.95
adam_eps = 1e-08
decay_rate = 0.1
rate_matrix = 0.1
rate_gain = 0.8

f32 = jnp.float32
bf16 = jnp.bfloat16

SHIFT = (0, 0, 0, 0, 2, 2, 2, 2, 2, 2, 0, 1, 2, 3, 0, 1, 2, 3)
ROW_TILES = (3, 9, 14, 15, 16, 17)
VMEM_LIMIT = 48 << 20


def normalize(h, gain):
    scale = lax.rsqrt(jnp.mean(h * h, axis=-1, keepdims=True) + norm_eps)
    return h * scale * gain


def gelu_tanh(u):
    return 0.5 * u * (1.0 + jnp.tanh(0.7978845608028654 * (u + 0.044715 * u * u * u)))


def matmul(left, right):
    return jnp.dot(left, right, preferred_element_type=f32)


def matmul_left(left, right):
    return lax.dot_general(left, right, (((0,), (0,)), ((), ())), preferred_element_type=f32)


def matmul_right(left, right):
    return lax.dot_general(left, right, (((1,), (1,)), ((), ())), preferred_element_type=f32)


def ranks_of(owners):
    order = jnp.arange(owners.shape[0])
    same = (owners[:, None] == owners[None, :]) & (order[None, :] < order[:, None])
    return jnp.sum(same.astype(jnp.int32), axis=1)


def segments(lengths, count):
    places = jnp.arange(count)
    end = jnp.zeros((), jnp.int32)
    seg = jnp.zeros((count,), jnp.int32)
    for item in range(lengths.shape[0]):
        end = end + lengths[item]
        seg = seg + (places >= end).astype(jnp.int32)
    return seg


def adam_update(weight, first, second, grad, rate, decay):
    first = beta_one * first + (1.0 - beta_one) * grad
    second = beta_two * second + (1.0 - beta_two) * grad * grad
    fix_one = 1.0 / (1.0 - beta_one**STEP)
    fix_two = 1.0 / (1.0 - beta_two**STEP)
    move = first * fix_one / (jnp.sqrt(second * fix_two) + adam_eps)
    return (weight - rate * (move + decay * weight), first, second)


def pack_columns(master, table, first_slot, slots):
    _, rows, columns = master.shape
    width = columns // 8

    def kernel(table_ref, in_ref, out_ref):
        slot = pl.program_id(0)
        for rank in range(8):
            start = pl.multiple_of(table_ref[slot * 8 + rank] * width, width)
            out_ref[rank, 0] = in_ref[0, :, pl.ds(start, width)].astype(bf16)

    return pl.pallas_call(
        kernel,
        out_shape=jax.ShapeDtypeStruct((8, slots, rows, width), bf16),
        grid_spec=pltpu.PrefetchScalarGridSpec(
            num_scalar_prefetch=1,
            grid=(slots,),
            in_specs=[pl.BlockSpec((1, rows, columns), lambda k, t: (first_slot + k, 0, 0))],
            out_specs=pl.BlockSpec((8, 1, rows, width), lambda k, t: (0, k, 0, 0)),
        ),
        compiler_params=pltpu.CompilerParams(vmem_limit_bytes=VMEM_LIMIT),
        name="pack_columns",
    )(table, master)


def pick_blocks(sources, which, index, count):
    _, rows, width = sources[0].shape
    n_src = len(sources)

    def kernel(which_ref, index_ref, *refs):
        place = pl.program_id(0) * 2 + pl.program_id(1)
        out_ref = refs[n_src]
        for number in range(n_src):

            @pl.when(which_ref[place] == number)
            def _():
                out_ref[...] = refs[number][0]

    def spec(number):
        def at(n, half, which, index):
            place = n * 2 + half
            return (jnp.where(which[place] == number, index[place], 0), 0, 0)

        return pl.BlockSpec((1, rows, width), at)

    return pl.pallas_call(
        kernel,
        out_shape=jax.ShapeDtypeStruct((2 * rows, count * width), bf16),
        grid_spec=pltpu.PrefetchScalarGridSpec(
            num_scalar_prefetch=2,
            grid=(count, 2),
            in_specs=[spec(number) for number in range(n_src)],
            out_specs=pl.BlockSpec((rows, width), lambda n, half, which, index: (half, n)),
        ),
        compiler_params=pltpu.CompilerParams(vmem_limit_bytes=VMEM_LIMIT),
        name="pick_blocks",
    )(which, index, *sources)


def pack_gradients(groups, which, column, rows, width, slots):
    n_src = len(groups)

    def kernel(which_ref, column_ref, *refs):
        place = pl.program_id(0) * slots + pl.program_id(1)
        out_ref = refs[n_src]
        for number in range(n_src):

            @pl.when(which_ref[place] == number)
            def _():
                out_ref[0, 0] = refs[number][...]

    def spec(number):
        def at(rank, k, which, column):
            place = rank * slots + k
            return (rank // 4, jnp.where(which[place] == number, column[place], 0))

        return pl.BlockSpec((rows, width), at)

    return pl.pallas_call(
        kernel,
        out_shape=jax.ShapeDtypeStruct((8, slots, rows, width), bf16),
        grid_spec=pltpu.PrefetchScalarGridSpec(
            num_scalar_prefetch=2,
            grid=(8, slots),
            in_specs=[spec(number) for number in range(n_src)],
            out_specs=pl.BlockSpec((1, 1, rows, width), lambda rank, k, which, column: (rank, k, 0, 0)),
        ),
        compiler_params=pltpu.CompilerParams(vmem_limit_bytes=VMEM_LIMIT),
        name="pack_gradients",
    )(which, column, *groups)


def adam_tiles(master, one, two, columns_from, rows_from, visit, mode, column_place, row_place, hold, previous=None):
    _, rows, columns = master.shape
    width = columns // 8
    n_visit = visit.shape[0]
    n_col, n_row = len(columns_from), len(rows_from)
    kept = () if previous is None else tuple(previous)

    def kernel(visit_ref, mode_ref, cp_ref, rp_ref, hold_ref, *refs):
        w_ref, m_ref, v_ref = refs[:3]
        grads = refs[3 : 3 + n_col + n_row]
        outs = refs[3 + n_col + n_row + len(kept) :]
        how = mode_ref[pl.program_id(0)]

        @pl.when(how == 1)
        def _():
            for ref in outs:
                ref[...] = jnp.zeros_like(ref)

        for number, grad_ref in enumerate(grads):

            @pl.when(how == number + 2)
            def _():
                grad = grad_ref[0].astype(f32)
                results = adam_update(w_ref[0], m_ref[0], v_ref[0], grad, rate_matrix, decay_rate)
                for ref, value in zip(outs, results, strict=True):
                    ref[0] = value

    def block_of(n, b, hold):
        return jnp.where(hold[n] == 1, 7, b)

    state = pl.BlockSpec((1, rows, width), lambda n, b, vi, mo, cp, rp, ho: (vi[n], 0, block_of(n, b, ho)))

    def column_spec(number):
        def at(n, b, vi, mo, cp, rp, ho):
            return (jnp.where(mo[n] == number + 2, cp[n * 8 + block_of(n, b, ho)], 0), 0, 0)

        return pl.BlockSpec((1, rows, width), at)

    def row_spec(number):
        def at(n, b, vi, mo, cp, rp, ho):
            taken = mo[n] == number + 2
            return (jnp.where(taken, rp[n], 0), 0, jnp.where(taken, block_of(n, b, ho), 0))

        return pl.BlockSpec((1, rows, width), at)

    shape = jax.ShapeDtypeStruct(master.shape, f32)
    n_before = 5 + 3 + n_col + n_row
    return pl.pallas_call(
        kernel,
        out_shape=(shape, shape, shape),
        grid_spec=pltpu.PrefetchScalarGridSpec(
            num_scalar_prefetch=5,
            grid=(n_visit, 8),
            in_specs=[
                state,
                state,
                state,
                *(column_spec(number) for number in range(n_col)),
                *(row_spec(n_col + number) for number in range(n_row)),
                *(pl.BlockSpec(memory_space=pl.ANY) for _ in kept),
            ],
            out_specs=(state, state, state),
        ),
        input_output_aliases={n_before + n: n for n in range(len(kept))},
        compiler_params=pltpu.CompilerParams(vmem_limit_bytes=VMEM_LIMIT),
        name="adam_tiles",
    )(visit, mode, column_place, row_place, hold, master, one, two, *columns_from, *rows_from, *kept)


def after(value, *others):
    return lax.optimization_barrier((value, *others))[0]


def swap(value, axis):
    return lax.ppermute(value, axis, [(0, 1), (1, 0)])


def gather_rows(value):
    half = value.shape[0] // 2
    over_x = swap(value, "x")
    over_y = swap(value, "y")
    far_low = swap(over_y[:half], "x")
    far_high = swap(over_x[half:], "y")
    four = jnp.concatenate([value, over_y, over_x, far_low, far_high], axis=0)
    return jnp.concatenate([four, swap(four, "c")], axis=0)


def scatter_rows(part):
    rows, width = part.shape[0] // 8, part.shape[1]
    half = width // 2
    part = part.reshape(2, 2, 2, rows, width)
    chip = part[0] + swap(part[1], "c")
    low, high = chip[..., :half], chip[..., half:]
    low_two = low[:, 0] + swap(low[:, 1].astype(bf16), "y").astype(f32)
    high_two = high[0] + swap(high[1].astype(bf16), "x").astype(f32)
    low_one = low_two[0] + swap(low_two[1].astype(bf16), "x").astype(f32)
    high_one = high_two[0] + swap(high_two[1].astype(bf16), "y").astype(f32)
    return jnp.concatenate([low_one, high_one], axis=1)


def flip_pairs(mask, keep=None):
    pairs = []
    for z in range(4):
        for place in range(8):
            target = place ^ mask
            if keep is None or keep(z, place, target):
                pairs.append((z * 8 + place, z * 8 + target))
    return pairs


ALL_AXES = ("z", "x", "y", "c")
PLANE = ("x", "y", "c")


def plane_body(
    tokens, cotangent, context, lengths, keep, owners, master, moment_one, moment_two, gains, gain_one, gain_two
):
    cap, rows, _ = master.shape
    count, width = tokens.shape
    heads_here = HEADS // 8
    head_dim = width // HEADS
    scale = head_dim ** (-0.5)
    block = width // 8
    z = lax.axis_index("z")
    x = lax.axis_index("x")
    f = lax.axis_index("y") * 2 + lax.axis_index("c")

    n_tiles = owners.shape[0]
    rank = ranks_of(owners)
    shift_of = np.array(SHIFT, np.int32)
    row_of = np.array([t in ROW_TILES for t in range(n_tiles)])
    all_slots = jnp.arange(4 * cap).reshape(4, cap)
    holds = (owners * cap + rank)[None, None, :] == all_slots[:, :, None]
    used_at = jnp.any(holds, axis=2)
    tile_at = jnp.sum(jnp.where(holds, np.arange(n_tiles, dtype=np.int32), 0), axis=2)
    shift_at = jnp.sum(jnp.where(holds, shift_of, 0), axis=2)
    row_at = jnp.any(holds & row_of, axis=2)
    mine = (jnp.arange(4) == f)[:, None]

    def my(value):
        return jnp.sum(jnp.where(mine, value.astype(jnp.int32), 0), axis=0)

    my_used, my_tile, my_shift, my_row = my(used_at), my(tile_at), my(shift_at), my(row_at)

    to_x = np.arange(8) // 4
    to_f = np.arange(8) % 4
    column_table = 2 * ((to_f[None, :] + my_shift[:, None]) % 4) + to_x[None, :]
    half_cap = cap // 2

    def exchange_columns(first, weights):
        table = column_table[first : first + half_cap].reshape(-1)
        got = lax.all_to_all(pack_columns(weights, table, first, half_cap), PLANE, 0, 0, tiled=True)
        return got.reshape(8 * half_cap, rows, block)

    received = [exchange_columns(0, master)]
    received.append(exchange_columns(half_cap, after(master, received[0])))

    def source_of(tile):
        if isinstance(tile, int):
            owner, slot = owners[tile], rank[tile]
        else:
            chosen = jnp.arange(n_tiles) == tile
            owner = jnp.sum(jnp.where(chosen, owners, 0))
            slot = jnp.sum(jnp.where(chosen, rank, 0))
        part = slot // half_cap
        return part, owner * half_cap + slot % half_cap

    def gather_columns(tiles, parts):
        which, index = [], []
        for tile in tiles:
            part, place = source_of(tile)
            for side in range(2):
                which.append(part)
                index.append(side * 4 * half_cap + place)
        local = pick_blocks(received[:parts], jnp.stack(which), jnp.stack(index), len(tiles))
        return lax.all_gather(local, "z", axis=0, tiled=True)

    w_qkv = gather_columns([0, 1, 2], 1)

    def my_block(tile):
        chosen = jnp.arange(n_tiles) == tile
        slot = jnp.sum(jnp.where(chosen, rank, 0))
        return lax.dynamic_index_in_dim(master, slot, 0, keepdims=False).astype(bf16)

    h0 = tokens.astype(f32)
    a_all = gather_rows(after(normalize(h0, gains[0]).astype(bf16), received[1]))

    def owner_of(tile):
        return jnp.sum(jnp.where(jnp.arange(n_tiles) == tile, owners, 0))

    def take_rows(tile_for, keep_pair, *earlier):
        found = None
        source = owner_of(tile_for(f)) ^ f
        for mask in range(4):
            got = after(my_block(tile_for(f ^ mask)), *earlier)
            if mask:
                got = lax.ppermute(got, ALL_AXES, flip_pairs(mask, keep_pair))
            found = got if found is None else jnp.where(source == mask, got, found)
        return found

    def self_or_cross(place):
        return jnp.where(place == z, 3, 9)

    def needs_outer(zz, place, target):
        return target % 4 in (zz, (zz + 2) % 4)

    outer = take_rows(self_or_cross, needs_outer, received[0])
    half_rows = rows // 2
    odd = z % 2
    to_pair = lax.dynamic_slice_in_dim(outer, (1 - odd) * half_rows, half_rows, 0)
    own_half = lax.dynamic_slice_in_dim(outer, odd * half_rows, half_rows, 0)
    pair_swap = [
        (zz * 8 + place, (zz ^ 1) * 8 + place)
        for zz in range(4)
        for place in range(8)
        if place % 4 in (zz, (zz + 2) % 4)
    ]
    from_pair = lax.ppermute(to_pair, ALL_AXES, pair_swap)
    has_outer = (f == z) | (f == (z + 2) % 4)
    outer_all = lax.all_gather(jnp.where(has_outer, own_half, from_pair), "z", axis=0, tiled=True)
    low_y = lax.axis_index("y") == 0
    w_self_out = jnp.where(low_y, outer_all[:rows], outer_all[rows:])
    w_cross_out = jnp.where(low_y, outer_all[rows:], outer_all[:rows])

    w_cross = gather_columns([4, 5, 7, 6, 8], 2)
    w_in = gather_columns([10 + (place - f) % 4 for place in range(4)], 2)
    slots, ctx_len, ctx_width = context.shape
    ctx_all = gather_rows(after(context.reshape(slots * ctx_len, ctx_width), a_all))
    out_rows = take_rows(lambda place: 14 + (z - place) % 4, None, ctx_all)
    w_out = lax.all_gather(out_rows, "z", axis=0, tiled=True)

    seg = segments(lengths[0], count)
    live = keep == 1
    code = seg * 2 + live.astype(jnp.int32)
    for axis in ("y", "x", "c"):
        code = jnp.concatenate([code, swap(code, axis)])
    seg_all = (code // 2).reshape(8, count)
    live_all = (code % 2 == 1).reshape(8, count)

    grad_out = cotangent.astype(f32) * live.astype(f32)[:, None]
    d_ff = gather_rows(after(grad_out.astype(bf16), out_rows))

    def split(value):
        return value.reshape(8, -1, heads_here, head_dim)

    qkv = matmul(a_all, w_qkv).astype(bf16)
    query, keys, values = (split(qkv[:, n * block : (n + 1) * block]) for n in range(3))
    places = jnp.arange(count)
    allowed = (seg_all[:, :, None] == seg_all[:, None, :]) & (
        live_all[:, None, :] | (places[:, None] == places[None, :])
    )

    def probabilities(left, right, mask):
        scores = jnp.einsum("bqhd,bkhd->bhqk", left, right, preferred_element_type=f32) * scale
        scores = jnp.where(mask[:, None], scores, -1e30)
        expo = jnp.exp(scores - jnp.max(scores, axis=-1, keepdims=True))
        return expo / jnp.sum(expo, axis=-1, keepdims=True)

    def weighted(probs, right):
        return jnp.einsum("bhqk,bkhd->bqhd", probs, right, preferred_element_type=f32)

    def joined(value):
        return value.astype(bf16).reshape(-1, block)

    probs = probabilities(query, keys, allowed)
    probs_low = probs.astype(bf16)
    attended = joined(weighted(probs_low, values))
    h1 = h0 + scatter_rows(matmul(attended, w_self_out))
    b_all = gather_rows(after(normalize(h1, gains[1]).astype(bf16), w_cross))

    w_cross_q = w_cross[:, :block]
    w_low = w_cross[:, block : 3 * block]
    w_high = w_cross[:, 3 * block :]
    ctx_low, ctx_high = ctx_all[:, :width], ctx_all[:, width:]
    ctx_kv = (matmul(ctx_low, w_low) + matmul(ctx_high, w_high)).astype(bf16)
    cross_q = split(matmul(b_all, w_cross_q).astype(bf16))
    cross_k, cross_v = split(ctx_kv[:, :block]), split(ctx_kv[:, block:])
    item = jnp.arange(slots * ctx_len) // ctx_len
    own_item = seg_all[:, :, None] == item[None, None, :]
    cross_p = probabilities(cross_q, cross_k, own_item)
    cross_low = cross_p.astype(bf16)
    cross_o = joined(weighted(cross_low, cross_v))
    h2 = h1 + scatter_rows(matmul(after(cross_o, w_in), w_cross_out))
    c_all = gather_rows(normalize(h2, gains[2]).astype(bf16))

    hidden = matmul(after(c_all, w_out), w_in)
    activated = gelu_tanh(hidden).astype(bf16)

    def sum_rows(value):
        return lax.psum_scatter(value, "z", scatter_dimension=0, tiled=True)

    def to_owners(value, keep_pair):
        moved = [lax.ppermute(value, ALL_AXES, flip_pairs(mask, keep_pair)) for mask in range(1, 4)]
        return jnp.stack([value, *moved])

    t_out = matmul_left(activated, d_ff).astype(bf16)
    g_out = sum_rows(t_out)
    d_act = matmul_right(after(d_ff, t_out), w_out)
    layer_out = (h2 + scatter_rows(matmul(activated, w_out))).astype(bf16)
    d_hidden = jax.vjp(gelu_tanh, hidden)[1](d_act)[0].astype(bf16)
    t_in = matmul_left(c_all, d_hidden).astype(bf16)
    g_in = sum_rows(t_in)
    part_two, gain_grad_two = jax.vjp(normalize, h2, gains[2])[1](scatter_rows(matmul_right(d_hidden, w_in)))
    dh2 = grad_out + part_two
    d_cross_out = gather_rows(after(dh2.astype(bf16), t_in, g_out))
    out_grads = to_owners(g_out, None)
    g_cross_out = matmul_left(cross_o, d_cross_out)

    def through(weights, d_out, left, right, probs, probs_low, values):
        d_mixed = split(matmul_right(d_out, weights).astype(bf16))
        d_probs = jnp.einsum("bqhd,bkhd->bhqk", d_mixed, values, preferred_element_type=f32)
        d_scores = (probs * (d_probs - jnp.sum(probs * d_probs, axis=-1, keepdims=True))).astype(bf16)
        d_left = joined(weighted(d_scores, right) * scale)
        d_right = joined(jnp.einsum("bhqk,bqhd->bkhd", d_scores, left, preferred_element_type=f32) * scale)
        d_values = joined(jnp.einsum("bhqk,bqhd->bkhd", probs_low, d_mixed, preferred_element_type=f32))
        return d_left, d_right, d_values

    d_cq, d_ck, d_cv = through(w_cross_out, d_cross_out, cross_q, cross_k, cross_p, cross_low, cross_v)
    d_ckv = jnp.concatenate([d_ck, d_cv], axis=1)
    t_cross = jnp.concatenate(
        [
            value.astype(bf16)
            for value in (matmul_left(b_all, d_cq), matmul_left(ctx_low, d_ckv), matmul_left(ctx_high, d_ckv))
        ],
        axis=1,
    )
    g_cross = sum_rows(t_cross)
    part_one, gain_grad_one = jax.vjp(normalize, h1, gains[1])[1](scatter_rows(matmul_right(d_cq, w_cross_q)))
    dh1 = dh2 + part_one
    d_self_out = gather_rows(after(dh1.astype(bf16), t_cross, g_in, out_grads))
    g_self_out = matmul_left(attended, d_self_out)
    g_outer = sum_rows(
        jnp.concatenate(
            [
                jnp.where(low_y, g_self_out, g_cross_out).astype(bf16),
                jnp.where(low_y, g_cross_out, g_self_out).astype(bf16),
            ],
            axis=0,
        )
    )
    d_q, d_k, d_v = through(w_self_out, d_self_out, query, keys, probs, probs_low, values)
    d_qkv = jnp.concatenate([d_q, d_k, d_v], axis=1)
    g_qkv = sum_rows(matmul_left(a_all, d_qkv).astype(bf16))
    part_zero, gain_grad_zero = jax.vjp(normalize, h0, gains[0])[1](scatter_rows(matmul_right(d_qkv, w_qkv)))
    grad_tokens = (dh1 + part_zero).astype(bf16)

    gain_total = lax.psum(jnp.stack([gain_grad_zero, gain_grad_one, gain_grad_two]), ALL_AXES)

    group_of = np.array([0, 0, 0, 0, 0, 0, 0, 0, 0, 0, 1, 1, 1, 1, 0, 0, 0, 0], np.int32)
    column_of = np.array([0, 0, 0, 0, 0, 1, 3, 2, 4, 0, 0, 1, 2, 3, 0, 0, 0, 0], np.int32)
    group_at = jnp.sum(jnp.where(holds, group_of, 0), axis=2)
    column_at = jnp.sum(jnp.where(holds, column_of, 0), axis=2)
    column_at = jnp.where(group_at == 1, (column_at + f) % 4, column_at)
    sent = pack_gradients(
        [g_cross, g_in],
        jnp.tile(group_at.reshape(-1), 2),
        jnp.tile(column_at.reshape(-1), 2),
        rows,
        block,
        cap,
    )
    early_grads = lax.all_to_all(sent, PLANE, 0, 0, tiled=True).reshape(8 * cap, rows, block)
    place = np.arange(8)
    source = (place % 2)[None, :] * 4 + ((place // 2)[None, :] - my_shift[:, None]) % 4
    row_source = ((z - my_shift) % 4) ^ f
    late = (my_used == 1) & ((my_tile < 4) | (my_tile == 9))
    early_mode = jnp.where(my_used == 0, 1, jnp.where(late, 0, jnp.where(my_row == 1, 3, 2)))
    states = (master, moment_one, moment_two)
    slot = np.arange(cap, dtype=np.int32)
    early = adam_tiles(
        *states,
        [early_grads],
        [out_grads],
        slot,
        after(early_mode, gain_total),
        (source * cap + slot[:, None]).reshape(-1),
        row_source,
        np.zeros(cap, np.int32),
    )

    back_swap = [(target, source) for source, target in pair_swap]
    other_half = lax.ppermute(g_outer, ALL_AXES, back_swap)
    outer_grad = jnp.where(
        odd == 0,
        jnp.concatenate([g_outer, other_half], axis=0),
        jnp.concatenate([other_half, g_outer], axis=0),
    )
    outer_grads = to_owners(after(outer_grad, early_grads), lambda zz, place, target: place % 4 in (zz, (zz + 2) % 4))
    by_tile = jnp.swapaxes(g_qkv.reshape(2, rows, 3, block), 1, 2)
    sent = jnp.broadcast_to(by_tile[:, None], (2, 4, 3, rows, block)).reshape(8, 3, rows, block)
    late_grads = lax.all_to_all(sent, PLANE, 0, 0, tiled=True).reshape(8 * 3, rows, block)

    n_late = 5
    order = jnp.sum(jnp.where(slot[None, :] < slot[:, None], late.astype(jnp.int32)[None, :], 0), axis=1)
    count_late = jnp.sum(late.astype(jnp.int32))
    step = np.arange(n_late)
    wanted = jnp.minimum(step, jnp.maximum(count_late - 1, 0))
    here = late[None, :] & (order[None, :] == wanted[:, None])

    def at_step(value):
        return jnp.sum(jnp.where(here, value.astype(jnp.int32)[None, :], 0), axis=1)

    hold = (step >= jnp.maximum(count_late, 1)).astype(jnp.int32)
    tile = at_step(my_tile)
    some = count_late > 0
    visit = jnp.where(some, at_step(slot), 0)
    first_mode = jnp.where(early_mode[0] == 3, 4, early_mode[0])
    late_mode = jnp.where(at_step(my_row) == 1, 5, 3)
    mode = jnp.where(hold == 1, 0, jnp.where(some, late_mode, first_mode))
    late_place = (place % 2)[None, :] * 4 + (place // 2)[None, :]
    column_place = jnp.where(some, late_place * 3 + tile[:, None], (source * cap + slot[:, None])[0][None, :])
    new_w, new_m, new_v = adam_tiles(
        *states,
        [early_grads, late_grads],
        [out_grads, outer_grads],
        visit,
        mode,
        column_place.reshape(-1),
        jnp.where(some, at_step(row_source), row_source[0]),
        hold,
        early,
    )
    new_g, new_gm, new_gv = adam_update(gains, gain_one, gain_two, gain_total, rate_gain, 0.0)
    return (layer_out, grad_tokens, new_w, new_m, new_v, new_g, new_gm, new_gv)


def whole_body(
    tokens, cotangent, context, lengths, keep, owners, master, moment_one, moment_two, gains, gain_one, gain_two
):
    cap = master.shape[0]
    n_tiles = owners.shape[0]
    slot_of = owners * cap + ranks_of(owners)
    owner_rows = lax.all_gather(master.astype(bf16), "fsdp", axis=0, tiled=True)
    tiles = [
        lax.all_gather(
            lax.dynamic_index_in_dim(owner_rows, slot_of[tile], 0, keepdims=False), "dp", axis=0, tiled=True
        )
        for tile in range(n_tiles)
    ]
    w_in = jnp.concatenate(tiles[10:14], axis=1)
    w_out = jnp.concatenate(tiles[14:18], axis=0)
    count, width = tokens.shape
    head_dim = width // HEADS
    scale = head_dim ** (-0.5)
    seg = segments(lengths[0], count)
    live = keep == 1
    places = jnp.arange(count)

    def split(value):
        return value.astype(bf16).reshape(-1, HEADS, head_dim)

    def joined(value):
        return value.astype(bf16).reshape(-1, width)

    def probabilities(left, right, mask):
        scores = jnp.einsum("qhd,khd->hqk", left, right, preferred_element_type=f32) * scale
        scores = jnp.where(mask[None], scores, -1e30)
        expo = jnp.exp(scores - jnp.max(scores, axis=-1, keepdims=True))
        return expo / jnp.sum(expo, axis=-1, keepdims=True)

    def weighted(probs, right):
        return jnp.einsum("hqk,khd->qhd", probs, right, preferred_element_type=f32)

    def through(weights, d_out, left, right, probs, values):
        d_mixed = split(matmul_right(d_out, weights))
        d_probs = jnp.einsum("qhd,khd->hqk", d_mixed, values, preferred_element_type=f32)
        d_scores = (probs * (d_probs - jnp.sum(probs * d_probs, axis=-1, keepdims=True))).astype(bf16)
        d_left = joined(weighted(d_scores, right) * scale)
        d_right = joined(jnp.einsum("hqk,qhd->khd", d_scores, left, preferred_element_type=f32) * scale)
        d_values = joined(jnp.einsum("hqk,qhd->khd", probs.astype(bf16), d_mixed, preferred_element_type=f32))
        return d_left, d_right, d_values

    h0 = tokens.astype(f32)
    a_in = normalize(h0, gains[0]).astype(bf16)
    query, keys, values = (split(matmul(a_in, tiles[n])) for n in range(3))
    allowed = (seg[:, None] == seg[None, :]) & (live[None, :] | (places[:, None] == places[None, :]))
    probs = probabilities(query, keys, allowed)
    attended = joined(weighted(probs.astype(bf16), values))
    h1 = h0 + matmul(attended, tiles[3])
    b_in = normalize(h1, gains[1]).astype(bf16)
    slots, ctx_len, ctx_width = context.shape
    ctx = context.reshape(slots * ctx_len, ctx_width)
    ctx_low, ctx_high = ctx[:, :width], ctx[:, width:]
    cross_q = split(matmul(b_in, tiles[4]))
    cross_k = split(matmul(ctx_low, tiles[5]) + matmul(ctx_high, tiles[6]))
    cross_v = split(matmul(ctx_low, tiles[7]) + matmul(ctx_high, tiles[8]))
    item = jnp.arange(slots * ctx_len) // ctx_len
    cross_p = probabilities(cross_q, cross_k, seg[:, None] == item[None, :])
    cross_o = joined(weighted(cross_p.astype(bf16), cross_v))
    h2 = h1 + matmul(cross_o, tiles[9])
    c_in = normalize(h2, gains[2]).astype(bf16)
    hidden = matmul(c_in, w_in)
    activated = gelu_tanh(hidden).astype(bf16)
    layer_out = (h2 + matmul(activated, w_out)).astype(bf16)
    grad_out = cotangent.astype(f32) * live.astype(f32)[:, None]
    d_ff = grad_out.astype(bf16)
    d_hidden = jax.vjp(gelu_tanh, hidden)[1](matmul_right(d_ff, w_out))[0].astype(bf16)
    part_two, gain_grad_two = jax.vjp(normalize, h2, gains[2])[1](matmul_right(d_hidden, w_in))
    dh2 = grad_out + part_two
    d_cross_out = dh2.astype(bf16)
    d_cq, d_ck, d_cv = through(tiles[9], d_cross_out, cross_q, cross_k, cross_p, cross_v)
    part_one, gain_grad_one = jax.vjp(normalize, h1, gains[1])[1](matmul_right(d_cq, tiles[4]))
    dh1 = dh2 + part_one
    d_self_out = dh1.astype(bf16)
    d_q, d_k, d_v = through(tiles[3], d_self_out, query, keys, probs, values)
    d_a = matmul_right(d_q, tiles[0]) + matmul_right(d_k, tiles[1]) + matmul_right(d_v, tiles[2])
    part_zero, gain_grad_zero = jax.vjp(normalize, h0, gains[0])[1](d_a)
    grad_tokens = (dh1 + part_zero).astype(bf16)
    pairs = [
        (a_in, d_q),
        (a_in, d_k),
        (a_in, d_v),
        (attended, d_self_out),
        (b_in, d_cq),
        (ctx_low, d_ck),
        (ctx_high, d_ck),
        (ctx_low, d_cv),
        (ctx_high, d_cv),
        (cross_o, d_cross_out),
    ]
    for part in range(4):
        pairs.append((c_in, d_hidden[:, part * width : (part + 1) * width]))
    for part in range(4):
        pairs.append((activated[:, part * width : (part + 1) * width], d_ff))
    total_slots = lax.axis_size("fsdp") * cap
    placed = jnp.zeros((total_slots,) + master.shape[1:], bf16)
    for tile, (left, right) in enumerate(pairs):
        term = lax.psum_scatter(
            matmul_left(left, right).astype(bf16), "dp", scatter_dimension=0, tiled=True
        )
        placed = lax.dynamic_update_index_in_dim(placed, term, slot_of[tile], 0)
    owned = lax.psum_scatter(placed, "fsdp", scatter_dimension=0, tiled=True).astype(f32)
    my_slots = lax.axis_index("fsdp") * cap + jnp.arange(cap)
    used = jnp.any(slot_of[None, :] == my_slots[:, None], axis=1)[:, None, None]
    updated = adam_update(master, moment_one, moment_two, owned, rate_matrix, decay_rate)
    new_w, new_m, new_v = (jnp.where(used, value, 0.0) for value in updated)
    gain_grads = jnp.stack([gain_grad_zero, gain_grad_one, gain_grad_two])
    gain_total = lax.psum(gain_grads, ("dp", "fsdp"))
    new_g, new_gm, new_gv = adam_update(gains, gain_one, gain_two, gain_total, rate_gain, 0.0)
    return (layer_out, grad_tokens, new_w, new_m, new_v, new_g, new_gm, new_gv)


def solution(mesh):
    planes = mesh.shape["dp"] == 8 and mesh.shape["fsdp"] == 4
    if planes:
        used = Mesh(mesh.devices.reshape(4, 2, 2, 2), ALL_AXES)
        dp, fsdp, body = ("z", "x"), ("y", "c"), plane_body
    else:
        used, dp, fsdp, body = mesh, ("dp",), ("fsdp",), whole_body
    rows = P(dp + fsdp, None)
    tiles = P(fsdp, dp, None)
    return jax.shard_map(
        body,
        mesh=used,
        in_specs=(rows, rows, P(dp + fsdp, None, None), rows, P(dp + fsdp), P(), tiles, tiles, tiles, P(), P(), P()),
        out_specs=(rows, rows, tiles, tiles, tiles, P(), P(), P()),
        check_vma=False,
    )
```

```python
import jax
import jax.numpy as jnp
import numpy as np
from jax import lax
from jax.experimental import pallas as pl
from jax.experimental.pallas import tpu as pltpu
from jax.sharding import Mesh
from jax.sharding import PartitionSpec as P

HEADS = 16
STEP = 10

norm_eps = 1e-06
beta_one = 0.9
beta_two = 0.95
adam_eps = 1e-08
decay_rate = 0.1
rate_matrix = 0.1
rate_gain = 0.8

f32 = jnp.float32
bf16 = jnp.bfloat16

SHIFT = (0, 0, 0, 0, 2, 2, 2, 2, 2, 2, 0, 1, 2, 3, 0, 1, 2, 3)
ROW_TILES = (3, 9, 14, 15, 16, 17)
VMEM_LIMIT = 48 << 20


def normalize(h, gain):
    scale = lax.rsqrt(jnp.mean(h * h, axis=-1, keepdims=True) + norm_eps)
    return h * scale * gain


def gelu_tanh(u):
    return 0.5 * u * (1.0 + jnp.tanh(0.7978845608028654 * (u + 0.044715 * u * u * u)))


def matmul(left, right):
    return jnp.dot(left, right, preferred_element_type=f32)


def matmul_left(left, right):
    return lax.dot_general(left, right, (((0,), (0,)), ((), ())), preferred_element_type=f32)


def matmul_right(left, right):
    return lax.dot_general(left, right, (((1,), (1,)), ((), ())), preferred_element_type=f32)


def ranks_of(owners):
    order = jnp.arange(owners.shape[0])
    same = (owners[:, None] == owners[None, :]) & (order[None, :] < order[:, None])
    return jnp.sum(same.astype(jnp.int32), axis=1)


def segments(lengths, count):
    places = jnp.arange(count)
    end = jnp.zeros((), jnp.int32)
    seg = jnp.zeros((count,), jnp.int32)
    for item in range(lengths.shape[0]):
        end = end + lengths[item]
        seg = seg + (places >= end).astype(jnp.int32)
    return seg


def adam_update(weight, first, second, grad, rate, decay):
    first = beta_one * first + (1.0 - beta_one) * grad
    second = beta_two * second + (1.0 - beta_two) * grad * grad
    fix_one = 1.0 / (1.0 - beta_one**STEP)
    fix_two = 1.0 / (1.0 - beta_two**STEP)
    move = first * fix_one / (jnp.sqrt(second * fix_two) + adam_eps)
    return (weight - rate * (move + decay * weight), first, second)


def pack_columns(master, table, first_slot, slots):
    _, rows, columns = master.shape
    width = columns // 8

    def kernel(table_ref, in_ref, out_ref):
        slot = pl.program_id(0)
        for rank in range(8):
            start = pl.multiple_of(table_ref[slot * 8 + rank] * width, width)
            out_ref[rank, 0] = in_ref[0, :, pl.ds(start, width)].astype(bf16)

    return pl.pallas_call(
        kernel,
        out_shape=jax.ShapeDtypeStruct((8, slots, rows, width), bf16),
        grid_spec=pltpu.PrefetchScalarGridSpec(
            num_scalar_prefetch=1,
            grid=(slots,),
            in_specs=[pl.BlockSpec((1, rows, columns), lambda k, t: (first_slot + k, 0, 0))],
            out_specs=pl.BlockSpec((8, 1, rows, width), lambda k, t: (0, k, 0, 0)),
        ),
        compiler_params=pltpu.CompilerParams(vmem_limit_bytes=VMEM_LIMIT),
        name="pack_columns",
    )(table, master)


def pick_blocks(sources, which, index, count):
    _, rows, width = sources[0].shape
    n_src = len(sources)

    def kernel(which_ref, index_ref, *refs):
        place = pl.program_id(0) * 2 + pl.program_id(1)
        out_ref = refs[n_src]
        for number in range(n_src):

            @pl.when(which_ref[place] == number)
            def _():
                out_ref[...] = refs[number][0]

    def spec(number):
        def at(n, half, which, index):
            place = n * 2 + half
            return (jnp.where(which[place] == number, index[place], 0), 0, 0)

        return pl.BlockSpec((1, rows, width), at)

    return pl.pallas_call(
        kernel,
        out_shape=jax.ShapeDtypeStruct((2 * rows, count * width), bf16),
        grid_spec=pltpu.PrefetchScalarGridSpec(
            num_scalar_prefetch=2,
            grid=(count, 2),
            in_specs=[spec(number) for number in range(n_src)],
            out_specs=pl.BlockSpec((rows, width), lambda n, half, which, index: (half, n)),
        ),
        compiler_params=pltpu.CompilerParams(vmem_limit_bytes=VMEM_LIMIT),
        name="pick_blocks",
    )(which, index, *sources)


def pack_gradients(groups, which, column, rows, width, slots):
    n_src = len(groups)

    def kernel(which_ref, column_ref, *refs):
        place = pl.program_id(0) * slots + pl.program_id(1)
        out_ref = refs[n_src]
        for number in range(n_src):

            @pl.when(which_ref[place] == number)
            def _():
                out_ref[0, 0] = refs[number][...]

    def spec(number):
        def at(rank, k, which, column):
            place = rank * slots + k
            return (rank // 4, jnp.where(which[place] == number, column[place], 0))

        return pl.BlockSpec((rows, width), at)

    return pl.pallas_call(
        kernel,
        out_shape=jax.ShapeDtypeStruct((8, slots, rows, width), bf16),
        grid_spec=pltpu.PrefetchScalarGridSpec(
            num_scalar_prefetch=2,
            grid=(8, slots),
            in_specs=[spec(number) for number in range(n_src)],
            out_specs=pl.BlockSpec((1, 1, rows, width), lambda rank, k, which, column: (rank, k, 0, 0)),
        ),
        compiler_params=pltpu.CompilerParams(vmem_limit_bytes=VMEM_LIMIT),
        name="pack_gradients",
    )(which, column, *groups)


def adam_tiles(master, one, two, columns_from, rows_from, visit, mode, column_place, row_place, hold, previous=None):
    _, rows, columns = master.shape
    width = columns // 8
    n_visit = visit.shape[0]
    n_col, n_row = len(columns_from), len(rows_from)
    kept = () if previous is None else tuple(previous)

    def kernel(visit_ref, mode_ref, cp_ref, rp_ref, hold_ref, *refs):
        w_ref, m_ref, v_ref = refs[:3]
        grads = refs[3 : 3 + n_col + n_row]
        outs = refs[3 + n_col + n_row + len(kept) :]
        how = mode_ref[pl.program_id(0)]

        @pl.when(how == 1)
        def _():
            for ref in outs:
                ref[...] = jnp.zeros_like(ref)

        for number, grad_ref in enumerate(grads):

            @pl.when(how == number + 2)
            def _():
                grad = grad_ref[0].astype(f32)
                results = adam_update(w_ref[0], m_ref[0], v_ref[0], grad, rate_matrix, decay_rate)
                for ref, value in zip(outs, results, strict=True):
                    ref[0] = value

    def block_of(n, b, hold):
        return jnp.where(hold[n] == 1, 7, b)

    state = pl.BlockSpec((1, rows, width), lambda n, b, vi, mo, cp, rp, ho: (vi[n], 0, block_of(n, b, ho)))

    def column_spec(number):
        def at(n, b, vi, mo, cp, rp, ho):
            return (jnp.where(mo[n] == number + 2, cp[n * 8 + block_of(n, b, ho)], 0), 0, 0)

        return pl.BlockSpec((1, rows, width), at)

    def row_spec(number):
        def at(n, b, vi, mo, cp, rp, ho):
            taken = mo[n] == number + 2
            return (jnp.where(taken, rp[n], 0), 0, jnp.where(taken, block_of(n, b, ho), 0))

        return pl.BlockSpec((1, rows, width), at)

    shape = jax.ShapeDtypeStruct(master.shape, f32)
    n_before = 5 + 3 + n_col + n_row
    return pl.pallas_call(
        kernel,
        out_shape=(shape, shape, shape),
        grid_spec=pltpu.PrefetchScalarGridSpec(
            num_scalar_prefetch=5,
            grid=(n_visit, 8),
            in_specs=[
                state,
                state,
                state,
                *(column_spec(number) for number in range(n_col)),
                *(row_spec(n_col + number) for number in range(n_row)),
                *(pl.BlockSpec(memory_space=pl.ANY) for _ in kept),
            ],
            out_specs=(state, state, state),
        ),
        input_output_aliases={n_before + n: n for n in range(len(kept))},
        compiler_params=pltpu.CompilerParams(vmem_limit_bytes=VMEM_LIMIT),
        name="adam_tiles",
    )(visit, mode, column_place, row_place, hold, master, one, two, *columns_from, *rows_from, *kept)


def after(value, *others):
    return lax.optimization_barrier((value, *others))[0]


def swap(value, axis):
    return lax.ppermute(value, axis, [(0, 1), (1, 0)])


def gather_rows(value):
    half = value.shape[0] // 2
    over_x = swap(value, "x")
    over_y = swap(value, "y")
    far_low = swap(over_y[:half], "x")
    far_high = swap(over_x[half:], "y")
    four = jnp.concatenate([value, over_y, over_x, far_low, far_high], axis=0)
    return jnp.concatenate([four, swap(four, "c")], axis=0)


def scatter_rows(part):
    rows, width = part.shape[0] // 8, part.shape[1]
    half = width // 2
    part = part.reshape(2, 2, 2, rows, width)
    chip = part[0] + swap(part[1], "c")
    low, high = chip[..., :half], chip[..., half:]
    low_two = low[:, 0] + swap(low[:, 1].astype(bf16), "y").astype(f32)
    high_two = high[0] + swap(high[1].astype(bf16), "x").astype(f32)
    low_one = low_two[0] + swap(low_two[1].astype(bf16), "x").astype(f32)
    high_one = high_two[0] + swap(high_two[1].astype(bf16), "y").astype(f32)
    return jnp.concatenate([low_one, high_one], axis=1)


def sum_everywhere(value):
    for axis in ("c", "y", "x"):
        value = value + swap(value, axis)
    for step in (1, 2):
        value = value + lax.ppermute(value, "z", [(z, z ^ step) for z in range(4)])
    return value


def flip_pairs(mask, keep=None):
    pairs = []
    for z in range(4):
        for place in range(8):
            target = place ^ mask
            if keep is None or keep(z, place, target):
                pairs.append((z * 8 + place, z * 8 + target))
    return pairs


ALL_AXES = ("z", "x", "y", "c")
PLANE = ("x", "y", "c")


def plane_body(
    tokens, cotangent, context, lengths, keep, owners, master, moment_one, moment_two, gains, gain_one, gain_two
):
    cap, rows, _ = master.shape
    count, width = tokens.shape
    heads_here = HEADS // 8
    head_dim = width // HEADS
    scale = head_dim ** (-0.5)
    block = width // 8
    z = lax.axis_index("z")
    x = lax.axis_index("x")
    f = lax.axis_index("y") * 2 + lax.axis_index("c")

    n_tiles = owners.shape[0]
    rank = ranks_of(owners)
    shift_of = np.array(SHIFT, np.int32)
    row_of = np.array([t in ROW_TILES for t in range(n_tiles)])
    all_slots = jnp.arange(4 * cap).reshape(4, cap)
    holds = (owners * cap + rank)[None, None, :] == all_slots[:, :, None]
    used_at = jnp.any(holds, axis=2)
    tile_at = jnp.sum(jnp.where(holds, np.arange(n_tiles, dtype=np.int32), 0), axis=2)
    shift_at = jnp.sum(jnp.where(holds, shift_of, 0), axis=2)
    row_at = jnp.any(holds & row_of, axis=2)
    mine = (jnp.arange(4) == f)[:, None]

    def my(value):
        return jnp.sum(jnp.where(mine, value.astype(jnp.int32), 0), axis=0)

    my_used, my_tile, my_shift, my_row = my(used_at), my(tile_at), my(shift_at), my(row_at)

    to_x = np.arange(8) // 4
    to_f = np.arange(8) % 4
    column_table = 2 * ((to_f[None, :] + my_shift[:, None]) % 4) + to_x[None, :]
    half_cap = cap // 2
    place = np.arange(4)

    def of_tiles(tiles, values):
        chosen = tiles[:, None] == np.arange(n_tiles)[None, :]
        return jnp.sum(jnp.where(chosen, values[None, :], 0), axis=1)

    column_tiles = jnp.concatenate([np.array([0, 1, 2, 4, 5, 7, 6, 8], np.int32), 10 + (place - f) % 4])
    column_part = jnp.repeat(of_tiles(column_tiles, rank // half_cap), 2)
    column_place = of_tiles(column_tiles, owners * half_cap + rank % half_cap)
    column_place = (column_place[:, None] + np.array([0, 4 * half_cap])[None, :]).reshape(-1)
    other_f = f ^ place
    outer_tiles = jnp.where(other_f == z, 3, 9)
    out_tiles = 14 + (z - other_f) % 4
    row_slots = of_tiles(jnp.concatenate([outer_tiles, out_tiles]), rank)
    row_owners = of_tiles(jnp.stack([outer_tiles[0], out_tiles[0]]), owners)

    def exchange_columns(first, weights):
        table = column_table[first : first + half_cap].reshape(-1)
        got = lax.all_to_all(pack_columns(weights, table, first, half_cap), PLANE, 0, 0, tiled=True)
        return got.reshape(8 * half_cap, rows, block)

    received = [exchange_columns(0, after(master, column_part, column_place, row_slots, row_owners))]
    received.append(exchange_columns(half_cap, after(master, received[0])))

    def columns_here(first, count, parts):
        chosen = slice(2 * first, 2 * (first + count))
        return pick_blocks(received[:parts], column_part[chosen], column_place[chosen], count)

    def gather_z(value):
        return lax.all_gather(value, "z", axis=0, tiled=True)

    w_qkv = gather_z(columns_here(0, 3, 1))

    def my_block(slot):
        return lax.dynamic_index_in_dim(master, slot, 0, keepdims=False).astype(bf16)

    h0 = tokens.astype(f32)
    a_all = gather_rows(after(normalize(h0, gains[0]).astype(bf16), received[1]))

    def take_rows(kind, keep_pair, *earlier):
        found = None
        source = row_owners[kind] ^ f
        for mask in range(4):
            got = after(my_block(row_slots[4 * kind + mask]), *earlier)
            if mask:
                got = lax.ppermute(got, ALL_AXES, flip_pairs(mask, keep_pair))
            found = got if found is None else jnp.where(source == mask, got, found)
        return found

    def needs_outer(zz, place, target):
        return target % 4 in (zz, (zz + 2) % 4)

    outer = take_rows(0, needs_outer, received[0])
    half_rows = rows // 2
    odd = z % 2
    to_pair = lax.dynamic_slice_in_dim(outer, (1 - odd) * half_rows, half_rows, 0)
    own_half = lax.dynamic_slice_in_dim(outer, odd * half_rows, half_rows, 0)
    pair_swap = [
        (zz * 8 + place, (zz ^ 1) * 8 + place)
        for zz in range(4)
        for place in range(8)
        if place % 4 in (zz, (zz + 2) % 4)
    ]
    from_pair = lax.ppermute(to_pair, ALL_AXES, pair_swap)
    has_outer = (f == z) | (f == (z + 2) % 4)
    outer_all = lax.all_gather(jnp.where(has_outer, own_half, from_pair), "z", axis=0, tiled=True)
    low_y = lax.axis_index("y") == 0
    w_self_out = jnp.where(low_y, outer_all[:rows], outer_all[rows:])
    w_cross_out = jnp.where(low_y, outer_all[rows:], outer_all[:rows])

    w_cross = gather_z(columns_here(3, 5, 2))
    w_in = gather_z(columns_here(8, 4, 2))
    slots, ctx_len, ctx_width = context.shape
    ctx_all = gather_rows(after(context.reshape(slots * ctx_len, ctx_width), a_all))
    out_rows = take_rows(1, None, ctx_all)
    w_out = gather_z(out_rows)

    seg = segments(lengths[0], count)
    live = keep == 1
    code = seg * 2 + live.astype(jnp.int32)
    for axis in ("y", "x", "c"):
        code = jnp.concatenate([code, swap(code, axis)])
    seg_all = (code // 2).reshape(8, count)
    live_all = (code % 2 == 1).reshape(8, count)

    grad_out = cotangent.astype(f32) * live.astype(f32)[:, None]
    d_ff = gather_rows(after(grad_out.astype(bf16), out_rows))

    present = owners[0] >= 0

    def gather_step(value):
        shape = jax.ShapeDtypeStruct((8 * value.shape[0], value.shape[1]), value.dtype)
        return lax.cond(present, gather_rows, lambda _: jnp.zeros(shape.shape, shape.dtype), value)

    def scatter_step(part):
        shape = (part.shape[0] // 8, part.shape[1])
        return lax.cond(present, scatter_rows, lambda _: jnp.zeros(shape, f32), part)

    def split(value):
        return value.reshape(8, -1, heads_here, head_dim)

    qkv = matmul(a_all, w_qkv)
    qkv = qkv.astype(bf16)
    query, keys, values = (split(qkv[:, n * block : (n + 1) * block]) for n in range(3))
    places = jnp.arange(count)
    allowed = (seg_all[:, :, None] == seg_all[:, None, :]) & (
        live_all[:, None, :] | (places[:, None] == places[None, :])
    )

    def probabilities(left, right, mask):
        scores = jnp.einsum("bqhd,bkhd->bhqk", left, right, preferred_element_type=f32) * scale
        scores = jnp.where(mask[:, None], scores, -1e30)
        expo = jnp.exp(scores - jnp.max(scores, axis=-1, keepdims=True))
        return expo / jnp.sum(expo, axis=-1, keepdims=True)

    def weighted(probs, right):
        return jnp.einsum("bhqk,bkhd->bqhd", probs, right, preferred_element_type=f32)

    def joined(value):
        return value.astype(bf16).reshape(-1, block)

    probs = probabilities(query, keys, allowed)
    probs_low = probs.astype(bf16)
    attended = joined(weighted(probs_low, values))
    part = matmul(attended, w_self_out)
    h1 = h0 + scatter_step(part)
    b_all = gather_step(normalize(h1, gains[1]).astype(bf16))

    w_cross_q = w_cross[:, :block]
    w_low = w_cross[:, block : 3 * block]
    w_high = w_cross[:, 3 * block :]
    ctx_low, ctx_high = ctx_all[:, :width], ctx_all[:, width:]
    ctx_kv = (matmul(ctx_low, w_low) + matmul(ctx_high, w_high)).astype(bf16)
    cross_q = matmul(b_all, w_cross_q)
    cross_q = split(cross_q.astype(bf16))
    cross_k, cross_v = split(ctx_kv[:, :block]), split(ctx_kv[:, block:])
    item = jnp.arange(slots * ctx_len) // ctx_len
    own_item = seg_all[:, :, None] == item[None, None, :]
    cross_p = probabilities(cross_q, cross_k, own_item)
    cross_low = cross_p.astype(bf16)
    cross_o = joined(weighted(cross_low, cross_v))
    h2 = h1 + scatter_step(matmul(cross_o, w_cross_out))
    c_all = gather_step(normalize(h2, gains[2]).astype(bf16))

    hidden = matmul(c_all, w_in)
    activated = gelu_tanh(hidden).astype(bf16)

    def sum_rows(value):
        return lax.psum_scatter(value, "z", scatter_dimension=0, tiled=True)

    def to_owners(value, keep_pair):
        moved = [lax.ppermute(value, ALL_AXES, flip_pairs(mask, keep_pair)) for mask in range(1, 4)]
        return jnp.stack([value, *moved])

    t_out = matmul_left(activated, d_ff).astype(bf16)
    g_out = sum_rows(t_out)
    d_act = matmul_right(after(d_ff, t_out), w_out)
    layer_out = (h2 + scatter_step(matmul(activated, w_out))).astype(bf16)
    d_hidden = jax.vjp(gelu_tanh, hidden)[1](d_act)[0].astype(bf16)
    t_in = matmul_left(c_all, d_hidden).astype(bf16)
    g_in = sum_rows(t_in)
    part = matmul_right(d_hidden, w_in)
    part_two, gain_grad_two = jax.vjp(normalize, h2, gains[2])[1](scatter_step(part))
    dh2 = grad_out + part_two
    d_cross_out = gather_step(after(dh2.astype(bf16), t_in))
    out_grads = to_owners(g_out, None)
    g_cross_out = matmul_left(cross_o, d_cross_out)

    def through(d_mixed, left, right, probs, probs_low, values):
        d_mixed = split(d_mixed.astype(bf16))
        d_probs = jnp.einsum("bqhd,bkhd->bhqk", d_mixed, values, preferred_element_type=f32)
        d_scores = (probs * (d_probs - jnp.sum(probs * d_probs, axis=-1, keepdims=True))).astype(bf16)
        d_left = joined(weighted(d_scores, right) * scale)
        d_right = joined(jnp.einsum("bhqk,bqhd->bkhd", d_scores, left, preferred_element_type=f32) * scale)
        d_values = joined(jnp.einsum("bhqk,bqhd->bkhd", probs_low, d_mixed, preferred_element_type=f32))
        return d_left, d_right, d_values

    d_cq, d_ck, d_cv = through(
        matmul_right(d_cross_out, w_cross_out), cross_q, cross_k, cross_p, cross_low, cross_v
    )
    d_ckv = jnp.concatenate([d_ck, d_cv], axis=1)
    t_cross = jnp.concatenate(
        [
            value.astype(bf16)
            for value in (matmul_left(b_all, d_cq), matmul_left(ctx_low, d_ckv), matmul_left(ctx_high, d_ckv))
        ],
        axis=1,
    )
    g_cross = sum_rows(t_cross)
    part = matmul_right(d_cq, w_cross_q)
    part_one, gain_grad_one = jax.vjp(normalize, h1, gains[1])[1](scatter_step(part))
    dh1 = dh2 + part_one
    d_self_out = gather_step(after(dh1.astype(bf16), t_cross, out_grads))
    g_self_out = matmul_left(attended, d_self_out)
    g_outer = sum_rows(
        jnp.concatenate(
            [
                jnp.where(low_y, g_self_out, g_cross_out).astype(bf16),
                jnp.where(low_y, g_cross_out, g_self_out).astype(bf16),
            ],
            axis=0,
        )
    )
    d_mixed = matmul_right(d_self_out, w_self_out)
    d_q, d_k, d_v = through(d_mixed, query, keys, probs, probs_low, values)
    d_qkv = jnp.concatenate([d_q, d_k, d_v], axis=1)
    g_qkv = sum_rows(matmul_left(a_all, d_qkv).astype(bf16))
    group_of = np.array([0, 0, 0, 0, 0, 0, 0, 0, 0, 0, 1, 1, 1, 1, 0, 0, 0, 0], np.int32)
    column_of = np.array([0, 0, 0, 0, 0, 1, 3, 2, 4, 0, 0, 1, 2, 3, 0, 0, 0, 0], np.int32)
    group_at = jnp.sum(jnp.where(holds, group_of, 0), axis=2)
    column_at = jnp.sum(jnp.where(holds, column_of, 0), axis=2)
    column_at = jnp.where(group_at == 1, (column_at + f) % 4, column_at)
    sent = pack_gradients(
        [g_cross, g_in],
        jnp.tile(group_at.reshape(-1), 2),
        jnp.tile(column_at.reshape(-1), 2),
        rows,
        block,
        cap,
    )
    early_grads = lax.all_to_all(sent, PLANE, 0, 0, tiled=True).reshape(8 * cap, rows, block)
    part = matmul_right(after(d_qkv, sent), w_qkv)
    part_zero, gain_grad_zero = jax.vjp(normalize, h0, gains[0])[1](scatter_step(part))
    grad_tokens = (dh1 + part_zero).astype(bf16)

    gain_total = sum_everywhere(jnp.stack([gain_grad_zero, gain_grad_one, gain_grad_two]))

    place = np.arange(8)
    source = (place % 2)[None, :] * 4 + ((place // 2)[None, :] - my_shift[:, None]) % 4
    row_source = ((z - my_shift) % 4) ^ f
    late = (my_used == 1) & ((my_tile < 4) | (my_tile == 9))
    early_mode = jnp.where(my_used == 0, 1, jnp.where(late, 0, jnp.where(my_row == 1, 3, 2)))
    states = (master, moment_one, moment_two)
    slot = np.arange(cap, dtype=np.int32)
    early = adam_tiles(
        *states,
        [early_grads],
        [out_grads],
        slot,
        after(early_mode, gain_total),
        (source * cap + slot[:, None]).reshape(-1),
        row_source,
        np.zeros(cap, np.int32),
    )

    back_swap = [(target, source) for source, target in pair_swap]
    other_half = lax.ppermute(g_outer, ALL_AXES, back_swap)
    outer_grad = jnp.where(
        odd == 0,
        jnp.concatenate([g_outer, other_half], axis=0),
        jnp.concatenate([other_half, g_outer], axis=0),
    )
    outer_grads = to_owners(after(outer_grad, early_grads), lambda zz, place, target: place % 4 in (zz, (zz + 2) % 4))
    by_tile = jnp.swapaxes(g_qkv.reshape(2, rows, 3, block), 1, 2)
    sent = jnp.broadcast_to(by_tile[:, None], (2, 4, 3, rows, block)).reshape(8, 3, rows, block)
    late_grads = lax.all_to_all(sent, PLANE, 0, 0, tiled=True).reshape(8 * 3, rows, block)

    n_late = 5
    order = jnp.sum(jnp.where(slot[None, :] < slot[:, None], late.astype(jnp.int32)[None, :], 0), axis=1)
    count_late = jnp.sum(late.astype(jnp.int32))
    step = np.arange(n_late)
    wanted = jnp.minimum(step, jnp.maximum(count_late - 1, 0))
    here = late[None, :] & (order[None, :] == wanted[:, None])

    def at_step(value):
        return jnp.sum(jnp.where(here, value.astype(jnp.int32)[None, :], 0), axis=1)

    hold = (step >= jnp.maximum(count_late, 1)).astype(jnp.int32)
    tile = at_step(my_tile)
    some = count_late > 0
    visit = jnp.where(some, at_step(slot), 0)
    first_mode = jnp.where(early_mode[0] == 3, 4, early_mode[0])
    late_mode = jnp.where(at_step(my_row) == 1, 5, 3)
    mode = jnp.where(hold == 1, 0, jnp.where(some, late_mode, first_mode))
    late_place = (place % 2)[None, :] * 4 + (place // 2)[None, :]
    column_place = jnp.where(some, late_place * 3 + tile[:, None], (source * cap + slot[:, None])[0][None, :])
    new_w, new_m, new_v = adam_tiles(
        *states,
        [early_grads, late_grads],
        [out_grads, outer_grads],
        visit,
        mode,
        column_place.reshape(-1),
        jnp.where(some, at_step(row_source), row_source[0]),
        hold,
        early,
    )
    new_g, new_gm, new_gv = adam_update(gains, gain_one, gain_two, gain_total, rate_gain, 0.0)
    return (layer_out, grad_tokens, new_w, new_m, new_v, new_g, new_gm, new_gv)


def whole_body(
    tokens, cotangent, context, lengths, keep, owners, master, moment_one, moment_two, gains, gain_one, gain_two
):
    cap = master.shape[0]
    n_tiles = owners.shape[0]
    slot_of = owners * cap + ranks_of(owners)
    owner_rows = lax.all_gather(master.astype(bf16), "fsdp", axis=0, tiled=True)
    tiles = [
        lax.all_gather(
            lax.dynamic_index_in_dim(owner_rows, slot_of[tile], 0, keepdims=False), "dp", axis=0, tiled=True
        )
        for tile in range(n_tiles)
    ]
    w_in = jnp.concatenate(tiles[10:14], axis=1)
    w_out = jnp.concatenate(tiles[14:18], axis=0)
    count, width = tokens.shape
    head_dim = width // HEADS
    scale = head_dim ** (-0.5)
    seg = segments(lengths[0], count)
    live = keep == 1
    places = jnp.arange(count)

    def split(value):
        return value.astype(bf16).reshape(-1, HEADS, head_dim)

    def joined(value):
        return value.astype(bf16).reshape(-1, width)

    def probabilities(left, right, mask):
        scores = jnp.einsum("qhd,khd->hqk", left, right, preferred_element_type=f32) * scale
        scores = jnp.where(mask[None], scores, -1e30)
        expo = jnp.exp(scores - jnp.max(scores, axis=-1, keepdims=True))
        return expo / jnp.sum(expo, axis=-1, keepdims=True)

    def weighted(probs, right):
        return jnp.einsum("hqk,khd->qhd", probs, right, preferred_element_type=f32)

    def through(weights, d_out, left, right, probs, values):
        d_mixed = split(matmul_right(d_out, weights))
        d_probs = jnp.einsum("qhd,khd->hqk", d_mixed, values, preferred_element_type=f32)
        d_scores = (probs * (d_probs - jnp.sum(probs * d_probs, axis=-1, keepdims=True))).astype(bf16)
        d_left = joined(weighted(d_scores, right) * scale)
        d_right = joined(jnp.einsum("hqk,qhd->khd", d_scores, left, preferred_element_type=f32) * scale)
        d_values = joined(jnp.einsum("hqk,qhd->khd", probs.astype(bf16), d_mixed, preferred_element_type=f32))
        return d_left, d_right, d_values

    h0 = tokens.astype(f32)
    a_in = normalize(h0, gains[0]).astype(bf16)
    query, keys, values = (split(matmul(a_in, tiles[n])) for n in range(3))
    allowed = (seg[:, None] == seg[None, :]) & (live[None, :] | (places[:, None] == places[None, :]))
    probs = probabilities(query, keys, allowed)
    attended = joined(weighted(probs.astype(bf16), values))
    h1 = h0 + matmul(attended, tiles[3])
    b_in = normalize(h1, gains[1]).astype(bf16)
    slots, ctx_len, ctx_width = context.shape
    ctx = context.reshape(slots * ctx_len, ctx_width)
    ctx_low, ctx_high = ctx[:, :width], ctx[:, width:]
    cross_q = split(matmul(b_in, tiles[4]))
    cross_k = split(matmul(ctx_low, tiles[5]) + matmul(ctx_high, tiles[6]))
    cross_v = split(matmul(ctx_low, tiles[7]) + matmul(ctx_high, tiles[8]))
    item = jnp.arange(slots * ctx_len) // ctx_len
    cross_p = probabilities(cross_q, cross_k, seg[:, None] == item[None, :])
    cross_o = joined(weighted(cross_p.astype(bf16), cross_v))
    h2 = h1 + matmul(cross_o, tiles[9])
    c_in = normalize(h2, gains[2]).astype(bf16)
    hidden = matmul(c_in, w_in)
    activated = gelu_tanh(hidden).astype(bf16)
    layer_out = (h2 + matmul(activated, w_out)).astype(bf16)
    grad_out = cotangent.astype(f32) * live.astype(f32)[:, None]
    d_ff = grad_out.astype(bf16)
    d_hidden = jax.vjp(gelu_tanh, hidden)[1](matmul_right(d_ff, w_out))[0].astype(bf16)
    part_two, gain_grad_two = jax.vjp(normalize, h2, gains[2])[1](matmul_right(d_hidden, w_in))
    dh2 = grad_out + part_two
    d_cross_out = dh2.astype(bf16)
    d_cq, d_ck, d_cv = through(tiles[9], d_cross_out, cross_q, cross_k, cross_p, cross_v)
    part_one, gain_grad_one = jax.vjp(normalize, h1, gains[1])[1](matmul_right(d_cq, tiles[4]))
    dh1 = dh2 + part_one
    d_self_out = dh1.astype(bf16)
    d_q, d_k, d_v = through(tiles[3], d_self_out, query, keys, probs, values)
    d_a = matmul_right(d_q, tiles[0]) + matmul_right(d_k, tiles[1]) + matmul_right(d_v, tiles[2])
    part_zero, gain_grad_zero = jax.vjp(normalize, h0, gains[0])[1](d_a)
    grad_tokens = (dh1 + part_zero).astype(bf16)
    pairs = [
        (a_in, d_q),
        (a_in, d_k),
        (a_in, d_v),
        (attended, d_self_out),
        (b_in, d_cq),
        (ctx_low, d_ck),
        (ctx_high, d_ck),
        (ctx_low, d_cv),
        (ctx_high, d_cv),
        (cross_o, d_cross_out),
    ]
    for part in range(4):
        pairs.append((c_in, d_hidden[:, part * width : (part + 1) * width]))
    for part in range(4):
        pairs.append((activated[:, part * width : (part + 1) * width], d_ff))
    total_slots = lax.axis_size("fsdp") * cap
    placed = jnp.zeros((total_slots,) + master.shape[1:], bf16)
    for tile, (left, right) in enumerate(pairs):
        term = lax.psum_scatter(
            matmul_left(left, right).astype(bf16), "dp", scatter_dimension=0, tiled=True
        )
        placed = lax.dynamic_update_index_in_dim(placed, term, slot_of[tile], 0)
    owned = lax.psum_scatter(placed, "fsdp", scatter_dimension=0, tiled=True).astype(f32)
    my_slots = lax.axis_index("fsdp") * cap + jnp.arange(cap)
    used = jnp.any(slot_of[None, :] == my_slots[:, None], axis=1)[:, None, None]
    updated = adam_update(master, moment_one, moment_two, owned, rate_matrix, decay_rate)
    new_w, new_m, new_v = (jnp.where(used, value, 0.0) for value in updated)
    gain_grads = jnp.stack([gain_grad_zero, gain_grad_one, gain_grad_two])
    gain_total = lax.psum(gain_grads, ("dp", "fsdp"))
    new_g, new_gm, new_gv = adam_update(gains, gain_one, gain_two, gain_total, rate_gain, 0.0)
    return (layer_out, grad_tokens, new_w, new_m, new_v, new_g, new_gm, new_gv)


def solution(mesh):
    planes = mesh.shape["dp"] == 8 and mesh.shape["fsdp"] == 4
    if planes:
        used = Mesh(mesh.devices.reshape(4, 2, 2, 2), ALL_AXES)
        dp, fsdp, body = ("z", "x"), ("y", "c"), plane_body
    else:
        used, dp, fsdp, body = mesh, ("dp",), ("fsdp",), whole_body
    rows = P(dp + fsdp, None)
    tiles = P(fsdp, dp, None)
    return jax.shard_map(
        body,
        mesh=used,
        in_specs=(rows, rows, P(dp + fsdp, None, None), rows, P(dp + fsdp), P(), tiles, tiles, tiles, P(), P(), P()),
        out_specs=(rows, rows, tiles, tiles, tiles, P(), P(), P()),
        check_vma=False,
    )
```

```python
import jax
import jax.numpy as jnp
import numpy as np
from jax import lax
from jax.experimental import pallas as pl
from jax.experimental.layout import Layout, with_layout_constraint
from jax.experimental.pallas import tpu as pltpu
from jax.sharding import Mesh
from jax.sharding import PartitionSpec as P

HEADS = 16
STEP = 10

norm_eps = 1e-06
beta_one = 0.9
beta_two = 0.95
adam_eps = 1e-08
decay_rate = 0.1
rate_matrix = 0.1
rate_gain = 0.8

f32 = jnp.float32
bf16 = jnp.bfloat16

SHIFT = (0, 0, 0, 0, 2, 2, 2, 2, 2, 2, 0, 1, 2, 3, 0, 1, 2, 3)
ROW_TILES = (3, 9, 14, 15, 16, 17)
VMEM_LIMIT = 48 << 20


def normalize(h, gain):
    scale = lax.rsqrt(jnp.mean(h * h, axis=-1, keepdims=True) + norm_eps)
    return h * scale * gain


def gelu_tanh(u):
    return 0.5 * u * (1.0 + jnp.tanh(0.7978845608028654 * (u + 0.044715 * u * u * u)))


def matmul(left, right):
    return jnp.dot(left, right, preferred_element_type=f32)


def matmul_left(left, right):
    return lax.dot_general(left, right, (((0,), (0,)), ((), ())), preferred_element_type=f32)


def matmul_right(left, right):
    return lax.dot_general(left, right, (((1,), (1,)), ((), ())), preferred_element_type=f32)


def ranks_of(owners):
    order = jnp.arange(owners.shape[0])
    same = (owners[:, None] == owners[None, :]) & (order[None, :] < order[:, None])
    return jnp.sum(same.astype(jnp.int32), axis=1)


def segments(lengths, count):
    places = jnp.arange(count)
    end = jnp.zeros((), jnp.int32)
    seg = jnp.zeros((count,), jnp.int32)
    for item in range(lengths.shape[0]):
        end = end + lengths[item]
        seg = seg + (places >= end).astype(jnp.int32)
    return seg


def adam_update(weight, first, second, grad, rate, decay):
    first = beta_one * first + (1.0 - beta_one) * grad
    second = beta_two * second + (1.0 - beta_two) * grad * grad
    fix_one = 1.0 / (1.0 - beta_one**STEP)
    fix_two = 1.0 / (1.0 - beta_two**STEP)
    move = first * fix_one / (jnp.sqrt(second * fix_two) + adam_eps)
    return (weight - rate * (move + decay * weight), first, second)


def pack_columns(master, table, first_slot, slots):
    _, rows, columns = master.shape
    width = columns // 8

    def kernel(table_ref, in_ref, out_ref):
        slot = pl.program_id(0)
        for rank in range(8):
            start = pl.multiple_of(table_ref[slot * 8 + rank] * width, width)
            out_ref[rank, 0] = in_ref[0, :, pl.ds(start, width)].astype(bf16)

    return pl.pallas_call(
        kernel,
        out_shape=jax.ShapeDtypeStruct((8, slots, rows, width), bf16),
        grid_spec=pltpu.PrefetchScalarGridSpec(
            num_scalar_prefetch=1,
            grid=(slots,),
            in_specs=[pl.BlockSpec((1, rows, columns), lambda k, t: (first_slot + k, 0, 0))],
            out_specs=pl.BlockSpec((8, 1, rows, width), lambda k, t: (0, k, 0, 0)),
        ),
        compiler_params=pltpu.CompilerParams(vmem_limit_bytes=VMEM_LIMIT),
        name="pack_columns",
    )(table, master)


def pick_blocks(sources, which, index, count):
    _, rows, width = sources[0].shape
    n_src = len(sources)

    def kernel(which_ref, index_ref, *refs):
        place = pl.program_id(0) * 2 + pl.program_id(1)
        out_ref = refs[n_src]
        for number in range(n_src):

            @pl.when(which_ref[place] == number)
            def _():
                out_ref[...] = refs[number][0]

    def spec(number):
        def at(n, half, which, index):
            place = n * 2 + half
            return (jnp.where(which[place] == number, index[place], 0), 0, 0)

        return pl.BlockSpec((1, rows, width), at)

    return pl.pallas_call(
        kernel,
        out_shape=jax.ShapeDtypeStruct((2 * rows, count * width), bf16),
        grid_spec=pltpu.PrefetchScalarGridSpec(
            num_scalar_prefetch=2,
            grid=(count, 2),
            in_specs=[spec(number) for number in range(n_src)],
            out_specs=pl.BlockSpec((rows, width), lambda n, half, which, index: (half, n)),
        ),
        compiler_params=pltpu.CompilerParams(vmem_limit_bytes=VMEM_LIMIT),
        name="pick_blocks",
    )(which, index, *sources)


def adam_tiles(master, one, two, columns_from, rows_from, visit, mode, column_place, row_place, hold, previous=None):
    _, rows, columns = master.shape
    width = columns // 8
    n_visit = visit.shape[0]
    n_col, n_row = len(columns_from), len(rows_from)
    kept = () if previous is None else tuple(previous)

    def kernel(visit_ref, mode_ref, cp_ref, rp_ref, hold_ref, *refs):
        w_ref, m_ref, v_ref = refs[:3]
        grads = refs[3 : 3 + n_col + n_row]
        outs = refs[3 + n_col + n_row + len(kept) :]
        how = mode_ref[pl.program_id(0)]

        @pl.when(how == 1)
        def _():
            for ref in outs:
                ref[...] = jnp.zeros_like(ref)

        for number, grad_ref in enumerate(grads):

            @pl.when(how == number + 2)
            def _():
                grad = grad_ref[0].astype(f32)
                results = adam_update(w_ref[0], m_ref[0], v_ref[0], grad, rate_matrix, decay_rate)
                for ref, value in zip(outs, results, strict=True):
                    ref[0] = value

    def block_of(n, b, hold):
        return jnp.where(hold[n] == 1, 7, b)

    state = pl.BlockSpec((1, rows, width), lambda n, b, vi, mo, cp, rp, ho: (vi[n], 0, block_of(n, b, ho)))

    def column_spec(number):
        def at(n, b, vi, mo, cp, rp, ho):
            place = jnp.where(mo[n] == number + 2, cp[n * 8 + block_of(n, b, ho)], 0)
            return (place // 8, 0, place % 8)

        return pl.BlockSpec((1, rows, width), at)

    def row_spec(number):
        def at(n, b, vi, mo, cp, rp, ho):
            taken = mo[n] == number + 2
            return (jnp.where(taken, rp[n], 0), 0, jnp.where(taken, block_of(n, b, ho), 0))

        return pl.BlockSpec((1, rows, width), at)

    shape = jax.ShapeDtypeStruct(master.shape, f32)
    n_before = 5 + 3 + n_col + n_row
    return pl.pallas_call(
        kernel,
        out_shape=(shape, shape, shape),
        grid_spec=pltpu.PrefetchScalarGridSpec(
            num_scalar_prefetch=5,
            grid=(n_visit, 8),
            in_specs=[
                state,
                state,
                state,
                *(column_spec(number) for number in range(n_col)),
                *(row_spec(n_col + number) for number in range(n_row)),
                *(pl.BlockSpec(memory_space=pl.ANY) for _ in kept),
            ],
            out_specs=(state, state, state),
        ),
        input_output_aliases={n_before + n: n for n in range(len(kept))},
        compiler_params=pltpu.CompilerParams(vmem_limit_bytes=VMEM_LIMIT),
        name="adam_tiles",
    )(visit, mode, column_place, row_place, hold, master, one, two, *columns_from, *rows_from, *kept)


def after(value, *others):
    return lax.optimization_barrier((value, *others))[0]


def swap(value, axis):
    return lax.ppermute(value, axis, [(0, 1), (1, 0)])


def gather_rows(value):
    half = value.shape[0] // 2
    over_x = swap(value, "x")
    over_y = swap(value, "y")
    far_low = swap(over_y[:half], "x")
    far_high = swap(over_x[half:], "y")
    four = jnp.concatenate([value, over_y, over_x, far_low, far_high], axis=0)
    return jnp.concatenate([four, swap(four, "c")], axis=0)


def spread_columns(value):
    rows = value.shape[0] // 2
    low = lax.axis_index("x") == 0
    upper, lower = value[:rows], value[rows:]
    two = jnp.stack([jnp.where(low, upper, lower), swap(jnp.where(low, lower, upper), "x")])
    four = jnp.concatenate([two, swap(two, "y")])
    return jnp.concatenate([four, swap(four, "c")])


def scatter_rows(part):
    rows, width = part.shape[0] // 8, part.shape[1]
    half = width // 2
    part = part.reshape(2, 2, 2, rows, width)
    chip = part[0] + swap(part[1], "c")
    low, high = chip[..., :half], chip[..., half:]
    low_two = low[:, 0] + swap(low[:, 1].astype(bf16), "y").astype(f32)
    high_two = high[0] + swap(high[1].astype(bf16), "x").astype(f32)
    low_one = low_two[0] + swap(low_two[1].astype(bf16), "x").astype(f32)
    high_one = high_two[0] + swap(high_two[1].astype(bf16), "y").astype(f32)
    return jnp.concatenate([low_one, high_one], axis=1)


def sum_everywhere(value):
    for axis in ("c", "y", "x"):
        value = value + swap(value, axis)
    for step in (1, 2):
        value = value + lax.ppermute(value, "z", [(z, z ^ step) for z in range(4)])
    return value


def flip_pairs(mask, keep=None):
    pairs = []
    for z in range(4):
        for place in range(8):
            target = place ^ mask
            if keep is None or keep(z, place, target):
                pairs.append((z * 8 + place, z * 8 + target))
    return pairs


ALL_AXES = ("z", "x", "y", "c")
PLANE = ("x", "y", "c")


def plane_body(
    tokens, cotangent, context, lengths, keep, owners, master, moment_one, moment_two, gains, gain_one, gain_two
):
    cap, rows, _ = master.shape
    count, width = tokens.shape
    heads_here = HEADS // 8
    head_dim = width // HEADS
    scale = head_dim ** (-0.5)
    block = width // 8
    z = lax.axis_index("z")
    x = lax.axis_index("x")
    f = lax.axis_index("y") * 2 + lax.axis_index("c")

    n_tiles = owners.shape[0]
    rank = ranks_of(owners)
    shift_of = np.array(SHIFT, np.int32)
    row_of = np.array([t in ROW_TILES for t in range(n_tiles)])
    all_slots = jnp.arange(4 * cap).reshape(4, cap)
    holds = (owners * cap + rank)[None, None, :] == all_slots[:, :, None]
    used_at = jnp.any(holds, axis=2)
    tile_at = jnp.sum(jnp.where(holds, np.arange(n_tiles, dtype=np.int32), 0), axis=2)
    shift_at = jnp.sum(jnp.where(holds, shift_of, 0), axis=2)
    row_at = jnp.any(holds & row_of, axis=2)
    mine = (jnp.arange(4) == f)[:, None]

    def my(value):
        return jnp.sum(jnp.where(mine, value.astype(jnp.int32), 0), axis=0)

    my_used, my_tile, my_shift, my_row = my(used_at), my(tile_at), my(shift_at), my(row_at)

    to_x = np.arange(8) // 4
    to_f = np.arange(8) % 4
    column_table = 2 * ((to_f[None, :] + my_shift[:, None]) % 4) + to_x[None, :]
    half_cap = cap // 2
    place = np.arange(4)

    def of_tiles(tiles, values):
        chosen = tiles[:, None] == np.arange(n_tiles)[None, :]
        return jnp.sum(jnp.where(chosen, values[None, :], 0), axis=1)

    column_tiles = jnp.concatenate([np.array([0, 1, 2, 4, 5, 7, 6, 8], np.int32), 10 + (place - f) % 4])
    column_part = jnp.repeat(of_tiles(column_tiles, rank // half_cap), 2)
    column_place = of_tiles(column_tiles, owners * half_cap + rank % half_cap)
    column_place = (column_place[:, None] + np.array([0, 4 * half_cap])[None, :]).reshape(-1)
    other_f = f ^ place
    outer_tiles = jnp.where(other_f == z, 3, 9)
    out_tiles = 14 + (z - other_f) % 4
    row_slots = of_tiles(jnp.concatenate([outer_tiles, out_tiles]), rank)
    row_owners = of_tiles(jnp.stack([outer_tiles[0], out_tiles[0]]), owners)

    def exchange_columns(first, weights):
        table = column_table[first : first + half_cap].reshape(-1)
        got = lax.all_to_all(pack_columns(weights, table, first, half_cap), PLANE, 0, 0, tiled=True)
        return got.reshape(8 * half_cap, rows, block)

    def my_block(slot):
        return lax.dynamic_index_in_dim(master, slot, 0, keepdims=False).astype(bf16)

    h0 = tokens.astype(f32)
    outer_blocks = [my_block(row_slots[mask]) for mask in range(4)]
    a_in = normalize(h0, gains[0]).astype(bf16)
    received = [exchange_columns(0, after(master, column_part, column_place, row_slots, row_owners))]
    received = [after(received[0], a_in, *outer_blocks)]

    def columns_here(first, count, parts):
        chosen = slice(2 * first, 2 * (first + count))
        return pick_blocks(received[:parts], column_part[chosen], column_place[chosen], count)

    def gather_z(value):
        return lax.all_gather(value, "z", axis=0, tiled=True)

    local = columns_here(0, 3, 1)
    w_qkv = gather_z(local)
    received.append(exchange_columns(half_cap, after(master, local)))
    a_all = gather_rows(after(a_in, local))

    def take_rows(kind, blocks, keep_pair, earlier):
        found = None
        source = row_owners[kind] ^ f
        for mask, got in enumerate(blocks):
            if mask:
                got = after(got, earlier)
                got = lax.ppermute(got, ALL_AXES, flip_pairs(mask, keep_pair))
            found = got if found is None else jnp.where(source == mask, got, found)
        return found

    def needs_outer(zz, place, target):
        return target % 4 in (zz, (zz + 2) % 4)

    outer = take_rows(0, outer_blocks, needs_outer, local)
    half_rows = rows // 2
    odd = z % 2
    to_pair = lax.dynamic_slice_in_dim(outer, (1 - odd) * half_rows, half_rows, 0)
    own_half = lax.dynamic_slice_in_dim(outer, odd * half_rows, half_rows, 0)
    pair_swap = [
        (zz * 8 + place, (zz ^ 1) * 8 + place)
        for zz in range(4)
        for place in range(8)
        if place % 4 in (zz, (zz + 2) % 4)
    ]
    from_pair = lax.ppermute(to_pair, ALL_AXES, pair_swap)
    has_outer = (f == z) | (f == (z + 2) % 4)
    outer_all = lax.all_gather(jnp.where(has_outer, own_half, from_pair), "z", axis=0, tiled=True)
    low_y = lax.axis_index("y") == 0
    w_self_out = jnp.where(low_y, outer_all[:rows], outer_all[rows:])
    w_cross_out = jnp.where(low_y, outer_all[rows:], outer_all[:rows])

    w_cross = gather_z(columns_here(3, 5, 2))
    w_in = gather_z(columns_here(8, 4, 2))
    slots, ctx_len, ctx_width = context.shape
    ctx = context.reshape(slots * ctx_len, ctx_width)
    ctx_x = swap(after(ctx, a_all), "x")
    ctx_y = swap(after(ctx, a_all), "y")

    seg = segments(lengths[0], count)
    live = keep == 1
    code = seg * 2 + live.astype(jnp.int32)
    for axis in ("y", "x", "c"):
        code = jnp.concatenate([code, swap(code, axis)])
    seg_all = (code // 2).reshape(8, count)
    live_all = (code % 2 == 1).reshape(8, count)

    grad_out = cotangent.astype(f32) * live.astype(f32)[:, None]
    present = owners[0] >= 0

    def chain_step(move, *values):
        shapes = jax.eval_shape(move, *values)
        idle = jax.tree.map(lambda leaf: jnp.zeros(leaf.shape, leaf.dtype), shapes)
        return lax.cond(present, move, lambda *_: idle, *values)

    def split(value):
        return value.reshape(8, -1, heads_here, head_dim)

    qkv = matmul(a_all, w_qkv)
    qkv = qkv.astype(bf16)
    query, keys, values = (split(qkv[:, n * block : (n + 1) * block]) for n in range(3))
    places = jnp.arange(count)
    allowed = (seg_all[:, :, None] == seg_all[:, None, :]) & (
        live_all[:, None, :] | (places[:, None] == places[None, :])
    )

    def probabilities(left, right, mask):
        scores = jnp.einsum("bqhd,bkhd->bhqk", left, right, preferred_element_type=f32) * scale
        scores = jnp.where(mask[:, None], scores, -1e30)
        expo = jnp.exp(scores - jnp.max(scores, axis=-1, keepdims=True))
        return expo / jnp.sum(expo, axis=-1, keepdims=True)

    def weighted(probs, right):
        return jnp.einsum("bhqk,bkhd->bqhd", probs, right, preferred_element_type=f32)

    def joined(value):
        return value.astype(bf16).reshape(-1, block)

    probs = probabilities(query, keys, allowed)
    probs_low = probs.astype(bf16)
    attended = joined(weighted(probs_low, values))
    half = slots * ctx_len // 2
    far_low = swap(after(ctx_y, attended)[:half], "x")
    far_high = swap(after(ctx_x, attended)[half:], "y")
    out_blocks = [my_block(row_slots[4 + mask]) for mask in range(4)]
    out_rows = take_rows(1, out_blocks, None, attended)
    w_out = gather_z(out_rows)
    h1 = h0 + chain_step(scatter_rows, matmul(attended, w_self_out))
    ctx_four = jnp.concatenate([ctx, ctx_y, ctx_x, far_low, far_high], axis=0)
    ctx_all = jnp.concatenate([ctx_four, swap(ctx_four, "c")], axis=0)
    b_all, d_ff = chain_step(
        lambda one, two: (gather_rows(one), gather_rows(two)),
        normalize(h1, gains[1]).astype(bf16),
        grad_out.astype(bf16),
    )

    w_cross_q = w_cross[:, :block]
    w_low = w_cross[:, block : 3 * block]
    w_high = w_cross[:, 3 * block :]
    ctx_low, ctx_high = ctx_all[:, :width], ctx_all[:, width:]
    ctx_kv = (matmul(ctx_low, w_low) + matmul(ctx_high, w_high)).astype(bf16)
    cross_q = matmul(b_all, w_cross_q)
    cross_q = split(cross_q.astype(bf16))
    cross_k, cross_v = split(ctx_kv[:, :block]), split(ctx_kv[:, block:])
    item = jnp.arange(slots * ctx_len) // ctx_len
    own_item = seg_all[:, :, None] == item[None, None, :]
    cross_p = probabilities(cross_q, cross_k, own_item)
    cross_low = cross_p.astype(bf16)
    cross_o = joined(weighted(cross_low, cross_v))
    h2 = h1 + chain_step(scatter_rows, matmul(cross_o, w_cross_out))
    c_all = chain_step(gather_rows, normalize(h2, gains[2]).astype(bf16))

    hidden = matmul(c_all, w_in)
    activated = gelu_tanh(hidden).astype(bf16)

    def sum_rows(value):
        value = with_layout_constraint(value, Layout(major_to_minor=(0, 1)))
        value = lax.psum_scatter(value, "z", scatter_dimension=0, tiled=True)
        return with_layout_constraint(value, Layout(major_to_minor=(0, 1)))

    def to_owners(value, keep_pair):
        moved = [lax.ppermute(value, ALL_AXES, flip_pairs(mask, keep_pair)) for mask in range(1, 4)]
        return jnp.stack([value, *moved])

    t_out = matmul_left(activated, d_ff).astype(bf16)
    g_out = sum_rows(t_out)
    d_act = matmul_right(after(d_ff, t_out), w_out)
    d_hidden = jax.vjp(gelu_tanh, hidden)[1](d_act)[0].astype(bf16)
    t_in = matmul_left(c_all, d_hidden).astype(bf16)
    g_in = sum_rows(t_in)
    d_c, mixed = chain_step(
        lambda one, two: (scatter_rows(one), scatter_rows(two)), matmul_right(d_hidden, w_in), matmul(activated, w_out)
    )
    layer_out = (h2 + mixed).astype(bf16)
    part_two, gain_grad_two = jax.vjp(normalize, h2, gains[2])[1](d_c)
    dh2 = grad_out + part_two
    d_cross_out = chain_step(gather_rows, after(dh2.astype(bf16), t_in))
    out_grads = to_owners(g_out, None)
    g_cross_out = matmul_left(cross_o, d_cross_out)

    def through(d_mixed, left, right, probs, probs_low, values):
        d_mixed = split(d_mixed.astype(bf16))
        d_probs = jnp.einsum("bqhd,bkhd->bhqk", d_mixed, values, preferred_element_type=f32)
        d_scores = (probs * (d_probs - jnp.sum(probs * d_probs, axis=-1, keepdims=True))).astype(bf16)
        d_left = joined(weighted(d_scores, right) * scale)
        d_right = joined(jnp.einsum("bhqk,bqhd->bkhd", d_scores, left, preferred_element_type=f32) * scale)
        d_values = joined(jnp.einsum("bhqk,bqhd->bkhd", probs_low, d_mixed, preferred_element_type=f32))
        return d_left, d_right, d_values

    d_cq, d_ck, d_cv = through(
        matmul_right(d_cross_out, w_cross_out), cross_q, cross_k, cross_p, cross_low, cross_v
    )
    d_ckv = jnp.concatenate([d_ck, d_cv], axis=1)
    t_cross = jnp.concatenate(
        [
            value.astype(bf16)
            for value in (matmul_left(b_all, d_cq), matmul_left(ctx_low, d_ckv), matmul_left(ctx_high, d_ckv))
        ],
        axis=1,
    )
    g_cross = sum_rows(t_cross)
    part = matmul_right(d_cq, w_cross_q)
    part_one, gain_grad_one = jax.vjp(normalize, h1, gains[1])[1](chain_step(scatter_rows, part))
    dh1 = dh2 + part_one
    d_self_out, in_grads = chain_step(
        lambda one, two: (gather_rows(one), spread_columns(two)), after(dh1.astype(bf16), t_cross, out_grads), g_in
    )
    g_self_out = matmul_left(attended, d_self_out)
    t_outer = jnp.concatenate(
        [
            jnp.where(low_y, g_self_out, g_cross_out).astype(bf16),
            jnp.where(low_y, g_cross_out, g_self_out).astype(bf16),
        ],
        axis=0,
    )
    g_outer = sum_rows(t_outer)
    d_mixed = matmul_right(after(d_self_out, t_outer), w_self_out)
    d_q, d_k, d_v = through(d_mixed, query, keys, probs, probs_low, values)
    d_qkv = jnp.concatenate([d_q, d_k, d_v], axis=1)
    g_qkv = sum_rows(matmul_left(a_all, d_qkv).astype(bf16))
    d_a, cross_grads = chain_step(
        lambda one, two: (scatter_rows(one), spread_columns(two)), matmul_right(d_qkv, w_qkv), g_cross
    )
    part_zero, gain_grad_zero = jax.vjp(normalize, h0, gains[0])[1](d_a)
    grad_tokens = (dh1 + part_zero).astype(bf16)

    gain_total = sum_everywhere(jnp.stack([gain_grad_zero, gain_grad_one, gain_grad_two]))

    place = np.arange(8)
    source_x, source_f = (place % 2)[None, :], ((place // 2)[None, :] - my_shift[:, None]) % 4
    other = source_f ^ f
    source = (other % 2) * 4 + (other // 2) * 2 + (source_x ^ x)
    column_of = np.array([0, 1, 2, 0, 0, 1, 3, 2, 4, 0, 0, 0, 0, 0, 0, 0, 0, 0], np.int32)
    my_column = jnp.sum(jnp.where(my_tile[:, None] == np.arange(n_tiles), column_of, 0), axis=1)
    in_layer = (my_tile >= 10)[:, None]
    column_place = source * 8 + jnp.where(in_layer, (place // 2)[None, :], my_column[:, None])
    row_source = ((z - my_shift) % 4) ^ f
    late = (my_used == 1) & ((my_tile < 4) | (my_tile == 9))
    early_mode = jnp.where(my_row == 1, 4, jnp.where(my_tile >= 10, 2, 3))
    early_mode = jnp.where(my_used == 0, 1, jnp.where(late, 0, early_mode))
    states = (master, moment_one, moment_two)
    slot = np.arange(cap, dtype=np.int32)
    by_tile = jnp.swapaxes(g_qkv.reshape(2, rows, 3, block), 1, 2)
    sent = jnp.broadcast_to(by_tile[:, None], (2, 4, 3, rows, block)).reshape(8, 3, rows, block)
    late_grads = lax.all_to_all(sent, PLANE, 0, 0, tiled=True).reshape(8 * 3, rows, block)
    early = adam_tiles(
        *states,
        [in_grads, cross_grads],
        [out_grads],
        slot,
        after(early_mode, gain_total, sent),
        column_place.reshape(-1),
        row_source,
        np.zeros(cap, np.int32),
    )

    back_swap = [(target, source) for source, target in pair_swap]
    other_half = lax.ppermute(g_outer, ALL_AXES, back_swap)
    outer_grad = jnp.where(
        odd == 0,
        jnp.concatenate([g_outer, other_half], axis=0),
        jnp.concatenate([other_half, g_outer], axis=0),
    )
    outer_grads = to_owners(outer_grad, lambda zz, place, target: place % 4 in (zz, (zz + 2) % 4))
    n_late = 5
    order = jnp.sum(jnp.where(slot[None, :] < slot[:, None], late.astype(jnp.int32)[None, :], 0), axis=1)
    count_late = jnp.sum(late.astype(jnp.int32))
    step = np.arange(n_late)
    wanted = jnp.minimum(step, jnp.maximum(count_late - 1, 0))
    here = late[None, :] & (order[None, :] == wanted[:, None])

    def at_step(value):
        return jnp.sum(jnp.where(here, value.astype(jnp.int32)[None, :], 0), axis=1)

    hold = (step >= jnp.maximum(count_late, 1)).astype(jnp.int32)
    tile = at_step(my_tile)
    some = count_late > 0
    visit = jnp.where(some, at_step(slot), 0)
    first_mode = jnp.where(early_mode[0] == 4, 5, early_mode[0])
    late_mode = jnp.where(at_step(my_row) == 1, 6, 4)
    mode = jnp.where(hold == 1, 0, jnp.where(some, late_mode, first_mode))
    late_place = ((place % 2)[None, :] * 4 + (place // 2)[None, :]) * 3 + tile[:, None]
    late_place = jnp.where(some, late_place * 8, column_place[:1])
    new_w, new_m, new_v = adam_tiles(
        *states,
        [in_grads, cross_grads, late_grads],
        [out_grads, outer_grads],
        visit,
        mode,
        late_place.reshape(-1),
        jnp.where(some, at_step(row_source), row_source[0]),
        hold,
        early,
    )
    new_g, new_gm, new_gv = adam_update(gains, gain_one, gain_two, gain_total, rate_gain, 0.0)
    return (layer_out, grad_tokens, new_w, new_m, new_v, new_g, new_gm, new_gv)


def whole_body(
    tokens, cotangent, context, lengths, keep, owners, master, moment_one, moment_two, gains, gain_one, gain_two
):
    cap = master.shape[0]
    n_tiles = owners.shape[0]
    slot_of = owners * cap + ranks_of(owners)
    owner_rows = lax.all_gather(master.astype(bf16), "fsdp", axis=0, tiled=True)
    tiles = [
        lax.all_gather(
            lax.dynamic_index_in_dim(owner_rows, slot_of[tile], 0, keepdims=False), "dp", axis=0, tiled=True
        )
        for tile in range(n_tiles)
    ]
    w_in = jnp.concatenate(tiles[10:14], axis=1)
    w_out = jnp.concatenate(tiles[14:18], axis=0)
    count, width = tokens.shape
    head_dim = width // HEADS
    scale = head_dim ** (-0.5)
    seg = segments(lengths[0], count)
    live = keep == 1
    places = jnp.arange(count)

    def split(value):
        return value.astype(bf16).reshape(-1, HEADS, head_dim)

    def joined(value):
        return value.astype(bf16).reshape(-1, width)

    def probabilities(left, right, mask):
        scores = jnp.einsum("qhd,khd->hqk", left, right, preferred_element_type=f32) * scale
        scores = jnp.where(mask[None], scores, -1e30)
        expo = jnp.exp(scores - jnp.max(scores, axis=-1, keepdims=True))
        return expo / jnp.sum(expo, axis=-1, keepdims=True)

    def weighted(probs, right):
        return jnp.einsum("hqk,khd->qhd", probs, right, preferred_element_type=f32)

    def through(weights, d_out, left, right, probs, values):
        d_mixed = split(matmul_right(d_out, weights))
        d_probs = jnp.einsum("qhd,khd->hqk", d_mixed, values, preferred_element_type=f32)
        d_scores = (probs * (d_probs - jnp.sum(probs * d_probs, axis=-1, keepdims=True))).astype(bf16)
        d_left = joined(weighted(d_scores, right) * scale)
        d_right = joined(jnp.einsum("hqk,qhd->khd", d_scores, left, preferred_element_type=f32) * scale)
        d_values = joined(jnp.einsum("hqk,qhd->khd", probs.astype(bf16), d_mixed, preferred_element_type=f32))
        return d_left, d_right, d_values

    h0 = tokens.astype(f32)
    a_in = normalize(h0, gains[0]).astype(bf16)
    query, keys, values = (split(matmul(a_in, tiles[n])) for n in range(3))
    allowed = (seg[:, None] == seg[None, :]) & (live[None, :] | (places[:, None] == places[None, :]))
    probs = probabilities(query, keys, allowed)
    attended = joined(weighted(probs.astype(bf16), values))
    h1 = h0 + matmul(attended, tiles[3])
    b_in = normalize(h1, gains[1]).astype(bf16)
    slots, ctx_len, ctx_width = context.shape
    ctx = context.reshape(slots * ctx_len, ctx_width)
    ctx_low, ctx_high = ctx[:, :width], ctx[:, width:]
    cross_q = split(matmul(b_in, tiles[4]))
    cross_k = split(matmul(ctx_low, tiles[5]) + matmul(ctx_high, tiles[6]))
    cross_v = split(matmul(ctx_low, tiles[7]) + matmul(ctx_high, tiles[8]))
    item = jnp.arange(slots * ctx_len) // ctx_len
    cross_p = probabilities(cross_q, cross_k, seg[:, None] == item[None, :])
    cross_o = joined(weighted(cross_p.astype(bf16), cross_v))
    h2 = h1 + matmul(cross_o, tiles[9])
    c_in = normalize(h2, gains[2]).astype(bf16)
    hidden = matmul(c_in, w_in)
    activated = gelu_tanh(hidden).astype(bf16)
    layer_out = (h2 + matmul(activated, w_out)).astype(bf16)
    grad_out = cotangent.astype(f32) * live.astype(f32)[:, None]
    d_ff = grad_out.astype(bf16)
    d_hidden = jax.vjp(gelu_tanh, hidden)[1](matmul_right(d_ff, w_out))[0].astype(bf16)
    part_two, gain_grad_two = jax.vjp(normalize, h2, gains[2])[1](matmul_right(d_hidden, w_in))
    dh2 = grad_out + part_two
    d_cross_out = dh2.astype(bf16)
    d_cq, d_ck, d_cv = through(tiles[9], d_cross_out, cross_q, cross_k, cross_p, cross_v)
    part_one, gain_grad_one = jax.vjp(normalize, h1, gains[1])[1](matmul_right(d_cq, tiles[4]))
    dh1 = dh2 + part_one
    d_self_out = dh1.astype(bf16)
    d_q, d_k, d_v = through(tiles[3], d_self_out, query, keys, probs, values)
    d_a = matmul_right(d_q, tiles[0]) + matmul_right(d_k, tiles[1]) + matmul_right(d_v, tiles[2])
    part_zero, gain_grad_zero = jax.vjp(normalize, h0, gains[0])[1](d_a)
    grad_tokens = (dh1 + part_zero).astype(bf16)
    pairs = [
        (a_in, d_q),
        (a_in, d_k),
        (a_in, d_v),
        (attended, d_self_out),
        (b_in, d_cq),
        (ctx_low, d_ck),
        (ctx_high, d_ck),
        (ctx_low, d_cv),
        (ctx_high, d_cv),
        (cross_o, d_cross_out),
    ]
    for part in range(4):
        pairs.append((c_in, d_hidden[:, part * width : (part + 1) * width]))
    for part in range(4):
        pairs.append((activated[:, part * width : (part + 1) * width], d_ff))
    total_slots = lax.axis_size("fsdp") * cap
    placed = jnp.zeros((total_slots,) + master.shape[1:], bf16)
    for tile, (left, right) in enumerate(pairs):
        term = lax.psum_scatter(
            matmul_left(left, right).astype(bf16), "dp", scatter_dimension=0, tiled=True
        )
        placed = lax.dynamic_update_index_in_dim(placed, term, slot_of[tile], 0)
    owned = lax.psum_scatter(placed, "fsdp", scatter_dimension=0, tiled=True).astype(f32)
    my_slots = lax.axis_index("fsdp") * cap + jnp.arange(cap)
    used = jnp.any(slot_of[None, :] == my_slots[:, None], axis=1)[:, None, None]
    updated = adam_update(master, moment_one, moment_two, owned, rate_matrix, decay_rate)
    new_w, new_m, new_v = (jnp.where(used, value, 0.0) for value in updated)
    gain_grads = jnp.stack([gain_grad_zero, gain_grad_one, gain_grad_two])
    gain_total = lax.psum(gain_grads, ("dp", "fsdp"))
    new_g, new_gm, new_gv = adam_update(gains, gain_one, gain_two, gain_total, rate_gain, 0.0)
    return (layer_out, grad_tokens, new_w, new_m, new_v, new_g, new_gm, new_gv)


def solution(mesh):
    planes = mesh.shape["dp"] == 8 and mesh.shape["fsdp"] == 4
    if planes:
        used = Mesh(mesh.devices.reshape(4, 2, 2, 2), ALL_AXES)
        dp, fsdp, body = ("z", "x"), ("y", "c"), plane_body
    else:
        used, dp, fsdp, body = mesh, ("dp",), ("fsdp",), whole_body
    rows = P(dp + fsdp, None)
    tiles = P(fsdp, dp, None)
    return jax.shard_map(
        body,
        mesh=used,
        in_specs=(rows, rows, P(dp + fsdp, None, None), rows, P(dp + fsdp), P(), tiles, tiles, tiles, P(), P(), P()),
        out_specs=(rows, rows, tiles, tiles, tiles, P(), P(), P()),
        check_vma=False,
    )
```

```python
import jax
import jax.numpy as jnp
import numpy as np
from jax import lax
from jax.experimental import pallas as pl
from jax.experimental.layout import Layout, with_layout_constraint
from jax.experimental.pallas import tpu as pltpu
from jax.sharding import Mesh
from jax.sharding import PartitionSpec as P

HEADS = 16
STEP = 10

norm_eps = 1e-06
beta_one = 0.9
beta_two = 0.95
adam_eps = 1e-08
decay_rate = 0.1
rate_matrix = 0.1
rate_gain = 0.8

f32 = jnp.float32
bf16 = jnp.bfloat16

SHIFT = (0, 0, 0, 0, 2, 2, 2, 2, 2, 2, 0, 1, 2, 3, 0, 1, 2, 3)
ROW_TILES = (3, 9, 14, 15, 16, 17)
VMEM_LIMIT = 48 << 20


def normalize(h, gain):
    scale = lax.rsqrt(jnp.mean(h * h, axis=-1, keepdims=True) + norm_eps)
    return h * scale * gain


def gelu_tanh(u):
    return 0.5 * u * (1.0 + jnp.tanh(0.7978845608028654 * (u + 0.044715 * u * u * u)))


def matmul(left, right):
    return jnp.dot(left, right, preferred_element_type=f32)


def matmul_left(left, right):
    return lax.dot_general(left, right, (((0,), (0,)), ((), ())), preferred_element_type=f32)


def matmul_right(left, right):
    return lax.dot_general(left, right, (((1,), (1,)), ((), ())), preferred_element_type=f32)


def ranks_of(owners):
    order = jnp.arange(owners.shape[0])
    same = (owners[:, None] == owners[None, :]) & (order[None, :] < order[:, None])
    return jnp.sum(same.astype(jnp.int32), axis=1)


def segments(lengths, count):
    places = jnp.arange(count)
    end = jnp.zeros((), jnp.int32)
    seg = jnp.zeros((count,), jnp.int32)
    for item in range(lengths.shape[0]):
        end = end + lengths[item]
        seg = seg + (places >= end).astype(jnp.int32)
    return seg


def adam_update(weight, first, second, grad, rate, decay):
    first = beta_one * first + (1.0 - beta_one) * grad
    second = beta_two * second + (1.0 - beta_two) * grad * grad
    fix_one = 1.0 / (1.0 - beta_one**STEP)
    fix_two = 1.0 / (1.0 - beta_two**STEP)
    move = first * fix_one / (jnp.sqrt(second * fix_two) + adam_eps)
    return (weight - rate * (move + decay * weight), first, second)


def pack_columns(master, table, first_slot, slots):
    _, rows, columns = master.shape
    width = columns // 8

    def kernel(table_ref, in_ref, out_ref):
        slot = pl.program_id(0)
        for rank in range(8):
            start = pl.multiple_of(table_ref[slot * 8 + rank] * width, width)
            out_ref[rank, 0] = in_ref[0, :, pl.ds(start, width)].astype(bf16)

    return pl.pallas_call(
        kernel,
        out_shape=jax.ShapeDtypeStruct((8, slots, rows, width), bf16),
        grid_spec=pltpu.PrefetchScalarGridSpec(
            num_scalar_prefetch=1,
            grid=(slots,),
            in_specs=[pl.BlockSpec((1, rows, columns), lambda k, t: (first_slot + k, 0, 0))],
            out_specs=pl.BlockSpec((8, 1, rows, width), lambda k, t: (0, k, 0, 0)),
        ),
        compiler_params=pltpu.CompilerParams(vmem_limit_bytes=VMEM_LIMIT),
        name="pack_columns",
    )(table, master)


def pick_blocks(sources, which, index, count):
    _, rows, width = sources[0].shape
    n_src = len(sources)

    def kernel(which_ref, index_ref, *refs):
        place = pl.program_id(0) * 2 + pl.program_id(1)
        out_ref = refs[n_src]
        for number in range(n_src):

            @pl.when(which_ref[place] == number)
            def _():
                out_ref[...] = refs[number][0]

    def spec(number):
        def at(n, half, which, index):
            place = n * 2 + half
            return (jnp.where(which[place] == number, index[place], 0), 0, 0)

        return pl.BlockSpec((1, rows, width), at)

    return pl.pallas_call(
        kernel,
        out_shape=jax.ShapeDtypeStruct((2 * rows, count * width), bf16),
        grid_spec=pltpu.PrefetchScalarGridSpec(
            num_scalar_prefetch=2,
            grid=(count, 2),
            in_specs=[spec(number) for number in range(n_src)],
            out_specs=pl.BlockSpec((rows, width), lambda n, half, which, index: (half, n)),
        ),
        compiler_params=pltpu.CompilerParams(vmem_limit_bytes=VMEM_LIMIT),
        name="pick_blocks",
    )(which, index, *sources)


def adam_tiles(master, one, two, columns_from, rows_from, visit, mode, column_place, row_place, hold, previous=None):
    _, rows, columns = master.shape
    width = columns // 8
    n_visit = visit.shape[0]
    n_col, n_row = len(columns_from), len(rows_from)
    kept = () if previous is None else tuple(previous)

    def kernel(visit_ref, mode_ref, cp_ref, rp_ref, hold_ref, *refs):
        w_ref, m_ref, v_ref = refs[:3]
        grads = refs[3 : 3 + n_col + n_row]
        outs = refs[3 + n_col + n_row + len(kept) :]
        how = mode_ref[pl.program_id(0)]

        @pl.when(how == 1)
        def _():
            for ref in outs:
                ref[...] = jnp.zeros_like(ref)

        for number, grad_ref in enumerate(grads):

            @pl.when(how == number + 2)
            def _():
                grad = grad_ref[0].astype(f32)
                results = adam_update(w_ref[0], m_ref[0], v_ref[0], grad, rate_matrix, decay_rate)
                for ref, value in zip(outs, results, strict=True):
                    ref[0] = value

    def block_of(n, b, hold):
        return jnp.where(hold[n] == 1, 7, b)

    state = pl.BlockSpec((1, rows, width), lambda n, b, vi, mo, cp, rp, ho: (vi[n], 0, block_of(n, b, ho)))

    def column_spec(number):
        def at(n, b, vi, mo, cp, rp, ho):
            place = jnp.where(mo[n] == number + 2, cp[n * 8 + block_of(n, b, ho)], 0)
            return (place // 8, 0, place % 8)

        return pl.BlockSpec((1, rows, width), at)

    def row_spec(number):
        def at(n, b, vi, mo, cp, rp, ho):
            taken = mo[n] == number + 2
            return (jnp.where(taken, rp[n], 0), 0, jnp.where(taken, block_of(n, b, ho), 0))

        return pl.BlockSpec((1, rows, width), at)

    shape = jax.ShapeDtypeStruct(master.shape, f32)
    n_before = 5 + 3 + n_col + n_row
    return pl.pallas_call(
        kernel,
        out_shape=(shape, shape, shape),
        grid_spec=pltpu.PrefetchScalarGridSpec(
            num_scalar_prefetch=5,
            grid=(n_visit, 8),
            in_specs=[
                state,
                state,
                state,
                *(column_spec(number) for number in range(n_col)),
                *(row_spec(n_col + number) for number in range(n_row)),
                *(pl.BlockSpec(memory_space=pl.ANY) for _ in kept),
            ],
            out_specs=(state, state, state),
        ),
        input_output_aliases={n_before + n: n for n in range(len(kept))},
        compiler_params=pltpu.CompilerParams(vmem_limit_bytes=VMEM_LIMIT),
        cost_estimate=pl.CostEstimate(
            flops=30 * n_visit * rows * columns, bytes_accessed=26 * n_visit * rows * columns, transcendentals=0
        ),
        name="adam_tiles",
    )(visit, mode, column_place, row_place, hold, master, one, two, *columns_from, *rows_from, *kept)


def after(value, *others):
    return lax.optimization_barrier((value, *others))[0]


def swap(value, axis):
    return lax.ppermute(value, axis, [(0, 1), (1, 0)])


def gather_rows(value):
    half = value.shape[0] // 2
    over_x = swap(value, "x")
    over_y = swap(value, "y")
    far_low = swap(over_y[:half], "x")
    far_high = swap(over_x[half:], "y")
    four = jnp.concatenate([value, over_y, over_x, far_low, far_high], axis=0)
    return jnp.concatenate([four, swap(four, "c")], axis=0)


def spread_columns(value):
    rows = value.shape[0] // 2
    low = lax.axis_index("x") == 0
    upper, lower = value[:rows], value[rows:]
    two = jnp.stack([jnp.where(low, upper, lower), swap(jnp.where(low, lower, upper), "x")])
    four = jnp.concatenate([two, swap(two, "y")])
    return jnp.concatenate([four, swap(four, "c")])


def scatter_rows(part):
    rows, width = part.shape[0] // 8, part.shape[1]
    half = width // 2
    part = part.reshape(2, 2, 2, rows, width)
    chip = part[0] + swap(part[1], "c")
    low, high = chip[..., :half], chip[..., half:]
    low_two = low[:, 0] + swap(low[:, 1].astype(bf16), "y").astype(f32)
    high_two = high[0] + swap(high[1].astype(bf16), "x").astype(f32)
    low_one = low_two[0] + swap(low_two[1].astype(bf16), "x").astype(f32)
    high_one = high_two[0] + swap(high_two[1].astype(bf16), "y").astype(f32)
    return jnp.concatenate([low_one, high_one], axis=1)


def sum_everywhere(value):
    for axis in ("c", "y", "x"):
        value = value + swap(value, axis)
    for step in (1, 2):
        value = value + lax.ppermute(value, "z", [(z, z ^ step) for z in range(4)])
    return value


def flip_pairs(mask, keep=None):
    pairs = []
    for z in range(4):
        for place in range(8):
            target = place ^ mask
            if keep is None or keep(z, place, target):
                pairs.append((z * 8 + place, z * 8 + target))
    return pairs


ALL_AXES = ("z", "x", "y", "c")
PLANE = ("x", "y", "c")


def plane_body(
    tokens, cotangent, context, lengths, keep, owners, master, moment_one, moment_two, gains, gain_one, gain_two
):
    cap, rows, _ = master.shape
    count, width = tokens.shape
    heads_here = HEADS // 8
    head_dim = width // HEADS
    scale = head_dim ** (-0.5)
    block = width // 8
    z = lax.axis_index("z")
    x = lax.axis_index("x")
    f = lax.axis_index("y") * 2 + lax.axis_index("c")

    n_tiles = owners.shape[0]
    rank = ranks_of(owners)
    shift_of = np.array(SHIFT, np.int32)
    row_of = np.array([t in ROW_TILES for t in range(n_tiles)])
    all_slots = jnp.arange(4 * cap).reshape(4, cap)
    holds = (owners * cap + rank)[None, None, :] == all_slots[:, :, None]
    used_at = jnp.any(holds, axis=2)
    tile_at = jnp.sum(jnp.where(holds, np.arange(n_tiles, dtype=np.int32), 0), axis=2)
    shift_at = jnp.sum(jnp.where(holds, shift_of, 0), axis=2)
    row_at = jnp.any(holds & row_of, axis=2)
    mine = (jnp.arange(4) == f)[:, None]

    def my(value):
        return jnp.sum(jnp.where(mine, value.astype(jnp.int32), 0), axis=0)

    my_used, my_tile, my_shift, my_row = my(used_at), my(tile_at), my(shift_at), my(row_at)

    to_x = np.arange(8) // 4
    to_f = np.arange(8) % 4
    column_table = 2 * ((to_f[None, :] + my_shift[:, None]) % 4) + to_x[None, :]
    half_cap = cap // 2
    place = np.arange(4)

    def of_tiles(tiles, values):
        chosen = tiles[:, None] == np.arange(n_tiles)[None, :]
        return jnp.sum(jnp.where(chosen, values[None, :], 0), axis=1)

    column_tiles = jnp.concatenate([np.array([0, 1, 2, 4, 5, 7, 6, 8], np.int32), 10 + (place - f) % 4])
    column_part = jnp.repeat(of_tiles(column_tiles, rank // half_cap), 2)
    column_place = of_tiles(column_tiles, owners * half_cap + rank % half_cap)
    column_place = (column_place[:, None] + np.array([0, 4 * half_cap])[None, :]).reshape(-1)
    other_f = f ^ place
    outer_tiles = jnp.where(other_f == z, 3, 9)
    out_tiles = 14 + (z - other_f) % 4
    row_slots = of_tiles(jnp.concatenate([outer_tiles, out_tiles]), rank)
    row_owners = of_tiles(jnp.stack([outer_tiles[0], out_tiles[0]]), owners)

    def exchange_columns(first, weights):
        table = column_table[first : first + half_cap].reshape(-1)
        got = lax.all_to_all(pack_columns(weights, table, first, half_cap), PLANE, 0, 0, tiled=True)
        return got.reshape(8 * half_cap, rows, block)

    def my_block(slot):
        return lax.dynamic_index_in_dim(master, slot, 0, keepdims=False).astype(bf16)

    h0 = tokens.astype(f32)
    outer_blocks = [my_block(row_slots[mask]) for mask in range(4)]
    a_in = normalize(h0, gains[0]).astype(bf16)
    received = [exchange_columns(0, after(master, column_part, column_place, row_slots, row_owners))]
    received = [after(received[0], a_in, *outer_blocks)]

    def columns_here(first, count, parts):
        chosen = slice(2 * first, 2 * (first + count))
        return pick_blocks(received[:parts], column_part[chosen], column_place[chosen], count)

    def gather_z(value):
        return lax.all_gather(value, "z", axis=0, tiled=True)

    local = columns_here(0, 3, 1)
    w_qkv = gather_z(local)
    a_all = gather_rows(after(a_in, local))
    received.append(exchange_columns(half_cap, after(master, a_all)))

    def take_rows(kind, blocks, keep_pair, earlier):
        found = None
        source = row_owners[kind] ^ f
        for mask, got in enumerate(blocks):
            if mask:
                got = after(got, earlier)
                got = lax.ppermute(got, ALL_AXES, flip_pairs(mask, keep_pair))
            found = got if found is None else jnp.where(source == mask, got, found)
        return found

    def needs_outer(zz, place, target):
        return target % 4 in (zz, (zz + 2) % 4)

    outer = take_rows(0, outer_blocks, needs_outer, local)
    half_rows = rows // 2
    odd = z % 2
    to_pair = lax.dynamic_slice_in_dim(outer, (1 - odd) * half_rows, half_rows, 0)
    own_half = lax.dynamic_slice_in_dim(outer, odd * half_rows, half_rows, 0)
    pair_swap = [
        (zz * 8 + place, (zz ^ 1) * 8 + place)
        for zz in range(4)
        for place in range(8)
        if place % 4 in (zz, (zz + 2) % 4)
    ]
    from_pair = lax.ppermute(to_pair, ALL_AXES, pair_swap)
    has_outer = (f == z) | (f == (z + 2) % 4)
    outer_all = lax.all_gather(jnp.where(has_outer, own_half, from_pair), "z", axis=0, tiled=True)
    low_y = lax.axis_index("y") == 0
    w_self_out = jnp.where(low_y, outer_all[:rows], outer_all[rows:])
    w_cross_out = jnp.where(low_y, outer_all[rows:], outer_all[:rows])

    w_cross = gather_z(columns_here(3, 5, 2))
    w_in = gather_z(columns_here(8, 4, 2))
    slots, ctx_len, ctx_width = context.shape
    ctx = context.reshape(slots * ctx_len, ctx_width)
    ctx_x = swap(after(ctx, received[1]), "x")
    ctx_y = swap(after(ctx, received[1]), "y")

    seg = segments(lengths[0], count)
    live = keep == 1
    code = seg * 2 + live.astype(jnp.int32)
    for axis in ("y", "x", "c"):
        code = jnp.concatenate([code, swap(code, axis)])
    seg_all = (code // 2).reshape(8, count)
    live_all = (code % 2 == 1).reshape(8, count)

    grad_out = cotangent.astype(f32) * live.astype(f32)[:, None]
    present = owners[0] >= 0

    def chain_step(move, *values):
        shapes = jax.eval_shape(move, *values)
        idle = jax.tree.map(lambda leaf: jnp.zeros(leaf.shape, leaf.dtype), shapes)
        return lax.cond(present, move, lambda *_: idle, *values)

    def split(value):
        return value.reshape(8, -1, heads_here, head_dim)

    qkv = matmul(a_all, w_qkv)
    qkv = qkv.astype(bf16)
    query, keys, values = (split(qkv[:, n * block : (n + 1) * block]) for n in range(3))
    places = jnp.arange(count)
    allowed = (seg_all[:, :, None] == seg_all[:, None, :]) & (
        live_all[:, None, :] | (places[:, None] == places[None, :])
    )

    def probabilities(left, right, mask):
        scores = jnp.einsum("bqhd,bkhd->bhqk", left, right, preferred_element_type=f32) * scale
        scores = jnp.where(mask[:, None], scores, -1e30)
        expo = jnp.exp(scores - jnp.max(scores, axis=-1, keepdims=True))
        return expo / jnp.sum(expo, axis=-1, keepdims=True)

    def weighted(probs, right):
        return jnp.einsum("bhqk,bkhd->bqhd", probs, right, preferred_element_type=f32)

    def joined(value):
        return value.astype(bf16).reshape(-1, block)

    probs = probabilities(query, keys, allowed)
    probs_low = probs.astype(bf16)
    attended = joined(weighted(probs_low, values))
    h1 = h0 + chain_step(scatter_rows, matmul(attended, w_self_out))
    half = slots * ctx_len // 2
    far_low = swap(after(ctx_y, h1)[:half], "x")
    far_high = swap(after(ctx_x, h1)[half:], "y")
    b_all, d_ff = chain_step(
        lambda one, two: (gather_rows(one), gather_rows(two)),
        normalize(h1, gains[1]).astype(bf16),
        grad_out.astype(bf16),
    )
    out_rows = take_rows(1, [my_block(row_slots[4 + mask]) for mask in range(4)], None, b_all)
    w_out = gather_z(out_rows)
    ctx_four = jnp.concatenate([ctx, ctx_y, ctx_x, far_low, far_high], axis=0)
    ctx_all = jnp.concatenate([ctx_four, swap(ctx_four, "c")], axis=0)

    w_cross_q = w_cross[:, :block]
    w_low = w_cross[:, block : 3 * block]
    w_high = w_cross[:, 3 * block :]
    ctx_low, ctx_high = ctx_all[:, :width], ctx_all[:, width:]
    ctx_kv = (matmul(ctx_low, w_low) + matmul(ctx_high, w_high)).astype(bf16)
    cross_q = matmul(b_all, w_cross_q)
    cross_q = split(cross_q.astype(bf16))
    cross_k, cross_v = split(ctx_kv[:, :block]), split(ctx_kv[:, block:])
    item = jnp.arange(slots * ctx_len) // ctx_len
    own_item = seg_all[:, :, None] == item[None, None, :]
    cross_p = probabilities(cross_q, cross_k, own_item)
    cross_low = cross_p.astype(bf16)
    cross_o = joined(weighted(cross_low, cross_v))
    h2 = h1 + chain_step(scatter_rows, matmul(cross_o, w_cross_out))
    c_all = chain_step(gather_rows, normalize(h2, gains[2]).astype(bf16))

    hidden = matmul(c_all, w_in)
    activated = gelu_tanh(hidden).astype(bf16)

    def sum_rows(value):
        value = with_layout_constraint(value, Layout(major_to_minor=(0, 1)))
        value = lax.psum_scatter(value, "z", scatter_dimension=0, tiled=True)
        return with_layout_constraint(value, Layout(major_to_minor=(0, 1)))

    def from_other(value, mask, keep_pair=None):
        return lax.ppermute(value, ALL_AXES, flip_pairs(mask, keep_pair))

    t_out = matmul_left(activated, d_ff).astype(bf16)
    g_out = sum_rows(t_out)
    d_act = matmul_right(after(d_ff, t_out), w_out)
    d_hidden = jax.vjp(gelu_tanh, hidden)[1](d_act)[0].astype(bf16)
    t_in = matmul_left(c_all, d_hidden).astype(bf16)
    g_in = sum_rows(t_in)
    d_c, mixed = chain_step(
        lambda one, two: (scatter_rows(one), scatter_rows(two)), matmul_right(d_hidden, w_in), matmul(activated, w_out)
    )
    layer_out = (h2 + mixed).astype(bf16)
    part_two, gain_grad_two = jax.vjp(normalize, h2, gains[2])[1](d_c)
    dh2 = grad_out + part_two
    d_cross_out, out_one, out_two = chain_step(
        lambda one, two: (gather_rows(one), from_other(two, 1), from_other(two, 2)),
        after(dh2.astype(bf16), t_in),
        g_out,
    )
    g_cross_out = matmul_left(cross_o, d_cross_out)

    def through(d_mixed, left, right, probs, probs_low, values):
        d_mixed = split(d_mixed.astype(bf16))
        d_probs = jnp.einsum("bqhd,bkhd->bhqk", d_mixed, values, preferred_element_type=f32)
        d_scores = (probs * (d_probs - jnp.sum(probs * d_probs, axis=-1, keepdims=True))).astype(bf16)
        d_left = joined(weighted(d_scores, right) * scale)
        d_right = joined(jnp.einsum("bhqk,bqhd->bkhd", d_scores, left, preferred_element_type=f32) * scale)
        d_values = joined(jnp.einsum("bhqk,bqhd->bkhd", probs_low, d_mixed, preferred_element_type=f32))
        return d_left, d_right, d_values

    d_cq, d_ck, d_cv = through(
        matmul_right(d_cross_out, w_cross_out), cross_q, cross_k, cross_p, cross_low, cross_v
    )
    d_ckv = jnp.concatenate([d_ck, d_cv], axis=1)
    t_cross = jnp.concatenate(
        [
            value.astype(bf16)
            for value in (matmul_left(b_all, d_cq), matmul_left(ctx_low, d_ckv), matmul_left(ctx_high, d_ckv))
        ],
        axis=1,
    )
    g_cross = sum_rows(t_cross)
    part = matmul_right(d_cq, w_cross_q)
    d_b, out_three = chain_step(lambda one, two: (scatter_rows(one), from_other(two, 3)), part, g_out)
    out_grads = jnp.stack([g_out, out_one, out_two, out_three])
    part_one, gain_grad_one = jax.vjp(normalize, h1, gains[1])[1](d_b)
    dh1 = dh2 + part_one
    d_self_out, in_grads = chain_step(
        lambda one, two: (gather_rows(one), spread_columns(two)), after(dh1.astype(bf16), t_cross), g_in
    )
    g_self_out = matmul_left(attended, d_self_out)
    t_outer = jnp.concatenate(
        [
            jnp.where(low_y, g_self_out, g_cross_out).astype(bf16),
            jnp.where(low_y, g_cross_out, g_self_out).astype(bf16),
        ],
        axis=0,
    )
    g_outer = sum_rows(after(t_outer, g_cross))
    d_mixed = matmul_right(after(d_self_out, t_outer, g_cross), w_self_out)
    d_q, d_k, d_v = through(d_mixed, query, keys, probs, probs_low, values)
    d_qkv = jnp.concatenate([d_q, d_k, d_v], axis=1)
    g_qkv = sum_rows(matmul_left(a_all, d_qkv).astype(bf16))

    def last_step(part, grads, gain_grad_one, gain_grad_two):
        part_zero, gain_grad_zero = jax.vjp(normalize, h0, gains[0])[1](scatter_rows(part))
        gain_grads = jnp.stack([gain_grad_zero, gain_grad_one, gain_grad_two])
        return part_zero, sum_everywhere(gain_grads), spread_columns(grads)

    part_zero, gain_total, cross_grads = chain_step(
        last_step, matmul_right(d_qkv, w_qkv), g_cross, gain_grad_one, gain_grad_two
    )
    grad_tokens = (dh1 + part_zero).astype(bf16)

    back_swap = [(target, source) for source, target in pair_swap]
    other_half = lax.ppermute(after(g_outer, cross_grads), ALL_AXES, back_swap)
    outer_grad = jnp.where(
        odd == 0,
        jnp.concatenate([g_outer, other_half], axis=0),
        jnp.concatenate([other_half, g_outer], axis=0),
    )
    by_tile = jnp.swapaxes(after(g_qkv, cross_grads).reshape(2, rows, 3, block), 1, 2)
    sent = jnp.broadcast_to(by_tile[:, None], (2, 4, 3, rows, block)).reshape(8, 3, rows, block)
    late_grads = lax.all_to_all(sent, PLANE, 0, 0, tiled=True).reshape(8 * 3, rows, block)
    place = np.arange(8)
    source_x, source_f = (place % 2)[None, :], ((place // 2)[None, :] - my_shift[:, None]) % 4
    other = source_f ^ f
    source = (other % 2) * 4 + (other // 2) * 2 + (source_x ^ x)
    column_of = np.array([0, 1, 2, 0, 0, 1, 3, 2, 4, 0, 0, 0, 0, 0, 0, 0, 0, 0], np.int32)
    my_column = jnp.sum(jnp.where(my_tile[:, None] == np.arange(n_tiles), column_of, 0), axis=1)
    in_layer = (my_tile >= 10)[:, None]
    column_place = source * 8 + jnp.where(in_layer, (place // 2)[None, :], my_column[:, None])
    row_source = ((z - my_shift) % 4) ^ f
    late = (my_used == 1) & ((my_tile < 4) | (my_tile == 9))
    early_mode = jnp.where(my_row == 1, 4, jnp.where(my_tile >= 10, 2, 3))
    early_mode = jnp.where(my_used == 0, 1, jnp.where(late, 0, early_mode))
    states = (master, moment_one, moment_two)
    slot = np.arange(cap, dtype=np.int32)
    early = None
    for first in (0, half_cap):
        chosen = slice(first, first + half_cap)
        early = adam_tiles(
            *states,
            [in_grads, cross_grads],
            [out_grads],
            slot[chosen],
            after(early_mode, outer_grad, sent)[chosen] if first else early_mode[chosen],
            column_place[chosen].reshape(-1),
            row_source[chosen],
            np.zeros(half_cap, np.int32),
            early,
        )

    outer_grads = jnp.stack(
        [outer_grad]
        + [from_other(outer_grad, mask, lambda zz, place, _: place % 4 in (zz, (zz + 2) % 4)) for mask in range(1, 4)]
    )
    n_late = 5
    order = jnp.sum(jnp.where(slot[None, :] < slot[:, None], late.astype(jnp.int32)[None, :], 0), axis=1)
    count_late = jnp.sum(late.astype(jnp.int32))
    step = np.arange(n_late)
    wanted = jnp.minimum(step, jnp.maximum(count_late - 1, 0))
    here = late[None, :] & (order[None, :] == wanted[:, None])

    def at_step(value):
        return jnp.sum(jnp.where(here, value.astype(jnp.int32)[None, :], 0), axis=1)

    hold = (step >= jnp.maximum(count_late, 1)).astype(jnp.int32)
    tile = at_step(my_tile)
    some = count_late > 0
    visit = jnp.where(some, at_step(slot), 0)
    first_mode = jnp.where(early_mode[0] == 4, 5, early_mode[0])
    late_mode = jnp.where(at_step(my_row) == 1, 6, 4)
    mode = jnp.where(hold == 1, 0, jnp.where(some, late_mode, first_mode))
    late_place = ((place % 2)[None, :] * 4 + (place // 2)[None, :]) * 3 + tile[:, None]
    late_place = jnp.where(some, late_place * 8, column_place[:1])
    new_w, new_m, new_v = adam_tiles(
        *states,
        [in_grads, cross_grads, late_grads],
        [out_grads, outer_grads],
        visit,
        mode,
        late_place.reshape(-1),
        jnp.where(some, at_step(row_source), row_source[0]),
        hold,
        early,
    )
    new_g, new_gm, new_gv = adam_update(gains, gain_one, gain_two, gain_total, rate_gain, 0.0)
    return (layer_out, grad_tokens, new_w, new_m, new_v, new_g, new_gm, new_gv)


def whole_body(
    tokens, cotangent, context, lengths, keep, owners, master, moment_one, moment_two, gains, gain_one, gain_two
):
    cap = master.shape[0]
    n_tiles = owners.shape[0]
    slot_of = owners * cap + ranks_of(owners)
    owner_rows = lax.all_gather(master.astype(bf16), "fsdp", axis=0, tiled=True)
    tiles = [
        lax.all_gather(
            lax.dynamic_index_in_dim(owner_rows, slot_of[tile], 0, keepdims=False), "dp", axis=0, tiled=True
        )
        for tile in range(n_tiles)
    ]
    w_in = jnp.concatenate(tiles[10:14], axis=1)
    w_out = jnp.concatenate(tiles[14:18], axis=0)
    count, width = tokens.shape
    head_dim = width // HEADS
    scale = head_dim ** (-0.5)
    seg = segments(lengths[0], count)
    live = keep == 1
    places = jnp.arange(count)

    def split(value):
        return value.astype(bf16).reshape(-1, HEADS, head_dim)

    def joined(value):
        return value.astype(bf16).reshape(-1, width)

    def probabilities(left, right, mask):
        scores = jnp.einsum("qhd,khd->hqk", left, right, preferred_element_type=f32) * scale
        scores = jnp.where(mask[None], scores, -1e30)
        expo = jnp.exp(scores - jnp.max(scores, axis=-1, keepdims=True))
        return expo / jnp.sum(expo, axis=-1, keepdims=True)

    def weighted(probs, right):
        return jnp.einsum("hqk,khd->qhd", probs, right, preferred_element_type=f32)

    def through(weights, d_out, left, right, probs, values):
        d_mixed = split(matmul_right(d_out, weights))
        d_probs = jnp.einsum("qhd,khd->hqk", d_mixed, values, preferred_element_type=f32)
        d_scores = (probs * (d_probs - jnp.sum(probs * d_probs, axis=-1, keepdims=True))).astype(bf16)
        d_left = joined(weighted(d_scores, right) * scale)
        d_right = joined(jnp.einsum("hqk,qhd->khd", d_scores, left, preferred_element_type=f32) * scale)
        d_values = joined(jnp.einsum("hqk,qhd->khd", probs.astype(bf16), d_mixed, preferred_element_type=f32))
        return d_left, d_right, d_values

    h0 = tokens.astype(f32)
    a_in = normalize(h0, gains[0]).astype(bf16)
    query, keys, values = (split(matmul(a_in, tiles[n])) for n in range(3))
    allowed = (seg[:, None] == seg[None, :]) & (live[None, :] | (places[:, None] == places[None, :]))
    probs = probabilities(query, keys, allowed)
    attended = joined(weighted(probs.astype(bf16), values))
    h1 = h0 + matmul(attended, tiles[3])
    b_in = normalize(h1, gains[1]).astype(bf16)
    slots, ctx_len, ctx_width = context.shape
    ctx = context.reshape(slots * ctx_len, ctx_width)
    ctx_low, ctx_high = ctx[:, :width], ctx[:, width:]
    cross_q = split(matmul(b_in, tiles[4]))
    cross_k = split(matmul(ctx_low, tiles[5]) + matmul(ctx_high, tiles[6]))
    cross_v = split(matmul(ctx_low, tiles[7]) + matmul(ctx_high, tiles[8]))
    item = jnp.arange(slots * ctx_len) // ctx_len
    cross_p = probabilities(cross_q, cross_k, seg[:, None] == item[None, :])
    cross_o = joined(weighted(cross_p.astype(bf16), cross_v))
    h2 = h1 + matmul(cross_o, tiles[9])
    c_in = normalize(h2, gains[2]).astype(bf16)
    hidden = matmul(c_in, w_in)
    activated = gelu_tanh(hidden).astype(bf16)
    layer_out = (h2 + matmul(activated, w_out)).astype(bf16)
    grad_out = cotangent.astype(f32) * live.astype(f32)[:, None]
    d_ff = grad_out.astype(bf16)
    d_hidden = jax.vjp(gelu_tanh, hidden)[1](matmul_right(d_ff, w_out))[0].astype(bf16)
    part_two, gain_grad_two = jax.vjp(normalize, h2, gains[2])[1](matmul_right(d_hidden, w_in))
    dh2 = grad_out + part_two
    d_cross_out = dh2.astype(bf16)
    d_cq, d_ck, d_cv = through(tiles[9], d_cross_out, cross_q, cross_k, cross_p, cross_v)
    part_one, gain_grad_one = jax.vjp(normalize, h1, gains[1])[1](matmul_right(d_cq, tiles[4]))
    dh1 = dh2 + part_one
    d_self_out = dh1.astype(bf16)
    d_q, d_k, d_v = through(tiles[3], d_self_out, query, keys, probs, values)
    d_a = matmul_right(d_q, tiles[0]) + matmul_right(d_k, tiles[1]) + matmul_right(d_v, tiles[2])
    part_zero, gain_grad_zero = jax.vjp(normalize, h0, gains[0])[1](d_a)
    grad_tokens = (dh1 + part_zero).astype(bf16)
    pairs = [
        (a_in, d_q),
        (a_in, d_k),
        (a_in, d_v),
        (attended, d_self_out),
        (b_in, d_cq),
        (ctx_low, d_ck),
        (ctx_high, d_ck),
        (ctx_low, d_cv),
        (ctx_high, d_cv),
        (cross_o, d_cross_out),
    ]
    for part in range(4):
        pairs.append((c_in, d_hidden[:, part * width : (part + 1) * width]))
    for part in range(4):
        pairs.append((activated[:, part * width : (part + 1) * width], d_ff))
    total_slots = lax.axis_size("fsdp") * cap
    placed = jnp.zeros((total_slots,) + master.shape[1:], bf16)
    for tile, (left, right) in enumerate(pairs):
        term = lax.psum_scatter(
            matmul_left(left, right).astype(bf16), "dp", scatter_dimension=0, tiled=True
        )
        placed = lax.dynamic_update_index_in_dim(placed, term, slot_of[tile], 0)
    owned = lax.psum_scatter(placed, "fsdp", scatter_dimension=0, tiled=True).astype(f32)
    my_slots = lax.axis_index("fsdp") * cap + jnp.arange(cap)
    used = jnp.any(slot_of[None, :] == my_slots[:, None], axis=1)[:, None, None]
    updated = adam_update(master, moment_one, moment_two, owned, rate_matrix, decay_rate)
    new_w, new_m, new_v = (jnp.where(used, value, 0.0) for value in updated)
    gain_grads = jnp.stack([gain_grad_zero, gain_grad_one, gain_grad_two])
    gain_total = lax.psum(gain_grads, ("dp", "fsdp"))
    new_g, new_gm, new_gv = adam_update(gains, gain_one, gain_two, gain_total, rate_gain, 0.0)
    return (layer_out, grad_tokens, new_w, new_m, new_v, new_g, new_gm, new_gv)


def solution(mesh):
    planes = mesh.shape["dp"] == 8 and mesh.shape["fsdp"] == 4
    if planes:
        used = Mesh(mesh.devices.reshape(4, 2, 2, 2), ALL_AXES)
        dp, fsdp, body = ("z", "x"), ("y", "c"), plane_body
    else:
        used, dp, fsdp, body = mesh, ("dp",), ("fsdp",), whole_body
    rows = P(dp + fsdp, None)
    tiles = P(fsdp, dp, None)
    return jax.shard_map(
        body,
        mesh=used,
        in_specs=(rows, rows, P(dp + fsdp, None, None), rows, P(dp + fsdp), P(), tiles, tiles, tiles, P(), P(), P()),
        out_specs=(rows, rows, tiles, tiles, tiles, P(), P(), P()),
        check_vma=False,
    )
```

```python
import jax
import jax.numpy as jnp
import numpy as np
from jax import lax
from jax.experimental import pallas as pl
from jax.experimental.layout import Layout, with_layout_constraint
from jax.experimental.pallas import tpu as pltpu
from jax.sharding import Mesh
from jax.sharding import PartitionSpec as P

HEADS = 16
STEP = 10

norm_eps = 1e-06
beta_one = 0.9
beta_two = 0.95
adam_eps = 1e-08
decay_rate = 0.1
rate_matrix = 0.1
rate_gain = 0.8

f32 = jnp.float32
bf16 = jnp.bfloat16

SHIFT = (0, 0, 0, 0, 2, 2, 2, 2, 2, 2, 0, 1, 2, 3, 0, 1, 2, 3)
ROW_TILES = (3, 9, 14, 15, 16, 17)
VMEM_LIMIT = 48 << 20


def normalize(h, gain):
    scale = lax.rsqrt(jnp.mean(h * h, axis=-1, keepdims=True) + norm_eps)
    return h * scale * gain


def gelu_tanh(u):
    return 0.5 * u * (1.0 + jnp.tanh(0.7978845608028654 * (u + 0.044715 * u * u * u)))


def matmul(left, right):
    return jnp.dot(left, right, preferred_element_type=f32)


def matmul_left(left, right):
    return lax.dot_general(left, right, (((0,), (0,)), ((), ())), preferred_element_type=f32)


def matmul_right(left, right):
    return lax.dot_general(left, right, (((1,), (1,)), ((), ())), preferred_element_type=f32)


def ranks_of(owners):
    order = jnp.arange(owners.shape[0])
    same = (owners[:, None] == owners[None, :]) & (order[None, :] < order[:, None])
    return jnp.sum(same.astype(jnp.int32), axis=1)


def segments(lengths, count):
    places = jnp.arange(count)
    end = jnp.zeros((), jnp.int32)
    seg = jnp.zeros((count,), jnp.int32)
    for item in range(lengths.shape[0]):
        end = end + lengths[item]
        seg = seg + (places >= end).astype(jnp.int32)
    return seg


def adam_update(weight, first, second, grad, rate, decay):
    first = beta_one * first + (1.0 - beta_one) * grad
    second = beta_two * second + (1.0 - beta_two) * grad * grad
    fix_one = 1.0 / (1.0 - beta_one**STEP)
    fix_two = 1.0 / (1.0 - beta_two**STEP)
    move = first * fix_one / (jnp.sqrt(second * fix_two) + adam_eps)
    return (weight - rate * (move + decay * weight), first, second)


def pack_columns(master, table, first_slot, slots):
    _, rows, columns = master.shape
    width = columns // 8

    def kernel(table_ref, in_ref, out_ref):
        slot = pl.program_id(0)
        for rank in range(8):
            start = pl.multiple_of(table_ref[slot * 8 + rank] * width, width)
            out_ref[rank, 0] = in_ref[0, :, pl.ds(start, width)].astype(bf16)

    return pl.pallas_call(
        kernel,
        out_shape=jax.ShapeDtypeStruct((8, slots, rows, width), bf16),
        grid_spec=pltpu.PrefetchScalarGridSpec(
            num_scalar_prefetch=1,
            grid=(slots,),
            in_specs=[pl.BlockSpec((1, rows, columns), lambda k, t: (first_slot + k, 0, 0))],
            out_specs=pl.BlockSpec((8, 1, rows, width), lambda k, t: (0, k, 0, 0)),
        ),
        compiler_params=pltpu.CompilerParams(vmem_limit_bytes=VMEM_LIMIT),
        name="pack_columns",
    )(table, master)


def pick_blocks(sources, which, index, count):
    _, rows, width = sources[0].shape
    n_src = len(sources)

    def kernel(which_ref, index_ref, *refs):
        place = pl.program_id(0) * 2 + pl.program_id(1)
        out_ref = refs[n_src]
        for number in range(n_src):

            @pl.when(which_ref[place] == number)
            def _():
                out_ref[...] = refs[number][0]

    def spec(number):
        def at(n, half, which, index):
            place = n * 2 + half
            return (jnp.where(which[place] == number, index[place], 0), 0, 0)

        return pl.BlockSpec((1, rows, width), at)

    return pl.pallas_call(
        kernel,
        out_shape=jax.ShapeDtypeStruct((2 * rows, count * width), bf16),
        grid_spec=pltpu.PrefetchScalarGridSpec(
            num_scalar_prefetch=2,
            grid=(count, 2),
            in_specs=[spec(number) for number in range(n_src)],
            out_specs=pl.BlockSpec((rows, width), lambda n, half, which, index: (half, n)),
        ),
        compiler_params=pltpu.CompilerParams(vmem_limit_bytes=VMEM_LIMIT),
        name="pick_blocks",
    )(which, index, *sources)


def adam_tiles(master, one, two, columns_from, rows_from, visit, mode, column_place, row_place, hold, previous=None):
    _, rows, columns = master.shape
    width = columns // 8
    n_visit = visit.shape[0]
    n_col, n_row = len(columns_from), len(rows_from)
    kept = () if previous is None else tuple(previous)

    def kernel(visit_ref, mode_ref, cp_ref, rp_ref, hold_ref, *refs):
        w_ref, m_ref, v_ref = refs[:3]
        grads = refs[3 : 3 + n_col + n_row]
        outs = refs[3 + n_col + n_row + len(kept) :]
        how = mode_ref[pl.program_id(0)]

        @pl.when(how == 1)
        def _():
            for ref in outs:
                ref[...] = jnp.zeros_like(ref)

        for number, grad_ref in enumerate(grads):

            @pl.when(how == number + 2)
            def _():
                grad = grad_ref[0].astype(f32)
                results = adam_update(w_ref[0], m_ref[0], v_ref[0], grad, rate_matrix, decay_rate)
                for ref, value in zip(outs, results, strict=True):
                    ref[0] = value

    def block_of(n, b, hold):
        return jnp.where(hold[n] == 1, 7, b)

    state = pl.BlockSpec((1, rows, width), lambda n, b, vi, mo, cp, rp, ho: (vi[n], 0, block_of(n, b, ho)))

    def column_spec(number):
        def at(n, b, vi, mo, cp, rp, ho):
            place = jnp.where(mo[n] == number + 2, cp[n * 8 + block_of(n, b, ho)], 0)
            return (place // 8, 0, place % 8)

        return pl.BlockSpec((1, rows, width), at)

    def row_spec(number):
        def at(n, b, vi, mo, cp, rp, ho):
            taken = mo[n] == number + 2
            return (jnp.where(taken, rp[n], 0), 0, jnp.where(taken, block_of(n, b, ho), 0))

        return pl.BlockSpec((1, rows, width), at)

    shape = jax.ShapeDtypeStruct(master.shape, f32)
    n_before = 5 + 3 + n_col + n_row
    return pl.pallas_call(
        kernel,
        out_shape=(shape, shape, shape),
        grid_spec=pltpu.PrefetchScalarGridSpec(
            num_scalar_prefetch=5,
            grid=(n_visit, 8),
            in_specs=[
                state,
                state,
                state,
                *(column_spec(number) for number in range(n_col)),
                *(row_spec(n_col + number) for number in range(n_row)),
                *(pl.BlockSpec(memory_space=pl.ANY) for _ in kept),
            ],
            out_specs=(state, state, state),
        ),
        input_output_aliases={n_before + n: n for n in range(len(kept))},
        compiler_params=pltpu.CompilerParams(vmem_limit_bytes=VMEM_LIMIT),
        cost_estimate=pl.CostEstimate(
            flops=30 * n_visit * rows * columns, bytes_accessed=26 * n_visit * rows * columns, transcendentals=0
        ),
        name="adam_tiles",
    )(visit, mode, column_place, row_place, hold, master, one, two, *columns_from, *rows_from, *kept)


def after(value, *others):
    return lax.optimization_barrier((value, *others))[0]


def swap(value, axis):
    return lax.ppermute(value, axis, [(0, 1), (1, 0)])


def gather_rows(value):
    half = value.shape[0] // 2
    over_x = swap(value, "x")
    over_y = swap(value, "y")
    far_low = swap(over_y[:half], "x")
    far_high = swap(over_x[half:], "y")
    four = jnp.concatenate([value, over_y, over_x, far_low, far_high], axis=0)
    return jnp.concatenate([four, swap(four, "c")], axis=0)


def spread_columns(value):
    rows = value.shape[0] // 2
    low = lax.axis_index("x") == 0
    upper, lower = value[:rows], value[rows:]
    two = jnp.stack([jnp.where(low, upper, lower), swap(jnp.where(low, lower, upper), "x")])
    four = jnp.concatenate([two, swap(two, "y")])
    return jnp.concatenate([four, swap(four, "c")])


def scatter_rows(part):
    rows, width = part.shape[0] // 8, part.shape[1]
    half = width // 2
    part = part.reshape(2, 2, 2, rows, width)
    chip = part[0] + swap(part[1], "c")
    low, high = chip[..., :half], chip[..., half:]
    low_two = low[:, 0] + swap(low[:, 1].astype(bf16), "y").astype(f32)
    high_two = high[0] + swap(high[1].astype(bf16), "x").astype(f32)
    low_one = low_two[0] + swap(low_two[1].astype(bf16), "x").astype(f32)
    high_one = high_two[0] + swap(high_two[1].astype(bf16), "y").astype(f32)
    return jnp.concatenate([low_one, high_one], axis=1)


def sum_everywhere(value):
    for axis in ("c", "y", "x"):
        value = value + swap(value, axis)
    for step in (1, 2):
        value = value + lax.ppermute(value, "z", [(z, z ^ step) for z in range(4)])
    return value


def flip_pairs(mask, keep=None):
    pairs = []
    for z in range(4):
        for place in range(8):
            target = place ^ mask
            if keep is None or keep(z, place, target):
                pairs.append((z * 8 + place, z * 8 + target))
    return pairs


ALL_AXES = ("z", "x", "y", "c")
PLANE = ("x", "y", "c")


def plane_body(
    tokens, cotangent, context, lengths, keep, owners, master, moment_one, moment_two, gains, gain_one, gain_two
):
    cap, rows, _ = master.shape
    count, width = tokens.shape
    heads_here = HEADS // 8
    head_dim = width // HEADS
    scale = head_dim ** (-0.5)
    block = width // 8
    z = lax.axis_index("z")
    x = lax.axis_index("x")
    f = lax.axis_index("y") * 2 + lax.axis_index("c")

    n_tiles = owners.shape[0]
    rank = ranks_of(owners)
    shift_of = np.array(SHIFT, np.int32)
    row_of = np.array([t in ROW_TILES for t in range(n_tiles)])
    all_slots = jnp.arange(4 * cap).reshape(4, cap)
    holds = (owners * cap + rank)[None, None, :] == all_slots[:, :, None]
    used_at = jnp.any(holds, axis=2)
    tile_at = jnp.sum(jnp.where(holds, np.arange(n_tiles, dtype=np.int32), 0), axis=2)
    shift_at = jnp.sum(jnp.where(holds, shift_of, 0), axis=2)
    row_at = jnp.any(holds & row_of, axis=2)
    mine = (jnp.arange(4) == f)[:, None]

    def my(value):
        return jnp.sum(jnp.where(mine, value.astype(jnp.int32), 0), axis=0)

    my_used, my_tile, my_shift, my_row = my(used_at), my(tile_at), my(shift_at), my(row_at)

    to_x = np.arange(8) // 4
    to_f = np.arange(8) % 4
    column_table = 2 * ((to_f[None, :] + my_shift[:, None]) % 4) + to_x[None, :]
    half_cap = cap // 2
    place = np.arange(4)

    def of_tiles(tiles, values):
        chosen = tiles[:, None] == np.arange(n_tiles)[None, :]
        return jnp.sum(jnp.where(chosen, values[None, :], 0), axis=1)

    column_tiles = jnp.concatenate([np.array([0, 1, 2, 4, 5, 7, 6, 8], np.int32), 10 + (place - f) % 4])
    column_part = jnp.repeat(of_tiles(column_tiles, rank // half_cap), 2)
    column_place = of_tiles(column_tiles, owners * half_cap + rank % half_cap)
    column_place = (column_place[:, None] + np.array([0, 4 * half_cap])[None, :]).reshape(-1)
    other_f = f ^ place
    outer_tiles = jnp.where(other_f == z, 3, 9)
    out_tiles = 14 + (z - other_f) % 4
    row_slots = of_tiles(jnp.concatenate([outer_tiles, out_tiles]), rank)
    row_owners = of_tiles(jnp.stack([outer_tiles[0], outer_tiles[2], out_tiles[0], out_tiles[2]]), owners)

    def exchange_columns(first, weights):
        table = column_table[first : first + half_cap].reshape(-1)
        got = lax.all_to_all(pack_columns(weights, table, first, half_cap), PLANE, 0, 0, tiled=True)
        return got.reshape(8 * half_cap, rows, block)

    def my_block(slot):
        return lax.dynamic_index_in_dim(master, slot, 0, keepdims=False).astype(bf16)

    h0 = tokens.astype(f32)
    outer_blocks = [my_block(row_slots[mask]) for mask in range(4)]
    out_blocks = [my_block(row_slots[4 + mask]) for mask in range(4)]
    a_in = normalize(h0, gains[0]).astype(bf16)
    received = [exchange_columns(0, after(master, column_part, column_place, row_slots, row_owners))]
    received = [after(received[0], a_in, *outer_blocks, *out_blocks)]

    def columns_here(first, count, parts):
        chosen = slice(2 * first, 2 * (first + count))
        return pick_blocks(received[:parts], column_part[chosen], column_place[chosen], count)

    def gather_z(value):
        return lax.all_gather(value, "z", axis=0, tiled=True)

    local = columns_here(0, 3, 1)
    w_qkv = gather_z(local)
    a_all = gather_rows(after(a_in, local))
    received.append(exchange_columns(half_cap, after(master, a_all)))

    def take_rows(kind, blocks, keep_pair):
        here, there = row_owners[2 * kind], row_owners[2 * kind + 1]
        core = f % 2
        from_core = swap(jnp.stack([blocks[1], blocks[3]]), "c")
        mine = jnp.where(here % 2 == core, blocks[0], from_core[0])
        across = jnp.where(there % 2 == core, blocks[2], from_core[1])
        from_y = lax.ppermute(across, ALL_AXES, flip_pairs(2, keep_pair))
        return jnp.where(here // 2 == f // 2, mine, from_y)

    def needs_outer(zz, place, target):
        return target % 4 in (zz, (zz + 2) % 4)

    outer = take_rows(0, [after(value, local) for value in outer_blocks], needs_outer)
    half_rows = rows // 2
    odd = z % 2
    to_pair = lax.dynamic_slice_in_dim(outer, (1 - odd) * half_rows, half_rows, 0)
    own_half = lax.dynamic_slice_in_dim(outer, odd * half_rows, half_rows, 0)
    pair_swap = [
        (zz * 8 + place, (zz ^ 1) * 8 + place)
        for zz in range(4)
        for place in range(8)
        if place % 4 in (zz, (zz + 2) % 4)
    ]
    from_pair = lax.ppermute(to_pair, ALL_AXES, pair_swap)
    has_outer = (f == z) | (f == (z + 2) % 4)
    outer_all = lax.all_gather(jnp.where(has_outer, own_half, from_pair), "z", axis=0, tiled=True)
    low_y = lax.axis_index("y") == 0
    w_self_out = jnp.where(low_y, outer_all[:rows], outer_all[rows:])
    w_cross_out = jnp.where(low_y, outer_all[rows:], outer_all[:rows])

    seg = segments(lengths[0], count)
    live = keep == 1
    code = seg * 2 + live.astype(jnp.int32)
    for axis in ("y", "x", "c"):
        code = jnp.concatenate([code, swap(code, axis)])
    seg_all = (code // 2).reshape(8, count)
    live_all = (code % 2 == 1).reshape(8, count)

    grad_out = cotangent.astype(f32) * live.astype(f32)[:, None]
    present = owners[0] >= 0

    def chain_step(move, *values):
        shapes = jax.eval_shape(move, *values)
        idle = jax.tree.map(lambda leaf: jnp.zeros(leaf.shape, leaf.dtype), shapes)
        return lax.cond(present, move, lambda *_: idle, *values)

    def split(value):
        return value.reshape(8, -1, heads_here, head_dim)

    qkv = matmul(a_all, w_qkv)
    qkv = qkv.astype(bf16)
    query, keys, values = (split(qkv[:, n * block : (n + 1) * block]) for n in range(3))
    places = jnp.arange(count)
    allowed = (seg_all[:, :, None] == seg_all[:, None, :]) & (
        live_all[:, None, :] | (places[:, None] == places[None, :])
    )

    def probabilities(left, right, mask):
        scores = jnp.einsum("bqhd,bkhd->bhqk", left, right, preferred_element_type=f32) * scale
        scores = jnp.where(mask[:, None], scores, -1e30)
        expo = jnp.exp(scores - jnp.max(scores, axis=-1, keepdims=True))
        return expo / jnp.sum(expo, axis=-1, keepdims=True)

    def weighted(probs, right):
        return jnp.einsum("bhqk,bkhd->bqhd", probs, right, preferred_element_type=f32)

    def joined(value):
        return value.astype(bf16).reshape(-1, block)

    probs = probabilities(query, keys, allowed)
    probs_low = probs.astype(bf16)
    attended = joined(weighted(probs_low, values))
    received[1] = after(received[1], attended)
    local_cross, local_in = columns_here(3, 5, 2), columns_here(8, 4, 2)
    w_cross = gather_z(local_cross)
    w_in = gather_z(local_in)
    slots, ctx_len, ctx_width = context.shape
    ctx = after(context.reshape(slots * ctx_len, ctx_width), local_cross, local_in)
    ctx_x, ctx_y = swap(ctx, "x"), swap(ctx, "y")
    out_rows = take_rows(1, [after(value, local_cross, local_in) for value in out_blocks], None)
    w_out = gather_z(out_rows)
    h1 = h0 + chain_step(scatter_rows, matmul(attended, w_self_out))
    half = slots * ctx_len // 2
    far_low = swap(after(ctx_y, h1)[:half], "x")
    far_high = swap(after(ctx_x, h1)[half:], "y")
    b_all, d_ff = chain_step(
        lambda one, two: (gather_rows(one), gather_rows(two)),
        normalize(h1, gains[1]).astype(bf16),
        grad_out.astype(bf16),
    )
    ctx_four = jnp.concatenate([ctx, ctx_y, ctx_x, far_low, far_high], axis=0)
    ctx_all = jnp.concatenate([ctx_four, swap(ctx_four, "c")], axis=0)

    w_cross_q = w_cross[:, :block]
    w_low = w_cross[:, block : 3 * block]
    w_high = w_cross[:, 3 * block :]
    ctx_low, ctx_high = ctx_all[:, :width], ctx_all[:, width:]
    ctx_kv = (matmul(ctx_low, w_low) + matmul(ctx_high, w_high)).astype(bf16)
    cross_q = matmul(b_all, w_cross_q)
    cross_q = split(cross_q.astype(bf16))
    cross_k, cross_v = split(ctx_kv[:, :block]), split(ctx_kv[:, block:])
    item = jnp.arange(slots * ctx_len) // ctx_len
    own_item = seg_all[:, :, None] == item[None, None, :]
    cross_p = probabilities(cross_q, cross_k, own_item)
    cross_low = cross_p.astype(bf16)
    cross_o = joined(weighted(cross_low, cross_v))
    h2 = h1 + chain_step(scatter_rows, matmul(cross_o, w_cross_out))
    c_all = chain_step(gather_rows, normalize(h2, gains[2]).astype(bf16))

    hidden = matmul(c_all, w_in)
    activated = gelu_tanh(hidden).astype(bf16)

    def sum_rows(value):
        value = with_layout_constraint(value, Layout(major_to_minor=(0, 1)))
        value = lax.psum_scatter(value, "z", scatter_dimension=0, tiled=True)
        return with_layout_constraint(value, Layout(major_to_minor=(0, 1)))

    def from_y(value, keep_pair=None):
        return jnp.stack([value, lax.ppermute(value, ALL_AXES, flip_pairs(2, keep_pair))])

    def with_core(pair):
        return jnp.concatenate([pair, swap(pair, "c")])

    t_out = matmul_left(activated, d_ff).astype(bf16)
    g_out = sum_rows(t_out)
    d_act = matmul_right(after(d_ff, t_out), w_out)
    d_hidden = jax.vjp(gelu_tanh, hidden)[1](d_act)[0].astype(bf16)
    t_in = matmul_left(c_all, d_hidden).astype(bf16)
    g_in = sum_rows(t_in)
    d_c, mixed = chain_step(
        lambda one, two: (scatter_rows(one), scatter_rows(two)), matmul_right(d_hidden, w_in), matmul(activated, w_out)
    )
    layer_out = (h2 + mixed).astype(bf16)
    part_two, gain_grad_two = jax.vjp(normalize, h2, gains[2])[1](d_c)
    dh2 = grad_out + part_two
    d_cross_out = chain_step(gather_rows, after(dh2.astype(bf16), t_in))
    g_cross_out = matmul_left(cross_o, d_cross_out)

    def through(d_mixed, left, right, probs, probs_low, values):
        d_mixed = split(d_mixed.astype(bf16))
        d_probs = jnp.einsum("bqhd,bkhd->bhqk", d_mixed, values, preferred_element_type=f32)
        d_scores = (probs * (d_probs - jnp.sum(probs * d_probs, axis=-1, keepdims=True))).astype(bf16)
        d_left = joined(weighted(d_scores, right) * scale)
        d_right = joined(jnp.einsum("bhqk,bqhd->bkhd", d_scores, left, preferred_element_type=f32) * scale)
        d_values = joined(jnp.einsum("bhqk,bqhd->bkhd", probs_low, d_mixed, preferred_element_type=f32))
        return d_left, d_right, d_values

    (d_cq, d_ck, d_cv), out_grads = chain_step(
        lambda one, two: (
            through(matmul_right(one, w_cross_out), cross_q, cross_k, cross_p, cross_low, cross_v),
            from_y(two),
        ),
        d_cross_out,
        g_out,
    )
    d_ckv = jnp.concatenate([d_ck, d_cv], axis=1)
    t_cross = jnp.concatenate(
        [
            value.astype(bf16)
            for value in (matmul_left(b_all, d_cq), matmul_left(ctx_low, d_ckv), matmul_left(ctx_high, d_ckv))
        ],
        axis=1,
    )
    g_cross = sum_rows(t_cross)
    part = matmul_right(d_cq, w_cross_q)
    d_b = chain_step(scatter_rows, part)
    part_one, gain_grad_one = jax.vjp(normalize, h1, gains[1])[1](d_b)
    dh1 = dh2 + part_one
    d_self_out = chain_step(gather_rows, after(dh1.astype(bf16), t_cross, g_in))
    g_self_out = matmul_left(attended, d_self_out)
    t_outer = jnp.concatenate(
        [
            jnp.where(low_y, g_self_out, g_cross_out).astype(bf16),
            jnp.where(low_y, g_cross_out, g_self_out).astype(bf16),
        ],
        axis=0,
    )
    g_outer = sum_rows(after(t_outer, g_cross))
    d_mixed = matmul_right(after(d_self_out, t_outer, g_cross), w_self_out)
    d_q, d_k, d_v = through(d_mixed, query, keys, probs, probs_low, values)
    d_qkv = jnp.concatenate([d_q, d_k, d_v], axis=1)
    g_qkv = sum_rows(matmul_left(a_all, d_qkv).astype(bf16))

    def last_step(part, in_sum, cross_sum, out_pair, gain_grad_one, gain_grad_two):
        part_zero, gain_grad_zero = jax.vjp(normalize, h0, gains[0])[1](scatter_rows(part))
        gain_grads = jnp.stack([gain_grad_zero, gain_grad_one, gain_grad_two])
        moved = spread_columns(in_sum), spread_columns(cross_sum), with_core(out_pair)
        return part_zero, sum_everywhere(gain_grads), *moved

    part_zero, gain_total, in_grads, cross_grads, out_grads = chain_step(
        last_step, matmul_right(d_qkv, w_qkv), g_in, g_cross, out_grads, gain_grad_one, gain_grad_two
    )
    grad_tokens = (dh1 + part_zero).astype(bf16)

    back_swap = [(target, source) for source, target in pair_swap]
    other_half = lax.ppermute(after(g_outer, cross_grads), ALL_AXES, back_swap)
    outer_grad = jnp.where(
        odd == 0,
        jnp.concatenate([g_outer, other_half], axis=0),
        jnp.concatenate([other_half, g_outer], axis=0),
    )
    by_tile = jnp.swapaxes(after(g_qkv, cross_grads).reshape(2, rows, 3, block), 1, 2)
    sent = jnp.broadcast_to(by_tile[:, None], (2, 4, 3, rows, block)).reshape(8, 3, rows, block)
    late_grads = lax.all_to_all(sent, PLANE, 0, 0, tiled=True).reshape(8 * 3, rows, block)
    place = np.arange(8)
    source_x, source_f = (place % 2)[None, :], ((place // 2)[None, :] - my_shift[:, None]) % 4
    other = source_f ^ f
    source = (other % 2) * 4 + (other // 2) * 2 + (source_x ^ x)
    column_of = np.array([0, 1, 2, 0, 0, 1, 3, 2, 4, 0, 0, 0, 0, 0, 0, 0, 0, 0], np.int32)
    my_column = jnp.sum(jnp.where(my_tile[:, None] == np.arange(n_tiles), column_of, 0), axis=1)
    in_layer = (my_tile >= 10)[:, None]
    column_place = source * 8 + jnp.where(in_layer, (place // 2)[None, :], my_column[:, None])
    other_row = ((z - my_shift) % 4) ^ f
    row_source = (other_row % 2) * 2 + other_row // 2
    late = (my_used == 1) & ((my_tile < 4) | (my_tile == 9))
    early_mode = jnp.where(my_row == 1, 4, jnp.where(my_tile >= 10, 2, 3))
    early_mode = jnp.where(my_used == 0, 1, jnp.where(late, 0, early_mode))
    states = (master, moment_one, moment_two)
    slot = np.arange(cap, dtype=np.int32)
    early = None
    for first in (0, half_cap):
        chosen = slice(first, first + half_cap)
        early = adam_tiles(
            *states,
            [in_grads, cross_grads],
            [out_grads],
            slot[chosen],
            after(early_mode, outer_grad, sent)[chosen] if first else early_mode[chosen],
            column_place[chosen].reshape(-1),
            row_source[chosen],
            np.zeros(half_cap, np.int32),
            early,
        )

    outer_grads = with_core(from_y(outer_grad, lambda zz, place, _: place % 4 in (zz, (zz + 2) % 4)))

    n_late = 5
    order = jnp.sum(jnp.where(slot[None, :] < slot[:, None], late.astype(jnp.int32)[None, :], 0), axis=1)
    count_late = jnp.sum(late.astype(jnp.int32))
    step = np.arange(n_late)
    wanted = jnp.minimum(step, jnp.maximum(count_late - 1, 0))
    here = late[None, :] & (order[None, :] == wanted[:, None])

    def at_step(value):
        return jnp.sum(jnp.where(here, value.astype(jnp.int32)[None, :], 0), axis=1)

    hold = (step >= jnp.maximum(count_late, 1)).astype(jnp.int32)
    tile = at_step(my_tile)
    some = count_late > 0
    visit = jnp.where(some, at_step(slot), 0)
    first_mode = jnp.where(early_mode[0] == 4, 5, early_mode[0])
    late_mode = jnp.where(at_step(my_row) == 1, 6, 4)
    mode = jnp.where(hold == 1, 0, jnp.where(some, late_mode, first_mode))
    late_place = ((place % 2)[None, :] * 4 + (place // 2)[None, :]) * 3 + tile[:, None]
    late_place = jnp.where(some, late_place * 8, column_place[:1])
    new_w, new_m, new_v = adam_tiles(
        *states,
        [in_grads, cross_grads, late_grads],
        [out_grads, outer_grads],
        visit,
        mode,
        late_place.reshape(-1),
        jnp.where(some, at_step(row_source), row_source[0]),
        hold,
        early,
    )
    new_g, new_gm, new_gv = adam_update(gains, gain_one, gain_two, gain_total, rate_gain, 0.0)
    return (layer_out, grad_tokens, new_w, new_m, new_v, new_g, new_gm, new_gv)


def whole_body(
    tokens, cotangent, context, lengths, keep, owners, master, moment_one, moment_two, gains, gain_one, gain_two
):
    cap = master.shape[0]
    n_tiles = owners.shape[0]
    slot_of = owners * cap + ranks_of(owners)
    owner_rows = lax.all_gather(master.astype(bf16), "fsdp", axis=0, tiled=True)
    tiles = [
        lax.all_gather(
            lax.dynamic_index_in_dim(owner_rows, slot_of[tile], 0, keepdims=False), "dp", axis=0, tiled=True
        )
        for tile in range(n_tiles)
    ]
    w_in = jnp.concatenate(tiles[10:14], axis=1)
    w_out = jnp.concatenate(tiles[14:18], axis=0)
    count, width = tokens.shape
    head_dim = width // HEADS
    scale = head_dim ** (-0.5)
    seg = segments(lengths[0], count)
    live = keep == 1
    places = jnp.arange(count)

    def split(value):
        return value.astype(bf16).reshape(-1, HEADS, head_dim)

    def joined(value):
        return value.astype(bf16).reshape(-1, width)

    def probabilities(left, right, mask):
        scores = jnp.einsum("qhd,khd->hqk", left, right, preferred_element_type=f32) * scale
        scores = jnp.where(mask[None], scores, -1e30)
        expo = jnp.exp(scores - jnp.max(scores, axis=-1, keepdims=True))
        return expo / jnp.sum(expo, axis=-1, keepdims=True)

    def weighted(probs, right):
        return jnp.einsum("hqk,khd->qhd", probs, right, preferred_element_type=f32)

    def through(weights, d_out, left, right, probs, values):
        d_mixed = split(matmul_right(d_out, weights))
        d_probs = jnp.einsum("qhd,khd->hqk", d_mixed, values, preferred_element_type=f32)
        d_scores = (probs * (d_probs - jnp.sum(probs * d_probs, axis=-1, keepdims=True))).astype(bf16)
        d_left = joined(weighted(d_scores, right) * scale)
        d_right = joined(jnp.einsum("hqk,qhd->khd", d_scores, left, preferred_element_type=f32) * scale)
        d_values = joined(jnp.einsum("hqk,qhd->khd", probs.astype(bf16), d_mixed, preferred_element_type=f32))
        return d_left, d_right, d_values

    h0 = tokens.astype(f32)
    a_in = normalize(h0, gains[0]).astype(bf16)
    query, keys, values = (split(matmul(a_in, tiles[n])) for n in range(3))
    allowed = (seg[:, None] == seg[None, :]) & (live[None, :] | (places[:, None] == places[None, :]))
    probs = probabilities(query, keys, allowed)
    attended = joined(weighted(probs.astype(bf16), values))
    h1 = h0 + matmul(attended, tiles[3])
    b_in = normalize(h1, gains[1]).astype(bf16)
    slots, ctx_len, ctx_width = context.shape
    ctx = context.reshape(slots * ctx_len, ctx_width)
    ctx_low, ctx_high = ctx[:, :width], ctx[:, width:]
    cross_q = split(matmul(b_in, tiles[4]))
    cross_k = split(matmul(ctx_low, tiles[5]) + matmul(ctx_high, tiles[6]))
    cross_v = split(matmul(ctx_low, tiles[7]) + matmul(ctx_high, tiles[8]))
    item = jnp.arange(slots * ctx_len) // ctx_len
    cross_p = probabilities(cross_q, cross_k, seg[:, None] == item[None, :])
    cross_o = joined(weighted(cross_p.astype(bf16), cross_v))
    h2 = h1 + matmul(cross_o, tiles[9])
    c_in = normalize(h2, gains[2]).astype(bf16)
    hidden = matmul(c_in, w_in)
    activated = gelu_tanh(hidden).astype(bf16)
    layer_out = (h2 + matmul(activated, w_out)).astype(bf16)
    grad_out = cotangent.astype(f32) * live.astype(f32)[:, None]
    d_ff = grad_out.astype(bf16)
    d_hidden = jax.vjp(gelu_tanh, hidden)[1](matmul_right(d_ff, w_out))[0].astype(bf16)
    part_two, gain_grad_two = jax.vjp(normalize, h2, gains[2])[1](matmul_right(d_hidden, w_in))
    dh2 = grad_out + part_two
    d_cross_out = dh2.astype(bf16)
    d_cq, d_ck, d_cv = through(tiles[9], d_cross_out, cross_q, cross_k, cross_p, cross_v)
    part_one, gain_grad_one = jax.vjp(normalize, h1, gains[1])[1](matmul_right(d_cq, tiles[4]))
    dh1 = dh2 + part_one
    d_self_out = dh1.astype(bf16)
    d_q, d_k, d_v = through(tiles[3], d_self_out, query, keys, probs, values)
    d_a = matmul_right(d_q, tiles[0]) + matmul_right(d_k, tiles[1]) + matmul_right(d_v, tiles[2])
    part_zero, gain_grad_zero = jax.vjp(normalize, h0, gains[0])[1](d_a)
    grad_tokens = (dh1 + part_zero).astype(bf16)
    pairs = [
        (a_in, d_q),
        (a_in, d_k),
        (a_in, d_v),
        (attended, d_self_out),
        (b_in, d_cq),
        (ctx_low, d_ck),
        (ctx_high, d_ck),
        (ctx_low, d_cv),
        (ctx_high, d_cv),
        (cross_o, d_cross_out),
    ]
    for part in range(4):
        pairs.append((c_in, d_hidden[:, part * width : (part + 1) * width]))
    for part in range(4):
        pairs.append((activated[:, part * width : (part + 1) * width], d_ff))
    total_slots = lax.axis_size("fsdp") * cap
    placed = jnp.zeros((total_slots,) + master.shape[1:], bf16)
    for tile, (left, right) in enumerate(pairs):
        term = lax.psum_scatter(
            matmul_left(left, right).astype(bf16), "dp", scatter_dimension=0, tiled=True
        )
        placed = lax.dynamic_update_index_in_dim(placed, term, slot_of[tile], 0)
    owned = lax.psum_scatter(placed, "fsdp", scatter_dimension=0, tiled=True).astype(f32)
    my_slots = lax.axis_index("fsdp") * cap + jnp.arange(cap)
    used = jnp.any(slot_of[None, :] == my_slots[:, None], axis=1)[:, None, None]
    updated = adam_update(master, moment_one, moment_two, owned, rate_matrix, decay_rate)
    new_w, new_m, new_v = (jnp.where(used, value, 0.0) for value in updated)
    gain_grads = jnp.stack([gain_grad_zero, gain_grad_one, gain_grad_two])
    gain_total = lax.psum(gain_grads, ("dp", "fsdp"))
    new_g, new_gm, new_gv = adam_update(gains, gain_one, gain_two, gain_total, rate_gain, 0.0)
    return (layer_out, grad_tokens, new_w, new_m, new_v, new_g, new_gm, new_gv)


def solution(mesh):
    planes = mesh.shape["dp"] == 8 and mesh.shape["fsdp"] == 4
    if planes:
        used = Mesh(mesh.devices.reshape(4, 2, 2, 2), ALL_AXES)
        dp, fsdp, body = ("z", "x"), ("y", "c"), plane_body
    else:
        used, dp, fsdp, body = mesh, ("dp",), ("fsdp",), whole_body
    rows = P(dp + fsdp, None)
    tiles = P(fsdp, dp, None)
    return jax.shard_map(
        body,
        mesh=used,
        in_specs=(rows, rows, P(dp + fsdp, None, None), rows, P(dp + fsdp), P(), tiles, tiles, tiles, P(), P(), P()),
        out_specs=(rows, rows, tiles, tiles, tiles, P(), P(), P()),
        check_vma=False,
    )
```

```python
import jax
import jax.numpy as jnp
import numpy as np
from jax import lax
from jax.experimental import pallas as pl
from jax.experimental.layout import Layout, with_layout_constraint
from jax.experimental.pallas import tpu as pltpu
from jax.sharding import Mesh
from jax.sharding import PartitionSpec as P

HEADS = 16
STEP = 10

norm_eps = 1e-06
beta_one = 0.9
beta_two = 0.95
adam_eps = 1e-08
decay_rate = 0.1
rate_matrix = 0.1
rate_gain = 0.8

f32 = jnp.float32
bf16 = jnp.bfloat16

SHIFT = (0, 0, 0, 0, 2, 2, 2, 2, 2, 2, 0, 1, 2, 3, 0, 1, 2, 3)
ROW_TILES = (3, 9, 14, 15, 16, 17)
VMEM_LIMIT = 48 << 20


def normalize(h, gain):
    scale = lax.rsqrt(jnp.mean(h * h, axis=-1, keepdims=True) + norm_eps)
    return h * scale * gain


def gelu_tanh(u):
    return 0.5 * u * (1.0 + jnp.tanh(0.7978845608028654 * (u + 0.044715 * u * u * u)))


def matmul(left, right):
    return jnp.dot(left, right, preferred_element_type=f32)


def matmul_left(left, right):
    return lax.dot_general(left, right, (((0,), (0,)), ((), ())), preferred_element_type=f32)


def matmul_right(left, right):
    return lax.dot_general(left, right, (((1,), (1,)), ((), ())), preferred_element_type=f32)


def ranks_of(owners):
    order = jnp.arange(owners.shape[0])
    same = (owners[:, None] == owners[None, :]) & (order[None, :] < order[:, None])
    return jnp.sum(same.astype(jnp.int32), axis=1)


def segments(lengths, count):
    places = jnp.arange(count)
    end = jnp.zeros((), jnp.int32)
    seg = jnp.zeros((count,), jnp.int32)
    for item in range(lengths.shape[0]):
        end = end + lengths[item]
        seg = seg + (places >= end).astype(jnp.int32)
    return seg


def adam_update(weight, first, second, grad, rate, decay):
    first = beta_one * first + (1.0 - beta_one) * grad
    second = beta_two * second + (1.0 - beta_two) * grad * grad
    fix_one = 1.0 / (1.0 - beta_one**STEP)
    fix_two = 1.0 / (1.0 - beta_two**STEP)
    move = first * fix_one / (jnp.sqrt(second * fix_two) + adam_eps)
    return (weight - rate * (move + decay * weight), first, second)


def pack_columns(master, table, first_slot, slots):
    _, rows, columns = master.shape
    width = columns // 8

    def kernel(table_ref, in_ref, out_ref):
        slot = pl.program_id(0)
        for rank in range(8):
            start = pl.multiple_of(table_ref[slot * 8 + rank] * width, width)
            out_ref[rank, 0] = in_ref[0, :, pl.ds(start, width)].astype(bf16)

    return pl.pallas_call(
        kernel,
        out_shape=jax.ShapeDtypeStruct((8, slots, rows, width), bf16),
        grid_spec=pltpu.PrefetchScalarGridSpec(
            num_scalar_prefetch=1,
            grid=(slots,),
            in_specs=[pl.BlockSpec((1, rows, columns), lambda k, t: (first_slot + k, 0, 0))],
            out_specs=pl.BlockSpec((8, 1, rows, width), lambda k, t: (0, k, 0, 0)),
        ),
        compiler_params=pltpu.CompilerParams(vmem_limit_bytes=VMEM_LIMIT),
        name="pack_columns",
    )(table, master)


def pick_blocks(sources, which, index, count):
    _, rows, width = sources[0].shape
    n_src = len(sources)

    def kernel(which_ref, index_ref, *refs):
        place = pl.program_id(0) * 2 + pl.program_id(1)
        out_ref = refs[n_src]
        for number in range(n_src):

            @pl.when(which_ref[place] == number)
            def _():
                out_ref[...] = refs[number][0]

    def spec(number):
        def at(n, half, which, index):
            place = n * 2 + half
            return (jnp.where(which[place] == number, index[place], 0), 0, 0)

        return pl.BlockSpec((1, rows, width), at)

    return pl.pallas_call(
        kernel,
        out_shape=jax.ShapeDtypeStruct((2 * rows, count * width), bf16),
        grid_spec=pltpu.PrefetchScalarGridSpec(
            num_scalar_prefetch=2,
            grid=(count, 2),
            in_specs=[spec(number) for number in range(n_src)],
            out_specs=pl.BlockSpec((rows, width), lambda n, half, which, index: (half, n)),
        ),
        compiler_params=pltpu.CompilerParams(vmem_limit_bytes=VMEM_LIMIT),
        name="pick_blocks",
    )(which, index, *sources)


def adam_tiles(master, one, two, columns_from, rows_from, visit, mode, column_place, row_place, hold, previous=None):
    _, rows, columns = master.shape
    width = columns // 8
    n_visit = visit.shape[0]
    n_col, n_row = len(columns_from), len(rows_from)
    kept = () if previous is None else tuple(previous)

    def kernel(visit_ref, mode_ref, cp_ref, rp_ref, hold_ref, *refs):
        w_ref, m_ref, v_ref = refs[:3]
        grads = refs[3 : 3 + n_col + n_row]
        outs = refs[3 + n_col + n_row + len(kept) :]
        how = mode_ref[pl.program_id(0)]

        @pl.when(how == 1)
        def _():
            for ref in outs:
                ref[...] = jnp.zeros_like(ref)

        for number, grad_ref in enumerate(grads):

            @pl.when(how == number + 2)
            def _():
                grad = grad_ref[0].astype(f32)
                results = adam_update(w_ref[0], m_ref[0], v_ref[0], grad, rate_matrix, decay_rate)
                for ref, value in zip(outs, results, strict=True):
                    ref[0] = value

    def block_of(n, b, hold):
        return jnp.where(hold[n] == 1, 7, b)

    state = pl.BlockSpec((1, rows, width), lambda n, b, vi, mo, cp, rp, ho: (vi[n], 0, block_of(n, b, ho)))

    def column_spec(number):
        def at(n, b, vi, mo, cp, rp, ho):
            place = jnp.where(mo[n] == number + 2, cp[n * 8 + block_of(n, b, ho)], 0)
            return (place // 8, 0, place % 8)

        return pl.BlockSpec((1, rows, width), at)

    def row_spec(number):
        def at(n, b, vi, mo, cp, rp, ho):
            taken = mo[n] == number + 2
            return (jnp.where(taken, rp[n], 0), 0, jnp.where(taken, block_of(n, b, ho), 0))

        return pl.BlockSpec((1, rows, width), at)

    shape = jax.ShapeDtypeStruct(master.shape, f32)
    n_before = 5 + 3 + n_col + n_row
    return pl.pallas_call(
        kernel,
        out_shape=(shape, shape, shape),
        grid_spec=pltpu.PrefetchScalarGridSpec(
            num_scalar_prefetch=5,
            grid=(n_visit, 8),
            in_specs=[
                state,
                state,
                state,
                *(column_spec(number) for number in range(n_col)),
                *(row_spec(n_col + number) for number in range(n_row)),
                *(pl.BlockSpec(memory_space=pl.ANY) for _ in kept),
            ],
            out_specs=(state, state, state),
        ),
        input_output_aliases={n_before + n: n for n in range(len(kept))},
        compiler_params=pltpu.CompilerParams(vmem_limit_bytes=VMEM_LIMIT),
        cost_estimate=pl.CostEstimate(
            flops=30 * n_visit * rows * columns, bytes_accessed=26 * n_visit * rows * columns, transcendentals=0
        ),
        name="adam_tiles",
    )(visit, mode, column_place, row_place, hold, master, one, two, *columns_from, *rows_from, *kept)


def after(value, *others):
    return lax.optimization_barrier((value, *others))[0]


def swap(value, axis):
    return lax.ppermute(value, axis, [(0, 1), (1, 0)])


def gather_rows(value):
    return gather_rest(value, swap(value, "x"), swap(value, "y"))


def gather_rest(value, over_x, over_y):
    half = value.shape[0] // 2
    far_low = swap(over_y[:half], "x")
    far_high = swap(over_x[half:], "y")
    four = jnp.concatenate([value, over_y, over_x, far_low, far_high], axis=0)
    return jnp.concatenate([four, swap(four, "c")], axis=0)


def spread_columns(value):
    rows = value.shape[0] // 2
    low = lax.axis_index("x") == 0
    upper, lower = value[:rows], value[rows:]
    two = jnp.stack([jnp.where(low, upper, lower), swap(jnp.where(low, lower, upper), "x")])
    four = jnp.concatenate([two, swap(two, "y")])
    return jnp.concatenate([four, swap(four, "c")])


def scatter_rows(part):
    rows, width = part.shape[0] // 8, part.shape[1]
    half = width // 2
    part = part.reshape(2, 2, 2, rows, width)
    chip = part[0] + swap(part[1], "c")
    low, high = chip[..., :half], chip[..., half:]
    low_two = low[:, 0] + swap(low[:, 1].astype(bf16), "y").astype(f32)
    high_two = high[0] + swap(high[1].astype(bf16), "x").astype(f32)
    low_one = low_two[0] + swap(low_two[1].astype(bf16), "x").astype(f32)
    high_one = high_two[0] + swap(high_two[1].astype(bf16), "y").astype(f32)
    return jnp.concatenate([low_one, high_one], axis=1)


def sum_everywhere(value):
    for axis in ("c", "y", "x"):
        value = value + swap(value, axis)
    for step in (1, 2):
        value = value + lax.ppermute(value, "z", [(z, z ^ step) for z in range(4)])
    return value


def flip_pairs(mask, keep=None):
    pairs = []
    for z in range(4):
        for place in range(8):
            target = place ^ mask
            if keep is None or keep(z, place, target):
                pairs.append((z * 8 + place, z * 8 + target))
    return pairs


ALL_AXES = ("z", "x", "y", "c")
PLANE = ("x", "y", "c")


def plane_body(
    tokens, cotangent, context, lengths, keep, owners, master, moment_one, moment_two, gains, gain_one, gain_two
):
    cap, rows, _ = master.shape
    count, width = tokens.shape
    heads_here = HEADS // 8
    head_dim = width // HEADS
    scale = head_dim ** (-0.5)
    block = width // 8
    z = lax.axis_index("z")
    x = lax.axis_index("x")
    f = lax.axis_index("y") * 2 + lax.axis_index("c")

    n_tiles = owners.shape[0]
    rank = ranks_of(owners)
    shift_of = np.array(SHIFT, np.int32)
    row_of = np.array([t in ROW_TILES for t in range(n_tiles)])
    all_slots = jnp.arange(4 * cap).reshape(4, cap)
    holds = (owners * cap + rank)[None, None, :] == all_slots[:, :, None]
    used_at = jnp.any(holds, axis=2)
    tile_at = jnp.sum(jnp.where(holds, np.arange(n_tiles, dtype=np.int32), 0), axis=2)
    shift_at = jnp.sum(jnp.where(holds, shift_of, 0), axis=2)
    row_at = jnp.any(holds & row_of, axis=2)
    mine = (jnp.arange(4) == f)[:, None]

    def my(value):
        return jnp.sum(jnp.where(mine, value.astype(jnp.int32), 0), axis=0)

    my_used, my_tile, my_shift, my_row = my(used_at), my(tile_at), my(shift_at), my(row_at)

    to_x = np.arange(8) // 4
    to_f = np.arange(8) % 4
    column_table = 2 * ((to_f[None, :] + my_shift[:, None]) % 4) + to_x[None, :]
    half_cap = cap // 2
    place = np.arange(4)

    def of_tiles(tiles, values):
        chosen = tiles[:, None] == np.arange(n_tiles)[None, :]
        return jnp.sum(jnp.where(chosen, values[None, :], 0), axis=1)

    column_tiles = jnp.concatenate([np.array([0, 1, 2, 4, 5, 7, 6, 8], np.int32), 10 + (place - f) % 4])
    column_part = jnp.repeat(of_tiles(column_tiles, rank // half_cap), 2)
    column_place = of_tiles(column_tiles, owners * half_cap + rank % half_cap)
    column_place = (column_place[:, None] + np.array([0, 4 * half_cap])[None, :]).reshape(-1)
    other_f = f ^ place
    outer_tiles = jnp.where(other_f == z, 3, 9)
    out_tiles = 14 + (z - other_f) % 4
    row_slots = of_tiles(jnp.concatenate([outer_tiles, out_tiles]), rank)
    row_owners = of_tiles(jnp.stack([outer_tiles[0], outer_tiles[2], out_tiles[0], out_tiles[2]]), owners)

    def exchange_columns(first, weights):
        table = column_table[first : first + half_cap].reshape(-1)
        got = lax.all_to_all(pack_columns(weights, table, first, half_cap), PLANE, 0, 0, tiled=True)
        return got.reshape(8 * half_cap, rows, block)

    def my_block(slot):
        return lax.dynamic_index_in_dim(master, slot, 0, keepdims=False).astype(bf16)

    h0 = tokens.astype(f32)
    outer_blocks = [my_block(row_slots[mask]) for mask in range(4)]
    out_blocks = [my_block(row_slots[4 + mask]) for mask in range(4)]
    a_in = normalize(h0, gains[0]).astype(bf16)
    received = [exchange_columns(0, after(master, column_part, column_place, row_slots, row_owners))]
    received = [after(received[0], a_in, *outer_blocks, *out_blocks)]

    def columns_here(first, count, parts):
        chosen = slice(2 * first, 2 * (first + count))
        return pick_blocks(received[:parts], column_part[chosen], column_place[chosen], count)

    def gather_z(value):
        return lax.all_gather(value, "z", axis=0, tiled=True)

    local = columns_here(0, 3, 1)
    w_qkv = gather_z(local)
    a_all = gather_rows(after(a_in, local))
    received.append(exchange_columns(half_cap, after(master, a_all)))

    def take_rows(kind, blocks, keep_pair):
        here, there = row_owners[2 * kind], row_owners[2 * kind + 1]
        core = f % 2
        from_core = swap(jnp.stack([blocks[1], blocks[3]]), "c")
        mine = jnp.where(here % 2 == core, blocks[0], from_core[0])
        across = jnp.where(there % 2 == core, blocks[2], from_core[1])
        from_y = lax.ppermute(across, ALL_AXES, flip_pairs(2, keep_pair))
        return jnp.where(here // 2 == f // 2, mine, from_y)

    def needs_outer(zz, place, target):
        return target % 4 in (zz, (zz + 2) % 4)

    outer = take_rows(0, [after(value, local) for value in outer_blocks], needs_outer)
    out_rows = take_rows(1, [after(value, local) for value in out_blocks], None)
    half_rows = rows // 2
    odd = z % 2
    to_pair = lax.dynamic_slice_in_dim(after(outer, a_all), (1 - odd) * half_rows, half_rows, 0)
    own_half = lax.dynamic_slice_in_dim(outer, odd * half_rows, half_rows, 0)
    pair_swap = [
        (zz * 8 + place, (zz ^ 1) * 8 + place)
        for zz in range(4)
        for place in range(8)
        if place % 4 in (zz, (zz + 2) % 4)
    ]
    from_pair = lax.ppermute(to_pair, ALL_AXES, pair_swap)
    has_outer = (f == z) | (f == (z + 2) % 4)
    outer_all = lax.all_gather(jnp.where(has_outer, own_half, from_pair), "z", axis=0, tiled=True)
    low_y = lax.axis_index("y") == 0
    w_self_out = jnp.where(low_y, outer_all[:rows], outer_all[rows:])
    w_cross_out = jnp.where(low_y, outer_all[rows:], outer_all[:rows])

    seg = segments(lengths[0], count)
    live = keep == 1
    code = seg * 2 + live.astype(jnp.int32)
    for axis in ("y", "x", "c"):
        code = jnp.concatenate([code, swap(code, axis)])
    seg_all = (code // 2).reshape(8, count)
    live_all = (code % 2 == 1).reshape(8, count)

    grad_out = cotangent.astype(f32) * live.astype(f32)[:, None]
    present = owners[0] >= 0

    def chain_step(move, *values):
        shapes = jax.eval_shape(move, *values)
        idle = jax.tree.map(lambda leaf: jnp.zeros(leaf.shape, leaf.dtype), shapes)
        return lax.cond(present, move, lambda *_: idle, *values)

    def split(value):
        return value.reshape(8, -1, heads_here, head_dim)

    qkv = matmul(a_all, w_qkv)
    qkv = qkv.astype(bf16)
    query, keys, values = (split(qkv[:, n * block : (n + 1) * block]) for n in range(3))
    places = jnp.arange(count)
    allowed = (seg_all[:, :, None] == seg_all[:, None, :]) & (
        live_all[:, None, :] | (places[:, None] == places[None, :])
    )

    def probabilities(left, right, mask):
        scores = jnp.einsum("bqhd,bkhd->bhqk", left, right, preferred_element_type=f32) * scale
        scores = jnp.where(mask[:, None], scores, -1e30)
        expo = jnp.exp(scores - jnp.max(scores, axis=-1, keepdims=True))
        return expo / jnp.sum(expo, axis=-1, keepdims=True)

    def weighted(probs, right):
        return jnp.einsum("bhqk,bkhd->bqhd", probs, right, preferred_element_type=f32)

    def joined(value):
        return value.astype(bf16).reshape(-1, block)

    probs = probabilities(query, keys, allowed)
    probs_low = probs.astype(bf16)
    mixed = weighted(probs_low, values).astype(bf16)
    attended = mixed.reshape(-1, block)
    received[1] = after(received[1], mixed)
    local_cross, local_in = columns_here(3, 5, 2), columns_here(8, 4, 2)
    w_cross = gather_z(local_cross)
    w_in = gather_z(local_in)
    w_out = gather_z(after(out_rows, local_cross, local_in))
    slots, ctx_len, ctx_width = context.shape
    ctx = context.reshape(slots * ctx_len, ctx_width)
    part = matmul(attended, w_self_out)
    h1, ctx_x, ctx_y = chain_step(
        lambda one, two: (scatter_rows(one), swap(two, "x"), swap(two, "y")), part, after(ctx, local_cross, local_in)
    )
    h1 = h0 + h1

    def with_context(one, two, own, over_x, over_y):
        return gather_rows(one), gather_rows(two), gather_rest(own, over_x, over_y)

    b_all, d_ff, ctx_all = chain_step(
        with_context, normalize(h1, gains[1]).astype(bf16), grad_out.astype(bf16), ctx, ctx_x, ctx_y
    )

    w_cross_q = w_cross[:, :block]
    w_low = w_cross[:, block : 3 * block]
    w_high = w_cross[:, 3 * block :]
    ctx_low, ctx_high = ctx_all[:, :width], ctx_all[:, width:]
    ctx_kv = (matmul(ctx_low, w_low) + matmul(ctx_high, w_high)).astype(bf16)
    cross_q = matmul(b_all, w_cross_q)
    cross_q = split(cross_q.astype(bf16))
    cross_k, cross_v = split(ctx_kv[:, :block]), split(ctx_kv[:, block:])
    item = jnp.arange(slots * ctx_len) // ctx_len
    own_item = seg_all[:, :, None] == item[None, None, :]
    cross_p = probabilities(cross_q, cross_k, own_item)
    cross_low = cross_p.astype(bf16)
    cross_o = joined(weighted(cross_low, cross_v))
    h2 = h1 + chain_step(scatter_rows, matmul(cross_o, w_cross_out))
    c_all = chain_step(gather_rows, normalize(h2, gains[2]).astype(bf16))

    hidden = matmul(c_all, w_in)
    activated = gelu_tanh(hidden).astype(bf16)

    def sum_rows(value):
        value = with_layout_constraint(value, Layout(major_to_minor=(0, 1)))
        value = lax.psum_scatter(value, "z", scatter_dimension=0, tiled=True)
        return with_layout_constraint(value, Layout(major_to_minor=(0, 1)))

    def from_y(value, keep_pair=None):
        return jnp.stack([value, lax.ppermute(value, ALL_AXES, flip_pairs(2, keep_pair))])

    def with_core(pair):
        return jnp.concatenate([pair, swap(pair, "c")])

    t_out = matmul_left(activated, d_ff).astype(bf16)
    g_out = sum_rows(t_out)
    d_act = matmul_right(after(d_ff, t_out), w_out)
    d_hidden = jax.vjp(gelu_tanh, hidden)[1](d_act)[0].astype(bf16)
    t_in = matmul_left(c_all, d_hidden).astype(bf16)
    g_in = sum_rows(t_in)
    d_c, out_sum = chain_step(
        lambda one, two: (scatter_rows(one), scatter_rows(two)), matmul_right(d_hidden, w_in), matmul(activated, w_out)
    )
    layer_out = (h2 + out_sum).astype(bf16)
    part_two, gain_grad_two = jax.vjp(normalize, h2, gains[2])[1](d_c)
    dh2 = grad_out + part_two
    d_cross_out = chain_step(gather_rows, after(dh2.astype(bf16), t_in))
    g_cross_out = matmul_left(cross_o, d_cross_out)

    def through(d_mixed, left, right, probs, probs_low, values):
        d_mixed = split(d_mixed.astype(bf16))
        d_probs = jnp.einsum("bqhd,bkhd->bhqk", d_mixed, values, preferred_element_type=f32)
        d_scores = (probs * (d_probs - jnp.sum(probs * d_probs, axis=-1, keepdims=True))).astype(bf16)
        d_left = joined(weighted(d_scores, right) * scale)
        d_right = joined(jnp.einsum("bhqk,bqhd->bkhd", d_scores, left, preferred_element_type=f32) * scale)
        d_values = joined(jnp.einsum("bhqk,bqhd->bkhd", probs_low, d_mixed, preferred_element_type=f32))
        return d_left, d_right, d_values

    (d_cq, d_ck, d_cv), out_grads = chain_step(
        lambda one, two: (
            through(matmul_right(one, w_cross_out), cross_q, cross_k, cross_p, cross_low, cross_v),
            from_y(two),
        ),
        d_cross_out,
        g_out,
    )
    d_ckv = jnp.concatenate([d_ck, d_cv], axis=1)
    t_cross = jnp.concatenate(
        [
            value.astype(bf16)
            for value in (matmul_left(b_all, d_cq), matmul_left(ctx_low, d_ckv), matmul_left(ctx_high, d_ckv))
        ],
        axis=1,
    )
    g_cross = sum_rows(t_cross)
    part = matmul_right(d_cq, w_cross_q)
    d_b = chain_step(scatter_rows, part)
    part_one, gain_grad_one = jax.vjp(normalize, h1, gains[1])[1](d_b)
    dh1 = dh2 + part_one
    d_self_out = chain_step(gather_rows, after(dh1.astype(bf16), t_cross, g_in))
    g_self_out = matmul_left(attended, d_self_out)
    t_outer = jnp.concatenate(
        [
            jnp.where(low_y, g_self_out, g_cross_out).astype(bf16),
            jnp.where(low_y, g_cross_out, g_self_out).astype(bf16),
        ],
        axis=0,
    )
    g_outer = sum_rows(after(t_outer, g_cross))
    (d_q, d_k, d_v), in_grads = chain_step(
        lambda one, two: (
            through(matmul_right(one, w_self_out), query, keys, probs, probs_low, values),
            spread_columns(two),
        ),
        after(d_self_out, t_outer, g_cross),
        g_in,
    )
    d_qkv = jnp.concatenate([d_q, d_k, d_v], axis=1)
    g_qkv = sum_rows(matmul_left(a_all, d_qkv).astype(bf16))

    back_swap = [(target, source) for source, target in pair_swap]

    def last_step(part, cross_sum, out_pair, half, gain_grad_one, gain_grad_two):
        part_zero, gain_grad_zero = jax.vjp(normalize, h0, gains[0])[1](scatter_rows(part))
        gain_grads = jnp.stack([gain_grad_zero, gain_grad_one, gain_grad_two])
        other_half = lax.ppermute(half, ALL_AXES, back_swap)
        in_order = jnp.where(odd == 0, jnp.stack([half, other_half]), jnp.stack([other_half, half]))
        outer_pair = from_y(in_order.reshape(rows, width), lambda zz, place, _: place % 4 in (zz, (zz + 2) % 4))
        moved = spread_columns(cross_sum), with_core(out_pair), with_core(outer_pair)
        return part_zero, sum_everywhere(gain_grads), *moved

    part_zero, gain_total, cross_grads, out_grads, outer_grads = chain_step(
        last_step, matmul_right(d_qkv, w_qkv), g_cross, out_grads, g_outer, gain_grad_one, gain_grad_two
    )
    grad_tokens = (dh1 + part_zero).astype(bf16)

    by_tile = jnp.swapaxes(after(g_qkv, cross_grads).reshape(2, rows, 3, block), 1, 2)
    sent = jnp.broadcast_to(by_tile[:, None], (2, 4, 3, rows, block)).reshape(8, 3, rows, block)
    late_grads = lax.all_to_all(sent, PLANE, 0, 0, tiled=True).reshape(8 * 3, rows, block)
    place = np.arange(8)
    source_x, source_f = (place % 2)[None, :], ((place // 2)[None, :] - my_shift[:, None]) % 4
    other = source_f ^ f
    source = (other % 2) * 4 + (other // 2) * 2 + (source_x ^ x)
    column_of = np.array([0, 1, 2, 0, 0, 1, 3, 2, 4, 0, 0, 0, 0, 0, 0, 0, 0, 0], np.int32)
    my_column = jnp.sum(jnp.where(my_tile[:, None] == np.arange(n_tiles), column_of, 0), axis=1)
    in_layer = (my_tile >= 10)[:, None]
    column_place = source * 8 + jnp.where(in_layer, (place // 2)[None, :], my_column[:, None])
    other_row = ((z - my_shift) % 4) ^ f
    row_source = (other_row % 2) * 2 + other_row // 2
    late = (my_used == 1) & ((my_tile < 4) | (my_tile == 9))
    early_mode = jnp.where(my_row == 1, 4, jnp.where(my_tile >= 10, 2, 3))
    early_mode = jnp.where(my_used == 0, 1, jnp.where(late, 0, early_mode))
    states = (master, moment_one, moment_two)
    slot = np.arange(cap, dtype=np.int32)
    early = None
    for first in (0, half_cap):
        chosen = slice(first, first + half_cap)
        early = adam_tiles(
            *states,
            [in_grads, cross_grads],
            [out_grads],
            slot[chosen],
            after(early_mode, sent)[chosen] if first else early_mode[chosen],
            column_place[chosen].reshape(-1),
            row_source[chosen],
            np.zeros(half_cap, np.int32),
            early,
        )

    n_late = 5
    order = jnp.sum(jnp.where(slot[None, :] < slot[:, None], late.astype(jnp.int32)[None, :], 0), axis=1)
    count_late = jnp.sum(late.astype(jnp.int32))
    step = np.arange(n_late)
    wanted = jnp.minimum(step, jnp.maximum(count_late - 1, 0))
    here = late[None, :] & (order[None, :] == wanted[:, None])

    def at_step(value):
        return jnp.sum(jnp.where(here, value.astype(jnp.int32)[None, :], 0), axis=1)

    hold = (step >= jnp.maximum(count_late, 1)).astype(jnp.int32)
    tile = at_step(my_tile)
    some = count_late > 0
    visit = jnp.where(some, at_step(slot), 0)
    first_mode = jnp.where(early_mode[0] == 4, 5, early_mode[0])
    late_mode = jnp.where(at_step(my_row) == 1, 6, 4)
    mode = jnp.where(hold == 1, 0, jnp.where(some, late_mode, first_mode))
    late_place = ((place % 2)[None, :] * 4 + (place // 2)[None, :]) * 3 + tile[:, None]
    late_place = jnp.where(some, late_place * 8, column_place[:1])
    new_w, new_m, new_v = adam_tiles(
        *states,
        [in_grads, cross_grads, late_grads],
        [out_grads, outer_grads],
        visit,
        mode,
        late_place.reshape(-1),
        jnp.where(some, at_step(row_source), row_source[0]),
        hold,
        early,
    )
    new_g, new_gm, new_gv = adam_update(gains, gain_one, gain_two, gain_total, rate_gain, 0.0)
    return (layer_out, grad_tokens, new_w, new_m, new_v, new_g, new_gm, new_gv)


def whole_body(
    tokens, cotangent, context, lengths, keep, owners, master, moment_one, moment_two, gains, gain_one, gain_two
):
    cap = master.shape[0]
    n_tiles = owners.shape[0]
    slot_of = owners * cap + ranks_of(owners)
    owner_rows = lax.all_gather(master.astype(bf16), "fsdp", axis=0, tiled=True)
    tiles = [
        lax.all_gather(
            lax.dynamic_index_in_dim(owner_rows, slot_of[tile], 0, keepdims=False), "dp", axis=0, tiled=True
        )
        for tile in range(n_tiles)
    ]
    w_in = jnp.concatenate(tiles[10:14], axis=1)
    w_out = jnp.concatenate(tiles[14:18], axis=0)
    count, width = tokens.shape
    head_dim = width // HEADS
    scale = head_dim ** (-0.5)
    seg = segments(lengths[0], count)
    live = keep == 1
    places = jnp.arange(count)

    def split(value):
        return value.astype(bf16).reshape(-1, HEADS, head_dim)

    def joined(value):
        return value.astype(bf16).reshape(-1, width)

    def probabilities(left, right, mask):
        scores = jnp.einsum("qhd,khd->hqk", left, right, preferred_element_type=f32) * scale
        scores = jnp.where(mask[None], scores, -1e30)
        expo = jnp.exp(scores - jnp.max(scores, axis=-1, keepdims=True))
        return expo / jnp.sum(expo, axis=-1, keepdims=True)

    def weighted(probs, right):
        return jnp.einsum("hqk,khd->qhd", probs, right, preferred_element_type=f32)

    def through(weights, d_out, left, right, probs, values):
        d_mixed = split(matmul_right(d_out, weights))
        d_probs = jnp.einsum("qhd,khd->hqk", d_mixed, values, preferred_element_type=f32)
        d_scores = (probs * (d_probs - jnp.sum(probs * d_probs, axis=-1, keepdims=True))).astype(bf16)
        d_left = joined(weighted(d_scores, right) * scale)
        d_right = joined(jnp.einsum("hqk,qhd->khd", d_scores, left, preferred_element_type=f32) * scale)
        d_values = joined(jnp.einsum("hqk,qhd->khd", probs.astype(bf16), d_mixed, preferred_element_type=f32))
        return d_left, d_right, d_values

    h0 = tokens.astype(f32)
    a_in = normalize(h0, gains[0]).astype(bf16)
    query, keys, values = (split(matmul(a_in, tiles[n])) for n in range(3))
    allowed = (seg[:, None] == seg[None, :]) & (live[None, :] | (places[:, None] == places[None, :]))
    probs = probabilities(query, keys, allowed)
    attended = joined(weighted(probs.astype(bf16), values))
    h1 = h0 + matmul(attended, tiles[3])
    b_in = normalize(h1, gains[1]).astype(bf16)
    slots, ctx_len, ctx_width = context.shape
    ctx = context.reshape(slots * ctx_len, ctx_width)
    ctx_low, ctx_high = ctx[:, :width], ctx[:, width:]
    cross_q = split(matmul(b_in, tiles[4]))
    cross_k = split(matmul(ctx_low, tiles[5]) + matmul(ctx_high, tiles[6]))
    cross_v = split(matmul(ctx_low, tiles[7]) + matmul(ctx_high, tiles[8]))
    item = jnp.arange(slots * ctx_len) // ctx_len
    cross_p = probabilities(cross_q, cross_k, seg[:, None] == item[None, :])
    cross_o = joined(weighted(cross_p.astype(bf16), cross_v))
    h2 = h1 + matmul(cross_o, tiles[9])
    c_in = normalize(h2, gains[2]).astype(bf16)
    hidden = matmul(c_in, w_in)
    activated = gelu_tanh(hidden).astype(bf16)
    layer_out = (h2 + matmul(activated, w_out)).astype(bf16)
    grad_out = cotangent.astype(f32) * live.astype(f32)[:, None]
    d_ff = grad_out.astype(bf16)
    d_hidden = jax.vjp(gelu_tanh, hidden)[1](matmul_right(d_ff, w_out))[0].astype(bf16)
    part_two, gain_grad_two = jax.vjp(normalize, h2, gains[2])[1](matmul_right(d_hidden, w_in))
    dh2 = grad_out + part_two
    d_cross_out = dh2.astype(bf16)
    d_cq, d_ck, d_cv = through(tiles[9], d_cross_out, cross_q, cross_k, cross_p, cross_v)
    part_one, gain_grad_one = jax.vjp(normalize, h1, gains[1])[1](matmul_right(d_cq, tiles[4]))
    dh1 = dh2 + part_one
    d_self_out = dh1.astype(bf16)
    d_q, d_k, d_v = through(tiles[3], d_self_out, query, keys, probs, values)
    d_a = matmul_right(d_q, tiles[0]) + matmul_right(d_k, tiles[1]) + matmul_right(d_v, tiles[2])
    part_zero, gain_grad_zero = jax.vjp(normalize, h0, gains[0])[1](d_a)
    grad_tokens = (dh1 + part_zero).astype(bf16)
    pairs = [
        (a_in, d_q),
        (a_in, d_k),
        (a_in, d_v),
        (attended, d_self_out),
        (b_in, d_cq),
        (ctx_low, d_ck),
        (ctx_high, d_ck),
        (ctx_low, d_cv),
        (ctx_high, d_cv),
        (cross_o, d_cross_out),
    ]
    for part in range(4):
        pairs.append((c_in, d_hidden[:, part * width : (part + 1) * width]))
    for part in range(4):
        pairs.append((activated[:, part * width : (part + 1) * width], d_ff))
    total_slots = lax.axis_size("fsdp") * cap
    placed = jnp.zeros((total_slots,) + master.shape[1:], bf16)
    for tile, (left, right) in enumerate(pairs):
        term = lax.psum_scatter(
            matmul_left(left, right).astype(bf16), "dp", scatter_dimension=0, tiled=True
        )
        placed = lax.dynamic_update_index_in_dim(placed, term, slot_of[tile], 0)
    owned = lax.psum_scatter(placed, "fsdp", scatter_dimension=0, tiled=True).astype(f32)
    my_slots = lax.axis_index("fsdp") * cap + jnp.arange(cap)
    used = jnp.any(slot_of[None, :] == my_slots[:, None], axis=1)[:, None, None]
    updated = adam_update(master, moment_one, moment_two, owned, rate_matrix, decay_rate)
    new_w, new_m, new_v = (jnp.where(used, value, 0.0) for value in updated)
    gain_grads = jnp.stack([gain_grad_zero, gain_grad_one, gain_grad_two])
    gain_total = lax.psum(gain_grads, ("dp", "fsdp"))
    new_g, new_gm, new_gv = adam_update(gains, gain_one, gain_two, gain_total, rate_gain, 0.0)
    return (layer_out, grad_tokens, new_w, new_m, new_v, new_g, new_gm, new_gv)


def solution(mesh):
    planes = mesh.shape["dp"] == 8 and mesh.shape["fsdp"] == 4
    if planes:
        used = Mesh(mesh.devices.reshape(4, 2, 2, 2), ALL_AXES)
        dp, fsdp, body = ("z", "x"), ("y", "c"), plane_body
    else:
        used, dp, fsdp, body = mesh, ("dp",), ("fsdp",), whole_body
    rows = P(dp + fsdp, None)
    tiles = P(fsdp, dp, None)
    return jax.shard_map(
        body,
        mesh=used,
        in_specs=(rows, rows, P(dp + fsdp, None, None), rows, P(dp + fsdp), P(), tiles, tiles, tiles, P(), P(), P()),
        out_specs=(rows, rows, tiles, tiles, tiles, P(), P(), P()),
        check_vma=False,
    )
```

```python
import jax
import jax.numpy as jnp
import numpy as np
from jax import lax
from jax.experimental import pallas as pl
from jax.experimental.layout import Layout, with_layout_constraint
from jax.experimental.pallas import tpu as pltpu
from jax.sharding import Mesh
from jax.sharding import PartitionSpec as P

HEADS = 16
STEP = 10

norm_eps = 1e-06
beta_one = 0.9
beta_two = 0.95
adam_eps = 1e-08
decay_rate = 0.1
rate_matrix = 0.1
rate_gain = 0.8

f32 = jnp.float32
bf16 = jnp.bfloat16

SHIFT = (0, 0, 0, 0, 2, 2, 2, 2, 2, 2, 0, 1, 2, 3, 0, 1, 2, 3)
ROW_TILES = (3, 9, 14, 15, 16, 17)
VMEM_LIMIT = 48 << 20


def normalize(h, gain):
    scale = lax.rsqrt(jnp.mean(h * h, axis=-1, keepdims=True) + norm_eps)
    return h * scale * gain


def gelu_tanh(u):
    return 0.5 * u * (1.0 + jnp.tanh(0.7978845608028654 * (u + 0.044715 * u * u * u)))


def matmul(left, right):
    return jnp.dot(left, right, preferred_element_type=f32)


def matmul_left(left, right):
    return lax.dot_general(left, right, (((0,), (0,)), ((), ())), preferred_element_type=f32)


def matmul_right(left, right):
    return lax.dot_general(left, right, (((1,), (1,)), ((), ())), preferred_element_type=f32)


def ranks_of(owners):
    order = jnp.arange(owners.shape[0])
    same = (owners[:, None] == owners[None, :]) & (order[None, :] < order[:, None])
    return jnp.sum(same.astype(jnp.int32), axis=1)


def segments(lengths, count):
    places = jnp.arange(count)
    end = jnp.zeros((), jnp.int32)
    seg = jnp.zeros((count,), jnp.int32)
    for item in range(lengths.shape[0]):
        end = end + lengths[item]
        seg = seg + (places >= end).astype(jnp.int32)
    return seg


def adam_update(weight, first, second, grad, rate, decay):
    first = beta_one * first + (1.0 - beta_one) * grad
    second = beta_two * second + (1.0 - beta_two) * grad * grad
    fix_one = 1.0 / (1.0 - beta_one**STEP)
    fix_two = 1.0 / (1.0 - beta_two**STEP)
    move = first * fix_one / (jnp.sqrt(second * fix_two) + adam_eps)
    return (weight - rate * (move + decay * weight), first, second)


def pack_columns(master, table, first_slot, slots):
    _, rows, columns = master.shape
    width = columns // 8

    def kernel(table_ref, in_ref, out_ref):
        slot = pl.program_id(0)
        for rank in range(8):
            start = pl.multiple_of(table_ref[slot * 8 + rank] * width, width)
            out_ref[rank, 0] = in_ref[0, :, pl.ds(start, width)].astype(bf16)

    return pl.pallas_call(
        kernel,
        out_shape=jax.ShapeDtypeStruct((8, slots, rows, width), bf16),
        grid_spec=pltpu.PrefetchScalarGridSpec(
            num_scalar_prefetch=1,
            grid=(slots,),
            in_specs=[pl.BlockSpec((1, rows, columns), lambda k, t: (first_slot + k, 0, 0))],
            out_specs=pl.BlockSpec((8, 1, rows, width), lambda k, t: (0, k, 0, 0)),
        ),
        compiler_params=pltpu.CompilerParams(vmem_limit_bytes=VMEM_LIMIT),
        name="pack_columns",
    )(table, master)


def pick_blocks(sources, which, index, count):
    _, rows, width = sources[0].shape
    n_src = len(sources)

    def kernel(which_ref, index_ref, *refs):
        place = pl.program_id(0) * 2 + pl.program_id(1)
        out_ref = refs[n_src]
        for number in range(n_src):

            @pl.when(which_ref[place] == number)
            def _():
                out_ref[...] = refs[number][0]

    def spec(number):
        def at(n, half, which, index):
            place = n * 2 + half
            return (jnp.where(which[place] == number, index[place], 0), 0, 0)

        return pl.BlockSpec((1, rows, width), at)

    return pl.pallas_call(
        kernel,
        out_shape=jax.ShapeDtypeStruct((2 * rows, count * width), bf16),
        grid_spec=pltpu.PrefetchScalarGridSpec(
            num_scalar_prefetch=2,
            grid=(count, 2),
            in_specs=[spec(number) for number in range(n_src)],
            out_specs=pl.BlockSpec((rows, width), lambda n, half, which, index: (half, n)),
        ),
        compiler_params=pltpu.CompilerParams(vmem_limit_bytes=VMEM_LIMIT),
        name="pick_blocks",
    )(which, index, *sources)


def pack_gradients(groups, which, column, rows, width, slots):
    n_src = len(groups)

    def kernel(which_ref, column_ref, *refs):
        place = pl.program_id(0) * slots + pl.program_id(1)
        out_ref = refs[n_src]
        for number in range(n_src):

            @pl.when(which_ref[place] == number)
            def _():
                out_ref[0, 0] = refs[number][...]

    def spec(number):
        def at(rank, k, which, column):
            place = rank * slots + k
            return (rank // 4, jnp.where(which[place] == number, column[place], 0))

        return pl.BlockSpec((rows, width), at)

    return pl.pallas_call(
        kernel,
        out_shape=jax.ShapeDtypeStruct((8, slots, rows, width), bf16),
        grid_spec=pltpu.PrefetchScalarGridSpec(
            num_scalar_prefetch=2,
            grid=(8, slots),
            in_specs=[spec(number) for number in range(n_src)],
            out_specs=pl.BlockSpec((1, 1, rows, width), lambda rank, k, which, column: (rank, k, 0, 0)),
        ),
        compiler_params=pltpu.CompilerParams(vmem_limit_bytes=VMEM_LIMIT),
        name="pack_gradients",
    )(which, column, *groups)


def adam_tiles(master, one, two, columns_from, rows_from, visit, mode, column_place, row_place, hold, previous=None):
    _, rows, columns = master.shape
    width = columns // 8
    n_visit = visit.shape[0]
    n_col, n_row = len(columns_from), len(rows_from)
    kept = () if previous is None else tuple(previous)

    def kernel(visit_ref, mode_ref, cp_ref, rp_ref, hold_ref, *refs):
        w_ref, m_ref, v_ref = refs[:3]
        grads = refs[3 : 3 + n_col + n_row]
        outs = refs[3 + n_col + n_row + len(kept) :]
        how = mode_ref[pl.program_id(0)]

        @pl.when(how == 1)
        def _():
            for ref in outs:
                ref[...] = jnp.zeros_like(ref)

        for number, grad_ref in enumerate(grads):

            @pl.when(how == number + 2)
            def _():
                grad = grad_ref[0].astype(f32)
                results = adam_update(w_ref[0], m_ref[0], v_ref[0], grad, rate_matrix, decay_rate)
                for ref, value in zip(outs, results, strict=True):
                    ref[0] = value

    def block_of(n, b, hold):
        return jnp.where(hold[n] == 1, 7, b)

    state = pl.BlockSpec((1, rows, width), lambda n, b, vi, mo, cp, rp, ho: (vi[n], 0, block_of(n, b, ho)))

    def column_spec(number):
        def at(n, b, vi, mo, cp, rp, ho):
            return (jnp.where(mo[n] == number + 2, cp[n * 8 + block_of(n, b, ho)], 0), 0, 0)

        return pl.BlockSpec((1, rows, width), at)

    def row_spec(number):
        def at(n, b, vi, mo, cp, rp, ho):
            taken = mo[n] == number + 2
            return (jnp.where(taken, rp[n], 0), 0, jnp.where(taken, block_of(n, b, ho), 0))

        return pl.BlockSpec((1, rows, width), at)

    shape = jax.ShapeDtypeStruct(master.shape, f32)
    n_before = 5 + 3 + n_col + n_row
    return pl.pallas_call(
        kernel,
        out_shape=(shape, shape, shape),
        grid_spec=pltpu.PrefetchScalarGridSpec(
            num_scalar_prefetch=5,
            grid=(n_visit, 8),
            in_specs=[
                state,
                state,
                state,
                *(column_spec(number) for number in range(n_col)),
                *(row_spec(n_col + number) for number in range(n_row)),
                *(pl.BlockSpec(memory_space=pl.ANY) for _ in kept),
            ],
            out_specs=(state, state, state),
        ),
        input_output_aliases={n_before + n: n for n in range(len(kept))},
        compiler_params=pltpu.CompilerParams(vmem_limit_bytes=VMEM_LIMIT),
        cost_estimate=pl.CostEstimate(
            flops=30 * n_visit * rows * columns, bytes_accessed=26 * n_visit * rows * columns, transcendentals=0
        ),
        name="adam_tiles",
    )(visit, mode, column_place, row_place, hold, master, one, two, *columns_from, *rows_from, *kept)


def after(value, *others):
    return lax.optimization_barrier((value, *others))[0]


def swap(value, axis):
    return lax.ppermute(value, axis, [(0, 1), (1, 0)])


def gather_rows(value):
    half = value.shape[0] // 2
    over_x = swap(value, "x")
    over_y = swap(value, "y")
    far_low = swap(over_y[:half], "x")
    far_high = swap(over_x[half:], "y")
    four = jnp.concatenate([value, over_y, over_x, far_low, far_high], axis=0)
    return jnp.concatenate([four, swap(four, "c")], axis=0)


def scatter_rows(part):
    rows, width = part.shape[0] // 8, part.shape[1]
    half = width // 2
    part = part.reshape(2, 2, 2, rows, width)
    chip = part[0] + swap(part[1], "c")
    low, high = chip[..., :half], chip[..., half:]
    low_two = low[:, 0] + swap(low[:, 1].astype(bf16), "y").astype(f32)
    high_two = high[0] + swap(high[1].astype(bf16), "x").astype(f32)
    low_one = low_two[0] + swap(low_two[1].astype(bf16), "x").astype(f32)
    high_one = high_two[0] + swap(high_two[1].astype(bf16), "y").astype(f32)
    return jnp.concatenate([low_one, high_one], axis=1)


def sum_everywhere(value):
    for axis in ("c", "y", "x"):
        value = value + swap(value, axis)
    for step in (1, 2):
        value = value + lax.ppermute(value, "z", [(z, z ^ step) for z in range(4)])
    return value


def flip_pairs(mask, keep=None):
    pairs = []
    for z in range(4):
        for place in range(8):
            target = place ^ mask
            if keep is None or keep(z, place, target):
                pairs.append((z * 8 + place, z * 8 + target))
    return pairs


ALL_AXES = ("z", "x", "y", "c")
PLANE = ("x", "y", "c")


def plane_body(
    tokens, cotangent, context, lengths, keep, owners, master, moment_one, moment_two, gains, gain_one, gain_two
):
    cap, rows, _ = master.shape
    count, width = tokens.shape
    heads_here = HEADS // 8
    head_dim = width // HEADS
    scale = head_dim ** (-0.5)
    block = width // 8
    z = lax.axis_index("z")
    x = lax.axis_index("x")
    f = lax.axis_index("y") * 2 + lax.axis_index("c")

    n_tiles = owners.shape[0]
    rank = ranks_of(owners)
    shift_of = np.array(SHIFT, np.int32)
    row_of = np.array([t in ROW_TILES for t in range(n_tiles)])
    all_slots = jnp.arange(4 * cap).reshape(4, cap)
    holds = (owners * cap + rank)[None, None, :] == all_slots[:, :, None]
    used_at = jnp.any(holds, axis=2)
    tile_at = jnp.sum(jnp.where(holds, np.arange(n_tiles, dtype=np.int32), 0), axis=2)
    shift_at = jnp.sum(jnp.where(holds, shift_of, 0), axis=2)
    row_at = jnp.any(holds & row_of, axis=2)
    mine = (jnp.arange(4) == f)[:, None]

    def my(value):
        return jnp.sum(jnp.where(mine, value.astype(jnp.int32), 0), axis=0)

    my_used, my_tile, my_shift, my_row = my(used_at), my(tile_at), my(shift_at), my(row_at)

    to_x = np.arange(8) // 4
    to_f = np.arange(8) % 4
    column_table = 2 * ((to_f[None, :] + my_shift[:, None]) % 4) + to_x[None, :]
    half_cap = cap // 2
    place = np.arange(4)

    def of_tiles(tiles, values):
        chosen = tiles[:, None] == np.arange(n_tiles)[None, :]
        return jnp.sum(jnp.where(chosen, values[None, :], 0), axis=1)

    column_tiles = jnp.concatenate([np.array([0, 1, 2, 4, 5, 7, 6, 8], np.int32), 10 + (place - f) % 4])
    column_part = jnp.repeat(of_tiles(column_tiles, rank // half_cap), 2)
    column_place = of_tiles(column_tiles, owners * half_cap + rank % half_cap)
    column_place = (column_place[:, None] + np.array([0, 4 * half_cap])[None, :]).reshape(-1)
    other_f = f ^ place
    outer_tiles = jnp.where(other_f == z, 3, 9)
    out_tiles = 14 + (z - other_f) % 4
    row_slots = of_tiles(jnp.concatenate([outer_tiles, out_tiles]), rank)
    row_owners = of_tiles(jnp.stack([outer_tiles[0], outer_tiles[2], out_tiles[0], out_tiles[2]]), owners)

    def pack_first(weights):
        return pack_columns(weights, column_table[:half_cap].reshape(-1), 0, half_cap)

    def pack_second(weights):
        return pack_columns(weights, column_table[half_cap:].reshape(-1), half_cap, half_cap)

    def my_block(slot):
        return lax.dynamic_index_in_dim(master, slot, 0, keepdims=False).astype(bf16)

    h0 = tokens.astype(f32)
    outer_blocks = [my_block(row_slots[mask]) for mask in range(4)]
    out_blocks = [my_block(row_slots[4 + mask]) for mask in range(4)]
    a_in = normalize(h0, gains[0]).astype(bf16)
    sent = pack_first(after(master, column_part, column_place, row_slots, row_owners))
    received = [lax.all_to_all(sent, PLANE, 0, 0, tiled=True).reshape(8 * half_cap, rows, block)]
    seg = segments(lengths[0], count)
    live = keep == 1
    code = seg * 2 + live.astype(jnp.int32)
    for axis in ("y", "x", "c"):
        code = jnp.concatenate([code, swap(code, axis)])
    seg_all = (code // 2).reshape(8, count)
    live_all = (code % 2 == 1).reshape(8, count)
    grad_out = cotangent.astype(f32) * live.astype(f32)[:, None]
    received = [after(received[0], a_in, code, *outer_blocks, *out_blocks)]

    def columns_here(first, count, parts):
        chosen = slice(2 * first, 2 * (first + count))
        return pick_blocks(received[:parts], column_part[chosen], column_place[chosen], count)

    def gather_z(value):
        return lax.all_gather(value, "z", axis=0, tiled=True)

    local = columns_here(0, 3, 1)
    w_qkv = gather_z(local)
    a_all = gather_rows(after(a_in, local))
    d_ff = gather_rows(after(grad_out.astype(bf16), local))
    sent = pack_second(after(master, a_all, d_ff))
    received.append(lax.all_to_all(sent, PLANE, 0, 0, tiled=True).reshape(8 * half_cap, rows, block))

    def take_rows(kind, blocks, keep_pair):
        here, there = row_owners[2 * kind], row_owners[2 * kind + 1]
        core = f % 2
        from_core = swap(jnp.stack([blocks[1], blocks[3]]), "c")
        mine = jnp.where(here % 2 == core, blocks[0], from_core[0])
        across = jnp.where(there % 2 == core, blocks[2], from_core[1])
        from_y = lax.ppermute(across, ALL_AXES, flip_pairs(2, keep_pair))
        return jnp.where(here // 2 == f // 2, mine, from_y)

    def needs_outer(zz, place, target):
        return target % 4 in (zz, (zz + 2) % 4)

    outer = take_rows(0, [after(value, local) for value in outer_blocks], needs_outer)
    out_rows = take_rows(1, [after(value, local) for value in out_blocks], None)
    half_rows = rows // 2
    odd = z % 2
    to_pair = lax.dynamic_slice_in_dim(after(outer, sent), (1 - odd) * half_rows, half_rows, 0)
    own_half = lax.dynamic_slice_in_dim(outer, odd * half_rows, half_rows, 0)
    pair_swap = [
        (zz * 8 + place, (zz ^ 1) * 8 + place)
        for zz in range(4)
        for place in range(8)
        if place % 4 in (zz, (zz + 2) % 4)
    ]
    from_pair = lax.ppermute(to_pair, ALL_AXES, pair_swap)
    has_outer = (f == z) | (f == (z + 2) % 4)
    outer_all = lax.all_gather(jnp.where(has_outer, own_half, from_pair), "z", axis=0, tiled=True)
    low_y = lax.axis_index("y") == 0
    w_self_out = jnp.where(low_y, outer_all[:rows], outer_all[rows:])
    w_cross_out = jnp.where(low_y, outer_all[rows:], outer_all[:rows])

    present = owners[0] >= 0

    def chain_step(move, *values):
        shapes = jax.eval_shape(move, *values)
        idle = jax.tree.map(lambda leaf: jnp.zeros(leaf.shape, leaf.dtype), shapes)
        return lax.cond(present, move, lambda *_: idle, *values)

    def split(value):
        return value.reshape(8, -1, heads_here, head_dim)

    qkv = matmul(a_all, w_qkv)
    qkv = qkv.astype(bf16)
    query, keys, values = (split(qkv[:, n * block : (n + 1) * block]) for n in range(3))
    places = jnp.arange(count)
    allowed = (seg_all[:, :, None] == seg_all[:, None, :]) & (
        live_all[:, None, :] | (places[:, None] == places[None, :])
    )

    def probabilities(left, right, mask):
        scores = jnp.einsum("bqhd,bkhd->bhqk", left, right, preferred_element_type=f32) * scale
        scores = jnp.where(mask[:, None], scores, -1e30)
        expo = jnp.exp(scores - jnp.max(scores, axis=-1, keepdims=True))
        return expo / jnp.sum(expo, axis=-1, keepdims=True)

    def weighted(probs, right):
        return jnp.einsum("bhqk,bkhd->bqhd", probs, right, preferred_element_type=f32)

    def joined(value):
        return value.astype(bf16).reshape(-1, block)

    probs = probabilities(query, keys, allowed)
    probs_low = probs.astype(bf16)
    mixed = weighted(probs_low, values).astype(bf16)
    attended = mixed.reshape(-1, block)
    received[1] = after(received[1], mixed)
    local_cross, local_in = columns_here(3, 5, 2), columns_here(8, 4, 2)
    w_cross = gather_z(local_cross)
    middle = width // 2
    halves = jnp.concatenate([out_rows[:, :middle], out_rows[:, middle:]], axis=0)
    w_layer = gather_z(jnp.concatenate([local_in, halves], axis=1))
    w_in = w_layer[:, : 4 * block]
    w_out = jnp.swapaxes(w_layer[:, 4 * block :].reshape(4, 2, rows, middle), 1, 2).reshape(4 * rows, width)

    slots, ctx_len, ctx_width = context.shape
    ctx = after(context.reshape(slots * ctx_len, ctx_width), local_cross, local_in)
    ctx_x, ctx_y = swap(ctx, "x"), swap(ctx, "y")
    h1 = h0 + chain_step(scatter_rows, matmul(attended, w_self_out))
    half = slots * ctx_len // 2
    far_low = swap(after(ctx_y, h1)[:half], "x")
    far_high = swap(after(ctx_x, h1)[half:], "y")
    b_all = chain_step(gather_rows, normalize(h1, gains[1]).astype(bf16))
    ctx_four = jnp.concatenate([ctx, ctx_y, ctx_x, far_low, far_high], axis=0)
    ctx_all = jnp.concatenate([ctx_four, swap(ctx_four, "c")], axis=0)

    w_cross_q = w_cross[:, :block]
    w_low = w_cross[:, block : 3 * block]
    w_high = w_cross[:, 3 * block :]
    ctx_low, ctx_high = ctx_all[:, :width], ctx_all[:, width:]
    ctx_kv = (matmul(ctx_low, w_low) + matmul(ctx_high, w_high)).astype(bf16)
    cross_q = matmul(b_all, w_cross_q)
    cross_q = split(cross_q.astype(bf16))
    cross_k, cross_v = split(ctx_kv[:, :block]), split(ctx_kv[:, block:])
    item = jnp.arange(slots * ctx_len) // ctx_len
    own_item = seg_all[:, :, None] == item[None, None, :]
    cross_p = probabilities(cross_q, cross_k, own_item)
    cross_low = cross_p.astype(bf16)
    cross_o = joined(weighted(cross_low, cross_v))
    h2 = h1 + chain_step(scatter_rows, matmul(cross_o, w_cross_out))
    c_all = chain_step(gather_rows, normalize(h2, gains[2]).astype(bf16))

    hidden = matmul(c_all, w_in)
    activated = gelu_tanh(hidden).astype(bf16)

    def sum_rows(value):
        value = with_layout_constraint(value, Layout(major_to_minor=(0, 1)))
        value = lax.psum_scatter(value, "z", scatter_dimension=0, tiled=True)
        return with_layout_constraint(value, Layout(major_to_minor=(0, 1)))

    def from_y(value, keep_pair=None):
        return jnp.stack([value, lax.ppermute(value, ALL_AXES, flip_pairs(2, keep_pair))])

    def with_core(pair):
        return jnp.concatenate([pair, swap(pair, "c")])

    t_out = matmul_left(activated, d_ff).astype(bf16)
    g_out = sum_rows(t_out)
    d_act = matmul_right(after(d_ff, t_out), w_out)
    d_hidden = jax.vjp(gelu_tanh, hidden)[1](d_act)[0].astype(bf16)
    t_in = matmul_left(c_all, d_hidden).astype(bf16)
    g_in = sum_rows(t_in)
    d_c, out_sum = chain_step(
        lambda one, two: (scatter_rows(one), scatter_rows(two)), matmul_right(d_hidden, w_in), matmul(activated, w_out)
    )
    layer_out = (h2 + out_sum).astype(bf16)
    part_two, gain_grad_two = jax.vjp(normalize, h2, gains[2])[1](d_c)
    dh2 = grad_out + part_two
    d_cross_out = chain_step(gather_rows, after(dh2.astype(bf16), t_in))
    g_cross_out = matmul_left(cross_o, d_cross_out)

    def through(d_mixed, left, right, probs, probs_low, values):
        d_mixed = split(d_mixed.astype(bf16))
        d_probs = jnp.einsum("bqhd,bkhd->bhqk", d_mixed, values, preferred_element_type=f32)
        d_scores = (probs * (d_probs - jnp.sum(probs * d_probs, axis=-1, keepdims=True))).astype(bf16)
        d_left = joined(weighted(d_scores, right) * scale)
        d_right = joined(jnp.einsum("bhqk,bqhd->bkhd", d_scores, left, preferred_element_type=f32) * scale)
        d_values = joined(jnp.einsum("bhqk,bqhd->bkhd", probs_low, d_mixed, preferred_element_type=f32))
        return d_left, d_right, d_values

    (d_cq, d_ck, d_cv), out_grads = chain_step(
        lambda one, two: (
            through(matmul_right(one, w_cross_out), cross_q, cross_k, cross_p, cross_low, cross_v),
            from_y(two),
        ),
        d_cross_out,
        g_out,
    )
    d_ckv = jnp.concatenate([d_ck, d_cv], axis=1)
    t_cross = jnp.concatenate(
        [
            value.astype(bf16)
            for value in (matmul_left(b_all, d_cq), matmul_left(ctx_low, d_ckv), matmul_left(ctx_high, d_ckv))
        ],
        axis=1,
    )
    g_cross = sum_rows(t_cross)
    part = matmul_right(d_cq, w_cross_q)
    d_b = chain_step(scatter_rows, part)
    part_one, gain_grad_one = jax.vjp(normalize, h1, gains[1])[1](d_b)
    dh1 = dh2 + part_one
    d_self_out = chain_step(gather_rows, after(dh1.astype(bf16), t_cross, g_in))
    g_self_out = matmul_left(attended, d_self_out)
    t_outer = jnp.concatenate(
        [
            jnp.where(low_y, g_self_out, g_cross_out).astype(bf16),
            jnp.where(low_y, g_cross_out, g_self_out).astype(bf16),
        ],
        axis=0,
    )
    g_outer = sum_rows(after(t_outer, g_cross))
    group_of = np.array([0, 0, 0, 0, 0, 0, 0, 0, 0, 0, 1, 1, 1, 1, 0, 0, 0, 0], np.int32)
    column_of = np.array([0, 0, 0, 0, 0, 1, 3, 2, 4, 0, 0, 1, 2, 3, 0, 0, 0, 0], np.int32)
    group_at = jnp.sum(jnp.where(holds, group_of, 0), axis=2)
    column_at = jnp.sum(jnp.where(holds, column_of, 0), axis=2)
    column_at = jnp.where(group_at == 1, (column_at + f) % 4, column_at)
    sent = pack_gradients(
        [g_cross, g_in], jnp.tile(group_at.reshape(-1), 2), jnp.tile(column_at.reshape(-1), 2), rows, block, cap
    )
    early_grads = lax.all_to_all(sent, PLANE, 0, 0, tiled=True).reshape(8 * cap, rows, block)
    d_mixed = matmul_right(after(d_self_out, t_outer, sent), w_self_out)
    d_q, d_k, d_v = through(d_mixed, query, keys, probs, probs_low, values)
    d_qkv = jnp.concatenate([d_q, d_k, d_v], axis=1)
    g_qkv = sum_rows(matmul_left(a_all, d_qkv).astype(bf16))

    def last_step(part, out_pair, gain_grad_one, gain_grad_two):
        part_zero, gain_grad_zero = jax.vjp(normalize, h0, gains[0])[1](scatter_rows(part))
        gain_grads = jnp.stack([gain_grad_zero, gain_grad_one, gain_grad_two])
        return part_zero, sum_everywhere(gain_grads), with_core(out_pair)

    part_zero, gain_total, out_grads = chain_step(
        last_step, matmul_right(d_qkv, w_qkv), out_grads, gain_grad_one, gain_grad_two
    )
    grad_tokens = (dh1 + part_zero).astype(bf16)

    by_tile = jnp.swapaxes(after(g_qkv, out_grads).reshape(2, rows, 3, block), 1, 2)
    sent = jnp.broadcast_to(by_tile[:, None], (2, 4, 3, rows, block)).reshape(8, 3, rows, block)
    late_grads = lax.all_to_all(sent, PLANE, 0, 0, tiled=True).reshape(8 * 3, rows, block)
    back_swap = [(target, source) for source, target in pair_swap]
    other_half = lax.ppermute(after(g_outer, out_grads), ALL_AXES, back_swap)
    outer_grad = jnp.where(
        odd == 0,
        jnp.concatenate([g_outer, other_half], axis=0),
        jnp.concatenate([other_half, g_outer], axis=0),
    )
    outer_pair = from_y(outer_grad, lambda zz, place, _: place % 4 in (zz, (zz + 2) % 4))
    outer_grads = with_core(outer_pair)

    place = np.arange(8)
    source_x, source_f = (place % 2)[None, :], ((place // 2)[None, :] - my_shift[:, None]) % 4
    slot = np.arange(cap, dtype=np.int32)
    column_place = (source_x * 4 + source_f) * cap + slot[:, None]
    other_row = ((z - my_shift) % 4) ^ f
    row_source = (other_row % 2) * 2 + other_row // 2
    late = (my_used == 1) & ((my_tile < 4) | (my_tile == 9))
    early_mode = jnp.where(my_used == 0, 1, jnp.where(late, 0, jnp.where(my_row == 1, 3, 2)))
    states = (master, moment_one, moment_two)
    early = None
    for first in (0, half_cap):
        chosen = slice(first, first + half_cap)
        early = adam_tiles(
            *states,
            [early_grads],
            [out_grads],
            slot[chosen],
            after(early_mode, outer_grad, sent)[chosen] if first else early_mode[chosen],
            column_place[chosen].reshape(-1),
            row_source[chosen],
            np.zeros(half_cap, np.int32),
            early,
        )

    n_late = 5
    order = jnp.sum(jnp.where(slot[None, :] < slot[:, None], late.astype(jnp.int32)[None, :], 0), axis=1)
    count_late = jnp.sum(late.astype(jnp.int32))
    step = np.arange(n_late)
    wanted = jnp.minimum(step, jnp.maximum(count_late - 1, 0))
    here = late[None, :] & (order[None, :] == wanted[:, None])

    def at_step(value):
        return jnp.sum(jnp.where(here, value.astype(jnp.int32)[None, :], 0), axis=1)

    hold = (step >= jnp.maximum(count_late, 1)).astype(jnp.int32)
    tile = at_step(my_tile)
    some = count_late > 0
    visit = jnp.where(some, at_step(slot), 0)
    first_mode = jnp.where(early_mode[0] == 3, 4, early_mode[0])
    late_mode = jnp.where(at_step(my_row) == 1, 5, 3)
    mode = jnp.where(hold == 1, 0, jnp.where(some, late_mode, first_mode))
    late_place = ((place % 2)[None, :] * 4 + (place // 2)[None, :]) * 3 + tile[:, None]
    late_place = jnp.where(some, late_place, column_place[:1])
    new_w, new_m, new_v = adam_tiles(
        *states,
        [early_grads, late_grads],
        [out_grads, outer_grads],
        visit,
        mode,
        late_place.reshape(-1),
        jnp.where(some, at_step(row_source), row_source[0]),
        hold,
        early,
    )
    new_g, new_gm, new_gv = adam_update(gains, gain_one, gain_two, gain_total, rate_gain, 0.0)
    return (layer_out, grad_tokens, new_w, new_m, new_v, new_g, new_gm, new_gv)


def whole_body(
    tokens, cotangent, context, lengths, keep, owners, master, moment_one, moment_two, gains, gain_one, gain_two
):
    cap = master.shape[0]
    n_tiles = owners.shape[0]
    slot_of = owners * cap + ranks_of(owners)
    owner_rows = lax.all_gather(master.astype(bf16), "fsdp", axis=0, tiled=True)
    tiles = [
        lax.all_gather(
            lax.dynamic_index_in_dim(owner_rows, slot_of[tile], 0, keepdims=False), "dp", axis=0, tiled=True
        )
        for tile in range(n_tiles)
    ]
    w_in = jnp.concatenate(tiles[10:14], axis=1)
    w_out = jnp.concatenate(tiles[14:18], axis=0)
    count, width = tokens.shape
    head_dim = width // HEADS
    scale = head_dim ** (-0.5)
    seg = segments(lengths[0], count)
    live = keep == 1
    places = jnp.arange(count)

    def split(value):
        return value.astype(bf16).reshape(-1, HEADS, head_dim)

    def joined(value):
        return value.astype(bf16).reshape(-1, width)

    def probabilities(left, right, mask):
        scores = jnp.einsum("qhd,khd->hqk", left, right, preferred_element_type=f32) * scale
        scores = jnp.where(mask[None], scores, -1e30)
        expo = jnp.exp(scores - jnp.max(scores, axis=-1, keepdims=True))
        return expo / jnp.sum(expo, axis=-1, keepdims=True)

    def weighted(probs, right):
        return jnp.einsum("hqk,khd->qhd", probs, right, preferred_element_type=f32)

    def through(weights, d_out, left, right, probs, values):
        d_mixed = split(matmul_right(d_out, weights))
        d_probs = jnp.einsum("qhd,khd->hqk", d_mixed, values, preferred_element_type=f32)
        d_scores = (probs * (d_probs - jnp.sum(probs * d_probs, axis=-1, keepdims=True))).astype(bf16)
        d_left = joined(weighted(d_scores, right) * scale)
        d_right = joined(jnp.einsum("hqk,qhd->khd", d_scores, left, preferred_element_type=f32) * scale)
        d_values = joined(jnp.einsum("hqk,qhd->khd", probs.astype(bf16), d_mixed, preferred_element_type=f32))
        return d_left, d_right, d_values

    h0 = tokens.astype(f32)
    a_in = normalize(h0, gains[0]).astype(bf16)
    query, keys, values = (split(matmul(a_in, tiles[n])) for n in range(3))
    allowed = (seg[:, None] == seg[None, :]) & (live[None, :] | (places[:, None] == places[None, :]))
    probs = probabilities(query, keys, allowed)
    attended = joined(weighted(probs.astype(bf16), values))
    h1 = h0 + matmul(attended, tiles[3])
    b_in = normalize(h1, gains[1]).astype(bf16)
    slots, ctx_len, ctx_width = context.shape
    ctx = context.reshape(slots * ctx_len, ctx_width)
    ctx_low, ctx_high = ctx[:, :width], ctx[:, width:]
    cross_q = split(matmul(b_in, tiles[4]))
    cross_k = split(matmul(ctx_low, tiles[5]) + matmul(ctx_high, tiles[6]))
    cross_v = split(matmul(ctx_low, tiles[7]) + matmul(ctx_high, tiles[8]))
    item = jnp.arange(slots * ctx_len) // ctx_len
    cross_p = probabilities(cross_q, cross_k, seg[:, None] == item[None, :])
    cross_o = joined(weighted(cross_p.astype(bf16), cross_v))
    h2 = h1 + matmul(cross_o, tiles[9])
    c_in = normalize(h2, gains[2]).astype(bf16)
    hidden = matmul(c_in, w_in)
    activated = gelu_tanh(hidden).astype(bf16)
    layer_out = (h2 + matmul(activated, w_out)).astype(bf16)
    grad_out = cotangent.astype(f32) * live.astype(f32)[:, None]
    d_ff = grad_out.astype(bf16)
    d_hidden = jax.vjp(gelu_tanh, hidden)[1](matmul_right(d_ff, w_out))[0].astype(bf16)
    part_two, gain_grad_two = jax.vjp(normalize, h2, gains[2])[1](matmul_right(d_hidden, w_in))
    dh2 = grad_out + part_two
    d_cross_out = dh2.astype(bf16)
    d_cq, d_ck, d_cv = through(tiles[9], d_cross_out, cross_q, cross_k, cross_p, cross_v)
    part_one, gain_grad_one = jax.vjp(normalize, h1, gains[1])[1](matmul_right(d_cq, tiles[4]))
    dh1 = dh2 + part_one
    d_self_out = dh1.astype(bf16)
    d_q, d_k, d_v = through(tiles[3], d_self_out, query, keys, probs, values)
    d_a = matmul_right(d_q, tiles[0]) + matmul_right(d_k, tiles[1]) + matmul_right(d_v, tiles[2])
    part_zero, gain_grad_zero = jax.vjp(normalize, h0, gains[0])[1](d_a)
    grad_tokens = (dh1 + part_zero).astype(bf16)
    pairs = [
        (a_in, d_q),
        (a_in, d_k),
        (a_in, d_v),
        (attended, d_self_out),
        (b_in, d_cq),
        (ctx_low, d_ck),
        (ctx_high, d_ck),
        (ctx_low, d_cv),
        (ctx_high, d_cv),
        (cross_o, d_cross_out),
    ]
    for part in range(4):
        pairs.append((c_in, d_hidden[:, part * width : (part + 1) * width]))
    for part in range(4):
        pairs.append((activated[:, part * width : (part + 1) * width], d_ff))
    total_slots = lax.axis_size("fsdp") * cap
    placed = jnp.zeros((total_slots,) + master.shape[1:], bf16)
    for tile, (left, right) in enumerate(pairs):
        term = lax.psum_scatter(
            matmul_left(left, right).astype(bf16), "dp", scatter_dimension=0, tiled=True
        )
        placed = lax.dynamic_update_index_in_dim(placed, term, slot_of[tile], 0)
    owned = lax.psum_scatter(placed, "fsdp", scatter_dimension=0, tiled=True).astype(f32)
    my_slots = lax.axis_index("fsdp") * cap + jnp.arange(cap)
    used = jnp.any(slot_of[None, :] == my_slots[:, None], axis=1)[:, None, None]
    updated = adam_update(master, moment_one, moment_two, owned, rate_matrix, decay_rate)
    new_w, new_m, new_v = (jnp.where(used, value, 0.0) for value in updated)
    gain_grads = jnp.stack([gain_grad_zero, gain_grad_one, gain_grad_two])
    gain_total = lax.psum(gain_grads, ("dp", "fsdp"))
    new_g, new_gm, new_gv = adam_update(gains, gain_one, gain_two, gain_total, rate_gain, 0.0)
    return (layer_out, grad_tokens, new_w, new_m, new_v, new_g, new_gm, new_gv)


def solution(mesh):
    planes = mesh.shape["dp"] == 8 and mesh.shape["fsdp"] == 4
    if planes:
        used = Mesh(mesh.devices.reshape(4, 2, 2, 2), ALL_AXES)
        dp, fsdp, body = ("z", "x"), ("y", "c"), plane_body
    else:
        used, dp, fsdp, body = mesh, ("dp",), ("fsdp",), whole_body
    rows = P(dp + fsdp, None)
    tiles = P(fsdp, dp, None)
    return jax.shard_map(
        body,
        mesh=used,
        in_specs=(rows, rows, P(dp + fsdp, None, None), rows, P(dp + fsdp), P(), tiles, tiles, tiles, P(), P(), P()),
        out_specs=(rows, rows, tiles, tiles, tiles, P(), P(), P()),
        check_vma=False,
    )
```

```python
import jax
import jax.numpy as jnp
import numpy as np
from jax import lax
from jax.experimental import pallas as pl
from jax.experimental.layout import Layout, with_layout_constraint
from jax.experimental.pallas import tpu as pltpu
from jax.sharding import Mesh
from jax.sharding import PartitionSpec as P

HEADS = 16
STEP = 10

norm_eps = 1e-06
beta_one = 0.9
beta_two = 0.95
adam_eps = 1e-08
decay_rate = 0.1
rate_matrix = 0.1
rate_gain = 0.8

f32 = jnp.float32
bf16 = jnp.bfloat16

SHIFT = (0, 0, 0, 0, 2, 2, 2, 2, 2, 2, 0, 1, 2, 3, 0, 1, 2, 3)
ROW_TILES = (3, 9, 14, 15, 16, 17)
VMEM_LIMIT = 48 << 20


def normalize(h, gain):
    scale = lax.rsqrt(jnp.mean(h * h, axis=-1, keepdims=True) + norm_eps)
    return h * scale * gain


def gelu_tanh(u):
    return 0.5 * u * (1.0 + jnp.tanh(0.7978845608028654 * (u + 0.044715 * u * u * u)))


def matmul(left, right):
    return jnp.dot(left, right, preferred_element_type=f32)


def matmul_left(left, right):
    return lax.dot_general(left, right, (((0,), (0,)), ((), ())), preferred_element_type=f32)


def matmul_right(left, right):
    return lax.dot_general(left, right, (((1,), (1,)), ((), ())), preferred_element_type=f32)


def ranks_of(owners):
    order = jnp.arange(owners.shape[0])
    same = (owners[:, None] == owners[None, :]) & (order[None, :] < order[:, None])
    return jnp.sum(same.astype(jnp.int32), axis=1)


def segments(lengths, count):
    places = jnp.arange(count)
    end = jnp.zeros((), jnp.int32)
    seg = jnp.zeros((count,), jnp.int32)
    for item in range(lengths.shape[0]):
        end = end + lengths[item]
        seg = seg + (places >= end).astype(jnp.int32)
    return seg


def adam_update(weight, first, second, grad, rate, decay):
    first = beta_one * first + (1.0 - beta_one) * grad
    second = beta_two * second + (1.0 - beta_two) * grad * grad
    fix_one = 1.0 / (1.0 - beta_one**STEP)
    fix_two = 1.0 / (1.0 - beta_two**STEP)
    move = first * fix_one / (jnp.sqrt(second * fix_two) + adam_eps)
    return (weight - rate * (move + decay * weight), first, second)


def pack_columns(master, table, first_slot, slots):
    _, rows, columns = master.shape
    width = columns // 8

    def kernel(table_ref, in_ref, out_ref):
        slot = pl.program_id(0)
        for rank in range(8):
            start = pl.multiple_of(table_ref[slot * 8 + rank] * width, width)
            out_ref[rank, 0] = in_ref[0, :, pl.ds(start, width)].astype(bf16)

    return pl.pallas_call(
        kernel,
        out_shape=jax.ShapeDtypeStruct((8, slots, rows, width), bf16),
        grid_spec=pltpu.PrefetchScalarGridSpec(
            num_scalar_prefetch=1,
            grid=(slots,),
            in_specs=[pl.BlockSpec((1, rows, columns), lambda k, t: (first_slot + k, 0, 0))],
            out_specs=pl.BlockSpec((8, 1, rows, width), lambda k, t: (0, k, 0, 0)),
        ),
        compiler_params=pltpu.CompilerParams(vmem_limit_bytes=VMEM_LIMIT),
        name="pack_columns",
    )(table, master)


def pick_blocks(sources, which, index, count):
    _, rows, width = sources[0].shape
    n_src = len(sources)

    def kernel(which_ref, index_ref, *refs):
        place = pl.program_id(0) * 2 + pl.program_id(1)
        out_ref = refs[n_src]
        for number in range(n_src):

            @pl.when(which_ref[place] == number)
            def _():
                out_ref[...] = refs[number][0]

    def spec(number):
        def at(n, half, which, index):
            place = n * 2 + half
            return (jnp.where(which[place] == number, index[place], 0), 0, 0)

        return pl.BlockSpec((1, rows, width), at)

    return pl.pallas_call(
        kernel,
        out_shape=jax.ShapeDtypeStruct((2 * rows, count * width), bf16),
        grid_spec=pltpu.PrefetchScalarGridSpec(
            num_scalar_prefetch=2,
            grid=(count, 2),
            in_specs=[spec(number) for number in range(n_src)],
            out_specs=pl.BlockSpec((rows, width), lambda n, half, which, index: (half, n)),
        ),
        compiler_params=pltpu.CompilerParams(vmem_limit_bytes=VMEM_LIMIT),
        name="pick_blocks",
    )(which, index, *sources)


def pack_gradients(groups, which, column, rows, width, slots):
    places = [(rank, k) for rank in range(8) for k in range(slots)]

    def kernel(which_ref, column_ref, *refs):
        out_ref, sems = refs[len(groups)], refs[len(groups) + 1]
        for place, (rank, k) in enumerate(places):
            for number in range(len(groups)):

                @pl.when(which_ref[place] == number)
                def _():
                    start = pl.multiple_of(column_ref[place] * width, width)
                    source = refs[number].at[pl.ds(rank // 4 * rows, rows), pl.ds(start, width)]
                    pltpu.make_async_copy(source, out_ref.at[rank, k], sems.at[place]).start()

        for place, (rank, k) in enumerate(places):
            source = refs[0].at[pl.ds(0, rows), pl.ds(0, width)]
            pltpu.make_async_copy(source, out_ref.at[rank, k], sems.at[place]).wait()

    return pl.pallas_call(
        kernel,
        out_shape=jax.ShapeDtypeStruct((8, slots, rows, width), bf16),
        in_specs=[pl.BlockSpec(memory_space=pltpu.SMEM)] * 2 + [pl.BlockSpec(memory_space=pl.ANY)] * len(groups),
        out_specs=pl.BlockSpec(memory_space=pl.ANY),
        scratch_shapes=[pltpu.SemaphoreType.DMA((len(places),))],
        name="pack_gradients",
    )(which, column, *groups)


def adam_tiles(master, one, two, columns_from, rows_from, visit, mode, column_place, row_place, hold, previous=None):
    _, rows, columns = master.shape
    width = columns // 8
    n_visit = visit.shape[0]
    n_col, n_row = len(columns_from), len(rows_from)
    kept = () if previous is None else tuple(previous)

    def kernel(visit_ref, mode_ref, cp_ref, rp_ref, hold_ref, *refs):
        w_ref, m_ref, v_ref = refs[:3]
        grads = refs[3 : 3 + n_col + n_row]
        outs = refs[3 + n_col + n_row + len(kept) :]
        how = mode_ref[pl.program_id(0)]

        @pl.when(how == 1)
        def _():
            for ref in outs:
                ref[...] = jnp.zeros_like(ref)

        for number, grad_ref in enumerate(grads):

            @pl.when(how == number + 2)
            def _():
                grad = grad_ref[0].astype(f32)
                results = adam_update(w_ref[0], m_ref[0], v_ref[0], grad, rate_matrix, decay_rate)
                for ref, value in zip(outs, results, strict=True):
                    ref[0] = value

    def block_of(n, b, hold):
        return jnp.where(hold[n] == 1, 7, b)

    state = pl.BlockSpec((1, rows, width), lambda n, b, vi, mo, cp, rp, ho: (vi[n], 0, block_of(n, b, ho)))

    def column_spec(number):
        def at(n, b, vi, mo, cp, rp, ho):
            return (jnp.where(mo[n] == number + 2, cp[n * 8 + block_of(n, b, ho)], 0), 0, 0)

        return pl.BlockSpec((1, rows, width), at)

    def row_spec(number):
        def at(n, b, vi, mo, cp, rp, ho):
            taken = mo[n] == number + 2
            return (jnp.where(taken, rp[n], 0), 0, jnp.where(taken, block_of(n, b, ho), 0))

        return pl.BlockSpec((1, rows, width), at)

    shape = jax.ShapeDtypeStruct(master.shape, f32)
    n_before = 5 + 3 + n_col + n_row
    return pl.pallas_call(
        kernel,
        out_shape=(shape, shape, shape),
        grid_spec=pltpu.PrefetchScalarGridSpec(
            num_scalar_prefetch=5,
            grid=(n_visit, 8),
            in_specs=[
                state,
                state,
                state,
                *(column_spec(number) for number in range(n_col)),
                *(row_spec(n_col + number) for number in range(n_row)),
                *(pl.BlockSpec(memory_space=pl.ANY) for _ in kept),
            ],
            out_specs=(state, state, state),
        ),
        input_output_aliases={n_before + n: n for n in range(len(kept))},
        compiler_params=pltpu.CompilerParams(vmem_limit_bytes=VMEM_LIMIT),
        cost_estimate=pl.CostEstimate(
            flops=30 * n_visit * rows * columns, bytes_accessed=26 * n_visit * rows * columns, transcendentals=0
        ),
        name="adam_tiles",
    )(visit, mode, column_place, row_place, hold, master, one, two, *columns_from, *rows_from, *kept)


def after(value, *others):
    return lax.optimization_barrier((value, *others))[0]


def swap(value, axis):
    return lax.ppermute(value, axis, [(0, 1), (1, 0)])


def gather_rows(value):
    half = value.shape[0] // 2
    over_x = swap(value, "x")
    over_y = swap(value, "y")
    far_low = swap(over_y[:half], "x")
    far_high = swap(over_x[half:], "y")
    four = jnp.concatenate([value, over_y, over_x, far_low, far_high], axis=0)
    return jnp.concatenate([four, swap(four, "c")], axis=0)


def scatter_rows(part):
    rows, width = part.shape[0] // 8, part.shape[1]
    half = width // 2
    part = part.reshape(2, 2, 2, rows, width)
    chip = part[0] + swap(part[1], "c")
    low, high = chip[..., :half], chip[..., half:]
    low_two = low[:, 0] + swap(low[:, 1].astype(bf16), "y").astype(f32)
    high_two = high[0] + swap(high[1].astype(bf16), "x").astype(f32)
    low_one = low_two[0] + swap(low_two[1].astype(bf16), "x").astype(f32)
    high_one = high_two[0] + swap(high_two[1].astype(bf16), "y").astype(f32)
    return jnp.concatenate([low_one, high_one], axis=1)


def sum_everywhere(value):
    for axis in ("c", "y", "x"):
        value = value + swap(value, axis)
    for step in (1, 2):
        value = value + lax.ppermute(value, "z", [(z, z ^ step) for z in range(4)])
    return value


def flip_pairs(mask, keep=None):
    pairs = []
    for z in range(4):
        for place in range(8):
            target = place ^ mask
            if keep is None or keep(z, place, target):
                pairs.append((z * 8 + place, z * 8 + target))
    return pairs


ALL_AXES = ("z", "x", "y", "c")
PLANE = ("x", "y", "c")


def plane_body(
    tokens, cotangent, context, lengths, keep, owners, master, moment_one, moment_two, gains, gain_one, gain_two
):
    cap, rows, _ = master.shape
    count, width = tokens.shape
    heads_here = HEADS // 8
    head_dim = width // HEADS
    scale = head_dim ** (-0.5)
    block = width // 8
    z = lax.axis_index("z")
    x = lax.axis_index("x")
    f = lax.axis_index("y") * 2 + lax.axis_index("c")

    n_tiles = owners.shape[0]
    rank = ranks_of(owners)
    shift_of = np.array(SHIFT, np.int32)
    row_of = np.array([t in ROW_TILES for t in range(n_tiles)])
    all_slots = jnp.arange(4 * cap).reshape(4, cap)
    holds = (owners * cap + rank)[None, None, :] == all_slots[:, :, None]
    used_at = jnp.any(holds, axis=2)
    tile_at = jnp.sum(jnp.where(holds, np.arange(n_tiles, dtype=np.int32), 0), axis=2)
    shift_at = jnp.sum(jnp.where(holds, shift_of, 0), axis=2)
    row_at = jnp.any(holds & row_of, axis=2)
    mine = (jnp.arange(4) == f)[:, None]

    def my(value):
        return jnp.sum(jnp.where(mine, value.astype(jnp.int32), 0), axis=0)

    my_used, my_tile, my_shift, my_row = my(used_at), my(tile_at), my(shift_at), my(row_at)

    to_x = np.arange(8) // 4
    to_f = np.arange(8) % 4
    column_table = 2 * ((to_f[None, :] + my_shift[:, None]) % 4) + to_x[None, :]
    half_cap = cap // 2
    place = np.arange(4)

    def of_tiles(tiles, values):
        chosen = tiles[:, None] == np.arange(n_tiles)[None, :]
        return jnp.sum(jnp.where(chosen, values[None, :], 0), axis=1)

    column_tiles = jnp.concatenate([np.array([0, 1, 2, 4, 5, 7, 6, 8], np.int32), 10 + (place - f) % 4])
    column_part = jnp.repeat(of_tiles(column_tiles, rank // half_cap), 2)
    column_place = of_tiles(column_tiles, owners * half_cap + rank % half_cap)
    column_place = (column_place[:, None] + np.array([0, 4 * half_cap])[None, :]).reshape(-1)
    other_f = f ^ place
    outer_tiles = jnp.where(other_f == z, 3, 9)
    out_tiles = 14 + (z - other_f) % 4
    row_slots = of_tiles(jnp.concatenate([outer_tiles, out_tiles]), rank)
    row_owners = of_tiles(jnp.stack([outer_tiles[0], outer_tiles[2], out_tiles[0], out_tiles[2]]), owners)

    def pack_first(weights):
        return pack_columns(weights, column_table[:half_cap].reshape(-1), 0, half_cap)

    def pack_second(weights):
        return pack_columns(weights, column_table[half_cap:].reshape(-1), half_cap, half_cap)

    def my_block(slot):
        return lax.dynamic_index_in_dim(master, slot, 0, keepdims=False).astype(bf16)

    h0 = tokens.astype(f32)
    outer_blocks = [my_block(row_slots[mask]) for mask in range(4)]
    out_blocks = [my_block(row_slots[4 + mask]) for mask in range(4)]
    a_in = normalize(h0, gains[0]).astype(bf16)
    sent = pack_first(after(master, column_part, column_place, row_slots, row_owners))
    received = [lax.all_to_all(sent, PLANE, 0, 0, tiled=True).reshape(8 * half_cap, rows, block)]
    seg = segments(lengths[0], count)
    live = keep == 1
    code = seg * 2 + live.astype(jnp.int32)
    for axis in ("y", "x", "c"):
        code = jnp.concatenate([code, swap(code, axis)])
    seg_all = (code // 2).reshape(8, count)
    live_all = (code % 2 == 1).reshape(8, count)
    grad_out = cotangent.astype(f32) * live.astype(f32)[:, None]
    received = [after(received[0], a_in, code, *outer_blocks, *out_blocks)]

    def columns_here(first, count, parts):
        chosen = slice(2 * first, 2 * (first + count))
        return pick_blocks(received[:parts], column_part[chosen], column_place[chosen], count)

    def gather_z(value):
        return lax.all_gather(value, "z", axis=0, tiled=True)

    local = columns_here(0, 3, 1)
    w_qkv = gather_z(local)

    def take_rows(kind, blocks, keep_pair):
        here, there = row_owners[2 * kind], row_owners[2 * kind + 1]
        core = f % 2
        from_core = swap(jnp.stack([blocks[1], blocks[3]]), "c")
        mine = jnp.where(here % 2 == core, blocks[0], from_core[0])
        across = jnp.where(there % 2 == core, blocks[2], from_core[1])
        from_y = lax.ppermute(across, ALL_AXES, flip_pairs(2, keep_pair))
        return jnp.where(here // 2 == f // 2, mine, from_y)

    def needs_outer(zz, place, target):
        return target % 4 in (zz, (zz + 2) % 4)

    outer = take_rows(0, [after(value, local) for value in outer_blocks], needs_outer)
    a_all = gather_rows(after(a_in, outer))
    d_ff = gather_rows(after(grad_out.astype(bf16), outer))
    out_rows = take_rows(1, [after(value, outer) for value in out_blocks], None)
    sent = pack_second(after(master, a_all, d_ff, out_rows))
    received.append(lax.all_to_all(sent, PLANE, 0, 0, tiled=True).reshape(8 * half_cap, rows, block))
    half_rows = rows // 2
    odd = z % 2
    to_pair = lax.dynamic_slice_in_dim(outer, (1 - odd) * half_rows, half_rows, 0)
    own_half = lax.dynamic_slice_in_dim(outer, odd * half_rows, half_rows, 0)
    pair_swap = [
        (zz * 8 + place, (zz ^ 1) * 8 + place)
        for zz in range(4)
        for place in range(8)
        if place % 4 in (zz, (zz + 2) % 4)
    ]
    from_pair = lax.ppermute(to_pair, ALL_AXES, pair_swap)
    has_outer = (f == z) | (f == (z + 2) % 4)
    outer_all = lax.all_gather(jnp.where(has_outer, own_half, from_pair), "z", axis=0, tiled=True)
    low_y = lax.axis_index("y") == 0
    w_self_out = jnp.where(low_y, outer_all[:rows], outer_all[rows:])
    w_cross_out = jnp.where(low_y, outer_all[rows:], outer_all[:rows])

    present = owners[0] >= 0

    def chain_step(move, *values):
        shapes = jax.eval_shape(move, *values)
        idle = jax.tree.map(lambda leaf: jnp.zeros(leaf.shape, leaf.dtype), shapes)
        return lax.cond(present, move, lambda *_: idle, *values)

    def split(value):
        return value.reshape(8, -1, heads_here, head_dim)

    qkv = matmul(a_all, w_qkv)
    qkv = qkv.astype(bf16)
    query, keys, values = (split(qkv[:, n * block : (n + 1) * block]) for n in range(3))
    places = jnp.arange(count)
    allowed = (seg_all[:, :, None] == seg_all[:, None, :]) & (
        live_all[:, None, :] | (places[:, None] == places[None, :])
    )

    def probabilities(left, right, mask):
        scores = jnp.einsum("bqhd,bkhd->bhqk", left, right, preferred_element_type=f32) * scale
        scores = jnp.where(mask[:, None], scores, -1e30)
        expo = jnp.exp(scores - jnp.max(scores, axis=-1, keepdims=True))
        return expo / jnp.sum(expo, axis=-1, keepdims=True)

    def weighted(probs, right):
        return jnp.einsum("bhqk,bkhd->bqhd", probs, right, preferred_element_type=f32)

    def joined(value):
        return value.astype(bf16).reshape(-1, block)

    probs = probabilities(query, keys, allowed)
    probs_low = probs.astype(bf16)
    mixed = weighted(probs_low, values).astype(bf16)
    attended = mixed.reshape(-1, block)
    received[1] = after(received[1], mixed)
    local_cross, local_in = columns_here(3, 5, 2), columns_here(8, 4, 2)
    w_cross = gather_z(local_cross)
    w_in = gather_z(local_in)
    w_out = gather_z(after(out_rows, local_cross, local_in))

    slots, ctx_len, ctx_width = context.shape
    ctx = after(context.reshape(slots * ctx_len, ctx_width), local_cross, local_in)
    ctx_x, ctx_y = swap(ctx, "x"), swap(ctx, "y")
    h1 = h0 + chain_step(scatter_rows, matmul(attended, w_self_out))

    def with_context(one, over_x, over_y):
        half = over_x.shape[0] // 2
        return gather_rows(one), swap(over_y[:half], "x"), swap(over_x[half:], "y")

    b_all, far_low, far_high = chain_step(with_context, normalize(h1, gains[1]).astype(bf16), ctx_x, ctx_y)

    def context_step(weights, *pieces):
        four = jnp.concatenate(pieces, axis=0)
        every = jnp.concatenate([four, swap(four, "c")], axis=0)
        low = matmul(every[:, :width], weights[:, block : 3 * block])
        return every, (low + matmul(every[:, width:], weights[:, 3 * block :])).astype(bf16)

    ctx_all, ctx_kv = chain_step(context_step, w_cross, ctx, ctx_y, ctx_x, far_low, far_high)
    w_cross_q = w_cross[:, :block]
    ctx_low, ctx_high = ctx_all[:, :width], ctx_all[:, width:]
    cross_q = matmul(b_all, w_cross_q)
    cross_q = split(cross_q.astype(bf16))
    cross_k, cross_v = split(ctx_kv[:, :block]), split(ctx_kv[:, block:])
    item = jnp.arange(slots * ctx_len) // ctx_len
    own_item = seg_all[:, :, None] == item[None, None, :]
    cross_p = probabilities(cross_q, cross_k, own_item)
    cross_low = cross_p.astype(bf16)
    cross_o = joined(weighted(cross_low, cross_v))
    h2 = h1 + chain_step(scatter_rows, matmul(cross_o, w_cross_out))
    c_all = chain_step(gather_rows, normalize(h2, gains[2]).astype(bf16))

    hidden = matmul(c_all, w_in)
    activated = gelu_tanh(hidden).astype(bf16)

    def sum_rows(value):
        value = with_layout_constraint(value, Layout(major_to_minor=(0, 1)))
        value = lax.psum_scatter(value, "z", scatter_dimension=0, tiled=True)
        return with_layout_constraint(value, Layout(major_to_minor=(0, 1)))

    def from_y(value, keep_pair=None):
        return jnp.stack([value, lax.ppermute(value, ALL_AXES, flip_pairs(2, keep_pair))])

    def with_core(pair):
        return jnp.concatenate([pair, swap(pair, "c")])

    t_out = matmul_left(activated, d_ff).astype(bf16)
    g_out = sum_rows(t_out)
    d_act = matmul_right(after(d_ff, t_out), w_out)
    d_hidden = jax.vjp(gelu_tanh, hidden)[1](d_act)[0].astype(bf16)
    t_in = matmul_left(c_all, d_hidden).astype(bf16)
    g_in = sum_rows(t_in)
    d_c, out_sum = chain_step(
        lambda one, two: (scatter_rows(one), scatter_rows(two)), matmul_right(d_hidden, w_in), matmul(activated, w_out)
    )
    layer_out = (h2 + out_sum).astype(bf16)
    part_two, gain_grad_two = jax.vjp(normalize, h2, gains[2])[1](d_c)
    dh2 = grad_out + part_two
    d_cross_out = chain_step(gather_rows, after(dh2.astype(bf16), t_in))
    g_cross_out = matmul_left(cross_o, d_cross_out)

    def through(d_mixed, left, right, probs, probs_low, values):
        d_mixed = split(d_mixed.astype(bf16))
        d_probs = jnp.einsum("bqhd,bkhd->bhqk", d_mixed, values, preferred_element_type=f32)
        d_scores = (probs * (d_probs - jnp.sum(probs * d_probs, axis=-1, keepdims=True))).astype(bf16)
        d_left = joined(weighted(d_scores, right) * scale)
        d_right = joined(jnp.einsum("bhqk,bqhd->bkhd", d_scores, left, preferred_element_type=f32) * scale)
        d_values = joined(jnp.einsum("bhqk,bqhd->bkhd", probs_low, d_mixed, preferred_element_type=f32))
        return d_left, d_right, d_values

    (d_cq, d_ck, d_cv), out_grads = chain_step(
        lambda one, two: (
            through(matmul_right(one, w_cross_out), cross_q, cross_k, cross_p, cross_low, cross_v),
            from_y(two),
        ),
        d_cross_out,
        g_out,
    )
    d_ckv = jnp.concatenate([d_ck, d_cv], axis=1)
    t_cross = jnp.concatenate(
        [
            value.astype(bf16)
            for value in (matmul_left(b_all, d_cq), matmul_left(ctx_low, d_ckv), matmul_left(ctx_high, d_ckv))
        ],
        axis=1,
    )
    g_cross = sum_rows(t_cross)
    part = matmul_right(d_cq, w_cross_q)
    d_b = chain_step(scatter_rows, part)
    part_one, gain_grad_one = jax.vjp(normalize, h1, gains[1])[1](d_b)
    dh1 = dh2 + part_one
    d_self_out = chain_step(gather_rows, after(dh1.astype(bf16), t_cross, g_in))
    g_self_out = matmul_left(attended, d_self_out)
    t_outer = jnp.concatenate(
        [
            jnp.where(low_y, g_self_out, g_cross_out).astype(bf16),
            jnp.where(low_y, g_cross_out, g_self_out).astype(bf16),
        ],
        axis=0,
    )
    g_outer = sum_rows(after(t_outer, g_cross))
    group_of = np.array([0, 0, 0, 0, 0, 0, 0, 0, 0, 0, 1, 1, 1, 1, 0, 0, 0, 0], np.int32)
    column_of = np.array([0, 0, 0, 0, 0, 1, 3, 2, 4, 0, 0, 1, 2, 3, 0, 0, 0, 0], np.int32)
    group_at = jnp.sum(jnp.where(holds, group_of, 0), axis=2)
    column_at = jnp.sum(jnp.where(holds, column_of, 0), axis=2)
    column_at = jnp.where(group_at == 1, (column_at + f) % 4, column_at)
    sent = pack_gradients(
        [g_cross, g_in], jnp.tile(group_at.reshape(-1), 2), jnp.tile(column_at.reshape(-1), 2), rows, block, cap
    )
    early_grads = lax.all_to_all(sent, PLANE, 0, 0, tiled=True).reshape(8 * cap, rows, block)

    def self_back(d_out):
        d_mixed = matmul_right(d_out, w_self_out)
        d_qkv = jnp.concatenate(through(d_mixed, query, keys, probs, probs_low, values), axis=1)
        return d_qkv, matmul_left(a_all, d_qkv).astype(bf16)

    d_qkv, t_qkv = chain_step(self_back, after(d_self_out, t_outer, sent))
    g_qkv = sum_rows(t_qkv)

    def last_step(part, out_pair, gain_grad_one, gain_grad_two):
        part_zero, gain_grad_zero = jax.vjp(normalize, h0, gains[0])[1](scatter_rows(part))
        gain_grads = jnp.stack([gain_grad_zero, gain_grad_one, gain_grad_two])
        return part_zero, sum_everywhere(gain_grads), with_core(out_pair)

    part_zero, gain_total, out_grads = chain_step(
        last_step, matmul_right(d_qkv, w_qkv), out_grads, gain_grad_one, gain_grad_two
    )
    grad_tokens = (dh1 + part_zero).astype(bf16)

    by_tile = jnp.swapaxes(after(g_qkv, out_grads).reshape(2, rows, 3, block), 1, 2)
    sent = jnp.broadcast_to(by_tile[:, None], (2, 4, 3, rows, block)).reshape(8, 3, rows, block)
    late_grads = lax.all_to_all(sent, PLANE, 0, 0, tiled=True).reshape(8 * 3, rows, block)
    back_swap = [(target, source) for source, target in pair_swap]
    other_half = lax.ppermute(after(g_outer, out_grads), ALL_AXES, back_swap)
    outer_grad = jnp.where(
        odd == 0,
        jnp.concatenate([g_outer, other_half], axis=0),
        jnp.concatenate([other_half, g_outer], axis=0),
    )
    outer_pair = from_y(outer_grad, lambda zz, place, _: place % 4 in (zz, (zz + 2) % 4))
    outer_grads = with_core(outer_pair)

    place = np.arange(8)
    source_x, source_f = (place % 2)[None, :], ((place // 2)[None, :] - my_shift[:, None]) % 4
    slot = np.arange(cap, dtype=np.int32)
    column_place = (source_x * 4 + source_f) * cap + slot[:, None]
    other_row = ((z - my_shift) % 4) ^ f
    row_source = (other_row % 2) * 2 + other_row // 2
    late = (my_used == 1) & ((my_tile < 4) | (my_tile == 9))
    early_mode = jnp.where(my_used == 0, 1, jnp.where(late, 0, jnp.where(my_row == 1, 3, 2)))
    states = (master, moment_one, moment_two)
    early = None
    for first in (0, half_cap):
        chosen = slice(first, first + half_cap)
        early = adam_tiles(
            *states,
            [early_grads],
            [out_grads],
            slot[chosen],
            after(early_mode, outer_grad, sent)[chosen] if first else early_mode[chosen],
            column_place[chosen].reshape(-1),
            row_source[chosen],
            np.zeros(half_cap, np.int32),
            early,
        )

    n_late = 5
    order = jnp.sum(jnp.where(slot[None, :] < slot[:, None], late.astype(jnp.int32)[None, :], 0), axis=1)
    count_late = jnp.sum(late.astype(jnp.int32))
    step = np.arange(n_late)
    wanted = jnp.minimum(step, jnp.maximum(count_late - 1, 0))
    here = late[None, :] & (order[None, :] == wanted[:, None])

    def at_step(value):
        return jnp.sum(jnp.where(here, value.astype(jnp.int32)[None, :], 0), axis=1)

    hold = (step >= jnp.maximum(count_late, 1)).astype(jnp.int32)
    tile = at_step(my_tile)
    some = count_late > 0
    visit = jnp.where(some, at_step(slot), 0)
    first_mode = jnp.where(early_mode[0] == 3, 4, early_mode[0])
    late_mode = jnp.where(at_step(my_row) == 1, 5, 3)
    mode = jnp.where(hold == 1, 0, jnp.where(some, late_mode, first_mode))
    late_place = ((place % 2)[None, :] * 4 + (place // 2)[None, :]) * 3 + tile[:, None]
    late_place = jnp.where(some, late_place, column_place[:1])
    new_w, new_m, new_v = adam_tiles(
        *states,
        [early_grads, late_grads],
        [out_grads, outer_grads],
        visit,
        mode,
        late_place.reshape(-1),
        jnp.where(some, at_step(row_source), row_source[0]),
        hold,
        early,
    )
    new_g, new_gm, new_gv = adam_update(gains, gain_one, gain_two, gain_total, rate_gain, 0.0)
    return (layer_out, grad_tokens, new_w, new_m, new_v, new_g, new_gm, new_gv)


def whole_body(
    tokens, cotangent, context, lengths, keep, owners, master, moment_one, moment_two, gains, gain_one, gain_two
):
    cap = master.shape[0]
    n_tiles = owners.shape[0]
    slot_of = owners * cap + ranks_of(owners)
    owner_rows = lax.all_gather(master.astype(bf16), "fsdp", axis=0, tiled=True)
    tiles = [
        lax.all_gather(
            lax.dynamic_index_in_dim(owner_rows, slot_of[tile], 0, keepdims=False), "dp", axis=0, tiled=True
        )
        for tile in range(n_tiles)
    ]
    w_in = jnp.concatenate(tiles[10:14], axis=1)
    w_out = jnp.concatenate(tiles[14:18], axis=0)
    count, width = tokens.shape
    head_dim = width // HEADS
    scale = head_dim ** (-0.5)
    seg = segments(lengths[0], count)
    live = keep == 1
    places = jnp.arange(count)

    def split(value):
        return value.astype(bf16).reshape(-1, HEADS, head_dim)

    def joined(value):
        return value.astype(bf16).reshape(-1, width)

    def probabilities(left, right, mask):
        scores = jnp.einsum("qhd,khd->hqk", left, right, preferred_element_type=f32) * scale
        scores = jnp.where(mask[None], scores, -1e30)
        expo = jnp.exp(scores - jnp.max(scores, axis=-1, keepdims=True))
        return expo / jnp.sum(expo, axis=-1, keepdims=True)

    def weighted(probs, right):
        return jnp.einsum("hqk,khd->qhd", probs, right, preferred_element_type=f32)

    def through(weights, d_out, left, right, probs, values):
        d_mixed = split(matmul_right(d_out, weights))
        d_probs = jnp.einsum("qhd,khd->hqk", d_mixed, values, preferred_element_type=f32)
        d_scores = (probs * (d_probs - jnp.sum(probs * d_probs, axis=-1, keepdims=True))).astype(bf16)
        d_left = joined(weighted(d_scores, right) * scale)
        d_right = joined(jnp.einsum("hqk,qhd->khd", d_scores, left, preferred_element_type=f32) * scale)
        d_values = joined(jnp.einsum("hqk,qhd->khd", probs.astype(bf16), d_mixed, preferred_element_type=f32))
        return d_left, d_right, d_values

    h0 = tokens.astype(f32)
    a_in = normalize(h0, gains[0]).astype(bf16)
    query, keys, values = (split(matmul(a_in, tiles[n])) for n in range(3))
    allowed = (seg[:, None] == seg[None, :]) & (live[None, :] | (places[:, None] == places[None, :]))
    probs = probabilities(query, keys, allowed)
    attended = joined(weighted(probs.astype(bf16), values))
    h1 = h0 + matmul(attended, tiles[3])
    b_in = normalize(h1, gains[1]).astype(bf16)
    slots, ctx_len, ctx_width = context.shape
    ctx = context.reshape(slots * ctx_len, ctx_width)
    ctx_low, ctx_high = ctx[:, :width], ctx[:, width:]
    cross_q = split(matmul(b_in, tiles[4]))
    cross_k = split(matmul(ctx_low, tiles[5]) + matmul(ctx_high, tiles[6]))
    cross_v = split(matmul(ctx_low, tiles[7]) + matmul(ctx_high, tiles[8]))
    item = jnp.arange(slots * ctx_len) // ctx_len
    cross_p = probabilities(cross_q, cross_k, seg[:, None] == item[None, :])
    cross_o = joined(weighted(cross_p.astype(bf16), cross_v))
    h2 = h1 + matmul(cross_o, tiles[9])
    c_in = normalize(h2, gains[2]).astype(bf16)
    hidden = matmul(c_in, w_in)
    activated = gelu_tanh(hidden).astype(bf16)
    layer_out = (h2 + matmul(activated, w_out)).astype(bf16)
    grad_out = cotangent.astype(f32) * live.astype(f32)[:, None]
    d_ff = grad_out.astype(bf16)
    d_hidden = jax.vjp(gelu_tanh, hidden)[1](matmul_right(d_ff, w_out))[0].astype(bf16)
    part_two, gain_grad_two = jax.vjp(normalize, h2, gains[2])[1](matmul_right(d_hidden, w_in))
    dh2 = grad_out + part_two
    d_cross_out = dh2.astype(bf16)
    d_cq, d_ck, d_cv = through(tiles[9], d_cross_out, cross_q, cross_k, cross_p, cross_v)
    part_one, gain_grad_one = jax.vjp(normalize, h1, gains[1])[1](matmul_right(d_cq, tiles[4]))
    dh1 = dh2 + part_one
    d_self_out = dh1.astype(bf16)
    d_q, d_k, d_v = through(tiles[3], d_self_out, query, keys, probs, values)
    d_a = matmul_right(d_q, tiles[0]) + matmul_right(d_k, tiles[1]) + matmul_right(d_v, tiles[2])
    part_zero, gain_grad_zero = jax.vjp(normalize, h0, gains[0])[1](d_a)
    grad_tokens = (dh1 + part_zero).astype(bf16)
    pairs = [
        (a_in, d_q),
        (a_in, d_k),
        (a_in, d_v),
        (attended, d_self_out),
        (b_in, d_cq),
        (ctx_low, d_ck),
        (ctx_high, d_ck),
        (ctx_low, d_cv),
        (ctx_high, d_cv),
        (cross_o, d_cross_out),
    ]
    for part in range(4):
        pairs.append((c_in, d_hidden[:, part * width : (part + 1) * width]))
    for part in range(4):
        pairs.append((activated[:, part * width : (part + 1) * width], d_ff))
    total_slots = lax.axis_size("fsdp") * cap
    placed = jnp.zeros((total_slots,) + master.shape[1:], bf16)
    for tile, (left, right) in enumerate(pairs):
        term = lax.psum_scatter(
            matmul_left(left, right).astype(bf16), "dp", scatter_dimension=0, tiled=True
        )
        placed = lax.dynamic_update_index_in_dim(placed, term, slot_of[tile], 0)
    owned = lax.psum_scatter(placed, "fsdp", scatter_dimension=0, tiled=True).astype(f32)
    my_slots = lax.axis_index("fsdp") * cap + jnp.arange(cap)
    used = jnp.any(slot_of[None, :] == my_slots[:, None], axis=1)[:, None, None]
    updated = adam_update(master, moment_one, moment_two, owned, rate_matrix, decay_rate)
    new_w, new_m, new_v = (jnp.where(used, value, 0.0) for value in updated)
    gain_grads = jnp.stack([gain_grad_zero, gain_grad_one, gain_grad_two])
    gain_total = lax.psum(gain_grads, ("dp", "fsdp"))
    new_g, new_gm, new_gv = adam_update(gains, gain_one, gain_two, gain_total, rate_gain, 0.0)
    return (layer_out, grad_tokens, new_w, new_m, new_v, new_g, new_gm, new_gv)


def solution(mesh):
    planes = mesh.shape["dp"] == 8 and mesh.shape["fsdp"] == 4
    if planes:
        used = Mesh(mesh.devices.reshape(4, 2, 2, 2), ALL_AXES)
        dp, fsdp, body = ("z", "x"), ("y", "c"), plane_body
    else:
        used, dp, fsdp, body = mesh, ("dp",), ("fsdp",), whole_body
    rows = P(dp + fsdp, None)
    tiles = P(fsdp, dp, None)
    return jax.shard_map(
        body,
        mesh=used,
        in_specs=(rows, rows, P(dp + fsdp, None, None), rows, P(dp + fsdp), P(), tiles, tiles, tiles, P(), P(), P()),
        out_specs=(rows, rows, tiles, tiles, tiles, P(), P(), P()),
        check_vma=False,
    )
```

```python
import jax
import jax.numpy as jnp
import numpy as np
from jax import lax
from jax.experimental import pallas as pl
from jax.experimental.layout import Layout, with_layout_constraint
from jax.experimental.pallas import tpu as pltpu
from jax.sharding import Mesh
from jax.sharding import PartitionSpec as P

HEADS = 16
STEP = 10

norm_eps = 1e-06
beta_one = 0.9
beta_two = 0.95
adam_eps = 1e-08
decay_rate = 0.1
rate_matrix = 0.1
rate_gain = 0.8

f32 = jnp.float32
bf16 = jnp.bfloat16

SHIFT = (0, 0, 0, 0, 2, 2, 2, 2, 2, 2, 0, 1, 2, 3, 0, 1, 2, 3)
ROW_TILES = (3, 9, 14, 15, 16, 17)
VMEM_LIMIT = 48 << 20


def normalize(h, gain):
    scale = lax.rsqrt(jnp.mean(h * h, axis=-1, keepdims=True) + norm_eps)
    return h * scale * gain


def gelu_tanh(u):
    return 0.5 * u * (1.0 + jnp.tanh(0.7978845608028654 * (u + 0.044715 * u * u * u)))


def matmul(left, right):
    return jnp.dot(left, right, preferred_element_type=f32)


def matmul_left(left, right):
    return lax.dot_general(left, right, (((0,), (0,)), ((), ())), preferred_element_type=f32)


def matmul_right(left, right):
    return lax.dot_general(left, right, (((1,), (1,)), ((), ())), preferred_element_type=f32)


def ranks_of(owners):
    order = jnp.arange(owners.shape[0])
    same = (owners[:, None] == owners[None, :]) & (order[None, :] < order[:, None])
    return jnp.sum(same.astype(jnp.int32), axis=1)


def segments(lengths, count):
    places = jnp.arange(count)
    end = jnp.zeros((), jnp.int32)
    seg = jnp.zeros((count,), jnp.int32)
    for item in range(lengths.shape[0]):
        end = end + lengths[item]
        seg = seg + (places >= end).astype(jnp.int32)
    return seg


def adam_update(weight, first, second, grad, rate, decay):
    first = beta_one * first + (1.0 - beta_one) * grad
    second = beta_two * second + (1.0 - beta_two) * grad * grad
    fix_one = 1.0 / (1.0 - beta_one**STEP)
    fix_two = 1.0 / (1.0 - beta_two**STEP)
    move = first * fix_one / (jnp.sqrt(second * fix_two) + adam_eps)
    return (weight - rate * (move + decay * weight), first, second)


def pack_columns(master, table, first_slot, slots):
    _, rows, columns = master.shape
    width = columns // 8

    def kernel(table_ref, in_ref, out_ref):
        slot = pl.program_id(0)
        for rank in range(8):
            start = pl.multiple_of(table_ref[slot * 8 + rank] * width, width)
            out_ref[rank, 0] = in_ref[0, :, pl.ds(start, width)].astype(bf16)

    return pl.pallas_call(
        kernel,
        out_shape=jax.ShapeDtypeStruct((8, slots, rows, width), bf16),
        grid_spec=pltpu.PrefetchScalarGridSpec(
            num_scalar_prefetch=1,
            grid=(slots,),
            in_specs=[pl.BlockSpec((1, rows, columns), lambda k, t: (first_slot + k, 0, 0))],
            out_specs=pl.BlockSpec((8, 1, rows, width), lambda k, t: (0, k, 0, 0)),
        ),
        compiler_params=pltpu.CompilerParams(vmem_limit_bytes=VMEM_LIMIT),
        name="pack_columns",
    )(table, master)


def pick_blocks(sources, which, index, count):
    _, rows, width = sources[0].shape
    n_src = len(sources)

    def kernel(which_ref, index_ref, *refs):
        place = pl.program_id(0) * 2 + pl.program_id(1)
        out_ref = refs[n_src]
        for number in range(n_src):

            @pl.when(which_ref[place] == number)
            def _():
                out_ref[...] = refs[number][0]

    def spec(number):
        def at(n, half, which, index):
            place = n * 2 + half
            return (jnp.where(which[place] == number, index[place], 0), 0, 0)

        return pl.BlockSpec((1, rows, width), at)

    return pl.pallas_call(
        kernel,
        out_shape=jax.ShapeDtypeStruct((2 * rows, count * width), bf16),
        grid_spec=pltpu.PrefetchScalarGridSpec(
            num_scalar_prefetch=2,
            grid=(count, 2),
            in_specs=[spec(number) for number in range(n_src)],
            out_specs=pl.BlockSpec((rows, width), lambda n, half, which, index: (half, n)),
        ),
        compiler_params=pltpu.CompilerParams(vmem_limit_bytes=VMEM_LIMIT),
        name="pick_blocks",
    )(which, index, *sources)


def pack_gradients(groups, which, column, rows, width, slots):
    n_src = len(groups)

    def kernel(which_ref, column_ref, *refs):
        rank = pl.program_id(0)
        out_ref = refs[n_src]
        for k in range(slots):
            start = pl.multiple_of(column_ref[rank * slots + k] * width, width)
            for number in range(n_src):

                @pl.when(which_ref[rank * slots + k] == number)
                def _():
                    out_ref[0, k] = refs[number][:, pl.ds(start, width)]

    return pl.pallas_call(
        kernel,
        out_shape=jax.ShapeDtypeStruct((8, slots, rows, width), bf16),
        grid_spec=pltpu.PrefetchScalarGridSpec(
            num_scalar_prefetch=2,
            grid=(8,),
            in_specs=[
                pl.BlockSpec((rows, group.shape[1]), lambda rank, which, column: (rank // 4, 0)) for group in groups
            ],
            out_specs=pl.BlockSpec((1, slots, rows, width), lambda rank, which, column: (rank, 0, 0, 0)),
        ),
        compiler_params=pltpu.CompilerParams(vmem_limit_bytes=VMEM_LIMIT),
        name="pack_gradients",
    )(which, column, *groups)


def adam_tiles(master, one, two, columns_from, rows_from, visit, mode, column_place, row_place, hold, previous=None):
    _, rows, columns = master.shape
    width = columns // 8
    n_visit = visit.shape[0]
    n_col, n_row = len(columns_from), len(rows_from)
    kept = () if previous is None else tuple(previous)

    def kernel(visit_ref, mode_ref, cp_ref, rp_ref, hold_ref, *refs):
        w_ref, m_ref, v_ref = refs[:3]
        grads = refs[3 : 3 + n_col + n_row]
        outs = refs[3 + n_col + n_row + len(kept) :]
        how = mode_ref[pl.program_id(0)]

        @pl.when(how == 1)
        def _():
            for ref in outs:
                ref[...] = jnp.zeros_like(ref)

        for number, grad_ref in enumerate(grads):

            @pl.when(how == number + 2)
            def _():
                grad = grad_ref[0].astype(f32)
                results = adam_update(w_ref[0], m_ref[0], v_ref[0], grad, rate_matrix, decay_rate)
                for ref, value in zip(outs, results, strict=True):
                    ref[0] = value

    def block_of(n, b, hold):
        return jnp.where(hold[n] == 1, 7, b)

    state = pl.BlockSpec((1, rows, width), lambda n, b, vi, mo, cp, rp, ho: (vi[n], 0, block_of(n, b, ho)))

    def column_spec(number):
        def at(n, b, vi, mo, cp, rp, ho):
            return (jnp.where(mo[n] == number + 2, cp[n * 8 + block_of(n, b, ho)], 0), 0, 0)

        return pl.BlockSpec((1, rows, width), at)

    def row_spec(number):
        def at(n, b, vi, mo, cp, rp, ho):
            taken = mo[n] == number + 2
            return (jnp.where(taken, rp[n], 0), 0, jnp.where(taken, block_of(n, b, ho), 0))

        return pl.BlockSpec((1, rows, width), at)

    shape = jax.ShapeDtypeStruct(master.shape, f32)
    n_before = 5 + 3 + n_col + n_row
    return pl.pallas_call(
        kernel,
        out_shape=(shape, shape, shape),
        grid_spec=pltpu.PrefetchScalarGridSpec(
            num_scalar_prefetch=5,
            grid=(n_visit, 8),
            in_specs=[
                state,
                state,
                state,
                *(column_spec(number) for number in range(n_col)),
                *(row_spec(n_col + number) for number in range(n_row)),
                *(pl.BlockSpec(memory_space=pl.ANY) for _ in kept),
            ],
            out_specs=(state, state, state),
        ),
        input_output_aliases={n_before + n: n for n in range(len(kept))},
        compiler_params=pltpu.CompilerParams(vmem_limit_bytes=VMEM_LIMIT),
        cost_estimate=pl.CostEstimate(
            flops=30 * n_visit * rows * columns, bytes_accessed=26 * n_visit * rows * columns, transcendentals=0
        ),
        name="adam_tiles",
    )(visit, mode, column_place, row_place, hold, master, one, two, *columns_from, *rows_from, *kept)


def after(value, *others):
    return lax.optimization_barrier((value, *others))[0]


def swap(value, axis):
    return lax.ppermute(value, axis, [(0, 1), (1, 0)])


def gather_rows(value):
    half = value.shape[0] // 2
    over_x = swap(value, "x")
    over_y = swap(value, "y")
    far_low = swap(over_y[:half], "x")
    far_high = swap(over_x[half:], "y")
    four = jnp.concatenate([value, over_y, over_x, far_low, far_high], axis=0)
    return jnp.concatenate([four, swap(four, "c")], axis=0)


def scatter_rows(part):
    rows, width = part.shape[0] // 8, part.shape[1]
    half = width // 2
    part = part.reshape(2, 2, 2, rows, width)
    chip = part[0] + swap(part[1], "c")
    low, high = chip[..., :half], chip[..., half:]
    low_two = low[:, 0] + swap(low[:, 1].astype(bf16), "y").astype(f32)
    high_two = high[0] + swap(high[1].astype(bf16), "x").astype(f32)
    low_one = low_two[0] + swap(low_two[1].astype(bf16), "x").astype(f32)
    high_one = high_two[0] + swap(high_two[1].astype(bf16), "y").astype(f32)
    return jnp.concatenate([low_one, high_one], axis=1)


def sum_everywhere(value):
    for axis in ("c", "y", "x"):
        value = value + swap(value, axis)
    for step in (1, 2):
        value = value + lax.ppermute(value, "z", [(z, z ^ step) for z in range(4)])
    return value


def flip_pairs(mask, keep=None):
    pairs = []
    for z in range(4):
        for place in range(8):
            target = place ^ mask
            if keep is None or keep(z, place, target):
                pairs.append((z * 8 + place, z * 8 + target))
    return pairs


ALL_AXES = ("z", "x", "y", "c")
PLANE = ("x", "y", "c")


def plane_body(
    tokens, cotangent, context, lengths, keep, owners, master, moment_one, moment_two, gains, gain_one, gain_two
):
    cap, rows, _ = master.shape
    count, width = tokens.shape
    heads_here = HEADS // 8
    head_dim = width // HEADS
    scale = head_dim ** (-0.5)
    block = width // 8
    z = lax.axis_index("z")
    x = lax.axis_index("x")
    f = lax.axis_index("y") * 2 + lax.axis_index("c")

    n_tiles = owners.shape[0]
    rank = ranks_of(owners)
    shift_of = np.array(SHIFT, np.int32)
    row_of = np.array([t in ROW_TILES for t in range(n_tiles)])
    all_slots = jnp.arange(4 * cap).reshape(4, cap)
    holds = (owners * cap + rank)[None, None, :] == all_slots[:, :, None]
    used_at = jnp.any(holds, axis=2)
    tile_at = jnp.sum(jnp.where(holds, np.arange(n_tiles, dtype=np.int32), 0), axis=2)
    shift_at = jnp.sum(jnp.where(holds, shift_of, 0), axis=2)
    row_at = jnp.any(holds & row_of, axis=2)
    mine = (jnp.arange(4) == f)[:, None]

    def my(value):
        return jnp.sum(jnp.where(mine, value.astype(jnp.int32), 0), axis=0)

    my_used, my_tile, my_shift, my_row = my(used_at), my(tile_at), my(shift_at), my(row_at)

    to_x = np.arange(8) // 4
    to_f = np.arange(8) % 4
    column_table = 2 * ((to_f[None, :] + my_shift[:, None]) % 4) + to_x[None, :]
    half_cap = cap // 2
    place = np.arange(4)

    def of_tiles(tiles, values):
        chosen = tiles[:, None] == np.arange(n_tiles)[None, :]
        return jnp.sum(jnp.where(chosen, values[None, :], 0), axis=1)

    column_tiles = jnp.concatenate([np.array([0, 1, 2, 4, 5, 7, 6, 8], np.int32), 10 + (place - f) % 4])
    column_part = jnp.repeat(of_tiles(column_tiles, rank // half_cap), 2)
    column_place = of_tiles(column_tiles, owners * half_cap + rank % half_cap)
    column_place = (column_place[:, None] + np.array([0, 4 * half_cap])[None, :]).reshape(-1)
    other_f = f ^ place
    outer_tiles = jnp.where(other_f == z, 3, 9)
    out_tiles = 14 + (z - other_f) % 4
    row_slots = of_tiles(jnp.concatenate([outer_tiles, out_tiles]), rank)
    row_owners = of_tiles(jnp.stack([outer_tiles[0], outer_tiles[2], out_tiles[0], out_tiles[2]]), owners)

    def pack_first(weights):
        return pack_columns(weights, column_table[:half_cap].reshape(-1), 0, half_cap)

    def pack_second(weights):
        return pack_columns(weights, column_table[half_cap:].reshape(-1), half_cap, half_cap)

    def my_block(slot):
        return lax.dynamic_index_in_dim(master, slot, 0, keepdims=False).astype(bf16)

    present = owners[0] >= 0

    def chain_step(move, *values):
        shapes = jax.eval_shape(move, *values)
        idle = jax.tree.map(lambda leaf: jnp.zeros(leaf.shape, leaf.dtype), shapes)
        return lax.cond(present, move, lambda *_: idle, *values)

    seg = segments(lengths[0], count)
    live = keep == 1
    code = seg * 2 + live.astype(jnp.int32)

    def spread_code(code):
        for axis in ("y", "x", "c"):
            code = jnp.concatenate([code, swap(code, axis)])
        return code

    code = chain_step(spread_code, code)
    seg_all = (code // 2).reshape(8, count)
    live_all = (code % 2 == 1).reshape(8, count)
    grad_out = cotangent.astype(f32) * live.astype(f32)[:, None]
    h0 = tokens.astype(f32)
    outer_blocks = [my_block(row_slots[mask]) for mask in range(4)]
    out_blocks = [my_block(row_slots[4 + mask]) for mask in range(4)]
    a_in = normalize(h0, gains[0]).astype(bf16)
    sent = pack_first(after(master, row_slots, row_owners))
    received = [lax.all_to_all(sent, PLANE, 0, 0, tiled=True).reshape(8 * half_cap, rows, block)]
    received = [after(received[0], code, a_in, *outer_blocks, *out_blocks)]

    def columns_here(first, count, parts):
        chosen = slice(2 * first, 2 * (first + count))
        return pick_blocks(received[:parts], column_part[chosen], column_place[chosen], count)

    def gather_z(value):
        return lax.all_gather(value, "z", axis=0, tiled=True)

    local = columns_here(0, 3, 1)
    w_qkv = gather_z(local)
    a_all = gather_rows(after(a_in, local))
    sent = pack_second(after(master, a_all))
    received.append(lax.all_to_all(sent, PLANE, 0, 0, tiled=True).reshape(8 * half_cap, rows, block))
    slots, ctx_len, ctx_width = context.shape
    ctx = after(context.reshape(slots * ctx_len, ctx_width), sent)
    ctx_x, ctx_y = swap(ctx, "x"), swap(ctx, "y")

    def take_rows(kind, blocks, keep_pair):
        here, there = row_owners[2 * kind], row_owners[2 * kind + 1]
        core = f % 2
        from_core = swap(jnp.stack([blocks[1], blocks[3]]), "c")
        mine = jnp.where(here % 2 == core, blocks[0], from_core[0])
        across = jnp.where(there % 2 == core, blocks[2], from_core[1])
        from_y = lax.ppermute(across, ALL_AXES, flip_pairs(2, keep_pair))
        return jnp.where(here // 2 == f // 2, mine, from_y)

    def needs_outer(zz, place, target):
        return target % 4 in (zz, (zz + 2) % 4)

    outer = take_rows(0, [after(value, local) for value in outer_blocks], needs_outer)
    half_rows = rows // 2
    odd = z % 2
    to_pair = lax.dynamic_slice_in_dim(outer, (1 - odd) * half_rows, half_rows, 0)
    own_half = lax.dynamic_slice_in_dim(outer, odd * half_rows, half_rows, 0)
    pair_swap = [
        (zz * 8 + place, (zz ^ 1) * 8 + place)
        for zz in range(4)
        for place in range(8)
        if place % 4 in (zz, (zz + 2) % 4)
    ]
    from_pair = lax.ppermute(to_pair, ALL_AXES, pair_swap)
    has_outer = (f == z) | (f == (z + 2) % 4)
    outer_all = lax.all_gather(jnp.where(has_outer, own_half, from_pair), "z", axis=0, tiled=True)
    low_y = lax.axis_index("y") == 0
    w_self_out = jnp.where(low_y, outer_all[:rows], outer_all[rows:])
    w_cross_out = jnp.where(low_y, outer_all[rows:], outer_all[:rows])

    def split(value):
        return value.reshape(8, -1, heads_here, head_dim)

    qkv = matmul(a_all, w_qkv)
    qkv = qkv.astype(bf16)
    query, keys, values = (split(qkv[:, n * block : (n + 1) * block]) for n in range(3))
    places = jnp.arange(count)
    allowed = (seg_all[:, :, None] == seg_all[:, None, :]) & (
        live_all[:, None, :] | (places[:, None] == places[None, :])
    )

    def probabilities(left, right, mask):
        scores = jnp.einsum("bqhd,bkhd->bhqk", left, right, preferred_element_type=f32) * scale
        scores = jnp.where(mask[:, None], scores, -1e30)
        expo = jnp.exp(scores - jnp.max(scores, axis=-1, keepdims=True))
        return expo / jnp.sum(expo, axis=-1, keepdims=True)

    def weighted(probs, right):
        return jnp.einsum("bhqk,bkhd->bqhd", probs, right, preferred_element_type=f32)

    def joined(value):
        return value.astype(bf16).reshape(-1, block)

    probs = probabilities(query, keys, allowed)
    probs_low = probs.astype(bf16)
    mixed = weighted(probs_low, values).astype(bf16)
    attended = mixed.reshape(-1, block)
    received[1] = after(received[1], mixed)
    local_cross, local_in = columns_here(3, 5, 2), columns_here(8, 4, 2)
    w_cross = gather_z(local_cross)
    w_in = gather_z(local_in)

    def first_step(one, over_x, over_y):
        half = over_x.shape[0] // 2
        return scatter_rows(one), swap(over_y[:half], "x"), swap(over_x[half:], "y")

    h1, far_low, far_high = chain_step(
        first_step, matmul(attended, w_self_out), after(ctx_x, local_in), after(ctx_y, local_in)
    )
    h1 = h0 + h1

    def second_step(one, *pieces):
        four = jnp.concatenate(pieces, axis=0)
        return gather_rows(one), four, swap(four, "c")

    b_all, ctx_here, ctx_there = chain_step(
        second_step, normalize(h1, gains[1]).astype(bf16), ctx, ctx_y, ctx_x, far_low, far_high
    )
    out_rows = take_rows(1, [after(value, b_all) for value in out_blocks], None)
    w_out = gather_z(out_rows)
    d_ff = gather_rows(after(grad_out.astype(bf16), b_all))

    w_cross_q = w_cross[:, :block]
    w_low = w_cross[:, block : 3 * block]
    w_high = w_cross[:, 3 * block :]
    ctx_kv = jnp.concatenate(
        [
            (matmul(part[:, :width], w_low) + matmul(part[:, width:], w_high)).astype(bf16)
            for part in (ctx_here, ctx_there)
        ],
        axis=0,
    )
    cross_q = matmul(b_all, w_cross_q)
    cross_q = split(cross_q.astype(bf16))
    cross_k, cross_v = split(ctx_kv[:, :block]), split(ctx_kv[:, block:])
    item = jnp.arange(slots * ctx_len) // ctx_len
    own_item = seg_all[:, :, None] == item[None, None, :]
    cross_p = probabilities(cross_q, cross_k, own_item)
    cross_low = cross_p.astype(bf16)
    cross_o = joined(weighted(cross_low, cross_v))
    h2, ctx_all = chain_step(
        lambda one, *pieces: (scatter_rows(one), jnp.concatenate(pieces, axis=0)),
        matmul(cross_o, w_cross_out),
        ctx_here,
        ctx_there,
    )
    ctx_low, ctx_high = ctx_all[:, :width], ctx_all[:, width:]
    h2 = h1 + h2
    c_all = chain_step(gather_rows, normalize(h2, gains[2]).astype(bf16))

    hidden = matmul(c_all, w_in)
    activated = gelu_tanh(hidden).astype(bf16)

    def sum_rows(value):
        value = with_layout_constraint(value, Layout(major_to_minor=(0, 1)))
        value = lax.psum_scatter(value, "z", scatter_dimension=0, tiled=True)
        return with_layout_constraint(value, Layout(major_to_minor=(0, 1)))

    def from_y(value, keep_pair=None):
        return jnp.stack([value, lax.ppermute(value, ALL_AXES, flip_pairs(2, keep_pair))])

    def with_core(pair):
        return jnp.concatenate([pair, swap(pair, "c")])

    t_out = matmul_left(activated, d_ff).astype(bf16)
    g_out = sum_rows(t_out)
    d_act = matmul_right(after(d_ff, t_out), w_out)
    d_hidden = jax.vjp(gelu_tanh, hidden)[1](d_act)[0].astype(bf16)
    t_in = matmul_left(c_all, d_hidden).astype(bf16)
    g_in = sum_rows(t_in)
    d_c, out_sum = chain_step(
        lambda one, two: (scatter_rows(one), scatter_rows(two)), matmul_right(d_hidden, w_in), matmul(activated, w_out)
    )
    layer_out = (h2 + out_sum).astype(bf16)
    part_two, gain_grad_two = jax.vjp(normalize, h2, gains[2])[1](d_c)
    dh2 = grad_out + part_two
    d_cross_out = chain_step(gather_rows, after(dh2.astype(bf16), t_in))
    g_cross_out = matmul_left(cross_o, d_cross_out)

    def through(d_mixed, left, right, probs, probs_low, values):
        d_mixed = split(d_mixed.astype(bf16))
        d_probs = jnp.einsum("bqhd,bkhd->bhqk", d_mixed, values, preferred_element_type=f32)
        d_scores = (probs * (d_probs - jnp.sum(probs * d_probs, axis=-1, keepdims=True))).astype(bf16)
        d_left = joined(weighted(d_scores, right) * scale)
        d_right = joined(jnp.einsum("bhqk,bqhd->bkhd", d_scores, left, preferred_element_type=f32) * scale)
        d_values = joined(jnp.einsum("bhqk,bqhd->bkhd", probs_low, d_mixed, preferred_element_type=f32))
        return d_left, d_right, d_values

    (d_cq, d_ck, d_cv), out_grads = chain_step(
        lambda one, two: (
            through(matmul_right(one, w_cross_out), cross_q, cross_k, cross_p, cross_low, cross_v),
            from_y(two),
        ),
        d_cross_out,
        g_out,
    )
    d_ckv = jnp.concatenate([d_ck, d_cv], axis=1)
    t_cross = jnp.concatenate(
        [
            value.astype(bf16)
            for value in (matmul_left(b_all, d_cq), matmul_left(ctx_low, d_ckv), matmul_left(ctx_high, d_ckv))
        ],
        axis=1,
    )
    g_cross = sum_rows(t_cross)
    part = matmul_right(d_cq, w_cross_q)
    d_b = chain_step(scatter_rows, part)
    part_one, gain_grad_one = jax.vjp(normalize, h1, gains[1])[1](d_b)
    dh1 = dh2 + part_one
    d_self_out = chain_step(gather_rows, after(dh1.astype(bf16), t_cross, g_in))
    g_self_out = matmul_left(attended, d_self_out)
    t_outer = jnp.concatenate(
        [
            jnp.where(low_y, g_self_out, g_cross_out).astype(bf16),
            jnp.where(low_y, g_cross_out, g_self_out).astype(bf16),
        ],
        axis=0,
    )
    g_outer = sum_rows(after(t_outer, g_cross))
    d_mixed = matmul_right(after(d_self_out, t_outer), w_self_out)
    d_q, d_k, d_v = through(d_mixed, query, keys, probs, probs_low, values)
    d_qkv = jnp.concatenate([d_q, d_k, d_v], axis=1)
    t_qkv = matmul_left(a_all, d_qkv).astype(bf16)
    g_qkv = sum_rows(t_qkv)
    group_of = np.array([0, 0, 0, 0, 0, 0, 0, 0, 0, 0, 1, 1, 1, 1, 0, 0, 0, 0], np.int32)
    column_of = np.array([0, 0, 0, 0, 0, 1, 3, 2, 4, 0, 0, 1, 2, 3, 0, 0, 0, 0], np.int32)
    group_at = jnp.sum(jnp.where(holds, group_of, 0), axis=2)
    column_at = jnp.sum(jnp.where(holds, column_of, 0), axis=2)
    column_at = jnp.where(group_at == 1, (column_at + f) % 4, column_at)
    sent = pack_gradients(
        [after(g_cross, t_qkv), g_in], jnp.tile(group_at.reshape(-1), 2), jnp.tile(column_at.reshape(-1), 2), rows, block, cap
    )
    early_grads = lax.all_to_all(sent, PLANE, 0, 0, tiled=True).reshape(8 * cap, rows, block)

    def last_step(part, out_pair, gain_grad_one, gain_grad_two):
        part_zero, gain_grad_zero = jax.vjp(normalize, h0, gains[0])[1](scatter_rows(part))
        gain_grads = jnp.stack([gain_grad_zero, gain_grad_one, gain_grad_two])
        return part_zero, sum_everywhere(gain_grads), with_core(out_pair)

    part_zero, gain_total, out_grads = chain_step(
        last_step, matmul_right(after(d_qkv, sent), w_qkv), out_grads, gain_grad_one, gain_grad_two
    )
    grad_tokens = (dh1 + part_zero).astype(bf16)

    by_tile = jnp.swapaxes(after(g_qkv, out_grads).reshape(2, rows, 3, block), 1, 2)
    sent = jnp.broadcast_to(by_tile[:, None], (2, 4, 3, rows, block)).reshape(8, 3, rows, block)
    late_grads = lax.all_to_all(sent, PLANE, 0, 0, tiled=True).reshape(8 * 3, rows, block)
    back_swap = [(target, source) for source, target in pair_swap]
    other_half = lax.ppermute(after(g_outer, out_grads), ALL_AXES, back_swap)
    outer_grad = jnp.where(
        odd == 0,
        jnp.concatenate([g_outer, other_half], axis=0),
        jnp.concatenate([other_half, g_outer], axis=0),
    )
    outer_pair = from_y(outer_grad, lambda zz, place, _: place % 4 in (zz, (zz + 2) % 4))
    outer_grads = with_core(outer_pair)

    place = np.arange(8)
    source_x, source_f = (place % 2)[None, :], ((place // 2)[None, :] - my_shift[:, None]) % 4
    slot = np.arange(cap, dtype=np.int32)
    column_place = (source_x * 4 + source_f) * cap + slot[:, None]
    other_row = ((z - my_shift) % 4) ^ f
    row_source = (other_row % 2) * 2 + other_row // 2
    late = (my_used == 1) & ((my_tile < 4) | (my_tile == 9))
    early_mode = jnp.where(my_used == 0, 1, jnp.where(late, 0, jnp.where(my_row == 1, 3, 2)))
    states = (master, moment_one, moment_two)
    early = None
    for first in (0, half_cap):
        chosen = slice(first, first + half_cap)
        early = adam_tiles(
            *states,
            [early_grads],
            [out_grads],
            slot[chosen],
            after(early_mode, outer_grad, sent)[chosen] if first else early_mode[chosen],
            column_place[chosen].reshape(-1),
            row_source[chosen],
            np.zeros(half_cap, np.int32),
            early,
        )

    n_late = 5
    order = jnp.sum(jnp.where(slot[None, :] < slot[:, None], late.astype(jnp.int32)[None, :], 0), axis=1)
    count_late = jnp.sum(late.astype(jnp.int32))
    step = np.arange(n_late)
    wanted = jnp.minimum(step, jnp.maximum(count_late - 1, 0))
    here = late[None, :] & (order[None, :] == wanted[:, None])

    def at_step(value):
        return jnp.sum(jnp.where(here, value.astype(jnp.int32)[None, :], 0), axis=1)

    hold = (step >= jnp.maximum(count_late, 1)).astype(jnp.int32)
    tile = at_step(my_tile)
    some = count_late > 0
    visit = jnp.where(some, at_step(slot), 0)
    first_mode = jnp.where(early_mode[0] == 3, 4, early_mode[0])
    late_mode = jnp.where(at_step(my_row) == 1, 5, 3)
    mode = jnp.where(hold == 1, 0, jnp.where(some, late_mode, first_mode))
    late_place = ((place % 2)[None, :] * 4 + (place // 2)[None, :]) * 3 + tile[:, None]
    late_place = jnp.where(some, late_place, column_place[:1])
    new_w, new_m, new_v = adam_tiles(
        *states,
        [early_grads, late_grads],
        [out_grads, outer_grads],
        visit,
        mode,
        late_place.reshape(-1),
        jnp.where(some, at_step(row_source), row_source[0]),
        hold,
        early,
    )
    new_g, new_gm, new_gv = adam_update(gains, gain_one, gain_two, gain_total, rate_gain, 0.0)
    return (layer_out, grad_tokens, new_w, new_m, new_v, new_g, new_gm, new_gv)


def whole_body(
    tokens, cotangent, context, lengths, keep, owners, master, moment_one, moment_two, gains, gain_one, gain_two
):
    cap = master.shape[0]
    n_tiles = owners.shape[0]
    slot_of = owners * cap + ranks_of(owners)
    owner_rows = lax.all_gather(master.astype(bf16), "fsdp", axis=0, tiled=True)
    tiles = [
        lax.all_gather(
            lax.dynamic_index_in_dim(owner_rows, slot_of[tile], 0, keepdims=False), "dp", axis=0, tiled=True
        )
        for tile in range(n_tiles)
    ]
    w_in = jnp.concatenate(tiles[10:14], axis=1)
    w_out = jnp.concatenate(tiles[14:18], axis=0)
    count, width = tokens.shape
    head_dim = width // HEADS
    scale = head_dim ** (-0.5)
    seg = segments(lengths[0], count)
    live = keep == 1
    places = jnp.arange(count)

    def split(value):
        return value.astype(bf16).reshape(-1, HEADS, head_dim)

    def joined(value):
        return value.astype(bf16).reshape(-1, width)

    def probabilities(left, right, mask):
        scores = jnp.einsum("qhd,khd->hqk", left, right, preferred_element_type=f32) * scale
        scores = jnp.where(mask[None], scores, -1e30)
        expo = jnp.exp(scores - jnp.max(scores, axis=-1, keepdims=True))
        return expo / jnp.sum(expo, axis=-1, keepdims=True)

    def weighted(probs, right):
        return jnp.einsum("hqk,khd->qhd", probs, right, preferred_element_type=f32)

    def through(weights, d_out, left, right, probs, values):
        d_mixed = split(matmul_right(d_out, weights))
        d_probs = jnp.einsum("qhd,khd->hqk", d_mixed, values, preferred_element_type=f32)
        d_scores = (probs * (d_probs - jnp.sum(probs * d_probs, axis=-1, keepdims=True))).astype(bf16)
        d_left = joined(weighted(d_scores, right) * scale)
        d_right = joined(jnp.einsum("hqk,qhd->khd", d_scores, left, preferred_element_type=f32) * scale)
        d_values = joined(jnp.einsum("hqk,qhd->khd", probs.astype(bf16), d_mixed, preferred_element_type=f32))
        return d_left, d_right, d_values

    h0 = tokens.astype(f32)
    a_in = normalize(h0, gains[0]).astype(bf16)
    query, keys, values = (split(matmul(a_in, tiles[n])) for n in range(3))
    allowed = (seg[:, None] == seg[None, :]) & (live[None, :] | (places[:, None] == places[None, :]))
    probs = probabilities(query, keys, allowed)
    attended = joined(weighted(probs.astype(bf16), values))
    h1 = h0 + matmul(attended, tiles[3])
    b_in = normalize(h1, gains[1]).astype(bf16)
    slots, ctx_len, ctx_width = context.shape
    ctx = context.reshape(slots * ctx_len, ctx_width)
    ctx_low, ctx_high = ctx[:, :width], ctx[:, width:]
    cross_q = split(matmul(b_in, tiles[4]))
    cross_k = split(matmul(ctx_low, tiles[5]) + matmul(ctx_high, tiles[6]))
    cross_v = split(matmul(ctx_low, tiles[7]) + matmul(ctx_high, tiles[8]))
    item = jnp.arange(slots * ctx_len) // ctx_len
    cross_p = probabilities(cross_q, cross_k, seg[:, None] == item[None, :])
    cross_o = joined(weighted(cross_p.astype(bf16), cross_v))
    h2 = h1 + matmul(cross_o, tiles[9])
    c_in = normalize(h2, gains[2]).astype(bf16)
    hidden = matmul(c_in, w_in)
    activated = gelu_tanh(hidden).astype(bf16)
    layer_out = (h2 + matmul(activated, w_out)).astype(bf16)
    grad_out = cotangent.astype(f32) * live.astype(f32)[:, None]
    d_ff = grad_out.astype(bf16)
    d_hidden = jax.vjp(gelu_tanh, hidden)[1](matmul_right(d_ff, w_out))[0].astype(bf16)
    part_two, gain_grad_two = jax.vjp(normalize, h2, gains[2])[1](matmul_right(d_hidden, w_in))
    dh2 = grad_out + part_two
    d_cross_out = dh2.astype(bf16)
    d_cq, d_ck, d_cv = through(tiles[9], d_cross_out, cross_q, cross_k, cross_p, cross_v)
    part_one, gain_grad_one = jax.vjp(normalize, h1, gains[1])[1](matmul_right(d_cq, tiles[4]))
    dh1 = dh2 + part_one
    d_self_out = dh1.astype(bf16)
    d_q, d_k, d_v = through(tiles[3], d_self_out, query, keys, probs, values)
    d_a = matmul_right(d_q, tiles[0]) + matmul_right(d_k, tiles[1]) + matmul_right(d_v, tiles[2])
    part_zero, gain_grad_zero = jax.vjp(normalize, h0, gains[0])[1](d_a)
    grad_tokens = (dh1 + part_zero).astype(bf16)
    pairs = [
        (a_in, d_q),
        (a_in, d_k),
        (a_in, d_v),
        (attended, d_self_out),
        (b_in, d_cq),
        (ctx_low, d_ck),
        (ctx_high, d_ck),
        (ctx_low, d_cv),
        (ctx_high, d_cv),
        (cross_o, d_cross_out),
    ]
    for part in range(4):
        pairs.append((c_in, d_hidden[:, part * width : (part + 1) * width]))
    for part in range(4):
        pairs.append((activated[:, part * width : (part + 1) * width], d_ff))
    total_slots = lax.axis_size("fsdp") * cap
    placed = jnp.zeros((total_slots,) + master.shape[1:], bf16)
    for tile, (left, right) in enumerate(pairs):
        term = lax.psum_scatter(
            matmul_left(left, right).astype(bf16), "dp", scatter_dimension=0, tiled=True
        )
        placed = lax.dynamic_update_index_in_dim(placed, term, slot_of[tile], 0)
    owned = lax.psum_scatter(placed, "fsdp", scatter_dimension=0, tiled=True).astype(f32)
    my_slots = lax.axis_index("fsdp") * cap + jnp.arange(cap)
    used = jnp.any(slot_of[None, :] == my_slots[:, None], axis=1)[:, None, None]
    updated = adam_update(master, moment_one, moment_two, owned, rate_matrix, decay_rate)
    new_w, new_m, new_v = (jnp.where(used, value, 0.0) for value in updated)
    gain_grads = jnp.stack([gain_grad_zero, gain_grad_one, gain_grad_two])
    gain_total = lax.psum(gain_grads, ("dp", "fsdp"))
    new_g, new_gm, new_gv = adam_update(gains, gain_one, gain_two, gain_total, rate_gain, 0.0)
    return (layer_out, grad_tokens, new_w, new_m, new_v, new_g, new_gm, new_gv)


def solution(mesh):
    planes = mesh.shape["dp"] == 8 and mesh.shape["fsdp"] == 4
    if planes:
        used = Mesh(mesh.devices.reshape(4, 2, 2, 2), ALL_AXES)
        dp, fsdp, body = ("z", "x"), ("y", "c"), plane_body
    else:
        used, dp, fsdp, body = mesh, ("dp",), ("fsdp",), whole_body
    rows = P(dp + fsdp, None)
    tiles = P(fsdp, dp, None)
    return jax.shard_map(
        body,
        mesh=used,
        in_specs=(rows, rows, P(dp + fsdp, None, None), rows, P(dp + fsdp), P(), tiles, tiles, tiles, P(), P(), P()),
        out_specs=(rows, rows, tiles, tiles, tiles, P(), P(), P()),
        check_vma=False,
    )
```

```python
import jax
import jax.numpy as jnp
import numpy as np
from jax import lax
from jax.experimental import pallas as pl
from jax.experimental.layout import Layout, with_layout_constraint
from jax.experimental.pallas import tpu as pltpu
from jax.sharding import Mesh
from jax.sharding import PartitionSpec as P

HEADS = 16
STEP = 10

norm_eps = 1e-06
beta_one = 0.9
beta_two = 0.95
adam_eps = 1e-08
decay_rate = 0.1
rate_matrix = 0.1
rate_gain = 0.8

f32 = jnp.float32
bf16 = jnp.bfloat16

SHIFT = (0, 0, 0, 0, 2, 2, 2, 2, 2, 2, 0, 1, 2, 3, 0, 1, 2, 3)
ROW_TILES = (3, 9, 14, 15, 16, 17)
VMEM_LIMIT = 48 << 20


def normalize(h, gain):
    scale = lax.rsqrt(jnp.mean(h * h, axis=-1, keepdims=True) + norm_eps)
    return h * scale * gain


def gelu_tanh(u):
    return 0.5 * u * (1.0 + jnp.tanh(0.7978845608028654 * (u + 0.044715 * u * u * u)))


def matmul(left, right):
    return jnp.dot(left, right, preferred_element_type=f32)


def matmul_left(left, right):
    return lax.dot_general(left, right, (((0,), (0,)), ((), ())), preferred_element_type=f32)


def matmul_right(left, right):
    return lax.dot_general(left, right, (((1,), (1,)), ((), ())), preferred_element_type=f32)


def ranks_of(owners):
    order = jnp.arange(owners.shape[0])
    same = (owners[:, None] == owners[None, :]) & (order[None, :] < order[:, None])
    return jnp.sum(same.astype(jnp.int32), axis=1)


def segments(lengths, count):
    places = jnp.arange(count)
    end = jnp.zeros((), jnp.int32)
    seg = jnp.zeros((count,), jnp.int32)
    for item in range(lengths.shape[0]):
        end = end + lengths[item]
        seg = seg + (places >= end).astype(jnp.int32)
    return seg


def adam_update(weight, first, second, grad, rate, decay):
    first = beta_one * first + (1.0 - beta_one) * grad
    second = beta_two * second + (1.0 - beta_two) * grad * grad
    fix_one = 1.0 / (1.0 - beta_one**STEP)
    fix_two = 1.0 / (1.0 - beta_two**STEP)
    move = first * fix_one / (jnp.sqrt(second * fix_two) + adam_eps)
    return (weight - rate * (move + decay * weight), first, second)


def pack_columns(master, table, first_slot, slots):
    _, rows, columns = master.shape
    width = columns // 8

    def kernel(table_ref, in_ref, out_ref):
        slot = pl.program_id(0)
        for rank in range(8):
            start = pl.multiple_of(table_ref[slot * 8 + rank] * width, width)
            out_ref[rank, 0] = in_ref[0, :, pl.ds(start, width)].astype(bf16)

    return pl.pallas_call(
        kernel,
        out_shape=jax.ShapeDtypeStruct((8, slots, rows, width), bf16),
        grid_spec=pltpu.PrefetchScalarGridSpec(
            num_scalar_prefetch=1,
            grid=(slots,),
            in_specs=[pl.BlockSpec((1, rows, columns), lambda k, t: (first_slot + k, 0, 0))],
            out_specs=pl.BlockSpec((8, 1, rows, width), lambda k, t: (0, k, 0, 0)),
        ),
        compiler_params=pltpu.CompilerParams(vmem_limit_bytes=VMEM_LIMIT),
        name="pack_columns",
    )(table, master)


def pick_blocks(sources, which, index, count):
    _, rows, width = sources[0].shape
    n_src = len(sources)

    def kernel(which_ref, index_ref, *refs):
        place = pl.program_id(0) * 2 + pl.program_id(1)
        out_ref = refs[n_src]
        for number in range(n_src):

            @pl.when(which_ref[place] == number)
            def _():
                out_ref[...] = refs[number][0]

    def spec(number):
        def at(n, half, which, index):
            place = n * 2 + half
            return (jnp.where(which[place] == number, index[place], 0), 0, 0)

        return pl.BlockSpec((1, rows, width), at)

    return pl.pallas_call(
        kernel,
        out_shape=jax.ShapeDtypeStruct((2 * rows, count * width), bf16),
        grid_spec=pltpu.PrefetchScalarGridSpec(
            num_scalar_prefetch=2,
            grid=(count, 2),
            in_specs=[spec(number) for number in range(n_src)],
            out_specs=pl.BlockSpec((rows, width), lambda n, half, which, index: (half, n)),
        ),
        compiler_params=pltpu.CompilerParams(vmem_limit_bytes=VMEM_LIMIT),
        name="pick_blocks",
    )(which, index, *sources)


def pack_gradients(groups, which, column, rows, width, slots):
    n_src = len(groups)

    def kernel(which_ref, column_ref, *refs):
        rank = pl.program_id(0)
        out_ref = refs[n_src]
        for k in range(slots):
            start = pl.multiple_of(column_ref[rank * slots + k] * width, width)
            for number in range(n_src):

                @pl.when(which_ref[rank * slots + k] == number)
                def _():
                    out_ref[0, k] = refs[number][:, pl.ds(start, width)]

    return pl.pallas_call(
        kernel,
        out_shape=jax.ShapeDtypeStruct((8, slots, rows, width), bf16),
        grid_spec=pltpu.PrefetchScalarGridSpec(
            num_scalar_prefetch=2,
            grid=(8,),
            in_specs=[
                pl.BlockSpec((rows, group.shape[1]), lambda rank, which, column: (rank // 4, 0)) for group in groups
            ],
            out_specs=pl.BlockSpec((1, slots, rows, width), lambda rank, which, column: (rank, 0, 0, 0)),
        ),
        compiler_params=pltpu.CompilerParams(vmem_limit_bytes=VMEM_LIMIT),
        name="pack_gradients",
    )(which, column, *groups)


def adam_tiles(master, one, two, columns_from, rows_from, visit, mode, column_place, row_place, hold, previous=None):
    _, rows, columns = master.shape
    width = columns // 8
    n_visit = visit.shape[0]
    n_col, n_row = len(columns_from), len(rows_from)
    kept = () if previous is None else tuple(previous)

    def kernel(visit_ref, mode_ref, cp_ref, rp_ref, hold_ref, *refs):
        w_ref, m_ref, v_ref = refs[:3]
        grads = refs[3 : 3 + n_col + n_row]
        outs = refs[3 + n_col + n_row + len(kept) :]
        how = mode_ref[pl.program_id(0)]

        @pl.when(how == 1)
        def _():
            for ref in outs:
                ref[...] = jnp.zeros_like(ref)

        for number, grad_ref in enumerate(grads):

            @pl.when(how == number + 2)
            def _():
                grad = grad_ref[0].astype(f32)
                results = adam_update(w_ref[0], m_ref[0], v_ref[0], grad, rate_matrix, decay_rate)
                for ref, value in zip(outs, results, strict=True):
                    ref[0] = value

    def block_of(n, b, hold):
        return jnp.where(hold[n] == 1, 7, b)

    state = pl.BlockSpec((1, rows, width), lambda n, b, vi, mo, cp, rp, ho: (vi[n], 0, block_of(n, b, ho)))

    def column_spec(number):
        def at(n, b, vi, mo, cp, rp, ho):
            place = jnp.where(mo[n] == number + 2, cp[n * 8 + block_of(n, b, ho)], 0)
            return (place // 8, 0, place % 8)

        return pl.BlockSpec((1, rows, width), at)

    def row_spec(number):
        def at(n, b, vi, mo, cp, rp, ho):
            taken = mo[n] == number + 2
            return (jnp.where(taken, rp[n], 0), 0, jnp.where(taken, block_of(n, b, ho), 0))

        return pl.BlockSpec((1, rows, width), at)

    shape = jax.ShapeDtypeStruct(master.shape, f32)
    n_before = 5 + 3 + n_col + n_row
    return pl.pallas_call(
        kernel,
        out_shape=(shape, shape, shape),
        grid_spec=pltpu.PrefetchScalarGridSpec(
            num_scalar_prefetch=5,
            grid=(n_visit, 8),
            in_specs=[
                state,
                state,
                state,
                *(column_spec(number) for number in range(n_col)),
                *(row_spec(n_col + number) for number in range(n_row)),
                *(pl.BlockSpec(memory_space=pl.ANY) for _ in kept),
            ],
            out_specs=(state, state, state),
        ),
        input_output_aliases={n_before + n: n for n in range(len(kept))},
        compiler_params=pltpu.CompilerParams(vmem_limit_bytes=VMEM_LIMIT),
        cost_estimate=pl.CostEstimate(
            flops=30 * n_visit * rows * columns, bytes_accessed=26 * n_visit * rows * columns, transcendentals=0
        ),
        name="adam_tiles",
    )(visit, mode, column_place, row_place, hold, master, one, two, *columns_from, *rows_from, *kept)


def after(value, *others):
    return lax.optimization_barrier((value, *others))[0]


def swap(value, axis):
    return lax.ppermute(value, axis, [(0, 1), (1, 0)])


def gather_rows(value):
    return gather_rest(value, swap(value, "x"), swap(value, "y"))


def gather_rest(value, over_x, over_y):
    half = value.shape[0] // 2
    far_low = swap(over_y[:half], "x")
    far_high = swap(over_x[half:], "y")
    four = jnp.concatenate([value, over_y, over_x, far_low, far_high], axis=0)
    return jnp.concatenate([four, swap(four, "c")], axis=0)


def scatter_rows(part):
    rows, width = part.shape[0] // 8, part.shape[1]
    half = width // 2
    part = part.reshape(2, 2, 2, rows, width)
    chip = part[0] + swap(part[1], "c")
    low, high = chip[..., :half], chip[..., half:]
    low_two = low[:, 0] + swap(low[:, 1].astype(bf16), "y").astype(f32)
    high_two = high[0] + swap(high[1].astype(bf16), "x").astype(f32)
    low_one = low_two[0] + swap(low_two[1].astype(bf16), "x").astype(f32)
    high_one = high_two[0] + swap(high_two[1].astype(bf16), "y").astype(f32)
    return jnp.concatenate([low_one, high_one], axis=1)


def sum_everywhere(value):
    def add_up(terms):
        while len(terms) > 1:
            terms = [terms[n] + terms[n + 1] for n in range(0, len(terms), 2)]
        return terms[0]

    value = add_up([value] + [lax.ppermute(value, ALL_AXES, flip_pairs(mask)) for mask in range(1, 8)])
    flips = [[(z, z ^ mask) for z in range(4)] for mask in range(1, 4)]
    return add_up([value] + [lax.ppermute(value, "z", pairs) for pairs in flips])


def flip_pairs(mask, keep=None):
    pairs = []
    for z in range(4):
        for place in range(8):
            target = place ^ mask
            if keep is None or keep(z, place, target):
                pairs.append((z * 8 + place, z * 8 + target))
    return pairs


ALL_AXES = ("z", "x", "y", "c")
PLANE = ("x", "y", "c")


def plane_body(
    tokens, cotangent, context, lengths, keep, owners, master, moment_one, moment_two, gains, gain_one, gain_two
):
    cap, rows, _ = master.shape
    count, width = tokens.shape
    heads_here = HEADS // 8
    head_dim = width // HEADS
    scale = head_dim ** (-0.5)
    block = width // 8
    z = lax.axis_index("z")
    x = lax.axis_index("x")
    f = lax.axis_index("y") * 2 + lax.axis_index("c")

    n_tiles = owners.shape[0]
    rank = ranks_of(owners)
    shift_of = np.array(SHIFT, np.int32)
    row_of = np.array([t in ROW_TILES for t in range(n_tiles)])
    all_slots = jnp.arange(4 * cap).reshape(4, cap)
    holds = (owners * cap + rank)[None, None, :] == all_slots[:, :, None]
    used_at = jnp.any(holds, axis=2)
    tile_at = jnp.sum(jnp.where(holds, np.arange(n_tiles, dtype=np.int32), 0), axis=2)
    shift_at = jnp.sum(jnp.where(holds, shift_of, 0), axis=2)
    row_at = jnp.any(holds & row_of, axis=2)
    mine = (jnp.arange(4) == f)[:, None]

    def my(value):
        return jnp.sum(jnp.where(mine, value.astype(jnp.int32), 0), axis=0)

    my_used, my_tile, my_shift, my_row = my(used_at), my(tile_at), my(shift_at), my(row_at)

    to_x = np.arange(8) // 4
    to_f = np.arange(8) % 4
    column_table = 2 * ((to_f[None, :] + my_shift[:, None]) % 4) + to_x[None, :]
    half_cap = cap // 2
    place = np.arange(4)

    def of_tiles(tiles, values):
        chosen = tiles[:, None] == np.arange(n_tiles)[None, :]
        return jnp.sum(jnp.where(chosen, values[None, :], 0), axis=1)

    column_tiles = jnp.concatenate([np.array([0, 1, 2, 4, 5, 7, 6, 8], np.int32), 10 + (place - f) % 4])
    column_part = jnp.repeat(of_tiles(column_tiles, rank // half_cap), 2)
    column_place = of_tiles(column_tiles, owners * half_cap + rank % half_cap)
    column_place = (column_place[:, None] + np.array([0, 4 * half_cap])[None, :]).reshape(-1)
    other_f = f ^ place
    outer_tiles = jnp.where(other_f == z, 3, 9)
    out_tiles = 14 + (z - other_f) % 4
    row_slots = of_tiles(jnp.concatenate([outer_tiles, out_tiles]), rank)
    row_owners = of_tiles(jnp.stack([outer_tiles[0], outer_tiles[2], out_tiles[0], out_tiles[2]]), owners)

    def pack_first(weights):
        return pack_columns(weights, column_table[:half_cap].reshape(-1), 0, half_cap)

    def pack_second(weights):
        return pack_columns(weights, column_table[half_cap:].reshape(-1), half_cap, half_cap)

    def my_block(slot):
        return lax.dynamic_index_in_dim(master, slot, 0, keepdims=False).astype(bf16)

    present = owners[0] >= 0

    def chain_step(move, *values):
        shapes = jax.eval_shape(move, *values)
        idle = jax.tree.map(lambda leaf: jnp.zeros(leaf.shape, leaf.dtype), shapes)
        return lax.cond(present, move, lambda *_: idle, *values)

    seg = segments(lengths[0], count)
    live = keep == 1
    code = seg * 2 + live.astype(jnp.int32)

    def spread_code(code):
        for axis in ("y", "x", "c"):
            code = jnp.concatenate([code, swap(code, axis)])
        return code

    grad_out = cotangent.astype(f32) * live.astype(f32)[:, None]
    h0 = tokens.astype(f32)
    outer_blocks = [my_block(row_slots[mask]) for mask in range(4)]
    out_blocks = [my_block(row_slots[4 + mask]) for mask in range(4)]
    a_in = normalize(h0, gains[0]).astype(bf16)
    sent = pack_first(after(master, row_slots, row_owners))
    received = [lax.all_to_all(sent, PLANE, 0, 0, tiled=True).reshape(8 * half_cap, rows, block)]
    code = chain_step(spread_code, after(code, a_in, *outer_blocks, *out_blocks))
    received = [after(received[0], code, a_in, *outer_blocks, *out_blocks)]
    seg_all = (code // 2).reshape(8, count)
    live_all = (code % 2 == 1).reshape(8, count)

    def columns_here(first, count, parts):
        chosen = slice(2 * first, 2 * (first + count))
        return pick_blocks(received[:parts], column_part[chosen], column_place[chosen], count)

    def gather_z(value):
        return lax.all_gather(value, "z", axis=0, tiled=True)

    local = columns_here(0, 3, 1)
    w_qkv = gather_z(local)
    a_ready = after(a_in, local)
    a_x, a_y = swap(a_ready, "x"), swap(a_ready, "y")
    a_all = gather_rest(a_in, a_x, a_y)
    sent = pack_second(after(master, a_x, a_y))
    received.append(lax.all_to_all(sent, PLANE, 0, 0, tiled=True).reshape(8 * half_cap, rows, block))
    slots, ctx_len, ctx_width = context.shape
    ctx = after(context.reshape(slots * ctx_len, ctx_width), sent)
    ctx_x, ctx_y = swap(ctx, "x"), swap(ctx, "y")

    def take_rows(kind, blocks, keep_pair):
        here, there = row_owners[2 * kind], row_owners[2 * kind + 1]
        core = f % 2
        from_core = swap(jnp.stack([blocks[1], blocks[3]]), "c")
        mine = jnp.where(here % 2 == core, blocks[0], from_core[0])
        across = jnp.where(there % 2 == core, blocks[2], from_core[1])
        from_y = lax.ppermute(across, ALL_AXES, flip_pairs(2, keep_pair))
        return jnp.where(here // 2 == f // 2, mine, from_y)

    def needs_outer(zz, place, target):
        return target % 4 in (zz, (zz + 2) % 4)

    outer = take_rows(0, [after(value, local) for value in outer_blocks], needs_outer)
    half_rows = rows // 2
    odd = z % 2
    to_pair = lax.dynamic_slice_in_dim(outer, (1 - odd) * half_rows, half_rows, 0)
    own_half = lax.dynamic_slice_in_dim(outer, odd * half_rows, half_rows, 0)
    pair_swap = [
        (zz * 8 + place, (zz ^ 1) * 8 + place)
        for zz in range(4)
        for place in range(8)
        if place % 4 in (zz, (zz + 2) % 4)
    ]
    from_pair = lax.ppermute(to_pair, ALL_AXES, pair_swap)
    has_outer = (f == z) | (f == (z + 2) % 4)
    outer_all = lax.all_gather(jnp.where(has_outer, own_half, from_pair), "z", axis=0, tiled=True)
    low_y = lax.axis_index("y") == 0
    w_self_out = jnp.where(low_y, outer_all[:rows], outer_all[rows:])
    w_cross_out = jnp.where(low_y, outer_all[rows:], outer_all[:rows])

    def split(value):
        return value.reshape(8, -1, heads_here, head_dim)

    qkv = matmul(after(a_all, received[1]), w_qkv)
    qkv = qkv.astype(bf16)
    query, keys, values = (split(qkv[:, n * block : (n + 1) * block]) for n in range(3))
    places = jnp.arange(count)
    allowed = (seg_all[:, :, None] == seg_all[:, None, :]) & (
        live_all[:, None, :] | (places[:, None] == places[None, :])
    )

    def probabilities(left, right, mask):
        scores = jnp.einsum("bqhd,bkhd->bhqk", left, right, preferred_element_type=f32) * scale
        scores = jnp.where(mask[:, None], scores, -1e30)
        expo = jnp.exp(scores - jnp.max(scores, axis=-1, keepdims=True))
        return expo / jnp.sum(expo, axis=-1, keepdims=True)

    def weighted(probs, right):
        return jnp.einsum("bhqk,bkhd->bqhd", probs, right, preferred_element_type=f32)

    def joined(value):
        return value.astype(bf16).reshape(-1, block)

    probs = probabilities(query, keys, allowed)
    probs_low = probs.astype(bf16)
    mixed = weighted(probs_low, values).astype(bf16)
    attended = mixed.reshape(-1, block)
    local_cross, local_in = columns_here(3, 5, 2), columns_here(8, 4, 2)
    w_cross = gather_z(local_cross)
    w_in = gather_z(local_in)

    def first_step(one, over_x, over_y):
        half = over_x.shape[0] // 2
        return scatter_rows(one), swap(over_y[:half], "x"), swap(over_x[half:], "y")

    h1, far_low, far_high = chain_step(
        first_step, matmul(attended, w_self_out), after(ctx_x, local_in), after(ctx_y, local_in)
    )
    h1 = h0 + h1

    def second_step(one, blocks, pieces):
        four = jnp.concatenate(pieces, axis=0)
        return gather_rows(one), take_rows(1, blocks, None), four, swap(four, "c")

    b_all, out_rows, ctx_here, ctx_there = chain_step(
        second_step, normalize(h1, gains[1]).astype(bf16), out_blocks, (ctx, ctx_y, ctx_x, far_low, far_high)
    )
    w_out = gather_z(out_rows)

    w_cross_q = w_cross[:, :block]
    w_low = w_cross[:, block : 3 * block]
    w_high = w_cross[:, 3 * block :]
    ctx_kv = jnp.concatenate(
        [
            (matmul(part[:, :width], w_low) + matmul(part[:, width:], w_high)).astype(bf16)
            for part in (ctx_here, ctx_there)
        ],
        axis=0,
    )
    cross_q = matmul(b_all, w_cross_q)
    cross_q = split(cross_q.astype(bf16))
    cross_k, cross_v = split(ctx_kv[:, :block]), split(ctx_kv[:, block:])
    item = jnp.arange(slots * ctx_len) // ctx_len
    own_item = seg_all[:, :, None] == item[None, None, :]
    cross_p = probabilities(cross_q, cross_k, own_item)
    cross_low = cross_p.astype(bf16)
    cross_o = joined(weighted(cross_low, cross_v))
    h2, ctx_all = chain_step(
        lambda one, *pieces: (scatter_rows(one), jnp.concatenate(pieces, axis=0)),
        matmul(cross_o, w_cross_out),
        ctx_here,
        ctx_there,
    )
    ctx_low, ctx_high = ctx_all[:, :width], ctx_all[:, width:]
    h2 = h1 + h2
    c_all, d_ff = chain_step(
        lambda one, two: (gather_rows(one), gather_rows(two)),
        normalize(h2, gains[2]).astype(bf16),
        grad_out.astype(bf16),
    )

    hidden = matmul(c_all, w_in)
    activated = gelu_tanh(hidden).astype(bf16)

    def sum_rows(value):
        value = with_layout_constraint(value, Layout(major_to_minor=(0, 1)))
        value = lax.psum_scatter(value, "z", scatter_dimension=0, tiled=True)
        return with_layout_constraint(value, Layout(major_to_minor=(0, 1)))

    def from_y(value, keep_pair=None):
        return jnp.stack([value, lax.ppermute(value, ALL_AXES, flip_pairs(2, keep_pair))])

    def with_core(pair):
        return jnp.concatenate([pair, swap(pair, "c")])

    t_out = matmul_left(activated, d_ff).astype(bf16)
    g_out = sum_rows(t_out)
    d_act = matmul_right(after(d_ff, t_out), w_out)
    d_hidden = jax.vjp(gelu_tanh, hidden)[1](d_act)[0].astype(bf16)
    t_in = matmul_left(c_all, d_hidden).astype(bf16)
    g_in = sum_rows(t_in)
    d_c, out_sum = chain_step(
        lambda one, two: (scatter_rows(one), scatter_rows(two)), matmul_right(d_hidden, w_in), matmul(activated, w_out)
    )
    layer_out = (h2 + out_sum).astype(bf16)
    part_two, gain_grad_two = jax.vjp(normalize, h2, gains[2])[1](d_c)
    dh2 = grad_out + part_two
    d_cross_out = chain_step(gather_rows, after(dh2.astype(bf16), t_in))
    g_cross_out = matmul_left(cross_o, d_cross_out)

    def through(d_mixed, left, right, probs, probs_low, values):
        d_mixed = split(d_mixed.astype(bf16))
        d_probs = jnp.einsum("bqhd,bkhd->bhqk", d_mixed, values, preferred_element_type=f32)
        d_scores = (probs * (d_probs - jnp.sum(probs * d_probs, axis=-1, keepdims=True))).astype(bf16)
        d_left = joined(weighted(d_scores, right) * scale)
        d_right = joined(jnp.einsum("bhqk,bqhd->bkhd", d_scores, left, preferred_element_type=f32) * scale)
        d_values = joined(jnp.einsum("bhqk,bqhd->bkhd", probs_low, d_mixed, preferred_element_type=f32))
        return d_left, d_right, d_values

    (d_cq, d_ck, d_cv), out_grads = chain_step(
        lambda one, two: (
            through(matmul_right(one, w_cross_out), cross_q, cross_k, cross_p, cross_low, cross_v),
            from_y(two),
        ),
        d_cross_out,
        g_out,
    )
    d_ckv = jnp.concatenate([d_ck, d_cv], axis=1)
    t_cross = jnp.concatenate(
        [
            value.astype(bf16)
            for value in (matmul_left(b_all, d_cq), matmul_left(ctx_low, d_ckv), matmul_left(ctx_high, d_ckv))
        ],
        axis=1,
    )
    g_cross = sum_rows(t_cross)
    part = matmul_right(d_cq, w_cross_q)
    d_b = chain_step(scatter_rows, part)
    part_one, gain_grad_one = jax.vjp(normalize, h1, gains[1])[1](d_b)
    dh1 = dh2 + part_one
    d_self_out = chain_step(gather_rows, after(dh1.astype(bf16), t_cross, g_in))
    g_self_out = matmul_left(attended, d_self_out)
    t_outer = jnp.concatenate(
        [
            jnp.where(low_y, g_self_out, g_cross_out).astype(bf16),
            jnp.where(low_y, g_cross_out, g_self_out).astype(bf16),
        ],
        axis=0,
    )
    g_outer = sum_rows(after(t_outer, g_cross))
    d_mixed = matmul_right(after(d_self_out, t_outer), w_self_out)
    d_q, d_k, d_v = through(d_mixed, query, keys, probs, probs_low, values)
    d_qkv = jnp.concatenate([d_q, d_k, d_v], axis=1)
    t_qkv = matmul_left(a_all, d_qkv).astype(bf16)
    g_qkv = sum_rows(t_qkv)
    group_of = np.array([0, 0, 0, 0, 0, 0, 0, 0, 0, 0, 1, 1, 1, 1, 0, 0, 0, 0], np.int32)
    column_of = np.array([0, 0, 0, 0, 0, 1, 3, 2, 4, 0, 0, 1, 2, 3, 0, 0, 0, 0], np.int32)
    group_at = jnp.sum(jnp.where(holds, group_of, 0), axis=2)
    column_at = jnp.sum(jnp.where(holds, column_of, 0), axis=2)
    column_at = jnp.where(group_at == 1, (column_at + f) % 4, column_at)
    sent = pack_gradients(
        [after(g_cross, t_qkv), g_in], jnp.tile(group_at.reshape(-1), 2), jnp.tile(column_at.reshape(-1), 2), rows, block, cap
    )
    early_grads = lax.all_to_all(sent, PLANE, 0, 0, tiled=True).reshape(8 * cap, rows, block)

    def last_step(part, out_pair, gain_grad_one, gain_grad_two):
        part_zero, gain_grad_zero = jax.vjp(normalize, h0, gains[0])[1](scatter_rows(part))
        gain_grads = jnp.stack([gain_grad_zero, gain_grad_one, gain_grad_two])
        return part_zero, sum_everywhere(gain_grads), with_core(out_pair)

    part_zero, gain_total, out_grads = chain_step(
        last_step, matmul_right(after(d_qkv, sent), w_qkv), out_grads, gain_grad_one, gain_grad_two
    )
    grad_tokens = (dh1 + part_zero).astype(bf16)

    upper, lower = g_qkv[:rows], g_qkv[rows:]
    same_x = jnp.where(x == 0, upper, lower)
    other_x = jnp.where(x == 0, lower, upper)
    moved = [lax.ppermute(same_x if mask < 4 else other_x, ALL_AXES, flip_pairs(mask)) for mask in range(1, 8)]
    late_grads = jnp.stack([same_x, *moved])
    back_swap = [(target, source) for source, target in pair_swap]
    other_half = lax.ppermute(after(g_outer, out_grads), ALL_AXES, back_swap)
    outer_grad = jnp.where(
        odd == 0,
        jnp.concatenate([g_outer, other_half], axis=0),
        jnp.concatenate([other_half, g_outer], axis=0),
    )
    outer_pair = from_y(outer_grad, lambda zz, place, _: place % 4 in (zz, (zz + 2) % 4))
    outer_grads = with_core(outer_pair)

    place = np.arange(8)
    source_x, source_f = (place % 2)[None, :], ((place // 2)[None, :] - my_shift[:, None]) % 4
    slot = np.arange(cap, dtype=np.int32)
    column_place = ((source_x * 4 + source_f) * cap + slot[:, None]) * 8
    other_row = ((z - my_shift) % 4) ^ f
    row_source = (other_row % 2) * 2 + other_row // 2
    late = (my_used == 1) & ((my_tile < 4) | (my_tile == 9))
    early_mode = jnp.where(my_used == 0, 1, jnp.where(late, 0, jnp.where(my_row == 1, 3, 2)))
    states = (master, moment_one, moment_two)
    early = None
    for first in (0, half_cap):
        chosen = slice(first, first + half_cap)
        early = adam_tiles(
            *states,
            [early_grads],
            [out_grads],
            slot[chosen],
            after(early_mode, outer_grad)[chosen] if first else early_mode[chosen],
            column_place[chosen].reshape(-1),
            row_source[chosen],
            np.zeros(half_cap, np.int32),
            early,
        )

    n_late = 5
    order = jnp.sum(jnp.where(slot[None, :] < slot[:, None], late.astype(jnp.int32)[None, :], 0), axis=1)
    count_late = jnp.sum(late.astype(jnp.int32))
    step = np.arange(n_late)
    wanted = jnp.minimum(step, jnp.maximum(count_late - 1, 0))
    here = late[None, :] & (order[None, :] == wanted[:, None])

    def at_step(value):
        return jnp.sum(jnp.where(here, value.astype(jnp.int32)[None, :], 0), axis=1)

    hold = (step >= jnp.maximum(count_late, 1)).astype(jnp.int32)
    tile = at_step(my_tile)
    some = count_late > 0
    visit = jnp.where(some, at_step(slot), 0)
    first_mode = jnp.where(early_mode[0] == 3, 4, early_mode[0])
    late_mode = jnp.where(at_step(my_row) == 1, 5, 3)
    mode = jnp.where(hold == 1, 0, jnp.where(some, late_mode, first_mode))
    late_place = (((place % 2)[None, :] ^ x) * 4 + ((place // 2)[None, :] ^ f)) * 8 + tile[:, None]
    late_place = jnp.where(some, late_place, column_place[:1])
    new_w, new_m, new_v = adam_tiles(
        *states,
        [early_grads, late_grads],
        [out_grads, outer_grads],
        visit,
        mode,
        late_place.reshape(-1),
        jnp.where(some, at_step(row_source), row_source[0]),
        hold,
        early,
    )
    new_g, new_gm, new_gv = adam_update(gains, gain_one, gain_two, gain_total, rate_gain, 0.0)
    return (layer_out, grad_tokens, new_w, new_m, new_v, new_g, new_gm, new_gv)


def whole_body(
    tokens, cotangent, context, lengths, keep, owners, master, moment_one, moment_two, gains, gain_one, gain_two
):
    cap = master.shape[0]
    n_tiles = owners.shape[0]
    slot_of = owners * cap + ranks_of(owners)
    owner_rows = lax.all_gather(master.astype(bf16), "fsdp", axis=0, tiled=True)
    tiles = [
        lax.all_gather(
            lax.dynamic_index_in_dim(owner_rows, slot_of[tile], 0, keepdims=False), "dp", axis=0, tiled=True
        )
        for tile in range(n_tiles)
    ]
    w_in = jnp.concatenate(tiles[10:14], axis=1)
    w_out = jnp.concatenate(tiles[14:18], axis=0)
    count, width = tokens.shape
    head_dim = width // HEADS
    scale = head_dim ** (-0.5)
    seg = segments(lengths[0], count)
    live = keep == 1
    places = jnp.arange(count)

    def split(value):
        return value.astype(bf16).reshape(-1, HEADS, head_dim)

    def joined(value):
        return value.astype(bf16).reshape(-1, width)

    def probabilities(left, right, mask):
        scores = jnp.einsum("qhd,khd->hqk", left, right, preferred_element_type=f32) * scale
        scores = jnp.where(mask[None], scores, -1e30)
        expo = jnp.exp(scores - jnp.max(scores, axis=-1, keepdims=True))
        return expo / jnp.sum(expo, axis=-1, keepdims=True)

    def weighted(probs, right):
        return jnp.einsum("hqk,khd->qhd", probs, right, preferred_element_type=f32)

    def through(weights, d_out, left, right, probs, values):
        d_mixed = split(matmul_right(d_out, weights))
        d_probs = jnp.einsum("qhd,khd->hqk", d_mixed, values, preferred_element_type=f32)
        d_scores = (probs * (d_probs - jnp.sum(probs * d_probs, axis=-1, keepdims=True))).astype(bf16)
        d_left = joined(weighted(d_scores, right) * scale)
        d_right = joined(jnp.einsum("hqk,qhd->khd", d_scores, left, preferred_element_type=f32) * scale)
        d_values = joined(jnp.einsum("hqk,qhd->khd", probs.astype(bf16), d_mixed, preferred_element_type=f32))
        return d_left, d_right, d_values

    h0 = tokens.astype(f32)
    a_in = normalize(h0, gains[0]).astype(bf16)
    query, keys, values = (split(matmul(a_in, tiles[n])) for n in range(3))
    allowed = (seg[:, None] == seg[None, :]) & (live[None, :] | (places[:, None] == places[None, :]))
    probs = probabilities(query, keys, allowed)
    attended = joined(weighted(probs.astype(bf16), values))
    h1 = h0 + matmul(attended, tiles[3])
    b_in = normalize(h1, gains[1]).astype(bf16)
    slots, ctx_len, ctx_width = context.shape
    ctx = context.reshape(slots * ctx_len, ctx_width)
    ctx_low, ctx_high = ctx[:, :width], ctx[:, width:]
    cross_q = split(matmul(b_in, tiles[4]))
    cross_k = split(matmul(ctx_low, tiles[5]) + matmul(ctx_high, tiles[6]))
    cross_v = split(matmul(ctx_low, tiles[7]) + matmul(ctx_high, tiles[8]))
    item = jnp.arange(slots * ctx_len) // ctx_len
    cross_p = probabilities(cross_q, cross_k, seg[:, None] == item[None, :])
    cross_o = joined(weighted(cross_p.astype(bf16), cross_v))
    h2 = h1 + matmul(cross_o, tiles[9])
    c_in = normalize(h2, gains[2]).astype(bf16)
    hidden = matmul(c_in, w_in)
    activated = gelu_tanh(hidden).astype(bf16)
    layer_out = (h2 + matmul(activated, w_out)).astype(bf16)
    grad_out = cotangent.astype(f32) * live.astype(f32)[:, None]
    d_ff = grad_out.astype(bf16)
    d_hidden = jax.vjp(gelu_tanh, hidden)[1](matmul_right(d_ff, w_out))[0].astype(bf16)
    part_two, gain_grad_two = jax.vjp(normalize, h2, gains[2])[1](matmul_right(d_hidden, w_in))
    dh2 = grad_out + part_two
    d_cross_out = dh2.astype(bf16)
    d_cq, d_ck, d_cv = through(tiles[9], d_cross_out, cross_q, cross_k, cross_p, cross_v)
    part_one, gain_grad_one = jax.vjp(normalize, h1, gains[1])[1](matmul_right(d_cq, tiles[4]))
    dh1 = dh2 + part_one
    d_self_out = dh1.astype(bf16)
    d_q, d_k, d_v = through(tiles[3], d_self_out, query, keys, probs, values)
    d_a = matmul_right(d_q, tiles[0]) + matmul_right(d_k, tiles[1]) + matmul_right(d_v, tiles[2])
    part_zero, gain_grad_zero = jax.vjp(normalize, h0, gains[0])[1](d_a)
    grad_tokens = (dh1 + part_zero).astype(bf16)
    pairs = [
        (a_in, d_q),
        (a_in, d_k),
        (a_in, d_v),
        (attended, d_self_out),
        (b_in, d_cq),
        (ctx_low, d_ck),
        (ctx_high, d_ck),
        (ctx_low, d_cv),
        (ctx_high, d_cv),
        (cross_o, d_cross_out),
    ]
    for part in range(4):
        pairs.append((c_in, d_hidden[:, part * width : (part + 1) * width]))
    for part in range(4):
        pairs.append((activated[:, part * width : (part + 1) * width], d_ff))
    total_slots = lax.axis_size("fsdp") * cap
    placed = jnp.zeros((total_slots,) + master.shape[1:], bf16)
    for tile, (left, right) in enumerate(pairs):
        term = lax.psum_scatter(
            matmul_left(left, right).astype(bf16), "dp", scatter_dimension=0, tiled=True
        )
        placed = lax.dynamic_update_index_in_dim(placed, term, slot_of[tile], 0)
    owned = lax.psum_scatter(placed, "fsdp", scatter_dimension=0, tiled=True).astype(f32)
    my_slots = lax.axis_index("fsdp") * cap + jnp.arange(cap)
    used = jnp.any(slot_of[None, :] == my_slots[:, None], axis=1)[:, None, None]
    updated = adam_update(master, moment_one, moment_two, owned, rate_matrix, decay_rate)
    new_w, new_m, new_v = (jnp.where(used, value, 0.0) for value in updated)
    gain_grads = jnp.stack([gain_grad_zero, gain_grad_one, gain_grad_two])
    gain_total = lax.psum(gain_grads, ("dp", "fsdp"))
    new_g, new_gm, new_gv = adam_update(gains, gain_one, gain_two, gain_total, rate_gain, 0.0)
    return (layer_out, grad_tokens, new_w, new_m, new_v, new_g, new_gm, new_gv)


def solution(mesh):
    planes = mesh.shape["dp"] == 8 and mesh.shape["fsdp"] == 4
    if planes:
        used = Mesh(mesh.devices.reshape(4, 2, 2, 2), ALL_AXES)
        dp, fsdp, body = ("z", "x"), ("y", "c"), plane_body
    else:
        used, dp, fsdp, body = mesh, ("dp",), ("fsdp",), whole_body
    rows = P(dp + fsdp, None)
    tiles = P(fsdp, dp, None)
    return jax.shard_map(
        body,
        mesh=used,
        in_specs=(rows, rows, P(dp + fsdp, None, None), rows, P(dp + fsdp), P(), tiles, tiles, tiles, P(), P(), P()),
        out_specs=(rows, rows, tiles, tiles, tiles, P(), P(), P()),
        check_vma=False,
    )
```

```python
import jax
import jax.numpy as jnp
import numpy as np
from jax import lax
from jax.experimental import pallas as pl
from jax.experimental.layout import Layout, with_layout_constraint
from jax.experimental.pallas import tpu as pltpu
from jax.sharding import Mesh
from jax.sharding import PartitionSpec as P

HEADS = 16
STEP = 10

norm_eps = 1e-06
beta_one = 0.9
beta_two = 0.95
adam_eps = 1e-08
decay_rate = 0.1
rate_matrix = 0.1
rate_gain = 0.8

f32 = jnp.float32
bf16 = jnp.bfloat16

SHIFT = (0, 0, 0, 0, 2, 2, 2, 2, 2, 2, 0, 1, 2, 3, 0, 1, 2, 3)
ROW_TILES = (3, 9, 14, 15, 16, 17)
VMEM_LIMIT = 48 << 20


def normalize(h, gain):
    scale = lax.rsqrt(jnp.mean(h * h, axis=-1, keepdims=True) + norm_eps)
    return h * scale * gain


def gelu_tanh(u):
    return 0.5 * u * (1.0 + jnp.tanh(0.7978845608028654 * (u + 0.044715 * u * u * u)))


def matmul(left, right):
    return jnp.dot(left, right, preferred_element_type=f32)


def matmul_left(left, right):
    return lax.dot_general(left, right, (((0,), (0,)), ((), ())), preferred_element_type=f32)


def matmul_right(left, right):
    return lax.dot_general(left, right, (((1,), (1,)), ((), ())), preferred_element_type=f32)


def ranks_of(owners):
    order = jnp.arange(owners.shape[0])
    same = (owners[:, None] == owners[None, :]) & (order[None, :] < order[:, None])
    return jnp.sum(same.astype(jnp.int32), axis=1)


def segments(lengths, count):
    places = jnp.arange(count)
    end = jnp.zeros((), jnp.int32)
    seg = jnp.zeros((count,), jnp.int32)
    for item in range(lengths.shape[0]):
        end = end + lengths[item]
        seg = seg + (places >= end).astype(jnp.int32)
    return seg


def adam_update(weight, first, second, grad, rate, decay):
    first = beta_one * first + (1.0 - beta_one) * grad
    second = beta_two * second + (1.0 - beta_two) * grad * grad
    fix_one = 1.0 / (1.0 - beta_one**STEP)
    fix_two = 1.0 / (1.0 - beta_two**STEP)
    move = first * fix_one / (jnp.sqrt(second * fix_two) + adam_eps)
    return (weight - rate * (move + decay * weight), first, second)


def pack_columns(master, table, first_slot, slots):
    _, rows, columns = master.shape
    width = columns // 8

    def kernel(table_ref, in_ref, out_ref):
        slot = pl.program_id(0)
        for rank in range(8):
            start = pl.multiple_of(table_ref[slot * 8 + rank] * width, width)
            out_ref[rank, 0] = in_ref[0, :, pl.ds(start, width)].astype(bf16)

    return pl.pallas_call(
        kernel,
        out_shape=jax.ShapeDtypeStruct((8, slots, rows, width), bf16),
        grid_spec=pltpu.PrefetchScalarGridSpec(
            num_scalar_prefetch=1,
            grid=(slots,),
            in_specs=[pl.BlockSpec((1, rows, columns), lambda k, t: (first_slot + k, 0, 0))],
            out_specs=pl.BlockSpec((8, 1, rows, width), lambda k, t: (0, k, 0, 0)),
        ),
        compiler_params=pltpu.CompilerParams(vmem_limit_bytes=VMEM_LIMIT),
        name="pack_columns",
    )(table, master)


def pick_blocks(sources, which, index, count):
    _, rows, width = sources[0].shape
    n_src = len(sources)

    def kernel(which_ref, index_ref, *refs):
        place = pl.program_id(0) * 2 + pl.program_id(1)
        out_ref = refs[n_src]
        for number in range(n_src):

            @pl.when(which_ref[place] == number)
            def _():
                out_ref[...] = refs[number][0]

    def spec(number):
        def at(n, half, which, index):
            place = n * 2 + half
            return (jnp.where(which[place] == number, index[place], 0), 0, 0)

        return pl.BlockSpec((1, rows, width), at)

    return pl.pallas_call(
        kernel,
        out_shape=jax.ShapeDtypeStruct((2 * rows, count * width), bf16),
        grid_spec=pltpu.PrefetchScalarGridSpec(
            num_scalar_prefetch=2,
            grid=(count, 2),
            in_specs=[spec(number) for number in range(n_src)],
            out_specs=pl.BlockSpec((rows, width), lambda n, half, which, index: (half, n)),
        ),
        compiler_params=pltpu.CompilerParams(vmem_limit_bytes=VMEM_LIMIT),
        name="pick_blocks",
    )(which, index, *sources)


def pack_gradients(groups, which, column, rows, width, slots):
    n_src = len(groups)

    def kernel(which_ref, column_ref, *refs):
        rank = pl.program_id(0)
        out_ref = refs[n_src]
        for k in range(slots):
            start = pl.multiple_of(column_ref[rank * slots + k] * width, width)
            for number in range(n_src):

                @pl.when(which_ref[rank * slots + k] == number)
                def _():
                    out_ref[0, k] = refs[number][:, pl.ds(start, width)]

    return pl.pallas_call(
        kernel,
        out_shape=jax.ShapeDtypeStruct((8, slots, rows, width), bf16),
        grid_spec=pltpu.PrefetchScalarGridSpec(
            num_scalar_prefetch=2,
            grid=(8,),
            in_specs=[
                pl.BlockSpec((rows, group.shape[1]), lambda rank, which, column: (rank // 4, 0)) for group in groups
            ],
            out_specs=pl.BlockSpec((1, slots, rows, width), lambda rank, which, column: (rank, 0, 0, 0)),
        ),
        compiler_params=pltpu.CompilerParams(vmem_limit_bytes=VMEM_LIMIT),
        name="pack_gradients",
    )(which, column, *groups)


def adam_tiles(master, one, two, columns_from, rows_from, visit, mode, column_place, row_place, hold, previous=None):
    _, rows, columns = master.shape
    width = columns // 8
    n_visit = visit.shape[0]
    n_col, n_row = len(columns_from), len(rows_from)
    kept = () if previous is None else tuple(previous[:3])

    def kernel(visit_ref, mode_ref, cp_ref, rp_ref, hold_ref, *refs):
        w_ref, m_ref, v_ref = refs[:3]
        grads = refs[3 : 3 + n_col + n_row]
        outs = refs[3 + n_col + n_row + len(kept) : -1]
        refs[-1][...] = jnp.zeros_like(refs[-1])
        how = mode_ref[pl.program_id(0)]

        @pl.when(how == 1)
        def _():
            for ref in outs:
                ref[...] = jnp.zeros_like(ref)

        for number, grad_ref in enumerate(grads):

            @pl.when(how == number + 2)
            def _():
                grad = grad_ref[0].astype(f32)
                results = adam_update(w_ref[0], m_ref[0], v_ref[0], grad, rate_matrix, decay_rate)
                for ref, value in zip(outs, results, strict=True):
                    ref[0] = value

    def block_of(n, b, hold):
        return jnp.where(hold[n] == 1, 7, b)

    state = pl.BlockSpec((1, rows, width), lambda n, b, vi, mo, cp, rp, ho: (vi[n], 0, block_of(n, b, ho)))

    def column_spec(number):
        def at(n, b, vi, mo, cp, rp, ho):
            return (jnp.where(mo[n] == number + 2, cp[n * 8 + block_of(n, b, ho)], 0), 0, 0)

        return pl.BlockSpec((1, rows, width), at)

    def row_spec(number):
        def at(n, b, vi, mo, cp, rp, ho):
            taken = mo[n] == number + 2
            return (jnp.where(taken, rp[n], 0), 0, jnp.where(taken, block_of(n, b, ho), 0))

        return pl.BlockSpec((1, rows, width), at)

    shape = jax.ShapeDtypeStruct(master.shape, f32)
    n_before = 5 + 3 + n_col + n_row
    return pl.pallas_call(
        kernel,
        out_shape=(shape, shape, shape, jax.ShapeDtypeStruct((8, 128), f32)),
        grid_spec=pltpu.PrefetchScalarGridSpec(
            num_scalar_prefetch=5,
            grid=(n_visit, 8),
            in_specs=[
                state,
                state,
                state,
                *(column_spec(number) for number in range(n_col)),
                *(row_spec(n_col + number) for number in range(n_row)),
                *(pl.BlockSpec(memory_space=pl.ANY) for _ in kept),
            ],
            out_specs=(state, state, state, pl.BlockSpec((8, 128), lambda *_: (0, 0))),
        ),
        input_output_aliases={n_before + n: n for n in range(len(kept))},
        compiler_params=pltpu.CompilerParams(vmem_limit_bytes=VMEM_LIMIT),
        cost_estimate=pl.CostEstimate(
            flops=30 * n_visit * rows * columns, bytes_accessed=26 * n_visit * rows * columns, transcendentals=0
        ),
        name="adam_tiles",
    )(visit, mode, column_place, row_place, hold, master, one, two, *columns_from, *rows_from, *kept)


def after(value, *others):
    return lax.optimization_barrier((value, *others))[0]


def swap(value, axis):
    return lax.ppermute(value, axis, [(0, 1), (1, 0)])


def gather_rows(value):
    half = value.shape[0] // 2
    over_x = swap(value, "x")
    over_y = swap(value, "y")
    far_low = swap(over_y[:half], "x")
    far_high = swap(over_x[half:], "y")
    four = jnp.concatenate([value, over_y, over_x, far_low, far_high], axis=0)
    return jnp.concatenate([four, swap(four, "c")], axis=0)


def scatter_rows(part):
    rows, width = part.shape[0] // 8, part.shape[1]
    half = width // 2
    part = part.reshape(2, 2, 2, rows, width)
    chip = part[0] + swap(part[1], "c")
    low, high = chip[..., :half], chip[..., half:]
    low_two = low[:, 0] + swap(low[:, 1].astype(bf16), "y").astype(f32)
    high_two = high[0] + swap(high[1].astype(bf16), "x").astype(f32)
    low_one = low_two[0] + swap(low_two[1].astype(bf16), "x").astype(f32)
    high_one = high_two[0] + swap(high_two[1].astype(bf16), "y").astype(f32)
    return jnp.concatenate([low_one, high_one], axis=1)


def sum_everywhere(value):
    for axis in ("c", "y", "x"):
        value = value + swap(value, axis)
    for step in (1, 2):
        value = value + lax.ppermute(value, "z", [(z, z ^ step) for z in range(4)])
    return value


def flip_pairs(mask, keep=None):
    pairs = []
    for z in range(4):
        for place in range(8):
            target = place ^ mask
            if keep is None or keep(z, place, target):
                pairs.append((z * 8 + place, z * 8 + target))
    return pairs


ALL_AXES = ("z", "x", "y", "c")
PLANE = ("x", "y", "c")


def plane_body(
    tokens, cotangent, context, lengths, keep, owners, master, moment_one, moment_two, gains, gain_one, gain_two
):
    cap, rows, _ = master.shape
    count, width = tokens.shape
    heads_here = HEADS // 8
    head_dim = width // HEADS
    scale = head_dim ** (-0.5)
    block = width // 8
    z = lax.axis_index("z")
    x = lax.axis_index("x")
    f = lax.axis_index("y") * 2 + lax.axis_index("c")

    n_tiles = owners.shape[0]
    rank = ranks_of(owners)
    shift_of = np.array(SHIFT, np.int32)
    row_of = np.array([t in ROW_TILES for t in range(n_tiles)])
    all_slots = jnp.arange(4 * cap).reshape(4, cap)
    holds = (owners * cap + rank)[None, None, :] == all_slots[:, :, None]
    used_at = jnp.any(holds, axis=2)
    tile_at = jnp.sum(jnp.where(holds, np.arange(n_tiles, dtype=np.int32), 0), axis=2)
    shift_at = jnp.sum(jnp.where(holds, shift_of, 0), axis=2)
    row_at = jnp.any(holds & row_of, axis=2)
    mine = (jnp.arange(4) == f)[:, None]

    def my(value):
        return jnp.sum(jnp.where(mine, value.astype(jnp.int32), 0), axis=0)

    my_used, my_tile, my_shift, my_row = my(used_at), my(tile_at), my(shift_at), my(row_at)

    to_x = np.arange(8) // 4
    to_f = np.arange(8) % 4
    column_table = 2 * ((to_f[None, :] + my_shift[:, None]) % 4) + to_x[None, :]
    half_cap = cap // 2
    place = np.arange(4)

    def of_tiles(tiles, values):
        chosen = tiles[:, None] == np.arange(n_tiles)[None, :]
        return jnp.sum(jnp.where(chosen, values[None, :], 0), axis=1)

    column_tiles = jnp.concatenate([np.array([0, 1, 2, 4, 5, 7, 6, 8], np.int32), 10 + (place - f) % 4])
    column_part = jnp.repeat(of_tiles(column_tiles, rank // half_cap), 2)
    column_place = of_tiles(column_tiles, owners * half_cap + rank % half_cap)
    column_place = (column_place[:, None] + np.array([0, 4 * half_cap])[None, :]).reshape(-1)
    other_f = f ^ place
    outer_tiles = jnp.where(other_f == z, 3, 9)
    out_tiles = 14 + (z - other_f) % 4
    row_slots = of_tiles(jnp.concatenate([outer_tiles, out_tiles]), rank)
    row_owners = of_tiles(jnp.stack([outer_tiles[0], outer_tiles[2], out_tiles[0], out_tiles[2]]), owners)

    def pack_first(weights):
        return pack_columns(weights, column_table[:half_cap].reshape(-1), 0, half_cap)

    def pack_second(weights):
        return pack_columns(weights, column_table[half_cap:].reshape(-1), half_cap, half_cap)

    def my_block(slot):
        return lax.dynamic_index_in_dim(master, slot, 0, keepdims=False).astype(bf16)

    present = owners[0] >= 0

    def chain_step(move, *values):
        shapes = jax.eval_shape(move, *values)
        idle = jax.tree.map(lambda leaf: jnp.zeros(leaf.shape, leaf.dtype), shapes)
        return lax.cond(present, move, lambda *_: idle, *values)

    h0 = tokens.astype(f32)
    outer_blocks = [my_block(row_slots[mask]) for mask in range(4)]
    out_blocks = [my_block(row_slots[4 + mask]) for mask in range(4)]
    a_in = normalize(h0, gains[0]).astype(bf16)
    sent = pack_first(after(master, column_part, column_place, row_slots, row_owners))
    received = [lax.all_to_all(sent, PLANE, 0, 0, tiled=True).reshape(8 * half_cap, rows, block)]
    seg = segments(lengths[0], count)
    live = keep == 1
    code = seg * 2 + live.astype(jnp.int32)

    def spread_code(code):
        for axis in ("y", "x", "c"):
            code = jnp.concatenate([code, swap(code, axis)])
        return code

    code = chain_step(spread_code, after(code, a_in, *outer_blocks, *out_blocks))
    seg_all = (code // 2).reshape(8, count)
    live_all = (code % 2 == 1).reshape(8, count)
    grad_out = cotangent.astype(f32) * live.astype(f32)[:, None]
    received = [after(received[0], a_in, code, *outer_blocks, *out_blocks)]

    def columns_here(first, count, parts):
        chosen = slice(2 * first, 2 * (first + count))
        return pick_blocks(received[:parts], column_part[chosen], column_place[chosen], count)

    def gather_z(value):
        return lax.all_gather(value, "z", axis=0, tiled=True)

    local = columns_here(0, 3, 1)
    w_qkv = gather_z(local)
    a_all = gather_rows(after(a_in, local))
    d_ff = gather_rows(after(grad_out.astype(bf16), local))
    sent = pack_second(after(master, a_all, d_ff))
    received.append(lax.all_to_all(sent, PLANE, 0, 0, tiled=True).reshape(8 * half_cap, rows, block))

    def take_rows(kind, blocks, keep_pair):
        here, there = row_owners[2 * kind], row_owners[2 * kind + 1]
        core = f % 2
        from_core = swap(jnp.stack([blocks[1], blocks[3]]), "c")
        mine = jnp.where(here % 2 == core, blocks[0], from_core[0])
        across = jnp.where(there % 2 == core, blocks[2], from_core[1])
        from_y = lax.ppermute(across, ALL_AXES, flip_pairs(2, keep_pair))
        return jnp.where(here // 2 == f // 2, mine, from_y)

    def needs_outer(zz, place, target):
        return target % 4 in (zz, (zz + 2) % 4)

    outer = take_rows(0, [after(value, local) for value in outer_blocks], needs_outer)
    out_rows = take_rows(1, [after(value, local) for value in out_blocks], None)
    half_rows = rows // 2
    odd = z % 2
    to_pair = lax.dynamic_slice_in_dim(after(outer, sent), (1 - odd) * half_rows, half_rows, 0)
    own_half = lax.dynamic_slice_in_dim(outer, odd * half_rows, half_rows, 0)
    pair_swap = [
        (zz * 8 + place, (zz ^ 1) * 8 + place)
        for zz in range(4)
        for place in range(8)
        if place % 4 in (zz, (zz + 2) % 4)
    ]
    from_pair = lax.ppermute(to_pair, ALL_AXES, pair_swap)
    has_outer = (f == z) | (f == (z + 2) % 4)
    outer_all = lax.all_gather(jnp.where(has_outer, own_half, from_pair), "z", axis=0, tiled=True)
    low_y = lax.axis_index("y") == 0
    w_self_out = jnp.where(low_y, outer_all[:rows], outer_all[rows:])
    w_cross_out = jnp.where(low_y, outer_all[rows:], outer_all[:rows])

    def split(value):
        return value.reshape(8, -1, heads_here, head_dim)

    qkv = matmul(a_all, w_qkv)
    qkv = qkv.astype(bf16)
    query, keys, values = (split(qkv[:, n * block : (n + 1) * block]) for n in range(3))
    places = jnp.arange(count)
    allowed = (seg_all[:, :, None] == seg_all[:, None, :]) & (
        live_all[:, None, :] | (places[:, None] == places[None, :])
    )

    def probabilities(left, right, mask):
        scores = jnp.einsum("bqhd,bkhd->bhqk", left, right, preferred_element_type=f32) * scale
        scores = jnp.where(mask[:, None], scores, -1e30)
        expo = jnp.exp(scores - jnp.max(scores, axis=-1, keepdims=True))
        return expo / jnp.sum(expo, axis=-1, keepdims=True)

    def weighted(probs, right):
        return jnp.einsum("bhqk,bkhd->bqhd", probs, right, preferred_element_type=f32)

    def joined(value):
        return value.astype(bf16).reshape(-1, block)

    probs = probabilities(query, keys, allowed)
    probs_low = probs.astype(bf16)
    mixed = weighted(probs_low, values).astype(bf16)
    attended = mixed.reshape(-1, block)
    received[1] = after(received[1], mixed)
    local_cross, local_in = columns_here(3, 5, 2), columns_here(8, 4, 2)
    w_cross = gather_z(local_cross)
    w_in = gather_z(local_in)

    w_out = gather_z(after(out_rows, local_cross, local_in))
    slots, ctx_len, ctx_width = context.shape
    ctx = after(context.reshape(slots * ctx_len, ctx_width), local_cross, local_in, out_rows)
    ctx_x, ctx_y = swap(ctx, "x"), swap(ctx, "y")
    h1 = h0 + chain_step(scatter_rows, matmul(after(attended, local_in), w_self_out))

    def second_step(one, own, over_x, over_y):
        half = over_x.shape[0] // 2
        far_low, far_high = swap(over_y[:half], "x"), swap(over_x[half:], "y")
        four = jnp.concatenate([own, over_y, over_x, far_low, far_high], axis=0)
        return gather_rows(one), four, swap(four, "c")

    b_all, ctx_here, ctx_there = chain_step(
        second_step, normalize(h1, gains[1]).astype(bf16), ctx, ctx_x, ctx_y
    )

    w_cross_q = w_cross[:, :block]
    w_low = w_cross[:, block : 3 * block]
    w_high = w_cross[:, 3 * block :]
    ctx_kv = jnp.concatenate(
        [
            (matmul(part[:, :width], w_low) + matmul(part[:, width:], w_high)).astype(bf16)
            for part in (ctx_here, ctx_there)
        ],
        axis=0,
    )
    cross_q = matmul(b_all, w_cross_q)
    cross_q = split(cross_q.astype(bf16))
    cross_k, cross_v = split(ctx_kv[:, :block]), split(ctx_kv[:, block:])
    item = jnp.arange(slots * ctx_len) // ctx_len
    own_item = seg_all[:, :, None] == item[None, None, :]
    cross_p = probabilities(cross_q, cross_k, own_item)
    cross_low = cross_p.astype(bf16)
    cross_o = joined(weighted(cross_low, cross_v))
    h2, ctx_all = chain_step(
        lambda one, *pieces: (scatter_rows(one), jnp.concatenate(pieces, axis=0)),
        matmul(cross_o, w_cross_out),
        ctx_here,
        ctx_there,
    )
    ctx_low, ctx_high = ctx_all[:, :width], ctx_all[:, width:]
    h2 = h1 + h2
    c_all = chain_step(gather_rows, normalize(h2, gains[2]).astype(bf16))

    hidden = matmul(c_all, w_in)
    activated = gelu_tanh(hidden).astype(bf16)

    def sum_rows(value):
        value = with_layout_constraint(value, Layout(major_to_minor=(0, 1)))
        value = lax.psum_scatter(value, "z", scatter_dimension=0, tiled=True)
        return with_layout_constraint(value, Layout(major_to_minor=(0, 1)))

    def from_y(value, keep_pair=None):
        return jnp.stack([value, lax.ppermute(value, ALL_AXES, flip_pairs(2, keep_pair))])

    def with_core(pair):
        return jnp.concatenate([pair, swap(pair, "c")])

    t_out = matmul_left(activated, d_ff).astype(bf16)
    g_out = sum_rows(t_out)
    d_act = matmul_right(after(d_ff, t_out), w_out)
    d_hidden = jax.vjp(gelu_tanh, hidden)[1](d_act)[0].astype(bf16)
    t_in = matmul_left(c_all, d_hidden).astype(bf16)
    g_in = sum_rows(t_in)
    d_c, out_sum = chain_step(
        lambda one, two: (scatter_rows(one), scatter_rows(two)), matmul_right(d_hidden, w_in), matmul(activated, w_out)
    )
    layer_out = (h2 + out_sum).astype(bf16)
    part_two, gain_grad_two = jax.vjp(normalize, h2, gains[2])[1](d_c)
    dh2 = grad_out + part_two
    d_cross_out = chain_step(gather_rows, after(dh2.astype(bf16), t_in))
    g_cross_out = matmul_left(cross_o, d_cross_out)

    def through(d_mixed, left, right, probs, probs_low, values):
        d_mixed = split(d_mixed.astype(bf16))
        d_probs = jnp.einsum("bqhd,bkhd->bhqk", d_mixed, values, preferred_element_type=f32)
        d_scores = (probs * (d_probs - jnp.sum(probs * d_probs, axis=-1, keepdims=True))).astype(bf16)
        d_left = joined(weighted(d_scores, right) * scale)
        d_right = joined(jnp.einsum("bhqk,bqhd->bkhd", d_scores, left, preferred_element_type=f32) * scale)
        d_values = joined(jnp.einsum("bhqk,bqhd->bkhd", probs_low, d_mixed, preferred_element_type=f32))
        return d_left, d_right, d_values

    (d_cq, d_ck, d_cv), out_grads = chain_step(
        lambda one, two: (
            through(matmul_right(one, w_cross_out), cross_q, cross_k, cross_p, cross_low, cross_v),
            from_y(two),
        ),
        d_cross_out,
        g_out,
    )
    d_ckv = jnp.concatenate([d_ck, d_cv], axis=1)
    t_cross = jnp.concatenate(
        [
            value.astype(bf16)
            for value in (matmul_left(b_all, d_cq), matmul_left(ctx_low, d_ckv), matmul_left(ctx_high, d_ckv))
        ],
        axis=1,
    )
    g_cross = sum_rows(t_cross)
    part = matmul_right(d_cq, w_cross_q)
    d_b = chain_step(scatter_rows, part)
    part_one, gain_grad_one = jax.vjp(normalize, h1, gains[1])[1](d_b)
    dh1 = dh2 + part_one
    d_self_out = chain_step(gather_rows, after(dh1.astype(bf16), t_cross, g_in))
    g_self_out = matmul_left(attended, d_self_out)
    t_outer = jnp.concatenate(
        [
            jnp.where(low_y, g_self_out, g_cross_out).astype(bf16),
            jnp.where(low_y, g_cross_out, g_self_out).astype(bf16),
        ],
        axis=0,
    )
    g_outer = sum_rows(after(t_outer, g_cross))
    d_mixed = matmul_right(after(d_self_out, t_outer), w_self_out)
    d_q, d_k, d_v = through(d_mixed, query, keys, probs, probs_low, values)
    d_qkv = jnp.concatenate([d_q, d_k, d_v], axis=1)
    t_qkv = matmul_left(a_all, d_qkv).astype(bf16)
    g_qkv = sum_rows(t_qkv)
    group_of = np.array([0, 0, 0, 0, 0, 0, 0, 0, 0, 0, 1, 1, 1, 1, 0, 0, 0, 0], np.int32)
    column_of = np.array([0, 0, 0, 0, 0, 1, 3, 2, 4, 0, 0, 1, 2, 3, 0, 0, 0, 0], np.int32)
    group_at = jnp.sum(jnp.where(holds, group_of, 0), axis=2)
    column_at = jnp.sum(jnp.where(holds, column_of, 0), axis=2)
    column_at = jnp.where(group_at == 1, (column_at + f) % 4, column_at)
    sent = pack_gradients(
        [after(g_cross, t_qkv), g_in], jnp.tile(group_at.reshape(-1), 2), jnp.tile(column_at.reshape(-1), 2), rows, block, cap
    )
    early_grads = lax.all_to_all(sent, PLANE, 0, 0, tiled=True).reshape(8 * cap, rows, block)

    def last_step(part, out_pair, gain_grad_one, gain_grad_two):
        part_zero, gain_grad_zero = jax.vjp(normalize, h0, gains[0])[1](scatter_rows(part))
        gain_grads = jnp.stack([gain_grad_zero, gain_grad_one, gain_grad_two])
        return part_zero, sum_everywhere(gain_grads), with_core(out_pair)

    part_zero, gain_total, out_grads = chain_step(
        last_step, matmul_right(after(d_qkv, sent), w_qkv), out_grads, gain_grad_one, gain_grad_two
    )
    grad_tokens = (dh1 + part_zero).astype(bf16)

    by_tile = jnp.swapaxes(after(g_qkv, out_grads).reshape(2, rows, 3, block), 1, 2)
    sent = jnp.broadcast_to(by_tile[:, None], (2, 4, 3, rows, block)).reshape(8, 3, rows, block)
    late_grads = lax.all_to_all(sent, PLANE, 0, 0, tiled=True).reshape(8 * 3, rows, block)
    back_swap = [(target, source) for source, target in pair_swap]
    other_half = lax.ppermute(after(g_outer, sent), ALL_AXES, back_swap)
    place = np.arange(8)
    source_x, source_f = (place % 2)[None, :], ((place // 2)[None, :] - my_shift[:, None]) % 4
    slot = np.arange(cap, dtype=np.int32)
    column_place = (source_x * 4 + source_f) * cap + slot[:, None]
    other_row = ((z - my_shift) % 4) ^ f
    row_source = (other_row % 2) * 2 + other_row // 2
    late = (my_used == 1) & ((my_tile < 4) | (my_tile == 9))
    early_mode = jnp.where(my_used == 0, 1, jnp.where(late, 0, jnp.where(my_row == 1, 3, 2)))
    states = (master, moment_one, moment_two)

    def adam_early(first, mode, previous):
        chosen = slice(first, first + half_cap)
        return adam_tiles(
            *states,
            [early_grads],
            [out_grads],
            slot[chosen],
            mode[chosen],
            column_place[chosen].reshape(-1),
            row_source[chosen],
            np.zeros(half_cap, np.int32),
            previous,
        )

    early = adam_early(0, early_mode, None)
    other_half = after(other_half, early[3])
    outer_grad = jnp.where(
        odd == 0,
        jnp.concatenate([g_outer, other_half], axis=0),
        jnp.concatenate([other_half, g_outer], axis=0),
    )
    outer_pair = from_y(outer_grad, lambda zz, place, _: place % 4 in (zz, (zz + 2) % 4))
    early = adam_early(half_cap, after(early_mode, outer_grad), early)
    outer_grads = with_core(outer_pair)

    n_late = 5
    order = jnp.sum(jnp.where(slot[None, :] < slot[:, None], late.astype(jnp.int32)[None, :], 0), axis=1)
    count_late = jnp.sum(late.astype(jnp.int32))
    step = np.arange(n_late)
    wanted = jnp.minimum(step, jnp.maximum(count_late - 1, 0))
    here = late[None, :] & (order[None, :] == wanted[:, None])

    def at_step(value):
        return jnp.sum(jnp.where(here, value.astype(jnp.int32)[None, :], 0), axis=1)

    hold = (step >= jnp.maximum(count_late, 1)).astype(jnp.int32)
    tile = at_step(my_tile)
    some = count_late > 0
    visit = jnp.where(some, at_step(slot), 0)
    first_mode = jnp.where(early_mode[0] == 3, 4, early_mode[0])
    late_mode = jnp.where(at_step(my_row) == 1, 5, 3)
    mode = jnp.where(hold == 1, 0, jnp.where(some, late_mode, first_mode))
    late_place = ((place % 2)[None, :] * 4 + (place // 2)[None, :]) * 3 + tile[:, None]
    late_place = jnp.where(some, late_place, column_place[:1])
    new_w, new_m, new_v, _ = adam_tiles(
        *states,
        [early_grads, late_grads],
        [out_grads, outer_grads],
        visit,
        mode,
        late_place.reshape(-1),
        jnp.where(some, at_step(row_source), row_source[0]),
        hold,
        early,
    )
    new_g, new_gm, new_gv = adam_update(gains, gain_one, gain_two, gain_total, rate_gain, 0.0)
    return (layer_out, grad_tokens, new_w, new_m, new_v, new_g, new_gm, new_gv)


def whole_body(
    tokens, cotangent, context, lengths, keep, owners, master, moment_one, moment_two, gains, gain_one, gain_two
):
    cap = master.shape[0]
    n_tiles = owners.shape[0]
    slot_of = owners * cap + ranks_of(owners)
    owner_rows = lax.all_gather(master.astype(bf16), "fsdp", axis=0, tiled=True)
    tiles = [
        lax.all_gather(
            lax.dynamic_index_in_dim(owner_rows, slot_of[tile], 0, keepdims=False), "dp", axis=0, tiled=True
        )
        for tile in range(n_tiles)
    ]
    w_in = jnp.concatenate(tiles[10:14], axis=1)
    w_out = jnp.concatenate(tiles[14:18], axis=0)
    count, width = tokens.shape
    head_dim = width // HEADS
    scale = head_dim ** (-0.5)
    seg = segments(lengths[0], count)
    live = keep == 1
    places = jnp.arange(count)

    def split(value):
        return value.astype(bf16).reshape(-1, HEADS, head_dim)

    def joined(value):
        return value.astype(bf16).reshape(-1, width)

    def probabilities(left, right, mask):
        scores = jnp.einsum("qhd,khd->hqk", left, right, preferred_element_type=f32) * scale
        scores = jnp.where(mask[None], scores, -1e30)
        expo = jnp.exp(scores - jnp.max(scores, axis=-1, keepdims=True))
        return expo / jnp.sum(expo, axis=-1, keepdims=True)

    def weighted(probs, right):
        return jnp.einsum("hqk,khd->qhd", probs, right, preferred_element_type=f32)

    def through(weights, d_out, left, right, probs, values):
        d_mixed = split(matmul_right(d_out, weights))
        d_probs = jnp.einsum("qhd,khd->hqk", d_mixed, values, preferred_element_type=f32)
        d_scores = (probs * (d_probs - jnp.sum(probs * d_probs, axis=-1, keepdims=True))).astype(bf16)
        d_left = joined(weighted(d_scores, right) * scale)
        d_right = joined(jnp.einsum("hqk,qhd->khd", d_scores, left, preferred_element_type=f32) * scale)
        d_values = joined(jnp.einsum("hqk,qhd->khd", probs.astype(bf16), d_mixed, preferred_element_type=f32))
        return d_left, d_right, d_values

    h0 = tokens.astype(f32)
    a_in = normalize(h0, gains[0]).astype(bf16)
    query, keys, values = (split(matmul(a_in, tiles[n])) for n in range(3))
    allowed = (seg[:, None] == seg[None, :]) & (live[None, :] | (places[:, None] == places[None, :]))
    probs = probabilities(query, keys, allowed)
    attended = joined(weighted(probs.astype(bf16), values))
    h1 = h0 + matmul(attended, tiles[3])
    b_in = normalize(h1, gains[1]).astype(bf16)
    slots, ctx_len, ctx_width = context.shape
    ctx = context.reshape(slots * ctx_len, ctx_width)
    ctx_low, ctx_high = ctx[:, :width], ctx[:, width:]
    cross_q = split(matmul(b_in, tiles[4]))
    cross_k = split(matmul(ctx_low, tiles[5]) + matmul(ctx_high, tiles[6]))
    cross_v = split(matmul(ctx_low, tiles[7]) + matmul(ctx_high, tiles[8]))
    item = jnp.arange(slots * ctx_len) // ctx_len
    cross_p = probabilities(cross_q, cross_k, seg[:, None] == item[None, :])
    cross_o = joined(weighted(cross_p.astype(bf16), cross_v))
    h2 = h1 + matmul(cross_o, tiles[9])
    c_in = normalize(h2, gains[2]).astype(bf16)
    hidden = matmul(c_in, w_in)
    activated = gelu_tanh(hidden).astype(bf16)
    layer_out = (h2 + matmul(activated, w_out)).astype(bf16)
    grad_out = cotangent.astype(f32) * live.astype(f32)[:, None]
    d_ff = grad_out.astype(bf16)
    d_hidden = jax.vjp(gelu_tanh, hidden)[1](matmul_right(d_ff, w_out))[0].astype(bf16)
    part_two, gain_grad_two = jax.vjp(normalize, h2, gains[2])[1](matmul_right(d_hidden, w_in))
    dh2 = grad_out + part_two
    d_cross_out = dh2.astype(bf16)
    d_cq, d_ck, d_cv = through(tiles[9], d_cross_out, cross_q, cross_k, cross_p, cross_v)
    part_one, gain_grad_one = jax.vjp(normalize, h1, gains[1])[1](matmul_right(d_cq, tiles[4]))
    dh1 = dh2 + part_one
    d_self_out = dh1.astype(bf16)
    d_q, d_k, d_v = through(tiles[3], d_self_out, query, keys, probs, values)
    d_a = matmul_right(d_q, tiles[0]) + matmul_right(d_k, tiles[1]) + matmul_right(d_v, tiles[2])
    part_zero, gain_grad_zero = jax.vjp(normalize, h0, gains[0])[1](d_a)
    grad_tokens = (dh1 + part_zero).astype(bf16)
    pairs = [
        (a_in, d_q),
        (a_in, d_k),
        (a_in, d_v),
        (attended, d_self_out),
        (b_in, d_cq),
        (ctx_low, d_ck),
        (ctx_high, d_ck),
        (ctx_low, d_cv),
        (ctx_high, d_cv),
        (cross_o, d_cross_out),
    ]
    for part in range(4):
        pairs.append((c_in, d_hidden[:, part * width : (part + 1) * width]))
    for part in range(4):
        pairs.append((activated[:, part * width : (part + 1) * width], d_ff))
    total_slots = lax.axis_size("fsdp") * cap
    placed = jnp.zeros((total_slots,) + master.shape[1:], bf16)
    for tile, (left, right) in enumerate(pairs):
        term = lax.psum_scatter(
            matmul_left(left, right).astype(bf16), "dp", scatter_dimension=0, tiled=True
        )
        placed = lax.dynamic_update_index_in_dim(placed, term, slot_of[tile], 0)
    owned = lax.psum_scatter(placed, "fsdp", scatter_dimension=0, tiled=True).astype(f32)
    my_slots = lax.axis_index("fsdp") * cap + jnp.arange(cap)
    used = jnp.any(slot_of[None, :] == my_slots[:, None], axis=1)[:, None, None]
    updated = adam_update(master, moment_one, moment_two, owned, rate_matrix, decay_rate)
    new_w, new_m, new_v = (jnp.where(used, value, 0.0) for value in updated)
    gain_grads = jnp.stack([gain_grad_zero, gain_grad_one, gain_grad_two])
    gain_total = lax.psum(gain_grads, ("dp", "fsdp"))
    new_g, new_gm, new_gv = adam_update(gains, gain_one, gain_two, gain_total, rate_gain, 0.0)
    return (layer_out, grad_tokens, new_w, new_m, new_v, new_g, new_gm, new_gv)


def solution(mesh):
    planes = mesh.shape["dp"] == 8 and mesh.shape["fsdp"] == 4
    if planes:
        used = Mesh(mesh.devices.reshape(4, 2, 2, 2), ALL_AXES)
        dp, fsdp, body = ("z", "x"), ("y", "c"), plane_body
    else:
        used, dp, fsdp, body = mesh, ("dp",), ("fsdp",), whole_body
    rows = P(dp + fsdp, None)
    tiles = P(fsdp, dp, None)
    return jax.shard_map(
        body,
        mesh=used,
        in_specs=(rows, rows, P(dp + fsdp, None, None), rows, P(dp + fsdp), P(), tiles, tiles, tiles, P(), P(), P()),
        out_specs=(rows, rows, tiles, tiles, tiles, P(), P(), P()),
        check_vma=False,
    )
```

```python
import jax
import jax.numpy as jnp
import numpy as np
from jax import lax
from jax.experimental import pallas as pl
from jax.experimental.layout import Layout, with_layout_constraint
from jax.experimental.pallas import tpu as pltpu
from jax.sharding import Mesh
from jax.sharding import PartitionSpec as P

HEADS = 16
STEP = 10

norm_eps = 1e-06
beta_one = 0.9
beta_two = 0.95
adam_eps = 1e-08
decay_rate = 0.1
rate_matrix = 0.1
rate_gain = 0.8

f32 = jnp.float32
bf16 = jnp.bfloat16

SHIFT = (0, 0, 0, 0, 2, 2, 2, 2, 2, 2, 0, 1, 2, 3, 0, 1, 2, 3)
ROW_TILES = (3, 9, 14, 15, 16, 17)
VMEM_LIMIT = 48 << 20


def normalize(h, gain):
    scale = lax.rsqrt(jnp.mean(h * h, axis=-1, keepdims=True) + norm_eps)
    return h * scale * gain


def gelu_tanh(u):
    return 0.5 * u * (1.0 + jnp.tanh(0.7978845608028654 * (u + 0.044715 * u * u * u)))


def matmul(left, right):
    return jnp.dot(left, right, preferred_element_type=f32)


def matmul_left(left, right):
    return lax.dot_general(left, right, (((0,), (0,)), ((), ())), preferred_element_type=f32)


def matmul_right(left, right):
    return lax.dot_general(left, right, (((1,), (1,)), ((), ())), preferred_element_type=f32)


def ranks_of(owners):
    order = jnp.arange(owners.shape[0])
    same = (owners[:, None] == owners[None, :]) & (order[None, :] < order[:, None])
    return jnp.sum(same.astype(jnp.int32), axis=1)


def segments(lengths, count):
    places = jnp.arange(count)
    end = jnp.zeros((), jnp.int32)
    seg = jnp.zeros((count,), jnp.int32)
    for item in range(lengths.shape[0]):
        end = end + lengths[item]
        seg = seg + (places >= end).astype(jnp.int32)
    return seg


def adam_update(weight, first, second, grad, rate, decay):
    first = beta_one * first + (1.0 - beta_one) * grad
    second = beta_two * second + (1.0 - beta_two) * grad * grad
    fix_one = 1.0 / (1.0 - beta_one**STEP)
    fix_two = 1.0 / (1.0 - beta_two**STEP)
    move = first * fix_one / (jnp.sqrt(second * fix_two) + adam_eps)
    return (weight - rate * (move + decay * weight), first, second)


def pack_columns(master, table, first_slot, slots):
    _, rows, columns = master.shape
    width = columns // 8

    def kernel(table_ref, in_ref, out_ref):
        slot = pl.program_id(0)
        for rank in range(8):
            start = pl.multiple_of(table_ref[slot * 8 + rank] * width, width)
            out_ref[rank, 0] = in_ref[0, :, pl.ds(start, width)].astype(bf16)

    return pl.pallas_call(
        kernel,
        out_shape=jax.ShapeDtypeStruct((8, slots, rows, width), bf16),
        grid_spec=pltpu.PrefetchScalarGridSpec(
            num_scalar_prefetch=1,
            grid=(slots,),
            in_specs=[pl.BlockSpec((1, rows, columns), lambda k, t: (first_slot + k, 0, 0))],
            out_specs=pl.BlockSpec((8, 1, rows, width), lambda k, t: (0, k, 0, 0)),
        ),
        compiler_params=pltpu.CompilerParams(vmem_limit_bytes=VMEM_LIMIT),
        name="pack_columns",
    )(table, master)


def pick_blocks(sources, which, index, count):
    _, rows, width = sources[0].shape
    n_src = len(sources)

    def kernel(which_ref, index_ref, *refs):
        place = pl.program_id(0) * 2 + pl.program_id(1)
        out_ref = refs[n_src]
        for number in range(n_src):

            @pl.when(which_ref[place] == number)
            def _():
                out_ref[...] = refs[number][0]

    def spec(number):
        def at(n, half, which, index):
            place = n * 2 + half
            return (jnp.where(which[place] == number, index[place], 0), 0, 0)

        return pl.BlockSpec((1, rows, width), at)

    return pl.pallas_call(
        kernel,
        out_shape=jax.ShapeDtypeStruct((2 * rows, count * width), bf16),
        grid_spec=pltpu.PrefetchScalarGridSpec(
            num_scalar_prefetch=2,
            grid=(count, 2),
            in_specs=[spec(number) for number in range(n_src)],
            out_specs=pl.BlockSpec((rows, width), lambda n, half, which, index: (half, n)),
        ),
        compiler_params=pltpu.CompilerParams(vmem_limit_bytes=VMEM_LIMIT),
        name="pick_blocks",
    )(which, index, *sources)


def pack_gradients(groups, which, column, rows, width, slots):
    n_src = len(groups)

    def kernel(which_ref, column_ref, *refs):
        rank = pl.program_id(0)
        out_ref = refs[n_src]
        for k in range(slots):
            start = pl.multiple_of(column_ref[rank * slots + k] * width, width)
            for number in range(n_src):

                @pl.when(which_ref[rank * slots + k] == number)
                def _():
                    out_ref[0, k] = refs[number][:, pl.ds(start, width)]

    return pl.pallas_call(
        kernel,
        out_shape=jax.ShapeDtypeStruct((8, slots, rows, width), bf16),
        grid_spec=pltpu.PrefetchScalarGridSpec(
            num_scalar_prefetch=2,
            grid=(8,),
            in_specs=[
                pl.BlockSpec((rows, group.shape[1]), lambda rank, which, column: (rank // 4, 0)) for group in groups
            ],
            out_specs=pl.BlockSpec((1, slots, rows, width), lambda rank, which, column: (rank, 0, 0, 0)),
        ),
        compiler_params=pltpu.CompilerParams(vmem_limit_bytes=VMEM_LIMIT),
        name="pack_gradients",
    )(which, column, *groups)


def adam_tiles(master, one, two, columns_from, rows_from, visit, mode, column_place, row_place, hold, previous=None):
    _, rows, columns = master.shape
    width = columns // 8
    n_visit = visit.shape[0]
    n_col, n_row = len(columns_from), len(rows_from)
    kept = () if previous is None else tuple(previous)

    def kernel(visit_ref, mode_ref, cp_ref, rp_ref, hold_ref, *refs):
        w_ref, m_ref, v_ref = refs[:3]
        grads = refs[3 : 3 + n_col + n_row]
        outs = refs[3 + n_col + n_row + len(kept) :]
        how = mode_ref[pl.program_id(0)]

        @pl.when(how == 1)
        def _():
            for ref in outs:
                ref[...] = jnp.zeros_like(ref)

        for number, grad_ref in enumerate(grads):

            @pl.when(how == number + 2)
            def _():
                grad = grad_ref[0].astype(f32)
                results = adam_update(w_ref[0], m_ref[0], v_ref[0], grad, rate_matrix, decay_rate)
                for ref, value in zip(outs, results, strict=True):
                    ref[0] = value

    def block_of(n, b, hold):
        return jnp.where(hold[n] == 1, 7, b)

    state = pl.BlockSpec((1, rows, width), lambda n, b, vi, mo, cp, rp, ho: (vi[n], 0, block_of(n, b, ho)))

    def column_spec(number):
        def at(n, b, vi, mo, cp, rp, ho):
            return (jnp.where(mo[n] == number + 2, cp[n * 8 + block_of(n, b, ho)], 0), 0, 0)

        return pl.BlockSpec((1, rows, width), at)

    def row_spec(number):
        def at(n, b, vi, mo, cp, rp, ho):
            taken = mo[n] == number + 2
            return (jnp.where(taken, rp[n], 0), 0, jnp.where(taken, block_of(n, b, ho), 0))

        return pl.BlockSpec((1, rows, width), at)

    shape = jax.ShapeDtypeStruct(master.shape, f32)
    n_before = 5 + 3 + n_col + n_row
    return pl.pallas_call(
        kernel,
        out_shape=(shape, shape, shape),
        grid_spec=pltpu.PrefetchScalarGridSpec(
            num_scalar_prefetch=5,
            grid=(n_visit, 8),
            in_specs=[
                state,
                state,
                state,
                *(column_spec(number) for number in range(n_col)),
                *(row_spec(n_col + number) for number in range(n_row)),
                *(pl.BlockSpec(memory_space=pl.ANY) for _ in kept),
            ],
            out_specs=(state, state, state),
        ),
        input_output_aliases={n_before + n: n for n in range(len(kept))},
        compiler_params=pltpu.CompilerParams(vmem_limit_bytes=VMEM_LIMIT),
        cost_estimate=pl.CostEstimate(
            flops=30 * n_visit * rows * columns, bytes_accessed=26 * n_visit * rows * columns, transcendentals=0
        ),
        name="adam_tiles",
    )(visit, mode, column_place, row_place, hold, master, one, two, *columns_from, *rows_from, *kept)


def after(value, *others):
    return lax.optimization_barrier((value, *others))[0]


def swap(value, axis):
    return lax.ppermute(value, axis, [(0, 1), (1, 0)])


def gather_rows(value):
    half = value.shape[0] // 2
    over_x = swap(value, "x")
    over_y = swap(value, "y")
    far_low = swap(over_y[:half], "x")
    far_high = swap(over_x[half:], "y")
    four = jnp.concatenate([value, over_y, over_x, far_low, far_high], axis=0)
    return jnp.concatenate([four, swap(four, "c")], axis=0)


def scatter_rows(part):
    rows, width = part.shape[0] // 8, part.shape[1]
    half = width // 2
    part = part.reshape(2, 2, 2, rows, width)
    chip = part[0] + swap(part[1], "c")
    low, high = chip[..., :half], chip[..., half:]
    low_two = low[:, 0] + swap(low[:, 1].astype(bf16), "y").astype(f32)
    high_two = high[0] + swap(high[1].astype(bf16), "x").astype(f32)
    low_one = low_two[0] + swap(low_two[1].astype(bf16), "x").astype(f32)
    high_one = high_two[0] + swap(high_two[1].astype(bf16), "y").astype(f32)
    return jnp.concatenate([low_one, high_one], axis=1)


def sum_everywhere(value):
    for axis in ("c", "y", "x"):
        value = value + swap(value, axis)
    for step in (1, 2):
        value = value + lax.ppermute(value, "z", [(z, z ^ step) for z in range(4)])
    return value


def flip_pairs(mask, keep=None):
    pairs = []
    for z in range(4):
        for place in range(8):
            target = place ^ mask
            if keep is None or keep(z, place, target):
                pairs.append((z * 8 + place, z * 8 + target))
    return pairs


ALL_AXES = ("z", "x", "y", "c")
PLANE = ("x", "y", "c")


def plane_body(
    tokens, cotangent, context, lengths, keep, owners, master, moment_one, moment_two, gains, gain_one, gain_two
):
    cap, rows, _ = master.shape
    count, width = tokens.shape
    heads_here = HEADS // 8
    head_dim = width // HEADS
    scale = head_dim ** (-0.5)
    block = width // 8
    z = lax.axis_index("z")
    x = lax.axis_index("x")
    f = lax.axis_index("y") * 2 + lax.axis_index("c")

    n_tiles = owners.shape[0]
    rank = ranks_of(owners)
    shift_of = np.array(SHIFT, np.int32)
    row_of = np.array([t in ROW_TILES for t in range(n_tiles)])
    all_slots = jnp.arange(4 * cap).reshape(4, cap)
    holds = (owners * cap + rank)[None, None, :] == all_slots[:, :, None]
    used_at = jnp.any(holds, axis=2)
    tile_at = jnp.sum(jnp.where(holds, np.arange(n_tiles, dtype=np.int32), 0), axis=2)
    shift_at = jnp.sum(jnp.where(holds, shift_of, 0), axis=2)
    row_at = jnp.any(holds & row_of, axis=2)
    mine = (jnp.arange(4) == f)[:, None]

    def my(value):
        return jnp.sum(jnp.where(mine, value.astype(jnp.int32), 0), axis=0)

    my_used, my_tile, my_shift, my_row = my(used_at), my(tile_at), my(shift_at), my(row_at)

    to_x = np.arange(8) // 4
    to_f = np.arange(8) % 4
    column_table = 2 * ((to_f[None, :] + my_shift[:, None]) % 4) + to_x[None, :]
    half_cap = cap // 2
    place = np.arange(4)

    def of_tiles(tiles, values):
        chosen = tiles[:, None] == np.arange(n_tiles)[None, :]
        return jnp.sum(jnp.where(chosen, values[None, :], 0), axis=1)

    column_tiles = jnp.concatenate([np.array([0, 1, 2, 4, 5, 7, 6, 8], np.int32), 10 + (place - f) % 4])
    column_part = jnp.repeat(of_tiles(column_tiles, rank // half_cap), 2)
    column_place = of_tiles(column_tiles, owners * half_cap + rank % half_cap)
    column_place = (column_place[:, None] + np.array([0, 4 * half_cap])[None, :]).reshape(-1)
    other_f = f ^ place
    outer_tiles = jnp.where(other_f == z, 3, 9)
    out_tiles = 14 + (z - other_f) % 4
    row_slots = of_tiles(jnp.concatenate([outer_tiles, out_tiles]), rank)
    row_owners = of_tiles(jnp.stack([outer_tiles[0], outer_tiles[2], out_tiles[0], out_tiles[2]]), owners)

    def pack_first(weights):
        return pack_columns(weights, column_table[:half_cap].reshape(-1), 0, half_cap)

    def pack_second(weights):
        return pack_columns(weights, column_table[half_cap:].reshape(-1), half_cap, half_cap)

    def my_block(slot):
        return lax.dynamic_index_in_dim(master, slot, 0, keepdims=False).astype(bf16)

    present = owners[0] >= 0

    def chain_step(move, *values):
        shapes = jax.eval_shape(move, *values)
        idle = jax.tree.map(lambda leaf: jnp.zeros(leaf.shape, leaf.dtype), shapes)
        return lax.cond(present, move, lambda *_: idle, *values)

    h0 = tokens.astype(f32)
    outer_blocks = [my_block(row_slots[mask]) for mask in range(4)]
    out_blocks = [my_block(row_slots[4 + mask]) for mask in range(4)]
    a_in = normalize(h0, gains[0]).astype(bf16)
    sent = pack_first(after(master, column_part, column_place, row_slots, row_owners))
    received = [lax.all_to_all(sent, PLANE, 0, 0, tiled=True).reshape(8 * half_cap, rows, block)]
    seg = segments(lengths[0], count)
    live = keep == 1
    code = seg * 2 + live.astype(jnp.int32)

    def spread_code(code):
        for axis in ("y", "x", "c"):
            code = jnp.concatenate([code, swap(code, axis)])
        return code

    code = chain_step(spread_code, after(code, a_in, *outer_blocks, *out_blocks))
    seg_all = (code // 2).reshape(8, count)
    live_all = (code % 2 == 1).reshape(8, count)
    grad_out = cotangent.astype(f32) * live.astype(f32)[:, None]
    received = [after(received[0], a_in, code, *outer_blocks, *out_blocks)]

    def columns_here(first, count, parts):
        chosen = slice(2 * first, 2 * (first + count))
        return pick_blocks(received[:parts], column_part[chosen], column_place[chosen], count)

    def gather_z(value):
        return lax.all_gather(value, "z", axis=0, tiled=True)

    local = columns_here(0, 3, 1)
    w_qkv = gather_z(local)
    a_all = gather_rows(after(a_in, local))
    d_ff = gather_rows(after(grad_out.astype(bf16), local))
    sent = pack_second(after(master, a_all, d_ff))
    received.append(lax.all_to_all(sent, PLANE, 0, 0, tiled=True).reshape(8 * half_cap, rows, block))

    def take_rows(kind, blocks, keep_pair):
        here, there = row_owners[2 * kind], row_owners[2 * kind + 1]
        core = f % 2
        from_core = swap(jnp.stack([blocks[1], blocks[3]]), "c")
        mine = jnp.where(here % 2 == core, blocks[0], from_core[0])
        across = jnp.where(there % 2 == core, blocks[2], from_core[1])
        from_y = lax.ppermute(across, ALL_AXES, flip_pairs(2, keep_pair))
        return jnp.where(here // 2 == f // 2, mine, from_y)

    def needs_outer(zz, place, target):
        return target % 4 in (zz, (zz + 2) % 4)

    outer = take_rows(0, [after(value, local) for value in outer_blocks], needs_outer)
    out_rows = take_rows(1, [after(value, local) for value in out_blocks], None)
    half_rows = rows // 2
    odd = z % 2
    to_pair = lax.dynamic_slice_in_dim(after(outer, sent), (1 - odd) * half_rows, half_rows, 0)
    own_half = lax.dynamic_slice_in_dim(outer, odd * half_rows, half_rows, 0)
    pair_swap = [
        (zz * 8 + place, (zz ^ 1) * 8 + place)
        for zz in range(4)
        for place in range(8)
        if place % 4 in (zz, (zz + 2) % 4)
    ]
    from_pair = lax.ppermute(to_pair, ALL_AXES, pair_swap)
    has_outer = (f == z) | (f == (z + 2) % 4)
    outer_all = lax.all_gather(jnp.where(has_outer, own_half, from_pair), "z", axis=0, tiled=True)
    low_y = lax.axis_index("y") == 0
    w_self_out = jnp.where(low_y, outer_all[:rows], outer_all[rows:])
    w_cross_out = jnp.where(low_y, outer_all[rows:], outer_all[:rows])

    def split(value):
        return value.reshape(8, -1, heads_here, head_dim)

    qkv = matmul(a_all, w_qkv)
    qkv = qkv.astype(bf16)
    query, keys, values = (split(qkv[:, n * block : (n + 1) * block]) for n in range(3))
    places = jnp.arange(count)
    allowed = (seg_all[:, :, None] == seg_all[:, None, :]) & (
        live_all[:, None, :] | (places[:, None] == places[None, :])
    )

    def probabilities(left, right, mask):
        scores = jnp.einsum("bqhd,bkhd->bhqk", left, right, preferred_element_type=f32) * scale
        scores = jnp.where(mask[:, None], scores, -1e30)
        expo = jnp.exp(scores - jnp.max(scores, axis=-1, keepdims=True))
        return expo / jnp.sum(expo, axis=-1, keepdims=True)

    def weighted(probs, right):
        return jnp.einsum("bhqk,bkhd->bqhd", probs, right, preferred_element_type=f32)

    def joined(value):
        return value.astype(bf16).reshape(-1, block)

    probs = probabilities(query, keys, allowed)
    probs_low = probs.astype(bf16)
    mixed = weighted(probs_low, values).astype(bf16)
    attended = mixed.reshape(-1, block)
    received[1] = after(received[1], mixed)
    local_cross, local_in = columns_here(3, 5, 2), columns_here(8, 4, 2)
    w_cross = gather_z(local_cross)
    w_in = gather_z(local_in)

    w_out = gather_z(after(out_rows, local_cross, local_in))
    slots, ctx_len, ctx_width = context.shape
    ctx = after(context.reshape(slots * ctx_len, ctx_width), local_cross, local_in, out_rows)
    ctx_x, ctx_y = swap(ctx, "x"), swap(ctx, "y")
    h1 = h0 + chain_step(scatter_rows, matmul(after(attended, local_in), w_self_out))

    def second_step(one, own, over_x, over_y):
        half = over_x.shape[0] // 2
        far_low, far_high = swap(over_y[:half], "x"), swap(over_x[half:], "y")
        four = jnp.concatenate([own, over_y, over_x, far_low, far_high], axis=0)
        return gather_rows(one), four, swap(four, "c")

    b_all, ctx_here, ctx_there = chain_step(
        second_step, normalize(h1, gains[1]).astype(bf16), ctx, ctx_x, ctx_y
    )

    w_cross_q = w_cross[:, :block]
    w_low = w_cross[:, block : 3 * block]
    w_high = w_cross[:, 3 * block :]
    ctx_kv = jnp.concatenate(
        [
            (matmul(part[:, :width], w_low) + matmul(part[:, width:], w_high)).astype(bf16)
            for part in (ctx_here, ctx_there)
        ],
        axis=0,
    )
    cross_q = matmul(b_all, w_cross_q)
    cross_q = split(cross_q.astype(bf16))
    cross_k, cross_v = split(ctx_kv[:, :block]), split(ctx_kv[:, block:])
    item = jnp.arange(slots * ctx_len) // ctx_len
    own_item = seg_all[:, :, None] == item[None, None, :]
    cross_p = probabilities(cross_q, cross_k, own_item)
    cross_low = cross_p.astype(bf16)
    cross_o = joined(weighted(cross_low, cross_v))
    h2, ctx_all = chain_step(
        lambda one, *pieces: (scatter_rows(one), jnp.concatenate(pieces, axis=0)),
        matmul(cross_o, w_cross_out),
        ctx_here,
        ctx_there,
    )
    ctx_low, ctx_high = ctx_all[:, :width], ctx_all[:, width:]
    h2 = h1 + h2
    c_all = chain_step(gather_rows, normalize(h2, gains[2]).astype(bf16))

    hidden = matmul(c_all, w_in)
    activated = gelu_tanh(hidden).astype(bf16)

    def sum_rows(value):
        value = with_layout_constraint(value, Layout(major_to_minor=(0, 1)))
        value = lax.psum_scatter(value, "z", scatter_dimension=0, tiled=True)
        return with_layout_constraint(value, Layout(major_to_minor=(0, 1)))

    def from_y(value, keep_pair=None):
        return jnp.stack([value, lax.ppermute(value, ALL_AXES, flip_pairs(2, keep_pair))])

    def with_core(pair):
        return jnp.concatenate([pair, swap(pair, "c")])

    t_out = matmul_left(activated, d_ff).astype(bf16)
    g_out = sum_rows(t_out)
    d_act = matmul_right(after(d_ff, t_out), w_out)
    d_hidden = jax.vjp(gelu_tanh, hidden)[1](d_act)[0].astype(bf16)
    t_in = matmul_left(c_all, d_hidden).astype(bf16)
    g_in = sum_rows(t_in)
    d_c, out_sum = chain_step(
        lambda one, two: (scatter_rows(one), scatter_rows(two)), matmul_right(d_hidden, w_in), matmul(activated, w_out)
    )
    layer_out = (h2 + out_sum).astype(bf16)
    part_two, gain_grad_two = jax.vjp(normalize, h2, gains[2])[1](d_c)
    dh2 = grad_out + part_two
    d_cross_out = chain_step(gather_rows, after(dh2.astype(bf16), t_in))
    g_cross_out = matmul_left(cross_o, d_cross_out)

    def through(d_mixed, left, right, probs, probs_low, values):
        d_mixed = split(d_mixed.astype(bf16))
        d_probs = jnp.einsum("bqhd,bkhd->bhqk", d_mixed, values, preferred_element_type=f32)
        d_scores = (probs * (d_probs - jnp.sum(probs * d_probs, axis=-1, keepdims=True))).astype(bf16)
        d_left = joined(weighted(d_scores, right) * scale)
        d_right = joined(jnp.einsum("bhqk,bqhd->bkhd", d_scores, left, preferred_element_type=f32) * scale)
        d_values = joined(jnp.einsum("bhqk,bqhd->bkhd", probs_low, d_mixed, preferred_element_type=f32))
        return d_left, d_right, d_values

    (d_cq, d_ck, d_cv), out_grads = chain_step(
        lambda one, two: (
            through(matmul_right(one, w_cross_out), cross_q, cross_k, cross_p, cross_low, cross_v),
            from_y(two),
        ),
        d_cross_out,
        g_out,
    )
    d_ckv = jnp.concatenate([d_ck, d_cv], axis=1)
    t_cross = jnp.concatenate(
        [
            value.astype(bf16)
            for value in (matmul_left(b_all, d_cq), matmul_left(ctx_low, d_ckv), matmul_left(ctx_high, d_ckv))
        ],
        axis=1,
    )
    g_cross = sum_rows(t_cross)
    part = matmul_right(d_cq, w_cross_q)
    d_b = chain_step(scatter_rows, part)
    part_one, gain_grad_one = jax.vjp(normalize, h1, gains[1])[1](d_b)
    dh1 = dh2 + part_one
    d_self_out = chain_step(gather_rows, after(dh1.astype(bf16), t_cross, g_in))
    g_self_out = matmul_left(attended, d_self_out)
    t_outer = jnp.concatenate(
        [
            jnp.where(low_y, g_self_out, g_cross_out).astype(bf16),
            jnp.where(low_y, g_cross_out, g_self_out).astype(bf16),
        ],
        axis=0,
    )
    g_outer = sum_rows(after(t_outer, g_cross))
    d_mixed = matmul_right(after(d_self_out, t_outer), w_self_out)
    d_q, d_k, d_v = through(d_mixed, query, keys, probs, probs_low, values)
    d_qkv = jnp.concatenate([d_q, d_k, d_v], axis=1)
    t_qkv = matmul_left(a_all, d_qkv).astype(bf16)
    g_qkv = sum_rows(t_qkv)
    group_of = np.array([0, 0, 0, 0, 0, 0, 0, 0, 0, 0, 1, 1, 1, 1, 0, 0, 0, 0], np.int32)
    column_of = np.array([0, 0, 0, 0, 0, 1, 3, 2, 4, 0, 0, 1, 2, 3, 0, 0, 0, 0], np.int32)
    group_at = jnp.sum(jnp.where(holds, group_of, 0), axis=2)
    column_at = jnp.sum(jnp.where(holds, column_of, 0), axis=2)
    column_at = jnp.where(group_at == 1, (column_at + f) % 4, column_at)
    sent = pack_gradients(
        [after(g_cross, t_qkv), g_in], jnp.tile(group_at.reshape(-1), 2), jnp.tile(column_at.reshape(-1), 2), rows, block, cap
    )
    early_grads = lax.all_to_all(sent, PLANE, 0, 0, tiled=True).reshape(8 * cap, rows, block)

    def last_step(part, out_pair, gain_grad_one, gain_grad_two):
        part_zero, gain_grad_zero = jax.vjp(normalize, h0, gains[0])[1](scatter_rows(part))
        gain_grads = jnp.stack([gain_grad_zero, gain_grad_one, gain_grad_two])
        return part_zero, sum_everywhere(gain_grads), with_core(out_pair)

    part_zero, gain_total, out_grads = chain_step(
        last_step, matmul_right(after(d_qkv, sent), w_qkv), out_grads, gain_grad_one, gain_grad_two
    )
    grad_tokens = (dh1 + part_zero).astype(bf16)

    by_tile = jnp.swapaxes(after(g_qkv, out_grads).reshape(2, rows, 3, block), 1, 2)
    sent = jnp.broadcast_to(by_tile[:, None], (2, 4, 3, rows, block)).reshape(8, 3, rows, block)
    late_grads = lax.all_to_all(sent, PLANE, 0, 0, tiled=True).reshape(8 * 3, rows, block)
    back_swap = [(target, source) for source, target in pair_swap]
    place = np.arange(8)
    source_x, source_f = (place % 2)[None, :], ((place // 2)[None, :] - my_shift[:, None]) % 4
    slot = np.arange(cap, dtype=np.int32)
    column_place = (source_x * 4 + source_f) * cap + slot[:, None]
    other_row = ((z - my_shift) % 4) ^ f
    row_source = (other_row % 2) * 2 + other_row // 2
    late = (my_used == 1) & ((my_tile < 4) | (my_tile == 9))
    early_mode = jnp.where(my_used == 0, 1, jnp.where(late, 0, jnp.where(my_row == 1, 3, 2)))
    states = (master, moment_one, moment_two)

    def early_step(early_grads, out_grads, half):
        other_half = lax.ppermute(half, ALL_AXES, back_swap)
        in_order = jnp.where(odd == 0, jnp.stack([half, other_half]), jnp.stack([other_half, half]))
        outer_pair = from_y(in_order.reshape(rows, width), lambda zz, place, _: place % 4 in (zz, (zz + 2) % 4))
        early = None
        for first in (0, half_cap):
            chosen = slice(first, first + half_cap)
            early = adam_tiles(
                *states,
                [early_grads],
                [out_grads],
                slot[chosen],
                early_mode[chosen],
                column_place[chosen].reshape(-1),
                row_source[chosen],
                np.zeros(half_cap, np.int32),
                early,
            )
        return *early, with_core(outer_pair)

    *early, outer_grads = chain_step(early_step, early_grads, out_grads, g_outer)

    n_late = 5
    order = jnp.sum(jnp.where(slot[None, :] < slot[:, None], late.astype(jnp.int32)[None, :], 0), axis=1)
    count_late = jnp.sum(late.astype(jnp.int32))
    step = np.arange(n_late)
    wanted = jnp.minimum(step, jnp.maximum(count_late - 1, 0))
    here = late[None, :] & (order[None, :] == wanted[:, None])

    def at_step(value):
        return jnp.sum(jnp.where(here, value.astype(jnp.int32)[None, :], 0), axis=1)

    hold = (step >= jnp.maximum(count_late, 1)).astype(jnp.int32)
    tile = at_step(my_tile)
    some = count_late > 0
    visit = jnp.where(some, at_step(slot), 0)
    first_mode = jnp.where(early_mode[0] == 3, 4, early_mode[0])
    late_mode = jnp.where(at_step(my_row) == 1, 5, 3)
    mode = jnp.where(hold == 1, 0, jnp.where(some, late_mode, first_mode))
    late_place = ((place % 2)[None, :] * 4 + (place // 2)[None, :]) * 3 + tile[:, None]
    late_place = jnp.where(some, late_place, column_place[:1])
    new_w, new_m, new_v = adam_tiles(
        *states,
        [early_grads, late_grads],
        [out_grads, outer_grads],
        visit,
        mode,
        late_place.reshape(-1),
        jnp.where(some, at_step(row_source), row_source[0]),
        hold,
        early,
    )
    new_g, new_gm, new_gv = adam_update(gains, gain_one, gain_two, gain_total, rate_gain, 0.0)
    return (layer_out, grad_tokens, new_w, new_m, new_v, new_g, new_gm, new_gv)


def whole_body(
    tokens, cotangent, context, lengths, keep, owners, master, moment_one, moment_two, gains, gain_one, gain_two
):
    cap = master.shape[0]
    n_tiles = owners.shape[0]
    slot_of = owners * cap + ranks_of(owners)
    owner_rows = lax.all_gather(master.astype(bf16), "fsdp", axis=0, tiled=True)
    tiles = [
        lax.all_gather(
            lax.dynamic_index_in_dim(owner_rows, slot_of[tile], 0, keepdims=False), "dp", axis=0, tiled=True
        )
        for tile in range(n_tiles)
    ]
    w_in = jnp.concatenate(tiles[10:14], axis=1)
    w_out = jnp.concatenate(tiles[14:18], axis=0)
    count, width = tokens.shape
    head_dim = width // HEADS
    scale = head_dim ** (-0.5)
    seg = segments(lengths[0], count)
    live = keep == 1
    places = jnp.arange(count)

    def split(value):
        return value.astype(bf16).reshape(-1, HEADS, head_dim)

    def joined(value):
        return value.astype(bf16).reshape(-1, width)

    def probabilities(left, right, mask):
        scores = jnp.einsum("qhd,khd->hqk", left, right, preferred_element_type=f32) * scale
        scores = jnp.where(mask[None], scores, -1e30)
        expo = jnp.exp(scores - jnp.max(scores, axis=-1, keepdims=True))
        return expo / jnp.sum(expo, axis=-1, keepdims=True)

    def weighted(probs, right):
        return jnp.einsum("hqk,khd->qhd", probs, right, preferred_element_type=f32)

    def through(weights, d_out, left, right, probs, values):
        d_mixed = split(matmul_right(d_out, weights))
        d_probs = jnp.einsum("qhd,khd->hqk", d_mixed, values, preferred_element_type=f32)
        d_scores = (probs * (d_probs - jnp.sum(probs * d_probs, axis=-1, keepdims=True))).astype(bf16)
        d_left = joined(weighted(d_scores, right) * scale)
        d_right = joined(jnp.einsum("hqk,qhd->khd", d_scores, left, preferred_element_type=f32) * scale)
        d_values = joined(jnp.einsum("hqk,qhd->khd", probs.astype(bf16), d_mixed, preferred_element_type=f32))
        return d_left, d_right, d_values

    h0 = tokens.astype(f32)
    a_in = normalize(h0, gains[0]).astype(bf16)
    query, keys, values = (split(matmul(a_in, tiles[n])) for n in range(3))
    allowed = (seg[:, None] == seg[None, :]) & (live[None, :] | (places[:, None] == places[None, :]))
    probs = probabilities(query, keys, allowed)
    attended = joined(weighted(probs.astype(bf16), values))
    h1 = h0 + matmul(attended, tiles[3])
    b_in = normalize(h1, gains[1]).astype(bf16)
    slots, ctx_len, ctx_width = context.shape
    ctx = context.reshape(slots * ctx_len, ctx_width)
    ctx_low, ctx_high = ctx[:, :width], ctx[:, width:]
    cross_q = split(matmul(b_in, tiles[4]))
    cross_k = split(matmul(ctx_low, tiles[5]) + matmul(ctx_high, tiles[6]))
    cross_v = split(matmul(ctx_low, tiles[7]) + matmul(ctx_high, tiles[8]))
    item = jnp.arange(slots * ctx_len) // ctx_len
    cross_p = probabilities(cross_q, cross_k, seg[:, None] == item[None, :])
    cross_o = joined(weighted(cross_p.astype(bf16), cross_v))
    h2 = h1 + matmul(cross_o, tiles[9])
    c_in = normalize(h2, gains[2]).astype(bf16)
    hidden = matmul(c_in, w_in)
    activated = gelu_tanh(hidden).astype(bf16)
    layer_out = (h2 + matmul(activated, w_out)).astype(bf16)
    grad_out = cotangent.astype(f32) * live.astype(f32)[:, None]
    d_ff = grad_out.astype(bf16)
    d_hidden = jax.vjp(gelu_tanh, hidden)[1](matmul_right(d_ff, w_out))[0].astype(bf16)
    part_two, gain_grad_two = jax.vjp(normalize, h2, gains[2])[1](matmul_right(d_hidden, w_in))
    dh2 = grad_out + part_two
    d_cross_out = dh2.astype(bf16)
    d_cq, d_ck, d_cv = through(tiles[9], d_cross_out, cross_q, cross_k, cross_p, cross_v)
    part_one, gain_grad_one = jax.vjp(normalize, h1, gains[1])[1](matmul_right(d_cq, tiles[4]))
    dh1 = dh2 + part_one
    d_self_out = dh1.astype(bf16)
    d_q, d_k, d_v = through(tiles[3], d_self_out, query, keys, probs, values)
    d_a = matmul_right(d_q, tiles[0]) + matmul_right(d_k, tiles[1]) + matmul_right(d_v, tiles[2])
    part_zero, gain_grad_zero = jax.vjp(normalize, h0, gains[0])[1](d_a)
    grad_tokens = (dh1 + part_zero).astype(bf16)
    pairs = [
        (a_in, d_q),
        (a_in, d_k),
        (a_in, d_v),
        (attended, d_self_out),
        (b_in, d_cq),
        (ctx_low, d_ck),
        (ctx_high, d_ck),
        (ctx_low, d_cv),
        (ctx_high, d_cv),
        (cross_o, d_cross_out),
    ]
    for part in range(4):
        pairs.append((c_in, d_hidden[:, part * width : (part + 1) * width]))
    for part in range(4):
        pairs.append((activated[:, part * width : (part + 1) * width], d_ff))
    total_slots = lax.axis_size("fsdp") * cap
    placed = jnp.zeros((total_slots,) + master.shape[1:], bf16)
    for tile, (left, right) in enumerate(pairs):
        term = lax.psum_scatter(
            matmul_left(left, right).astype(bf16), "dp", scatter_dimension=0, tiled=True
        )
        placed = lax.dynamic_update_index_in_dim(placed, term, slot_of[tile], 0)
    owned = lax.psum_scatter(placed, "fsdp", scatter_dimension=0, tiled=True).astype(f32)
    my_slots = lax.axis_index("fsdp") * cap + jnp.arange(cap)
    used = jnp.any(slot_of[None, :] == my_slots[:, None], axis=1)[:, None, None]
    updated = adam_update(master, moment_one, moment_two, owned, rate_matrix, decay_rate)
    new_w, new_m, new_v = (jnp.where(used, value, 0.0) for value in updated)
    gain_grads = jnp.stack([gain_grad_zero, gain_grad_one, gain_grad_two])
    gain_total = lax.psum(gain_grads, ("dp", "fsdp"))
    new_g, new_gm, new_gv = adam_update(gains, gain_one, gain_two, gain_total, rate_gain, 0.0)
    return (layer_out, grad_tokens, new_w, new_m, new_v, new_g, new_gm, new_gv)


def solution(mesh):
    planes = mesh.shape["dp"] == 8 and mesh.shape["fsdp"] == 4
    if planes:
        used = Mesh(mesh.devices.reshape(4, 2, 2, 2), ALL_AXES)
        dp, fsdp, body = ("z", "x"), ("y", "c"), plane_body
    else:
        used, dp, fsdp, body = mesh, ("dp",), ("fsdp",), whole_body
    rows = P(dp + fsdp, None)
    tiles = P(fsdp, dp, None)
    return jax.shard_map(
        body,
        mesh=used,
        in_specs=(rows, rows, P(dp + fsdp, None, None), rows, P(dp + fsdp), P(), tiles, tiles, tiles, P(), P(), P()),
        out_specs=(rows, rows, tiles, tiles, tiles, P(), P(), P()),
        check_vma=False,
    )
```

```python
import jax
import jax.numpy as jnp
import numpy as np
from jax import lax
from jax.experimental import pallas as pl
from jax.experimental.layout import Layout, with_layout_constraint
from jax.experimental.pallas import tpu as pltpu
from jax.sharding import Mesh
from jax.sharding import PartitionSpec as P

HEADS = 16
STEP = 10

norm_eps = 1e-06
beta_one = 0.9
beta_two = 0.95
adam_eps = 1e-08
decay_rate = 0.1
rate_matrix = 0.1
rate_gain = 0.8

f32 = jnp.float32
bf16 = jnp.bfloat16

SHIFT = (0, 0, 0, 0, 2, 2, 2, 2, 2, 2, 0, 1, 2, 3, 0, 1, 2, 3)
ROW_TILES = (3, 9, 14, 15, 16, 17)
VMEM_LIMIT = 48 << 20


def normalize(h, gain):
    scale = lax.rsqrt(jnp.mean(h * h, axis=-1, keepdims=True) + norm_eps)
    return h * scale * gain


def gelu_tanh(u):
    return 0.5 * u * (1.0 + jnp.tanh(0.7978845608028654 * (u + 0.044715 * u * u * u)))


def matmul(left, right):
    return jnp.dot(left, right, preferred_element_type=f32)


def matmul_left(left, right):
    return lax.dot_general(left, right, (((0,), (0,)), ((), ())), preferred_element_type=f32)


def matmul_right(left, right):
    return lax.dot_general(left, right, (((1,), (1,)), ((), ())), preferred_element_type=f32)


def ranks_of(owners):
    order = jnp.arange(owners.shape[0])
    same = (owners[:, None] == owners[None, :]) & (order[None, :] < order[:, None])
    return jnp.sum(same.astype(jnp.int32), axis=1)


def segments(lengths, count):
    places = jnp.arange(count)
    end = jnp.zeros((), jnp.int32)
    seg = jnp.zeros((count,), jnp.int32)
    for item in range(lengths.shape[0]):
        end = end + lengths[item]
        seg = seg + (places >= end).astype(jnp.int32)
    return seg


def adam_update(weight, first, second, grad, rate, decay):
    first = beta_one * first + (1.0 - beta_one) * grad
    second = beta_two * second + (1.0 - beta_two) * grad * grad
    fix_one = 1.0 / (1.0 - beta_one**STEP)
    fix_two = 1.0 / (1.0 - beta_two**STEP)
    move = first * fix_one / (jnp.sqrt(second * fix_two) + adam_eps)
    return (weight - rate * (move + decay * weight), first, second)


def pack_columns(master, table, first_slot, slots):
    _, rows, columns = master.shape
    width = columns // 8

    def kernel(table_ref, in_ref, out_ref):
        slot = pl.program_id(0)
        for rank in range(8):
            start = pl.multiple_of(table_ref[slot * 8 + rank] * width, width)
            out_ref[rank, 0] = in_ref[0, :, pl.ds(start, width)].astype(bf16)

    return pl.pallas_call(
        kernel,
        out_shape=jax.ShapeDtypeStruct((8, slots, rows, width), bf16),
        grid_spec=pltpu.PrefetchScalarGridSpec(
            num_scalar_prefetch=1,
            grid=(slots,),
            in_specs=[pl.BlockSpec((1, rows, columns), lambda k, t: (first_slot + k, 0, 0))],
            out_specs=pl.BlockSpec((8, 1, rows, width), lambda k, t: (0, k, 0, 0)),
        ),
        compiler_params=pltpu.CompilerParams(vmem_limit_bytes=VMEM_LIMIT),
        name="pack_columns",
    )(table, master)


def pick_blocks(sources, which, index, count):
    _, rows, width = sources[0].shape
    n_src = len(sources)

    def kernel(which_ref, index_ref, *refs):
        place = pl.program_id(0) * 2 + pl.program_id(1)
        out_ref = refs[n_src]
        for number in range(n_src):

            @pl.when(which_ref[place] == number)
            def _():
                out_ref[...] = refs[number][0]

    def spec(number):
        def at(n, half, which, index):
            place = n * 2 + half
            return (jnp.where(which[place] == number, index[place], 0), 0, 0)

        return pl.BlockSpec((1, rows, width), at)

    return pl.pallas_call(
        kernel,
        out_shape=jax.ShapeDtypeStruct((2 * rows, count * width), bf16),
        grid_spec=pltpu.PrefetchScalarGridSpec(
            num_scalar_prefetch=2,
            grid=(count, 2),
            in_specs=[spec(number) for number in range(n_src)],
            out_specs=pl.BlockSpec((rows, width), lambda n, half, which, index: (half, n)),
        ),
        compiler_params=pltpu.CompilerParams(vmem_limit_bytes=VMEM_LIMIT),
        name="pick_blocks",
    )(which, index, *sources)


def pack_gradients(groups, which, column, rows, width, slots):
    n_src = len(groups)

    def kernel(which_ref, column_ref, *refs):
        rank = pl.program_id(0)
        out_ref = refs[n_src]
        for k in range(slots):
            start = pl.multiple_of(column_ref[rank * slots + k] * width, width)
            for number in range(n_src):

                @pl.when(which_ref[rank * slots + k] == number)
                def _():
                    out_ref[0, k] = refs[number][:, pl.ds(start, width)]

    return pl.pallas_call(
        kernel,
        out_shape=jax.ShapeDtypeStruct((8, slots, rows, width), bf16),
        grid_spec=pltpu.PrefetchScalarGridSpec(
            num_scalar_prefetch=2,
            grid=(8,),
            in_specs=[
                pl.BlockSpec((rows, group.shape[1]), lambda rank, which, column: (rank // 4, 0)) for group in groups
            ],
            out_specs=pl.BlockSpec((1, slots, rows, width), lambda rank, which, column: (rank, 0, 0, 0)),
        ),
        compiler_params=pltpu.CompilerParams(vmem_limit_bytes=VMEM_LIMIT),
        name="pack_gradients",
    )(which, column, *groups)


def adam_tiles(master, one, two, columns_from, rows_from, visit, mode, column_place, row_place, hold, previous=None):
    _, rows, columns = master.shape
    width = columns // 8
    n_visit = visit.shape[0]
    n_col, n_row = len(columns_from), len(rows_from)
    kept = () if previous is None else tuple(previous)

    def kernel(visit_ref, mode_ref, cp_ref, rp_ref, hold_ref, *refs):
        w_ref, m_ref, v_ref = refs[:3]
        grads = refs[3 : 3 + n_col + n_row]
        outs = refs[3 + n_col + n_row + len(kept) :]
        how = mode_ref[pl.program_id(0)]

        @pl.when(how == 1)
        def _():
            for ref in outs:
                ref[...] = jnp.zeros_like(ref)

        for number, grad_ref in enumerate(grads):

            @pl.when(how == number + 2)
            def _():
                grad = grad_ref[0].astype(f32)
                results = adam_update(w_ref[0], m_ref[0], v_ref[0], grad, rate_matrix, decay_rate)
                for ref, value in zip(outs, results, strict=True):
                    ref[0] = value

    def block_of(n, b, hold):
        return jnp.where(hold[n] == 1, 7, b)

    state = pl.BlockSpec((1, rows, width), lambda n, b, vi, mo, cp, rp, ho: (vi[n], 0, block_of(n, b, ho)))

    def column_spec(number):
        def at(n, b, vi, mo, cp, rp, ho):
            return (jnp.where(mo[n] == number + 2, cp[n * 8 + block_of(n, b, ho)], 0), 0, 0)

        return pl.BlockSpec((1, rows, width), at)

    def row_spec(number):
        def at(n, b, vi, mo, cp, rp, ho):
            taken = mo[n] == number + 2
            return (jnp.where(taken, rp[n], 0), 0, jnp.where(taken, block_of(n, b, ho), 0))

        return pl.BlockSpec((1, rows, width), at)

    shape = jax.ShapeDtypeStruct(master.shape, f32)
    n_before = 5 + 3 + n_col + n_row
    return pl.pallas_call(
        kernel,
        out_shape=(shape, shape, shape),
        grid_spec=pltpu.PrefetchScalarGridSpec(
            num_scalar_prefetch=5,
            grid=(n_visit, 8),
            in_specs=[
                state,
                state,
                state,
                *(column_spec(number) for number in range(n_col)),
                *(row_spec(n_col + number) for number in range(n_row)),
                *(pl.BlockSpec(memory_space=pl.ANY) for _ in kept),
            ],
            out_specs=(state, state, state),
        ),
        input_output_aliases={n_before + n: n for n in range(len(kept))},
        compiler_params=pltpu.CompilerParams(vmem_limit_bytes=VMEM_LIMIT),
        cost_estimate=pl.CostEstimate(
            flops=30 * n_visit * rows * columns, bytes_accessed=26 * n_visit * rows * columns, transcendentals=0
        ),
        name="adam_tiles",
    )(visit, mode, column_place, row_place, hold, master, one, two, *columns_from, *rows_from, *kept)


def after(value, *others):
    return lax.optimization_barrier((value, *others))[0]


def swap(value, axis):
    return lax.ppermute(value, axis, [(0, 1), (1, 0)])


def gather_rows(value):
    half = value.shape[0] // 2
    over_x = swap(value, "x")
    over_y = swap(value, "y")
    far_low = swap(over_y[:half], "x")
    far_high = swap(over_x[half:], "y")
    four = jnp.concatenate([value, over_y, over_x, far_low, far_high], axis=0)
    return jnp.concatenate([four, swap(four, "c")], axis=0)


def scatter_rows(part):
    rows, width = part.shape[0] // 8, part.shape[1]
    half = width // 2
    part = part.reshape(2, 2, 2, rows, width)
    chip = part[0] + swap(part[1], "c")
    low, high = chip[..., :half], chip[..., half:]
    low_two = low[:, 0] + swap(low[:, 1].astype(bf16), "y").astype(f32)
    high_two = high[0] + swap(high[1].astype(bf16), "x").astype(f32)
    low_one = low_two[0] + swap(low_two[1].astype(bf16), "x").astype(f32)
    high_one = high_two[0] + swap(high_two[1].astype(bf16), "y").astype(f32)
    return jnp.concatenate([low_one, high_one], axis=1)


def sum_everywhere(value):
    for axis in ("c", "y", "x"):
        value = value + swap(value, axis)
    for step in (1, 2):
        value = value + lax.ppermute(value, "z", [(z, z ^ step) for z in range(4)])
    return value


def flip_pairs(mask, keep=None):
    pairs = []
    for z in range(4):
        for place in range(8):
            target = place ^ mask
            if keep is None or keep(z, place, target):
                pairs.append((z * 8 + place, z * 8 + target))
    return pairs


ALL_AXES = ("z", "x", "y", "c")
PLANE = ("x", "y", "c")


def plane_body(
    tokens, cotangent, context, lengths, keep, owners, master, moment_one, moment_two, gains, gain_one, gain_two
):
    cap, rows, _ = master.shape
    count, width = tokens.shape
    heads_here = HEADS // 8
    head_dim = width // HEADS
    scale = head_dim ** (-0.5)
    block = width // 8
    z = lax.axis_index("z")
    x = lax.axis_index("x")
    f = lax.axis_index("y") * 2 + lax.axis_index("c")

    n_tiles = owners.shape[0]
    rank = ranks_of(owners)
    shift_of = np.array(SHIFT, np.int32)
    row_of = np.array([t in ROW_TILES for t in range(n_tiles)])
    all_slots = jnp.arange(4 * cap).reshape(4, cap)
    holds = (owners * cap + rank)[None, None, :] == all_slots[:, :, None]
    used_at = jnp.any(holds, axis=2)
    tile_at = jnp.sum(jnp.where(holds, np.arange(n_tiles, dtype=np.int32), 0), axis=2)
    shift_at = jnp.sum(jnp.where(holds, shift_of, 0), axis=2)
    row_at = jnp.any(holds & row_of, axis=2)
    mine = (jnp.arange(4) == f)[:, None]

    def my(value):
        return jnp.sum(jnp.where(mine, value.astype(jnp.int32), 0), axis=0)

    my_used, my_tile, my_shift, my_row = my(used_at), my(tile_at), my(shift_at), my(row_at)

    to_x = np.arange(8) // 4
    to_f = np.arange(8) % 4
    column_table = 2 * ((to_f[None, :] + my_shift[:, None]) % 4) + to_x[None, :]
    half_cap = cap // 2
    place = np.arange(4)

    def of_tiles(tiles, values):
        chosen = tiles[:, None] == np.arange(n_tiles)[None, :]
        return jnp.sum(jnp.where(chosen, values[None, :], 0), axis=1)

    column_tiles = jnp.concatenate([np.array([0, 1, 2, 4, 5, 7, 6, 8], np.int32), 10 + (place - f) % 4])
    column_part = jnp.repeat(of_tiles(column_tiles, rank // half_cap), 2)
    column_place = of_tiles(column_tiles, owners * half_cap + rank % half_cap)
    column_place = (column_place[:, None] + np.array([0, 4 * half_cap])[None, :]).reshape(-1)
    other_f = f ^ place
    outer_tiles = jnp.where(other_f == z, 3, 9)
    out_tiles = 14 + (z - other_f) % 4
    row_slots = of_tiles(jnp.concatenate([outer_tiles, out_tiles]), rank)
    row_owners = of_tiles(jnp.stack([outer_tiles[0], outer_tiles[2], out_tiles[0], out_tiles[2]]), owners)

    def pack_first(weights):
        return pack_columns(weights, column_table[:half_cap].reshape(-1), 0, half_cap)

    def pack_second(weights):
        return pack_columns(weights, column_table[half_cap:].reshape(-1), half_cap, half_cap)

    def my_block(slot):
        return lax.dynamic_index_in_dim(master, slot, 0, keepdims=False).astype(bf16)

    present = owners[0] >= 0

    def chain_step(move, *values):
        shapes = jax.eval_shape(move, *values)
        idle = jax.tree.map(lambda leaf: jnp.zeros(leaf.shape, leaf.dtype), shapes)
        return lax.cond(present, move, lambda *_: idle, *values)

    h0 = tokens.astype(f32)
    outer_blocks = [my_block(row_slots[mask]) for mask in range(4)]
    out_blocks = [my_block(row_slots[4 + mask]) for mask in range(4)]
    a_in = normalize(h0, gains[0]).astype(bf16)
    sent = pack_first(after(master, column_part, column_place, row_slots, row_owners))
    received = [lax.all_to_all(sent, PLANE, 0, 0, tiled=True).reshape(8 * half_cap, rows, block)]
    seg = segments(lengths[0], count)
    live = keep == 1
    code = seg * 2 + live.astype(jnp.int32)

    def spread_code(code):
        for axis in ("y", "x", "c"):
            code = jnp.concatenate([code, swap(code, axis)])
        return code

    code = chain_step(spread_code, after(code, a_in, *outer_blocks, *out_blocks))
    seg_all = (code // 2).reshape(8, count)
    live_all = (code % 2 == 1).reshape(8, count)
    grad_out = cotangent.astype(f32) * live.astype(f32)[:, None]
    received = [after(received[0], a_in, code, *outer_blocks, *out_blocks)]

    def columns_here(first, count, parts):
        chosen = slice(2 * first, 2 * (first + count))
        return pick_blocks(received[:parts], column_part[chosen], column_place[chosen], count)

    def gather_z(value):
        return lax.all_gather(value, "z", axis=0, tiled=True)

    local = columns_here(0, 3, 1)
    w_qkv = gather_z(local)
    a_all = gather_rows(after(a_in, local))
    d_ff = gather_rows(after(grad_out.astype(bf16), local))
    sent = pack_second(after(master, a_all, d_ff))
    received.append(lax.all_to_all(sent, PLANE, 0, 0, tiled=True).reshape(8 * half_cap, rows, block))

    def take_rows(kind, blocks, keep_pair):
        here, there = row_owners[2 * kind], row_owners[2 * kind + 1]
        core = f % 2
        from_core = swap(jnp.stack([blocks[1], blocks[3]]), "c")
        mine = jnp.where(here % 2 == core, blocks[0], from_core[0])
        across = jnp.where(there % 2 == core, blocks[2], from_core[1])
        from_y = lax.ppermute(across, ALL_AXES, flip_pairs(2, keep_pair))
        return jnp.where(here // 2 == f // 2, mine, from_y)

    def needs_outer(zz, place, target):
        return target % 4 in (zz, (zz + 2) % 4)

    outer = take_rows(0, [after(value, local) for value in outer_blocks], needs_outer)
    out_rows = take_rows(1, [after(value, local) for value in out_blocks], None)
    half_rows = rows // 2
    odd = z % 2
    to_pair = lax.dynamic_slice_in_dim(after(outer, sent), (1 - odd) * half_rows, half_rows, 0)
    own_half = lax.dynamic_slice_in_dim(outer, odd * half_rows, half_rows, 0)
    pair_swap = [
        (zz * 8 + place, (zz ^ 1) * 8 + place)
        for zz in range(4)
        for place in range(8)
        if place % 4 in (zz, (zz + 2) % 4)
    ]
    from_pair = lax.ppermute(to_pair, ALL_AXES, pair_swap)
    has_outer = (f == z) | (f == (z + 2) % 4)
    outer_all = lax.all_gather(jnp.where(has_outer, own_half, from_pair), "z", axis=0, tiled=True)
    low_y = lax.axis_index("y") == 0
    w_self_out = jnp.where(low_y, outer_all[:rows], outer_all[rows:])
    w_cross_out = jnp.where(low_y, outer_all[rows:], outer_all[:rows])

    def split(value):
        return value.reshape(8, -1, heads_here, head_dim)

    qkv = matmul(a_all, w_qkv)
    qkv = qkv.astype(bf16)
    query, keys, values = (split(qkv[:, n * block : (n + 1) * block]) for n in range(3))
    places = jnp.arange(count)
    allowed = (seg_all[:, :, None] == seg_all[:, None, :]) & (
        live_all[:, None, :] | (places[:, None] == places[None, :])
    )

    def probabilities(left, right, mask):
        scores = jnp.einsum("bqhd,bkhd->bhqk", left, right, preferred_element_type=f32) * scale
        scores = jnp.where(mask[:, None], scores, -1e30)
        expo = jnp.exp(scores - jnp.max(scores, axis=-1, keepdims=True))
        return expo / jnp.sum(expo, axis=-1, keepdims=True)

    def weighted(probs, right):
        return jnp.einsum("bhqk,bkhd->bqhd", probs, right, preferred_element_type=f32)

    def joined(value):
        return value.astype(bf16).reshape(-1, block)

    probs = probabilities(query, keys, allowed)
    probs_low = probs.astype(bf16)
    mixed = weighted(probs_low, values).astype(bf16)
    attended = mixed.reshape(-1, block)
    received[1] = after(received[1], mixed)
    local_cross, local_in = columns_here(3, 5, 2), columns_here(8, 4, 2)
    w_cross = gather_z(local_cross)
    w_in = gather_z(local_in)

    w_out = gather_z(after(out_rows, local_cross, local_in))
    slots, ctx_len, ctx_width = context.shape
    ctx = after(context.reshape(slots * ctx_len, ctx_width), local_cross, local_in, out_rows)
    ctx_x, ctx_y = swap(ctx, "x"), swap(ctx, "y")
    h1 = h0 + chain_step(scatter_rows, matmul(after(attended, local_in), w_self_out))

    def second_step(one, own, over_x, over_y):
        half = over_x.shape[0] // 2
        far_low, far_high = swap(over_y[:half], "x"), swap(over_x[half:], "y")
        four = jnp.concatenate([own, over_y, over_x, far_low, far_high], axis=0)
        return gather_rows(one), four, swap(four, "c")

    b_all, ctx_here, ctx_there = chain_step(
        second_step, normalize(h1, gains[1]).astype(bf16), ctx, ctx_x, ctx_y
    )

    w_cross_q = w_cross[:, :block]
    w_low = w_cross[:, block : 3 * block]
    w_high = w_cross[:, 3 * block :]
    ctx_kv = jnp.concatenate(
        [
            (matmul(part[:, :width], w_low) + matmul(part[:, width:], w_high)).astype(bf16)
            for part in (ctx_here, ctx_there)
        ],
        axis=0,
    )
    cross_q = matmul(b_all, w_cross_q)
    cross_q = split(cross_q.astype(bf16))
    cross_k, cross_v = split(ctx_kv[:, :block]), split(ctx_kv[:, block:])
    item = jnp.arange(slots * ctx_len) // ctx_len
    own_item = seg_all[:, :, None] == item[None, None, :]
    cross_p = probabilities(cross_q, cross_k, own_item)
    cross_low = cross_p.astype(bf16)
    cross_o = joined(weighted(cross_low, cross_v))
    h2, ctx_all = chain_step(
        lambda one, *pieces: (scatter_rows(one), jnp.concatenate(pieces, axis=0)),
        matmul(cross_o, w_cross_out),
        ctx_here,
        ctx_there,
    )
    ctx_low, ctx_high = ctx_all[:, :width], ctx_all[:, width:]
    h2 = h1 + h2
    c_all = chain_step(gather_rows, normalize(h2, gains[2]).astype(bf16))

    hidden = matmul(c_all, w_in)
    activated = gelu_tanh(hidden).astype(bf16)

    def sum_rows(value):
        value = with_layout_constraint(value, Layout(major_to_minor=(0, 1)))
        value = lax.psum_scatter(value, "z", scatter_dimension=0, tiled=True)
        return with_layout_constraint(value, Layout(major_to_minor=(0, 1)))

    def from_y(value, keep_pair=None):
        return jnp.stack([value, lax.ppermute(value, ALL_AXES, flip_pairs(2, keep_pair))])

    def with_core(pair):
        return jnp.concatenate([pair, swap(pair, "c")])

    t_out = matmul_left(activated, d_ff).astype(bf16)
    g_out = sum_rows(t_out)
    d_act = matmul_right(after(d_ff, t_out), w_out)
    d_hidden = jax.vjp(gelu_tanh, hidden)[1](d_act)[0].astype(bf16)
    t_in = matmul_left(c_all, d_hidden).astype(bf16)
    g_in = sum_rows(t_in)
    d_c, out_sum = chain_step(
        lambda one, two: (scatter_rows(one), scatter_rows(two)), matmul_right(d_hidden, w_in), matmul(activated, w_out)
    )
    layer_out = (h2 + out_sum).astype(bf16)
    part_two, gain_grad_two = jax.vjp(normalize, h2, gains[2])[1](d_c)
    dh2 = grad_out + part_two
    d_cross_out = chain_step(gather_rows, after(dh2.astype(bf16), t_in))
    g_cross_out = matmul_left(cross_o, d_cross_out)

    def through(d_mixed, left, right, probs, probs_low, values):
        d_mixed = split(d_mixed.astype(bf16))
        d_probs = jnp.einsum("bqhd,bkhd->bhqk", d_mixed, values, preferred_element_type=f32)
        d_scores = (probs * (d_probs - jnp.sum(probs * d_probs, axis=-1, keepdims=True))).astype(bf16)
        d_left = joined(weighted(d_scores, right) * scale)
        d_right = joined(jnp.einsum("bhqk,bqhd->bkhd", d_scores, left, preferred_element_type=f32) * scale)
        d_values = joined(jnp.einsum("bhqk,bqhd->bkhd", probs_low, d_mixed, preferred_element_type=f32))
        return d_left, d_right, d_values

    (d_cq, d_ck, d_cv), out_grads = chain_step(
        lambda one, two: (
            through(matmul_right(one, w_cross_out), cross_q, cross_k, cross_p, cross_low, cross_v),
            from_y(two),
        ),
        d_cross_out,
        g_out,
    )
    d_ckv = jnp.concatenate([d_ck, d_cv], axis=1)
    t_cross = jnp.concatenate(
        [
            value.astype(bf16)
            for value in (matmul_left(b_all, d_cq), matmul_left(ctx_low, d_ckv), matmul_left(ctx_high, d_ckv))
        ],
        axis=1,
    )
    g_cross = sum_rows(t_cross)
    part = matmul_right(d_cq, w_cross_q)
    d_b = chain_step(scatter_rows, part)
    part_one, gain_grad_one = jax.vjp(normalize, h1, gains[1])[1](d_b)
    dh1 = dh2 + part_one
    d_self_out = chain_step(gather_rows, after(dh1.astype(bf16), t_cross, g_in))
    g_self_out = matmul_left(attended, d_self_out)
    t_outer = jnp.concatenate(
        [
            jnp.where(low_y, g_self_out, g_cross_out).astype(bf16),
            jnp.where(low_y, g_cross_out, g_self_out).astype(bf16),
        ],
        axis=0,
    )
    g_outer = sum_rows(after(t_outer, g_cross))
    d_mixed = matmul_right(after(d_self_out, t_outer), w_self_out)
    d_q, d_k, d_v = through(d_mixed, query, keys, probs, probs_low, values)
    d_qkv = jnp.concatenate([d_q, d_k, d_v], axis=1)
    t_qkv = matmul_left(a_all, d_qkv).astype(bf16)
    g_qkv = sum_rows(t_qkv)
    group_of = np.array([0, 0, 0, 0, 0, 0, 0, 0, 0, 0, 1, 1, 1, 1, 0, 0, 0, 0], np.int32)
    column_of = np.array([0, 0, 0, 0, 0, 1, 3, 2, 4, 0, 0, 1, 2, 3, 0, 0, 0, 0], np.int32)
    group_at = jnp.sum(jnp.where(holds, group_of, 0), axis=2)
    column_at = jnp.sum(jnp.where(holds, column_of, 0), axis=2)
    column_at = jnp.where(group_at == 1, (column_at + f) % 4, column_at)
    sent = pack_gradients(
        [after(g_cross, t_qkv), g_in], jnp.tile(group_at.reshape(-1), 2), jnp.tile(column_at.reshape(-1), 2), rows, block, cap
    )
    early_grads = lax.all_to_all(sent, PLANE, 0, 0, tiled=True).reshape(8 * cap, rows, block)

    def last_step(part, out_pair, gain_grad_one, gain_grad_two):
        part_zero, gain_grad_zero = jax.vjp(normalize, h0, gains[0])[1](scatter_rows(part))
        gain_grads = jnp.stack([gain_grad_zero, gain_grad_one, gain_grad_two])
        return part_zero, sum_everywhere(gain_grads), with_core(out_pair)

    part_zero, gain_total, out_grads = chain_step(
        last_step, matmul_right(after(d_qkv, sent), w_qkv), out_grads, gain_grad_one, gain_grad_two
    )
    grad_tokens = (dh1 + part_zero).astype(bf16)

    by_tile = jnp.swapaxes(after(g_qkv, out_grads).reshape(2, rows, 3, block), 1, 2)
    sent = jnp.broadcast_to(by_tile[:, None], (2, 4, 3, rows, block)).reshape(8, 3, rows, block)
    late_grads = lax.all_to_all(sent, PLANE, 0, 0, tiled=True).reshape(8 * 3, rows, block)
    back_swap = [(target, source) for source, target in pair_swap]
    place = np.arange(8)
    source_x, source_f = (place % 2)[None, :], ((place // 2)[None, :] - my_shift[:, None]) % 4
    slot = np.arange(cap, dtype=np.int32)
    column_place = (source_x * 4 + source_f) * cap + slot[:, None]
    other_row = ((z - my_shift) % 4) ^ f
    row_source = (other_row % 2) * 2 + other_row // 2
    late = (my_used == 1) & ((my_tile < 4) | (my_tile == 9))
    early_mode = jnp.where(my_used == 0, 1, jnp.where(late, 0, jnp.where(my_row == 1, 3, 2)))
    states = (master, moment_one, moment_two)

    def early_step(early_grads, out_grads, half):
        other_half = lax.ppermute(half, ALL_AXES, back_swap)
        in_order = jnp.where(odd == 0, jnp.stack([half, other_half]), jnp.stack([other_half, half]))
        in_order = in_order.reshape(rows, width)
        counts = jnp.where(f % 2 == z % 2, in_order, swap(in_order, "c"))
        early = None
        for first in (0, half_cap):
            chosen = slice(first, first + half_cap)
            early = adam_tiles(
                *states,
                [early_grads],
                [out_grads],
                slot[chosen],
                early_mode[chosen],
                column_place[chosen].reshape(-1),
                row_source[chosen],
                np.zeros(half_cap, np.int32),
                early,
            )
        return *early, from_y(counts)

    *early, outer_grads = chain_step(early_step, early_grads, out_grads, g_outer)

    n_late = 5
    order = jnp.sum(jnp.where(slot[None, :] < slot[:, None], late.astype(jnp.int32)[None, :], 0), axis=1)
    count_late = jnp.sum(late.astype(jnp.int32))
    step = np.arange(n_late)
    wanted = jnp.minimum(step, jnp.maximum(count_late - 1, 0))
    here = late[None, :] & (order[None, :] == wanted[:, None])

    def at_step(value):
        return jnp.sum(jnp.where(here, value.astype(jnp.int32)[None, :], 0), axis=1)

    hold = (step >= jnp.maximum(count_late, 1)).astype(jnp.int32)
    tile = at_step(my_tile)
    some = count_late > 0
    visit = jnp.where(some, at_step(slot), 0)
    first_mode = jnp.where(early_mode[0] == 3, 4, early_mode[0])
    late_mode = jnp.where(at_step(my_row) == 1, 5, 3)
    mode = jnp.where(hold == 1, 0, jnp.where(some, late_mode, first_mode))
    late_place = ((place % 2)[None, :] * 4 + (place // 2)[None, :]) * 3 + tile[:, None]
    late_place = jnp.where(some, late_place, column_place[:1])
    new_w, new_m, new_v = adam_tiles(
        *states,
        [early_grads, late_grads],
        [out_grads, outer_grads],
        visit,
        mode,
        late_place.reshape(-1),
        jnp.where(some, at_step(other_row // 2), row_source[0]),
        hold,
        early,
    )
    new_g, new_gm, new_gv = adam_update(gains, gain_one, gain_two, gain_total, rate_gain, 0.0)
    return (layer_out, grad_tokens, new_w, new_m, new_v, new_g, new_gm, new_gv)


def whole_body(
    tokens, cotangent, context, lengths, keep, owners, master, moment_one, moment_two, gains, gain_one, gain_two
):
    cap = master.shape[0]
    n_tiles = owners.shape[0]
    slot_of = owners * cap + ranks_of(owners)
    owner_rows = lax.all_gather(master.astype(bf16), "fsdp", axis=0, tiled=True)
    tiles = [
        lax.all_gather(
            lax.dynamic_index_in_dim(owner_rows, slot_of[tile], 0, keepdims=False), "dp", axis=0, tiled=True
        )
        for tile in range(n_tiles)
    ]
    w_in = jnp.concatenate(tiles[10:14], axis=1)
    w_out = jnp.concatenate(tiles[14:18], axis=0)
    count, width = tokens.shape
    head_dim = width // HEADS
    scale = head_dim ** (-0.5)
    seg = segments(lengths[0], count)
    live = keep == 1
    places = jnp.arange(count)

    def split(value):
        return value.astype(bf16).reshape(-1, HEADS, head_dim)

    def joined(value):
        return value.astype(bf16).reshape(-1, width)

    def probabilities(left, right, mask):
        scores = jnp.einsum("qhd,khd->hqk", left, right, preferred_element_type=f32) * scale
        scores = jnp.where(mask[None], scores, -1e30)
        expo = jnp.exp(scores - jnp.max(scores, axis=-1, keepdims=True))
        return expo / jnp.sum(expo, axis=-1, keepdims=True)

    def weighted(probs, right):
        return jnp.einsum("hqk,khd->qhd", probs, right, preferred_element_type=f32)

    def through(weights, d_out, left, right, probs, values):
        d_mixed = split(matmul_right(d_out, weights))
        d_probs = jnp.einsum("qhd,khd->hqk", d_mixed, values, preferred_element_type=f32)
        d_scores = (probs * (d_probs - jnp.sum(probs * d_probs, axis=-1, keepdims=True))).astype(bf16)
        d_left = joined(weighted(d_scores, right) * scale)
        d_right = joined(jnp.einsum("hqk,qhd->khd", d_scores, left, preferred_element_type=f32) * scale)
        d_values = joined(jnp.einsum("hqk,qhd->khd", probs.astype(bf16), d_mixed, preferred_element_type=f32))
        return d_left, d_right, d_values

    h0 = tokens.astype(f32)
    a_in = normalize(h0, gains[0]).astype(bf16)
    query, keys, values = (split(matmul(a_in, tiles[n])) for n in range(3))
    allowed = (seg[:, None] == seg[None, :]) & (live[None, :] | (places[:, None] == places[None, :]))
    probs = probabilities(query, keys, allowed)
    attended = joined(weighted(probs.astype(bf16), values))
    h1 = h0 + matmul(attended, tiles[3])
    b_in = normalize(h1, gains[1]).astype(bf16)
    slots, ctx_len, ctx_width = context.shape
    ctx = context.reshape(slots * ctx_len, ctx_width)
    ctx_low, ctx_high = ctx[:, :width], ctx[:, width:]
    cross_q = split(matmul(b_in, tiles[4]))
    cross_k = split(matmul(ctx_low, tiles[5]) + matmul(ctx_high, tiles[6]))
    cross_v = split(matmul(ctx_low, tiles[7]) + matmul(ctx_high, tiles[8]))
    item = jnp.arange(slots * ctx_len) // ctx_len
    cross_p = probabilities(cross_q, cross_k, seg[:, None] == item[None, :])
    cross_o = joined(weighted(cross_p.astype(bf16), cross_v))
    h2 = h1 + matmul(cross_o, tiles[9])
    c_in = normalize(h2, gains[2]).astype(bf16)
    hidden = matmul(c_in, w_in)
    activated = gelu_tanh(hidden).astype(bf16)
    layer_out = (h2 + matmul(activated, w_out)).astype(bf16)
    grad_out = cotangent.astype(f32) * live.astype(f32)[:, None]
    d_ff = grad_out.astype(bf16)
    d_hidden = jax.vjp(gelu_tanh, hidden)[1](matmul_right(d_ff, w_out))[0].astype(bf16)
    part_two, gain_grad_two = jax.vjp(normalize, h2, gains[2])[1](matmul_right(d_hidden, w_in))
    dh2 = grad_out + part_two
    d_cross_out = dh2.astype(bf16)
    d_cq, d_ck, d_cv = through(tiles[9], d_cross_out, cross_q, cross_k, cross_p, cross_v)
    part_one, gain_grad_one = jax.vjp(normalize, h1, gains[1])[1](matmul_right(d_cq, tiles[4]))
    dh1 = dh2 + part_one
    d_self_out = dh1.astype(bf16)
    d_q, d_k, d_v = through(tiles[3], d_self_out, query, keys, probs, values)
    d_a = matmul_right(d_q, tiles[0]) + matmul_right(d_k, tiles[1]) + matmul_right(d_v, tiles[2])
    part_zero, gain_grad_zero = jax.vjp(normalize, h0, gains[0])[1](d_a)
    grad_tokens = (dh1 + part_zero).astype(bf16)
    pairs = [
        (a_in, d_q),
        (a_in, d_k),
        (a_in, d_v),
        (attended, d_self_out),
        (b_in, d_cq),
        (ctx_low, d_ck),
        (ctx_high, d_ck),
        (ctx_low, d_cv),
        (ctx_high, d_cv),
        (cross_o, d_cross_out),
    ]
    for part in range(4):
        pairs.append((c_in, d_hidden[:, part * width : (part + 1) * width]))
    for part in range(4):
        pairs.append((activated[:, part * width : (part + 1) * width], d_ff))
    total_slots = lax.axis_size("fsdp") * cap
    placed = jnp.zeros((total_slots,) + master.shape[1:], bf16)
    for tile, (left, right) in enumerate(pairs):
        term = lax.psum_scatter(
            matmul_left(left, right).astype(bf16), "dp", scatter_dimension=0, tiled=True
        )
        placed = lax.dynamic_update_index_in_dim(placed, term, slot_of[tile], 0)
    owned = lax.psum_scatter(placed, "fsdp", scatter_dimension=0, tiled=True).astype(f32)
    my_slots = lax.axis_index("fsdp") * cap + jnp.arange(cap)
    used = jnp.any(slot_of[None, :] == my_slots[:, None], axis=1)[:, None, None]
    updated = adam_update(master, moment_one, moment_two, owned, rate_matrix, decay_rate)
    new_w, new_m, new_v = (jnp.where(used, value, 0.0) for value in updated)
    gain_grads = jnp.stack([gain_grad_zero, gain_grad_one, gain_grad_two])
    gain_total = lax.psum(gain_grads, ("dp", "fsdp"))
    new_g, new_gm, new_gv = adam_update(gains, gain_one, gain_two, gain_total, rate_gain, 0.0)
    return (layer_out, grad_tokens, new_w, new_m, new_v, new_g, new_gm, new_gv)


def solution(mesh):
    planes = mesh.shape["dp"] == 8 and mesh.shape["fsdp"] == 4
    if planes:
        used = Mesh(mesh.devices.reshape(4, 2, 2, 2), ALL_AXES)
        dp, fsdp, body = ("z", "x"), ("y", "c"), plane_body
    else:
        used, dp, fsdp, body = mesh, ("dp",), ("fsdp",), whole_body
    rows = P(dp + fsdp, None)
    tiles = P(fsdp, dp, None)
    return jax.shard_map(
        body,
        mesh=used,
        in_specs=(rows, rows, P(dp + fsdp, None, None), rows, P(dp + fsdp), P(), tiles, tiles, tiles, P(), P(), P()),
        out_specs=(rows, rows, tiles, tiles, tiles, P(), P(), P()),
        check_vma=False,
    )
```

```python
import jax
import jax.numpy as jnp
import numpy as np
from jax import lax
from jax.experimental import pallas as pl
from jax.experimental.layout import Layout, with_layout_constraint
from jax.experimental.pallas import tpu as pltpu
from jax.sharding import Mesh
from jax.sharding import PartitionSpec as P

HEADS = 16
STEP = 10

norm_eps = 1e-06
beta_one = 0.9
beta_two = 0.95
adam_eps = 1e-08
decay_rate = 0.1
rate_matrix = 0.1
rate_gain = 0.8

f32 = jnp.float32
bf16 = jnp.bfloat16

SHIFT = (0, 0, 0, 0, 2, 2, 2, 2, 2, 2, 0, 1, 2, 3, 0, 1, 2, 3)
ROW_TILES = (3, 9, 14, 15, 16, 17)
VMEM_LIMIT = 48 << 20


def normalize(h, gain):
    scale = lax.rsqrt(jnp.mean(h * h, axis=-1, keepdims=True) + norm_eps)
    return h * scale * gain


def gelu_tanh(u):
    return 0.5 * u * (1.0 + jnp.tanh(0.7978845608028654 * (u + 0.044715 * u * u * u)))


def matmul(left, right):
    return jnp.dot(left, right, preferred_element_type=f32)


def matmul_left(left, right):
    return lax.dot_general(left, right, (((0,), (0,)), ((), ())), preferred_element_type=f32)


def matmul_right(left, right):
    return lax.dot_general(left, right, (((1,), (1,)), ((), ())), preferred_element_type=f32)


def ranks_of(owners):
    order = jnp.arange(owners.shape[0])
    same = (owners[:, None] == owners[None, :]) & (order[None, :] < order[:, None])
    return jnp.sum(same.astype(jnp.int32), axis=1)


def segments(lengths, count):
    places = jnp.arange(count)
    end = jnp.zeros((), jnp.int32)
    seg = jnp.zeros((count,), jnp.int32)
    for item in range(lengths.shape[0]):
        end = end + lengths[item]
        seg = seg + (places >= end).astype(jnp.int32)
    return seg


def adam_update(weight, first, second, grad, rate, decay):
    first = beta_one * first + (1.0 - beta_one) * grad
    second = beta_two * second + (1.0 - beta_two) * grad * grad
    fix_one = 1.0 / (1.0 - beta_one**STEP)
    fix_two = 1.0 / (1.0 - beta_two**STEP)
    move = first * fix_one / (jnp.sqrt(second * fix_two) + adam_eps)
    return (weight - rate * (move + decay * weight), first, second)


def pack_columns(master, table, first_slot, slots):
    _, rows, columns = master.shape
    width = columns // 8

    def kernel(table_ref, in_ref, out_ref):
        slot = pl.program_id(0)
        for rank in range(8):
            start = pl.multiple_of(table_ref[slot * 8 + rank] * width, width)
            out_ref[rank, 0] = in_ref[0, :, pl.ds(start, width)].astype(bf16)

    return pl.pallas_call(
        kernel,
        out_shape=jax.ShapeDtypeStruct((8, slots, rows, width), bf16),
        grid_spec=pltpu.PrefetchScalarGridSpec(
            num_scalar_prefetch=1,
            grid=(slots,),
            in_specs=[pl.BlockSpec((1, rows, columns), lambda k, t: (first_slot + k, 0, 0))],
            out_specs=pl.BlockSpec((8, 1, rows, width), lambda k, t: (0, k, 0, 0)),
        ),
        compiler_params=pltpu.CompilerParams(vmem_limit_bytes=VMEM_LIMIT),
        name="pack_columns",
    )(table, master)


def pick_blocks(sources, which, index, count):
    _, rows, width = sources[0].shape
    n_src = len(sources)

    def kernel(which_ref, index_ref, *refs):
        place = pl.program_id(0) * 2 + pl.program_id(1)
        out_ref = refs[n_src]
        for number in range(n_src):

            @pl.when(which_ref[place] == number)
            def _():
                out_ref[...] = refs[number][0]

    def spec(number):
        def at(n, half, which, index):
            place = n * 2 + half
            return (jnp.where(which[place] == number, index[place], 0), 0, 0)

        return pl.BlockSpec((1, rows, width), at)

    return pl.pallas_call(
        kernel,
        out_shape=jax.ShapeDtypeStruct((2 * rows, count * width), bf16),
        grid_spec=pltpu.PrefetchScalarGridSpec(
            num_scalar_prefetch=2,
            grid=(count, 2),
            in_specs=[spec(number) for number in range(n_src)],
            out_specs=pl.BlockSpec((rows, width), lambda n, half, which, index: (half, n)),
        ),
        compiler_params=pltpu.CompilerParams(vmem_limit_bytes=VMEM_LIMIT),
        name="pick_blocks",
    )(which, index, *sources)


def pack_gradients(groups, which, column, rows, width, slots):
    n_src = len(groups)

    def kernel(which_ref, column_ref, *refs):
        rank = pl.program_id(0)
        out_ref = refs[n_src]
        for k in range(slots):
            start = pl.multiple_of(column_ref[rank * slots + k] * width, width)
            for number in range(n_src):

                @pl.when(which_ref[rank * slots + k] == number)
                def _():
                    out_ref[0, k] = refs[number][:, pl.ds(start, width)]

    return pl.pallas_call(
        kernel,
        out_shape=jax.ShapeDtypeStruct((8, slots, rows, width), bf16),
        grid_spec=pltpu.PrefetchScalarGridSpec(
            num_scalar_prefetch=2,
            grid=(8,),
            in_specs=[
                pl.BlockSpec((rows, group.shape[1]), lambda rank, which, column: (rank // 4, 0)) for group in groups
            ],
            out_specs=pl.BlockSpec((1, slots, rows, width), lambda rank, which, column: (rank, 0, 0, 0)),
        ),
        compiler_params=pltpu.CompilerParams(vmem_limit_bytes=VMEM_LIMIT),
        name="pack_gradients",
    )(which, column, *groups)


def adam_tiles(master, one, two, columns_from, rows_from, visit, mode, column_place, row_place, hold, previous=None):
    _, rows, columns = master.shape
    width = columns // 8
    n_visit = visit.shape[0]
    n_col, n_row = len(columns_from), len(rows_from)
    kept = () if previous is None else tuple(previous)

    def kernel(visit_ref, mode_ref, cp_ref, rp_ref, hold_ref, *refs):
        w_ref, m_ref, v_ref = refs[:3]
        grads = refs[3 : 3 + n_col + n_row]
        outs = refs[3 + n_col + n_row + len(kept) :]
        how = mode_ref[pl.program_id(0)]

        @pl.when(how == 1)
        def _():
            for ref in outs:
                ref[...] = jnp.zeros_like(ref)

        for number, grad_ref in enumerate(grads):

            @pl.when(how == number + 2)
            def _():
                grad = grad_ref[0].astype(f32)
                results = adam_update(w_ref[0], m_ref[0], v_ref[0], grad, rate_matrix, decay_rate)
                for ref, value in zip(outs, results, strict=True):
                    ref[0] = value

    def block_of(n, b, hold):
        return jnp.where(hold[n] == 1, 7, b)

    state = pl.BlockSpec((1, rows, width), lambda n, b, vi, mo, cp, rp, ho: (vi[n], 0, block_of(n, b, ho)))

    def column_spec(number):
        def at(n, b, vi, mo, cp, rp, ho):
            return (jnp.where(mo[n] == number + 2, cp[n * 8 + block_of(n, b, ho)], 0), 0, 0)

        return pl.BlockSpec((1, rows, width), at)

    def row_spec(number):
        def at(n, b, vi, mo, cp, rp, ho):
            taken = mo[n] == number + 2
            return (jnp.where(taken, rp[n], 0), 0, jnp.where(taken, block_of(n, b, ho), 0))

        return pl.BlockSpec((1, rows, width), at)

    shape = jax.ShapeDtypeStruct(master.shape, f32)
    n_before = 5 + 3 + n_col + n_row
    return pl.pallas_call(
        kernel,
        out_shape=(shape, shape, shape),
        grid_spec=pltpu.PrefetchScalarGridSpec(
            num_scalar_prefetch=5,
            grid=(n_visit, 8),
            in_specs=[
                state,
                state,
                state,
                *(column_spec(number) for number in range(n_col)),
                *(row_spec(n_col + number) for number in range(n_row)),
                *(pl.BlockSpec(memory_space=pl.ANY) for _ in kept),
            ],
            out_specs=(state, state, state),
        ),
        input_output_aliases={n_before + n: n for n in range(len(kept))},
        compiler_params=pltpu.CompilerParams(vmem_limit_bytes=VMEM_LIMIT),
        cost_estimate=pl.CostEstimate(
            flops=30 * n_visit * rows * columns, bytes_accessed=26 * n_visit * rows * columns, transcendentals=0
        ),
        name="adam_tiles",
    )(visit, mode, column_place, row_place, hold, master, one, two, *columns_from, *rows_from, *kept)


def after(value, *others):
    return lax.optimization_barrier((value, *others))[0]


def swap(value, axis):
    return lax.ppermute(value, axis, [(0, 1), (1, 0)])


def gather_rows(value):
    half = value.shape[0] // 2
    over_x = swap(value, "x")
    over_y = swap(value, "y")
    far_low = swap(over_y[:half], "x")
    far_high = swap(over_x[half:], "y")
    four = jnp.concatenate([value, over_y, over_x, far_low, far_high], axis=0)
    return jnp.concatenate([four, swap(four, "c")], axis=0)


def scatter_rows(part):
    rows, width = part.shape[0] // 8, part.shape[1]
    half = width // 2
    part = part.reshape(2, 2, 2, rows, width)
    chip = part[0] + swap(part[1], "c")
    low, high = chip[..., :half], chip[..., half:]
    low_two = low[:, 0] + swap(low[:, 1].astype(bf16), "y").astype(f32)
    high_two = high[0] + swap(high[1].astype(bf16), "x").astype(f32)
    low_one = low_two[0] + swap(low_two[1].astype(bf16), "x").astype(f32)
    high_one = high_two[0] + swap(high_two[1].astype(bf16), "y").astype(f32)
    return jnp.concatenate([low_one, high_one], axis=1)


def sum_everywhere(value):
    for axis in ("c", "y", "x"):
        value = value + swap(value, axis)
    for step in (1, 2):
        value = value + lax.ppermute(value, "z", [(z, z ^ step) for z in range(4)])
    return value


def flip_pairs(mask, keep=None):
    pairs = []
    for z in range(4):
        for place in range(8):
            target = place ^ mask
            if keep is None or keep(z, place, target):
                pairs.append((z * 8 + place, z * 8 + target))
    return pairs


ALL_AXES = ("z", "x", "y", "c")
PLANE = ("x", "y", "c")


def plane_body(
    tokens, cotangent, context, lengths, keep, owners, master, moment_one, moment_two, gains, gain_one, gain_two
):
    cap, rows, _ = master.shape
    count, width = tokens.shape
    heads_here = HEADS // 8
    head_dim = width // HEADS
    scale = head_dim ** (-0.5)
    block = width // 8
    z = lax.axis_index("z")
    x = lax.axis_index("x")
    f = lax.axis_index("y") * 2 + lax.axis_index("c")

    n_tiles = owners.shape[0]
    rank = ranks_of(owners)
    shift_of = np.array(SHIFT, np.int32)
    row_of = np.array([t in ROW_TILES for t in range(n_tiles)])
    all_slots = jnp.arange(4 * cap).reshape(4, cap)
    holds = (owners * cap + rank)[None, None, :] == all_slots[:, :, None]
    used_at = jnp.any(holds, axis=2)
    tile_at = jnp.sum(jnp.where(holds, np.arange(n_tiles, dtype=np.int32), 0), axis=2)
    shift_at = jnp.sum(jnp.where(holds, shift_of, 0), axis=2)
    row_at = jnp.any(holds & row_of, axis=2)
    mine = (jnp.arange(4) == f)[:, None]

    def my(value):
        return jnp.sum(jnp.where(mine, value.astype(jnp.int32), 0), axis=0)

    my_used, my_tile, my_shift, my_row = my(used_at), my(tile_at), my(shift_at), my(row_at)

    to_x = np.arange(8) // 4
    to_f = np.arange(8) % 4
    column_table = 2 * ((to_f[None, :] + my_shift[:, None]) % 4) + to_x[None, :]
    half_cap = cap // 2
    place = np.arange(4)

    def of_tiles(tiles, values):
        chosen = tiles[:, None] == np.arange(n_tiles)[None, :]
        return jnp.sum(jnp.where(chosen, values[None, :], 0), axis=1)

    column_tiles = jnp.concatenate([np.array([0, 1, 2, 4, 5, 7, 6, 8], np.int32), 10 + (place - f) % 4])
    column_part = jnp.repeat(of_tiles(column_tiles, rank // half_cap), 2)
    column_place = of_tiles(column_tiles, owners * half_cap + rank % half_cap)
    column_place = (column_place[:, None] + np.array([0, 4 * half_cap])[None, :]).reshape(-1)
    other_f = f ^ place
    outer_tiles = jnp.where(other_f == z, 3, 9)
    out_tiles = 14 + (z - other_f) % 4
    row_slots = of_tiles(jnp.concatenate([outer_tiles, out_tiles]), rank)
    row_owners = of_tiles(jnp.stack([outer_tiles[0], outer_tiles[2], out_tiles[0], out_tiles[2]]), owners)

    def pack_first(weights):
        return pack_columns(weights, column_table[:half_cap].reshape(-1), 0, half_cap)

    def pack_second(weights):
        return pack_columns(weights, column_table[half_cap:].reshape(-1), half_cap, half_cap)

    def my_block(slot):
        return lax.dynamic_index_in_dim(master, slot, 0, keepdims=False).astype(bf16)

    present = owners[0] >= 0

    def chain_step(move, *values):
        shapes = jax.eval_shape(move, *values)
        idle = jax.tree.map(lambda leaf: jnp.zeros(leaf.shape, leaf.dtype), shapes)
        return lax.cond(present, move, lambda *_: idle, *values)

    h0 = tokens.astype(f32)
    outer_blocks = [my_block(row_slots[mask]) for mask in range(4)]
    out_blocks = [my_block(row_slots[4 + mask]) for mask in range(4)]
    a_in = normalize(h0, gains[0]).astype(bf16)
    sent = pack_first(after(master, column_part, column_place, row_slots, row_owners))
    received = [lax.all_to_all(sent, PLANE, 0, 0, tiled=True).reshape(8 * half_cap, rows, block)]
    seg = segments(lengths[0], count)
    live = keep == 1
    code = seg * 2 + live.astype(jnp.int32)

    def spread_code(code):
        for axis in ("y", "x", "c"):
            code = jnp.concatenate([code, swap(code, axis)])
        return code

    code = chain_step(spread_code, after(code, a_in, *outer_blocks, *out_blocks))
    seg_all = (code // 2).reshape(8, count)
    live_all = (code % 2 == 1).reshape(8, count)
    grad_out = cotangent.astype(f32) * live.astype(f32)[:, None]
    received = [after(received[0], a_in, code, *outer_blocks, *out_blocks)]

    def columns_here(first, count, parts):
        chosen = slice(2 * first, 2 * (first + count))
        return pick_blocks(received[:parts], column_part[chosen], column_place[chosen], count)

    def gather_z(value):
        return lax.all_gather(value, "z", axis=0, tiled=True)

    local = columns_here(0, 3, 1)
    w_qkv = gather_z(local)
    a_all = gather_rows(after(a_in, local))
    d_ff = gather_rows(after(grad_out.astype(bf16), local))
    def meet_on_chip(kind, blocks):
        here, there = row_owners[2 * kind], row_owners[2 * kind + 1]
        core = f % 2
        from_core = swap(jnp.stack([blocks[1], blocks[3]]), "c")
        mine = jnp.where(here % 2 == core, blocks[0], from_core[0])
        return mine, jnp.where(there % 2 == core, blocks[2], from_core[1])

    def mine_or_over_y(kind, mine, over_y):
        return jnp.where(row_owners[2 * kind] // 2 == f // 2, mine, over_y)

    out_mine, out_across = meet_on_chip(1, [after(value, local) for value in out_blocks])
    sent = pack_second(after(master, a_all, d_ff, out_across))
    received.append(lax.all_to_all(sent, PLANE, 0, 0, tiled=True).reshape(8 * half_cap, rows, block))

    def needs_outer(zz, place, target):
        return target % 4 in (zz, (zz + 2) % 4)

    outer_mine, across = meet_on_chip(0, [after(value, local) for value in outer_blocks])
    outer = mine_or_over_y(0, outer_mine, lax.ppermute(across, ALL_AXES, flip_pairs(2, needs_outer)))
    half_rows = rows // 2
    odd = z % 2
    to_pair = lax.dynamic_slice_in_dim(after(outer, sent), (1 - odd) * half_rows, half_rows, 0)
    own_half = lax.dynamic_slice_in_dim(outer, odd * half_rows, half_rows, 0)
    pair_swap = [
        (zz * 8 + place, (zz ^ 1) * 8 + place)
        for zz in range(4)
        for place in range(8)
        if place % 4 in (zz, (zz + 2) % 4)
    ]
    from_pair = lax.ppermute(to_pair, ALL_AXES, pair_swap)
    has_outer = (f == z) | (f == (z + 2) % 4)
    outer_all = lax.all_gather(jnp.where(has_outer, own_half, from_pair), "z", axis=0, tiled=True)
    low_y = lax.axis_index("y") == 0
    w_self_out = jnp.where(low_y, outer_all[:rows], outer_all[rows:])
    w_cross_out = jnp.where(low_y, outer_all[rows:], outer_all[:rows])

    def split(value):
        return value.reshape(8, -1, heads_here, head_dim)

    qkv = matmul(a_all, w_qkv)
    qkv = qkv.astype(bf16)
    query, keys, values = (split(qkv[:, n * block : (n + 1) * block]) for n in range(3))
    places = jnp.arange(count)
    allowed = (seg_all[:, :, None] == seg_all[:, None, :]) & (
        live_all[:, None, :] | (places[:, None] == places[None, :])
    )

    def probabilities(left, right, mask):
        scores = jnp.einsum("bqhd,bkhd->bhqk", left, right, preferred_element_type=f32) * scale
        scores = jnp.where(mask[:, None], scores, -1e30)
        expo = jnp.exp(scores - jnp.max(scores, axis=-1, keepdims=True))
        return expo / jnp.sum(expo, axis=-1, keepdims=True)

    def weighted(probs, right):
        return jnp.einsum("bhqk,bkhd->bqhd", probs, right, preferred_element_type=f32)

    def joined(value):
        return value.astype(bf16).reshape(-1, block)

    probs = probabilities(query, keys, allowed)
    probs_low = probs.astype(bf16)
    mixed = weighted(probs_low, values).astype(bf16)
    attended = mixed.reshape(-1, block)
    received[1] = after(received[1], mixed)
    local_cross, local_in = columns_here(3, 5, 2), columns_here(8, 4, 2)
    w_cross = gather_z(local_cross)
    w_in = gather_z(local_in)

    slots, ctx_len, ctx_width = context.shape
    ctx = after(context.reshape(slots * ctx_len, ctx_width), local_cross, local_in)
    ctx_x, ctx_y = swap(ctx, "x"), swap(ctx, "y")
    h1, over_y = chain_step(
        lambda one, two: (scatter_rows(one), swap(two, "y")), matmul(after(attended, local_in), w_self_out), out_across
    )
    h1 = h0 + h1
    w_out = gather_z(mine_or_over_y(1, out_mine, over_y))

    def second_step(one, own, over_x, over_y):
        half = over_x.shape[0] // 2
        far_low, far_high = swap(over_y[:half], "x"), swap(over_x[half:], "y")
        four = jnp.concatenate([own, over_y, over_x, far_low, far_high], axis=0)
        return gather_rows(one), four, swap(four, "c")

    b_all, ctx_here, ctx_there = chain_step(
        second_step, normalize(h1, gains[1]).astype(bf16), ctx, ctx_x, ctx_y
    )

    w_cross_q = w_cross[:, :block]
    w_low = w_cross[:, block : 3 * block]
    w_high = w_cross[:, 3 * block :]
    ctx_kv = jnp.concatenate(
        [
            (matmul(part[:, :width], w_low) + matmul(part[:, width:], w_high)).astype(bf16)
            for part in (ctx_here, ctx_there)
        ],
        axis=0,
    )
    cross_q = matmul(b_all, w_cross_q)
    cross_q = split(cross_q.astype(bf16))
    cross_k, cross_v = split(ctx_kv[:, :block]), split(ctx_kv[:, block:])
    item = jnp.arange(slots * ctx_len) // ctx_len
    own_item = seg_all[:, :, None] == item[None, None, :]
    cross_p = probabilities(cross_q, cross_k, own_item)
    cross_low = cross_p.astype(bf16)
    cross_o = joined(weighted(cross_low, cross_v))
    h2, ctx_all = chain_step(
        lambda one, *pieces: (scatter_rows(one), jnp.concatenate(pieces, axis=0)),
        matmul(cross_o, w_cross_out),
        ctx_here,
        ctx_there,
    )
    ctx_low, ctx_high = ctx_all[:, :width], ctx_all[:, width:]
    h2 = h1 + h2
    c_all = chain_step(gather_rows, normalize(h2, gains[2]).astype(bf16))

    hidden = matmul(c_all, w_in)
    activated = gelu_tanh(hidden).astype(bf16)

    def sum_rows(value):
        value = with_layout_constraint(value, Layout(major_to_minor=(0, 1)))
        value = lax.psum_scatter(value, "z", scatter_dimension=0, tiled=True)
        return with_layout_constraint(value, Layout(major_to_minor=(0, 1)))

    def from_y(value, keep_pair=None):
        return jnp.stack([value, lax.ppermute(value, ALL_AXES, flip_pairs(2, keep_pair))])

    def with_core(pair):
        return jnp.concatenate([pair, swap(pair, "c")])

    t_out = matmul_left(activated, d_ff).astype(bf16)
    g_out = sum_rows(t_out)
    d_act = matmul_right(after(d_ff, t_out), w_out)
    d_hidden = jax.vjp(gelu_tanh, hidden)[1](d_act)[0].astype(bf16)
    t_in = matmul_left(c_all, d_hidden).astype(bf16)
    g_in = sum_rows(t_in)
    d_c, out_sum = chain_step(
        lambda one, two: (scatter_rows(one), scatter_rows(two)), matmul_right(d_hidden, w_in), matmul(activated, w_out)
    )
    layer_out = (h2 + out_sum).astype(bf16)
    part_two, gain_grad_two = jax.vjp(normalize, h2, gains[2])[1](d_c)
    dh2 = grad_out + part_two
    d_cross_out = chain_step(gather_rows, after(dh2.astype(bf16), t_in))
    g_cross_out = matmul_left(cross_o, d_cross_out)

    def through(d_mixed, left, right, probs, probs_low, values):
        d_mixed = split(d_mixed.astype(bf16))
        d_probs = jnp.einsum("bqhd,bkhd->bhqk", d_mixed, values, preferred_element_type=f32)
        d_scores = (probs * (d_probs - jnp.sum(probs * d_probs, axis=-1, keepdims=True))).astype(bf16)
        d_left = joined(weighted(d_scores, right) * scale)
        d_right = joined(jnp.einsum("bhqk,bqhd->bkhd", d_scores, left, preferred_element_type=f32) * scale)
        d_values = joined(jnp.einsum("bhqk,bqhd->bkhd", probs_low, d_mixed, preferred_element_type=f32))
        return d_left, d_right, d_values

    (d_cq, d_ck, d_cv), out_grads = chain_step(
        lambda one, two: (
            through(matmul_right(one, w_cross_out), cross_q, cross_k, cross_p, cross_low, cross_v),
            from_y(two),
        ),
        d_cross_out,
        g_out,
    )
    d_ckv = jnp.concatenate([d_ck, d_cv], axis=1)
    t_cross = jnp.concatenate(
        [
            value.astype(bf16)
            for value in (matmul_left(b_all, d_cq), matmul_left(ctx_low, d_ckv), matmul_left(ctx_high, d_ckv))
        ],
        axis=1,
    )
    g_cross = sum_rows(t_cross)
    part = matmul_right(d_cq, w_cross_q)
    d_b = chain_step(scatter_rows, part)
    part_one, gain_grad_one = jax.vjp(normalize, h1, gains[1])[1](d_b)
    dh1 = dh2 + part_one
    d_self_out = chain_step(gather_rows, after(dh1.astype(bf16), t_cross, g_in))
    g_self_out = matmul_left(attended, d_self_out)
    t_outer = jnp.concatenate(
        [
            jnp.where(low_y, g_self_out, g_cross_out).astype(bf16),
            jnp.where(low_y, g_cross_out, g_self_out).astype(bf16),
        ],
        axis=0,
    )
    g_outer = sum_rows(after(t_outer, g_cross))
    d_mixed = matmul_right(after(d_self_out, t_outer), w_self_out)
    d_q, d_k, d_v = through(d_mixed, query, keys, probs, probs_low, values)
    d_qkv = jnp.concatenate([d_q, d_k, d_v], axis=1)
    t_qkv = matmul_left(a_all, d_qkv).astype(bf16)
    g_qkv = sum_rows(t_qkv)
    group_of = np.array([0, 0, 0, 0, 0, 0, 0, 0, 0, 0, 1, 1, 1, 1, 0, 0, 0, 0], np.int32)
    column_of = np.array([0, 0, 0, 0, 0, 1, 3, 2, 4, 0, 0, 1, 2, 3, 0, 0, 0, 0], np.int32)
    group_at = jnp.sum(jnp.where(holds, group_of, 0), axis=2)
    column_at = jnp.sum(jnp.where(holds, column_of, 0), axis=2)
    column_at = jnp.where(group_at == 1, (column_at + f) % 4, column_at)
    sent = pack_gradients(
        [after(g_cross, t_qkv), g_in], jnp.tile(group_at.reshape(-1), 2), jnp.tile(column_at.reshape(-1), 2), rows, block, cap
    )
    early_grads = lax.all_to_all(sent, PLANE, 0, 0, tiled=True).reshape(8 * cap, rows, block)

    def last_step(part, out_pair, gain_grad_one, gain_grad_two):
        part_zero, gain_grad_zero = jax.vjp(normalize, h0, gains[0])[1](scatter_rows(part))
        gain_grads = jnp.stack([gain_grad_zero, gain_grad_one, gain_grad_two])
        return part_zero, sum_everywhere(gain_grads), with_core(out_pair)

    part_zero, gain_total, out_grads = chain_step(
        last_step, matmul_right(after(d_qkv, sent), w_qkv), out_grads, gain_grad_one, gain_grad_two
    )
    grad_tokens = (dh1 + part_zero).astype(bf16)

    by_tile = jnp.swapaxes(after(g_qkv, out_grads).reshape(2, rows, 3, block), 1, 2)
    sent = jnp.broadcast_to(by_tile[:, None], (2, 4, 3, rows, block)).reshape(8, 3, rows, block)
    late_grads = lax.all_to_all(sent, PLANE, 0, 0, tiled=True).reshape(8 * 3, rows, block)
    back_swap = [(target, source) for source, target in pair_swap]
    place = np.arange(8)
    source_x, source_f = (place % 2)[None, :], ((place // 2)[None, :] - my_shift[:, None]) % 4
    slot = np.arange(cap, dtype=np.int32)
    column_place = (source_x * 4 + source_f) * cap + slot[:, None]
    other_row = ((z - my_shift) % 4) ^ f
    row_source = (other_row % 2) * 2 + other_row // 2
    late = (my_used == 1) & ((my_tile < 4) | (my_tile == 9))
    early_mode = jnp.where(my_used == 0, 1, jnp.where(late, 0, jnp.where(my_row == 1, 3, 2)))
    states = (master, moment_one, moment_two)

    def early_step(early_grads, out_grads, half):
        other_half = lax.ppermute(half, ALL_AXES, back_swap)
        in_order = jnp.where(odd == 0, jnp.stack([half, other_half]), jnp.stack([other_half, half]))
        in_order = in_order.reshape(rows, width)
        counts = jnp.where(f % 2 == z % 2, in_order, swap(in_order, "c"))
        early = None
        for first in (0, half_cap):
            chosen = slice(first, first + half_cap)
            early = adam_tiles(
                *states,
                [early_grads],
                [out_grads],
                slot[chosen],
                early_mode[chosen],
                column_place[chosen].reshape(-1),
                row_source[chosen],
                np.zeros(half_cap, np.int32),
                early,
            )
        return *early, from_y(counts)

    *early, outer_grads = chain_step(early_step, early_grads, out_grads, g_outer)

    n_late = 5
    order = jnp.sum(jnp.where(slot[None, :] < slot[:, None], late.astype(jnp.int32)[None, :], 0), axis=1)
    count_late = jnp.sum(late.astype(jnp.int32))
    step = np.arange(n_late)
    wanted = jnp.minimum(step, jnp.maximum(count_late - 1, 0))
    here = late[None, :] & (order[None, :] == wanted[:, None])

    def at_step(value):
        return jnp.sum(jnp.where(here, value.astype(jnp.int32)[None, :], 0), axis=1)

    hold = (step >= jnp.maximum(count_late, 1)).astype(jnp.int32)
    tile = at_step(my_tile)
    some = count_late > 0
    visit = jnp.where(some, at_step(slot), 0)
    first_mode = jnp.where(early_mode[0] == 3, 4, early_mode[0])
    late_mode = jnp.where(at_step(my_row) == 1, 5, 3)
    mode = jnp.where(hold == 1, 0, jnp.where(some, late_mode, first_mode))
    late_place = ((place % 2)[None, :] * 4 + (place // 2)[None, :]) * 3 + tile[:, None]
    late_place = jnp.where(some, late_place, column_place[:1])
    new_w, new_m, new_v = adam_tiles(
        *states,
        [early_grads, late_grads],
        [out_grads, outer_grads],
        visit,
        mode,
        late_place.reshape(-1),
        jnp.where(some, at_step(other_row // 2), row_source[0]),
        hold,
        early,
    )
    new_g, new_gm, new_gv = adam_update(gains, gain_one, gain_two, gain_total, rate_gain, 0.0)
    return (layer_out, grad_tokens, new_w, new_m, new_v, new_g, new_gm, new_gv)


def whole_body(
    tokens, cotangent, context, lengths, keep, owners, master, moment_one, moment_two, gains, gain_one, gain_two
):
    cap = master.shape[0]
    n_tiles = owners.shape[0]
    slot_of = owners * cap + ranks_of(owners)
    owner_rows = lax.all_gather(master.astype(bf16), "fsdp", axis=0, tiled=True)
    tiles = [
        lax.all_gather(
            lax.dynamic_index_in_dim(owner_rows, slot_of[tile], 0, keepdims=False), "dp", axis=0, tiled=True
        )
        for tile in range(n_tiles)
    ]
    w_in = jnp.concatenate(tiles[10:14], axis=1)
    w_out = jnp.concatenate(tiles[14:18], axis=0)
    count, width = tokens.shape
    head_dim = width // HEADS
    scale = head_dim ** (-0.5)
    seg = segments(lengths[0], count)
    live = keep == 1
    places = jnp.arange(count)

    def split(value):
        return value.astype(bf16).reshape(-1, HEADS, head_dim)

    def joined(value):
        return value.astype(bf16).reshape(-1, width)

    def probabilities(left, right, mask):
        scores = jnp.einsum("qhd,khd->hqk", left, right, preferred_element_type=f32) * scale
        scores = jnp.where(mask[None], scores, -1e30)
        expo = jnp.exp(scores - jnp.max(scores, axis=-1, keepdims=True))
        return expo / jnp.sum(expo, axis=-1, keepdims=True)

    def weighted(probs, right):
        return jnp.einsum("hqk,khd->qhd", probs, right, preferred_element_type=f32)

    def through(weights, d_out, left, right, probs, values):
        d_mixed = split(matmul_right(d_out, weights))
        d_probs = jnp.einsum("qhd,khd->hqk", d_mixed, values, preferred_element_type=f32)
        d_scores = (probs * (d_probs - jnp.sum(probs * d_probs, axis=-1, keepdims=True))).astype(bf16)
        d_left = joined(weighted(d_scores, right) * scale)
        d_right = joined(jnp.einsum("hqk,qhd->khd", d_scores, left, preferred_element_type=f32) * scale)
        d_values = joined(jnp.einsum("hqk,qhd->khd", probs.astype(bf16), d_mixed, preferred_element_type=f32))
        return d_left, d_right, d_values

    h0 = tokens.astype(f32)
    a_in = normalize(h0, gains[0]).astype(bf16)
    query, keys, values = (split(matmul(a_in, tiles[n])) for n in range(3))
    allowed = (seg[:, None] == seg[None, :]) & (live[None, :] | (places[:, None] == places[None, :]))
    probs = probabilities(query, keys, allowed)
    attended = joined(weighted(probs.astype(bf16), values))
    h1 = h0 + matmul(attended, tiles[3])
    b_in = normalize(h1, gains[1]).astype(bf16)
    slots, ctx_len, ctx_width = context.shape
    ctx = context.reshape(slots * ctx_len, ctx_width)
    ctx_low, ctx_high = ctx[:, :width], ctx[:, width:]
    cross_q = split(matmul(b_in, tiles[4]))
    cross_k = split(matmul(ctx_low, tiles[5]) + matmul(ctx_high, tiles[6]))
    cross_v = split(matmul(ctx_low, tiles[7]) + matmul(ctx_high, tiles[8]))
    item = jnp.arange(slots * ctx_len) // ctx_len
    cross_p = probabilities(cross_q, cross_k, seg[:, None] == item[None, :])
    cross_o = joined(weighted(cross_p.astype(bf16), cross_v))
    h2 = h1 + matmul(cross_o, tiles[9])
    c_in = normalize(h2, gains[2]).astype(bf16)
    hidden = matmul(c_in, w_in)
    activated = gelu_tanh(hidden).astype(bf16)
    layer_out = (h2 + matmul(activated, w_out)).astype(bf16)
    grad_out = cotangent.astype(f32) * live.astype(f32)[:, None]
    d_ff = grad_out.astype(bf16)
    d_hidden = jax.vjp(gelu_tanh, hidden)[1](matmul_right(d_ff, w_out))[0].astype(bf16)
    part_two, gain_grad_two = jax.vjp(normalize, h2, gains[2])[1](matmul_right(d_hidden, w_in))
    dh2 = grad_out + part_two
    d_cross_out = dh2.astype(bf16)
    d_cq, d_ck, d_cv = through(tiles[9], d_cross_out, cross_q, cross_k, cross_p, cross_v)
    part_one, gain_grad_one = jax.vjp(normalize, h1, gains[1])[1](matmul_right(d_cq, tiles[4]))
    dh1 = dh2 + part_one
    d_self_out = dh1.astype(bf16)
    d_q, d_k, d_v = through(tiles[3], d_self_out, query, keys, probs, values)
    d_a = matmul_right(d_q, tiles[0]) + matmul_right(d_k, tiles[1]) + matmul_right(d_v, tiles[2])
    part_zero, gain_grad_zero = jax.vjp(normalize, h0, gains[0])[1](d_a)
    grad_tokens = (dh1 + part_zero).astype(bf16)
    pairs = [
        (a_in, d_q),
        (a_in, d_k),
        (a_in, d_v),
        (attended, d_self_out),
        (b_in, d_cq),
        (ctx_low, d_ck),
        (ctx_high, d_ck),
        (ctx_low, d_cv),
        (ctx_high, d_cv),
        (cross_o, d_cross_out),
    ]
    for part in range(4):
        pairs.append((c_in, d_hidden[:, part * width : (part + 1) * width]))
    for part in range(4):
        pairs.append((activated[:, part * width : (part + 1) * width], d_ff))
    total_slots = lax.axis_size("fsdp") * cap
    placed = jnp.zeros((total_slots,) + master.shape[1:], bf16)
    for tile, (left, right) in enumerate(pairs):
        term = lax.psum_scatter(
            matmul_left(left, right).astype(bf16), "dp", scatter_dimension=0, tiled=True
        )
        placed = lax.dynamic_update_index_in_dim(placed, term, slot_of[tile], 0)
    owned = lax.psum_scatter(placed, "fsdp", scatter_dimension=0, tiled=True).astype(f32)
    my_slots = lax.axis_index("fsdp") * cap + jnp.arange(cap)
    used = jnp.any(slot_of[None, :] == my_slots[:, None], axis=1)[:, None, None]
    updated = adam_update(master, moment_one, moment_two, owned, rate_matrix, decay_rate)
    new_w, new_m, new_v = (jnp.where(used, value, 0.0) for value in updated)
    gain_grads = jnp.stack([gain_grad_zero, gain_grad_one, gain_grad_two])
    gain_total = lax.psum(gain_grads, ("dp", "fsdp"))
    new_g, new_gm, new_gv = adam_update(gains, gain_one, gain_two, gain_total, rate_gain, 0.0)
    return (layer_out, grad_tokens, new_w, new_m, new_v, new_g, new_gm, new_gv)


def solution(mesh):
    planes = mesh.shape["dp"] == 8 and mesh.shape["fsdp"] == 4
    if planes:
        used = Mesh(mesh.devices.reshape(4, 2, 2, 2), ALL_AXES)
        dp, fsdp, body = ("z", "x"), ("y", "c"), plane_body
    else:
        used, dp, fsdp, body = mesh, ("dp",), ("fsdp",), whole_body
    rows = P(dp + fsdp, None)
    tiles = P(fsdp, dp, None)
    return jax.shard_map(
        body,
        mesh=used,
        in_specs=(rows, rows, P(dp + fsdp, None, None), rows, P(dp + fsdp), P(), tiles, tiles, tiles, P(), P(), P()),
        out_specs=(rows, rows, tiles, tiles, tiles, P(), P(), P()),
        check_vma=False,
    )
```

```python
import jax
import jax.numpy as jnp
import numpy as np
from jax import lax
from jax.experimental import pallas as pl
from jax.experimental.layout import Layout, with_layout_constraint
from jax.experimental.pallas import tpu as pltpu
from jax.sharding import Mesh
from jax.sharding import PartitionSpec as P

HEADS = 16
STEP = 10

norm_eps = 1e-06
beta_one = 0.9
beta_two = 0.95
adam_eps = 1e-08
decay_rate = 0.1
rate_matrix = 0.1
rate_gain = 0.8

f32 = jnp.float32
bf16 = jnp.bfloat16

SHIFT = (0, 0, 0, 0, 2, 2, 2, 2, 2, 2, 0, 1, 2, 3, 0, 1, 2, 3)
ROW_TILES = (3, 9, 14, 15, 16, 17)
VMEM_LIMIT = 48 << 20


def normalize(h, gain):
    scale = lax.rsqrt(jnp.mean(h * h, axis=-1, keepdims=True) + norm_eps)
    return h * scale * gain


def gelu_tanh(u):
    return 0.5 * u * (1.0 + jnp.tanh(0.7978845608028654 * (u + 0.044715 * u * u * u)))


def matmul(left, right):
    return jnp.dot(left, right, preferred_element_type=f32)


def matmul_left(left, right):
    return lax.dot_general(left, right, (((0,), (0,)), ((), ())), preferred_element_type=f32)


def matmul_right(left, right):
    return lax.dot_general(left, right, (((1,), (1,)), ((), ())), preferred_element_type=f32)


def ranks_of(owners):
    order = jnp.arange(owners.shape[0])
    same = (owners[:, None] == owners[None, :]) & (order[None, :] < order[:, None])
    return jnp.sum(same.astype(jnp.int32), axis=1)


def segments(lengths, count):
    places = jnp.arange(count)
    end = jnp.zeros((), jnp.int32)
    seg = jnp.zeros((count,), jnp.int32)
    for item in range(lengths.shape[0]):
        end = end + lengths[item]
        seg = seg + (places >= end).astype(jnp.int32)
    return seg


def adam_update(weight, first, second, grad, rate, decay):
    first = beta_one * first + (1.0 - beta_one) * grad
    second = beta_two * second + (1.0 - beta_two) * grad * grad
    fix_one = 1.0 / (1.0 - beta_one**STEP)
    fix_two = 1.0 / (1.0 - beta_two**STEP)
    move = first * fix_one / (jnp.sqrt(second * fix_two) + adam_eps)
    return (weight - rate * (move + decay * weight), first, second)


def pack_columns(master, table, first_slot, slots):
    _, rows, columns = master.shape
    width = columns // 8

    def kernel(table_ref, in_ref, out_ref):
        slot = pl.program_id(0)
        for rank in range(8):
            start = pl.multiple_of(table_ref[slot * 8 + rank] * width, width)
            out_ref[rank, 0] = in_ref[0, :, pl.ds(start, width)].astype(bf16)

    return pl.pallas_call(
        kernel,
        out_shape=jax.ShapeDtypeStruct((8, slots, rows, width), bf16),
        grid_spec=pltpu.PrefetchScalarGridSpec(
            num_scalar_prefetch=1,
            grid=(slots,),
            in_specs=[pl.BlockSpec((1, rows, columns), lambda k, t: (first_slot + k, 0, 0))],
            out_specs=pl.BlockSpec((8, 1, rows, width), lambda k, t: (0, k, 0, 0)),
        ),
        compiler_params=pltpu.CompilerParams(vmem_limit_bytes=VMEM_LIMIT),
        name="pack_columns",
    )(table, master)


def pick_blocks(sources, which, index, count):
    _, rows, width = sources[0].shape
    n_src = len(sources)

    def kernel(which_ref, index_ref, *refs):
        place = pl.program_id(0) * 2 + pl.program_id(1)
        out_ref = refs[n_src]
        for number in range(n_src):

            @pl.when(which_ref[place] == number)
            def _():
                out_ref[...] = refs[number][0]

    def spec(number):
        def at(n, half, which, index):
            place = n * 2 + half
            return (jnp.where(which[place] == number, index[place], 0), 0, 0)

        return pl.BlockSpec((1, rows, width), at)

    return pl.pallas_call(
        kernel,
        out_shape=jax.ShapeDtypeStruct((2 * rows, count * width), bf16),
        grid_spec=pltpu.PrefetchScalarGridSpec(
            num_scalar_prefetch=2,
            grid=(count, 2),
            in_specs=[spec(number) for number in range(n_src)],
            out_specs=pl.BlockSpec((rows, width), lambda n, half, which, index: (half, n)),
        ),
        compiler_params=pltpu.CompilerParams(vmem_limit_bytes=VMEM_LIMIT),
        name="pick_blocks",
    )(which, index, *sources)


def pack_gradients(groups, which, column, rows, width, slots):
    n_src = len(groups)

    def kernel(which_ref, column_ref, *refs):
        rank = pl.program_id(0)
        out_ref = refs[n_src]
        for k in range(slots):
            start = pl.multiple_of(column_ref[rank * slots + k] * width, width)
            for number in range(n_src):

                @pl.when(which_ref[rank * slots + k] == number)
                def _():
                    out_ref[0, k] = refs[number][:, pl.ds(start, width)]

    return pl.pallas_call(
        kernel,
        out_shape=jax.ShapeDtypeStruct((8, slots, rows, width), bf16),
        grid_spec=pltpu.PrefetchScalarGridSpec(
            num_scalar_prefetch=2,
            grid=(8,),
            in_specs=[
                pl.BlockSpec((rows, group.shape[1]), lambda rank, which, column: (rank // 4, 0)) for group in groups
            ],
            out_specs=pl.BlockSpec((1, slots, rows, width), lambda rank, which, column: (rank, 0, 0, 0)),
        ),
        compiler_params=pltpu.CompilerParams(vmem_limit_bytes=VMEM_LIMIT),
        name="pack_gradients",
    )(which, column, *groups)


def adam_tiles(master, one, two, columns_from, rows_from, visit, mode, column_place, row_place, hold, previous=None):
    _, rows, columns = master.shape
    width = columns // 8
    n_visit = visit.shape[0]
    n_col, n_row = len(columns_from), len(rows_from)
    kept = () if previous is None else tuple(previous)

    def kernel(visit_ref, mode_ref, cp_ref, rp_ref, hold_ref, *refs):
        w_ref, m_ref, v_ref = refs[:3]
        grads = refs[3 : 3 + n_col + n_row]
        outs = refs[3 + n_col + n_row + len(kept) :]
        how = mode_ref[pl.program_id(0)]

        @pl.when(how == 1)
        def _():
            for ref in outs:
                ref[...] = jnp.zeros_like(ref)

        for number, grad_ref in enumerate(grads):

            @pl.when(how == number + 2)
            def _():
                grad = grad_ref[0].astype(f32)
                results = adam_update(w_ref[0], m_ref[0], v_ref[0], grad, rate_matrix, decay_rate)
                for ref, value in zip(outs, results, strict=True):
                    ref[0] = value

    def block_of(n, b, hold):
        return jnp.where(hold[n] == 1, 7, b)

    state = pl.BlockSpec((1, rows, width), lambda n, b, vi, mo, cp, rp, ho: (vi[n], 0, block_of(n, b, ho)))

    def column_spec(number):
        def at(n, b, vi, mo, cp, rp, ho):
            return (jnp.where(mo[n] == number + 2, cp[n * 8 + block_of(n, b, ho)], 0), 0, 0)

        return pl.BlockSpec((1, rows, width), at)

    def row_spec(number):
        def at(n, b, vi, mo, cp, rp, ho):
            taken = mo[n] == number + 2
            return (jnp.where(taken, rp[n], 0), 0, jnp.where(taken, block_of(n, b, ho), 0))

        return pl.BlockSpec((1, rows, width), at)

    shape = jax.ShapeDtypeStruct(master.shape, f32)
    n_before = 5 + 3 + n_col + n_row
    return pl.pallas_call(
        kernel,
        out_shape=(shape, shape, shape),
        grid_spec=pltpu.PrefetchScalarGridSpec(
            num_scalar_prefetch=5,
            grid=(n_visit, 8),
            in_specs=[
                state,
                state,
                state,
                *(column_spec(number) for number in range(n_col)),
                *(row_spec(n_col + number) for number in range(n_row)),
                *(pl.BlockSpec(memory_space=pl.ANY) for _ in kept),
            ],
            out_specs=(state, state, state),
        ),
        input_output_aliases={n_before + n: n for n in range(len(kept))},
        compiler_params=pltpu.CompilerParams(vmem_limit_bytes=VMEM_LIMIT),
        cost_estimate=pl.CostEstimate(
            flops=30 * n_visit * rows * columns, bytes_accessed=26 * n_visit * rows * columns, transcendentals=0
        ),
        name="adam_tiles",
    )(visit, mode, column_place, row_place, hold, master, one, two, *columns_from, *rows_from, *kept)


def after(value, *others):
    return lax.optimization_barrier((value, *others))[0]


def swap(value, axis):
    return lax.ppermute(value, axis, [(0, 1), (1, 0)])


def gather_rows(value):
    half = value.shape[0] // 2
    over_x = swap(value, "x")
    over_y = swap(value, "y")
    far_low = swap(over_y[:half], "x")
    far_high = swap(over_x[half:], "y")
    four = jnp.concatenate([value, over_y, over_x, far_low, far_high], axis=0)
    return jnp.concatenate([four, swap(four, "c")], axis=0)


def scatter_rows(part):
    rows, width = part.shape[0] // 8, part.shape[1]
    half = width // 2
    part = part.reshape(2, 2, 2, rows, width)
    chip = part[0] + swap(part[1], "c")
    low, high = chip[..., :half], chip[..., half:]
    low_two = low[:, 0] + swap(low[:, 1].astype(bf16), "y").astype(f32)
    high_two = high[0] + swap(high[1].astype(bf16), "x").astype(f32)
    low_one = low_two[0] + swap(low_two[1].astype(bf16), "x").astype(f32)
    high_one = high_two[0] + swap(high_two[1].astype(bf16), "y").astype(f32)
    return jnp.concatenate([low_one, high_one], axis=1)


def sum_everywhere(value):
    for axis in ("c", "y", "x"):
        value = value + swap(value, axis)
    for step in (1, 2):
        value = value + lax.ppermute(value, "z", [(z, z ^ step) for z in range(4)])
    return value


def flip_pairs(mask, keep=None):
    pairs = []
    for z in range(4):
        for place in range(8):
            target = place ^ mask
            if keep is None or keep(z, place, target):
                pairs.append((z * 8 + place, z * 8 + target))
    return pairs


ALL_AXES = ("z", "x", "y", "c")
PLANE = ("x", "y", "c")


def plane_body(
    tokens, cotangent, context, lengths, keep, owners, master, moment_one, moment_two, gains, gain_one, gain_two
):
    cap, rows, _ = master.shape
    count, width = tokens.shape
    heads_here = HEADS // 8
    head_dim = width // HEADS
    scale = head_dim ** (-0.5)
    block = width // 8
    z = lax.axis_index("z")
    x = lax.axis_index("x")
    f = lax.axis_index("y") * 2 + lax.axis_index("c")

    n_tiles = owners.shape[0]
    rank = ranks_of(owners)
    shift_of = np.array(SHIFT, np.int32)
    row_of = np.array([t in ROW_TILES for t in range(n_tiles)])
    all_slots = jnp.arange(4 * cap).reshape(4, cap)
    holds = (owners * cap + rank)[None, None, :] == all_slots[:, :, None]
    used_at = jnp.any(holds, axis=2)
    tile_at = jnp.sum(jnp.where(holds, np.arange(n_tiles, dtype=np.int32), 0), axis=2)
    shift_at = jnp.sum(jnp.where(holds, shift_of, 0), axis=2)
    row_at = jnp.any(holds & row_of, axis=2)
    mine = (jnp.arange(4) == f)[:, None]

    def my(value):
        return jnp.sum(jnp.where(mine, value.astype(jnp.int32), 0), axis=0)

    my_used, my_tile, my_shift, my_row = my(used_at), my(tile_at), my(shift_at), my(row_at)

    to_x = np.arange(8) // 4
    to_f = np.arange(8) % 4
    column_table = 2 * ((to_f[None, :] + my_shift[:, None]) % 4) + to_x[None, :]
    half_cap = cap // 2
    place = np.arange(4)

    def of_tiles(tiles, values):
        chosen = tiles[:, None] == np.arange(n_tiles)[None, :]
        return jnp.sum(jnp.where(chosen, values[None, :], 0), axis=1)

    column_tiles = jnp.concatenate([np.array([0, 1, 2, 4, 5, 7, 6, 8], np.int32), 10 + (place - f) % 4])
    column_part = jnp.repeat(of_tiles(column_tiles, rank // half_cap), 2)
    column_place = of_tiles(column_tiles, owners * half_cap + rank % half_cap)
    column_place = (column_place[:, None] + np.array([0, 4 * half_cap])[None, :]).reshape(-1)
    other_f = f ^ place
    outer_tiles = jnp.where(other_f == z, 3, 9)
    out_tiles = 14 + (z - other_f) % 4
    row_slots = of_tiles(jnp.concatenate([outer_tiles, out_tiles]), rank)
    row_owners = of_tiles(jnp.stack([outer_tiles[0], outer_tiles[2], out_tiles[0], out_tiles[2]]), owners)

    def pack_first(weights):
        return pack_columns(weights, column_table[:half_cap].reshape(-1), 0, half_cap)

    def pack_second(weights):
        return pack_columns(weights, column_table[half_cap:].reshape(-1), half_cap, half_cap)

    def my_block(slot):
        return lax.dynamic_index_in_dim(master, slot, 0, keepdims=False).astype(bf16)

    present = owners[0] >= 0

    def chain_step(move, *values):
        shapes = jax.eval_shape(move, *values)
        idle = jax.tree.map(lambda leaf: jnp.zeros(leaf.shape, leaf.dtype), shapes)
        return lax.cond(present, move, lambda *_: idle, *values)

    h0 = tokens.astype(f32)
    outer_blocks = [my_block(row_slots[mask]) for mask in range(4)]
    out_blocks = [my_block(row_slots[4 + mask]) for mask in range(4)]
    a_in = normalize(h0, gains[0]).astype(bf16)
    sent = pack_first(after(master, column_part, column_place, row_slots, row_owners))
    received = [lax.all_to_all(sent, PLANE, 0, 0, tiled=True).reshape(8 * half_cap, rows, block)]
    seg = segments(lengths[0], count)
    live = keep == 1
    code = seg * 2 + live.astype(jnp.int32)

    def spread_code(code):
        for axis in ("y", "x", "c"):
            code = jnp.concatenate([code, swap(code, axis)])
        return code

    code = chain_step(spread_code, after(code, a_in, *outer_blocks, *out_blocks))
    seg_all = (code // 2).reshape(8, count)
    live_all = (code % 2 == 1).reshape(8, count)
    grad_out = cotangent.astype(f32) * live.astype(f32)[:, None]
    received = [after(received[0], a_in, code, *outer_blocks, *out_blocks)]

    def columns_here(first, count, parts):
        chosen = slice(2 * first, 2 * (first + count))
        return pick_blocks(received[:parts], column_part[chosen], column_place[chosen], count)

    def gather_z(value):
        return lax.all_gather(value, "z", axis=0, tiled=True)

    local = columns_here(0, 3, 1)
    w_qkv = gather_z(local)
    a_all = gather_rows(after(a_in, local))
    d_ff = gather_rows(after(grad_out.astype(bf16), local))
    def meet_on_chip(kind, blocks):
        here, there = row_owners[2 * kind], row_owners[2 * kind + 1]
        core = f % 2
        from_core = swap(jnp.stack([blocks[1], blocks[3]]), "c")
        mine = jnp.where(here % 2 == core, blocks[0], from_core[0])
        return mine, jnp.where(there % 2 == core, blocks[2], from_core[1])

    def mine_or_over_y(kind, mine, over_y):
        return jnp.where(row_owners[2 * kind] // 2 == f // 2, mine, over_y)

    out_mine, out_across = meet_on_chip(1, [after(value, local) for value in out_blocks])
    sent = pack_second(after(master, a_all, d_ff, out_across))
    received.append(lax.all_to_all(sent, PLANE, 0, 0, tiled=True).reshape(8 * half_cap, rows, block))

    def needs_outer(zz, place, target):
        return target % 4 in (zz, (zz + 2) % 4)

    outer_mine, across = meet_on_chip(0, [after(value, local) for value in outer_blocks])
    outer = mine_or_over_y(0, outer_mine, lax.ppermute(across, ALL_AXES, flip_pairs(2, needs_outer)))
    half_rows = rows // 2
    odd = z % 2
    to_pair = lax.dynamic_slice_in_dim(after(outer, sent), (1 - odd) * half_rows, half_rows, 0)
    own_half = lax.dynamic_slice_in_dim(outer, odd * half_rows, half_rows, 0)
    pair_swap = [
        (zz * 8 + place, (zz ^ 1) * 8 + place)
        for zz in range(4)
        for place in range(8)
        if place % 4 in (zz, (zz + 2) % 4)
    ]
    from_pair = lax.ppermute(to_pair, ALL_AXES, pair_swap)
    has_outer = (f == z) | (f == (z + 2) % 4)
    outer_all = lax.all_gather(jnp.where(has_outer, own_half, from_pair), "z", axis=0, tiled=True)
    low_y = lax.axis_index("y") == 0
    w_self_out = jnp.where(low_y, outer_all[:rows], outer_all[rows:])
    w_cross_out = jnp.where(low_y, outer_all[rows:], outer_all[:rows])

    def split(value):
        return value.reshape(8, -1, heads_here, head_dim)

    qkv = matmul(a_all, w_qkv)
    qkv = qkv.astype(bf16)
    query, keys, values = (split(qkv[:, n * block : (n + 1) * block]) for n in range(3))
    places = jnp.arange(count)
    allowed = (seg_all[:, :, None] == seg_all[:, None, :]) & (
        live_all[:, None, :] | (places[:, None] == places[None, :])
    )

    def probabilities(left, right, mask):
        scores = jnp.einsum("bqhd,bkhd->bhqk", left, right, preferred_element_type=f32) * scale
        scores = jnp.where(mask[:, None], scores, -1e30)
        expo = jnp.exp(scores - jnp.max(scores, axis=-1, keepdims=True))
        return expo / jnp.sum(expo, axis=-1, keepdims=True)

    def weighted(probs, right):
        return jnp.einsum("bhqk,bkhd->bqhd", probs, right, preferred_element_type=f32)

    def joined(value):
        return value.astype(bf16).reshape(-1, block)

    probs = probabilities(query, keys, allowed)
    probs_low = probs.astype(bf16)
    mixed = weighted(probs_low, values).astype(bf16)
    attended = mixed.reshape(-1, block)
    received[1] = after(received[1], mixed)
    local_cross, local_in = columns_here(3, 5, 2), columns_here(8, 4, 2)
    w_cross = gather_z(local_cross)
    w_in = gather_z(local_in)

    slots, ctx_len, ctx_width = context.shape
    ctx = after(context.reshape(slots * ctx_len, ctx_width), local_cross, local_in)
    ctx_x, ctx_y = swap(ctx, "x"), swap(ctx, "y")
    h1 = h0 + chain_step(scatter_rows, matmul(after(attended, local_in), w_self_out))

    def second_step(one, own, over_x, over_y):
        half = over_x.shape[0] // 2
        far_low, far_high = swap(over_y[:half], "x"), swap(over_x[half:], "y")
        four = jnp.concatenate([own, over_y, over_x, far_low, far_high], axis=0)
        return gather_rows(one), four, swap(four, "c")

    b_all, ctx_here, ctx_there = chain_step(
        second_step, normalize(h1, gains[1]).astype(bf16), ctx, ctx_x, ctx_y
    )

    w_cross_q = w_cross[:, :block]

    def keys_step(here, there, weights, moved):
        w_low, w_high = weights[:, block : 3 * block], weights[:, 3 * block :]
        parts = [
            (matmul(part[:, :width], w_low) + matmul(part[:, width:], w_high)).astype(bf16) for part in (here, there)
        ]
        return jnp.concatenate(parts, axis=0), swap(moved, "y")

    ctx_kv, over_y = chain_step(keys_step, ctx_here, ctx_there, w_cross, out_across)
    w_out = gather_z(mine_or_over_y(1, out_mine, over_y))
    cross_q = matmul(b_all, w_cross_q)
    cross_q = split(cross_q.astype(bf16))
    cross_k, cross_v = split(ctx_kv[:, :block]), split(ctx_kv[:, block:])
    item = jnp.arange(slots * ctx_len) // ctx_len
    own_item = seg_all[:, :, None] == item[None, None, :]
    cross_p = probabilities(cross_q, cross_k, own_item)
    cross_low = cross_p.astype(bf16)
    cross_o = joined(weighted(cross_low, cross_v))
    h2, ctx_all = chain_step(
        lambda one, *pieces: (scatter_rows(one), jnp.concatenate(pieces, axis=0)),
        matmul(cross_o, w_cross_out),
        ctx_here,
        ctx_there,
    )
    ctx_low, ctx_high = ctx_all[:, :width], ctx_all[:, width:]
    h2 = h1 + h2
    c_all = chain_step(gather_rows, normalize(h2, gains[2]).astype(bf16))

    hidden = matmul(c_all, w_in)
    activated = gelu_tanh(hidden).astype(bf16)

    def sum_rows(value):
        value = with_layout_constraint(value, Layout(major_to_minor=(0, 1)))
        value = lax.psum_scatter(value, "z", scatter_dimension=0, tiled=True)
        return with_layout_constraint(value, Layout(major_to_minor=(0, 1)))

    def from_y(value, keep_pair=None):
        return jnp.stack([value, lax.ppermute(value, ALL_AXES, flip_pairs(2, keep_pair))])

    def with_core(pair):
        return jnp.concatenate([pair, swap(pair, "c")])

    t_out = matmul_left(activated, d_ff).astype(bf16)
    g_out = sum_rows(t_out)
    d_act = matmul_right(after(d_ff, t_out), w_out)
    d_hidden = jax.vjp(gelu_tanh, hidden)[1](d_act)[0].astype(bf16)
    t_in = matmul_left(c_all, d_hidden).astype(bf16)
    g_in = sum_rows(t_in)
    d_c, out_sum = chain_step(
        lambda one, two: (scatter_rows(one), scatter_rows(two)), matmul_right(d_hidden, w_in), matmul(activated, w_out)
    )
    layer_out = (h2 + out_sum).astype(bf16)
    part_two, gain_grad_two = jax.vjp(normalize, h2, gains[2])[1](d_c)
    dh2 = grad_out + part_two
    d_cross_out = chain_step(gather_rows, after(dh2.astype(bf16), t_in))
    g_cross_out = matmul_left(cross_o, d_cross_out)

    def through(d_mixed, left, right, probs, probs_low, values):
        d_mixed = split(d_mixed.astype(bf16))
        d_probs = jnp.einsum("bqhd,bkhd->bhqk", d_mixed, values, preferred_element_type=f32)
        d_scores = (probs * (d_probs - jnp.sum(probs * d_probs, axis=-1, keepdims=True))).astype(bf16)
        d_left = joined(weighted(d_scores, right) * scale)
        d_right = joined(jnp.einsum("bhqk,bqhd->bkhd", d_scores, left, preferred_element_type=f32) * scale)
        d_values = joined(jnp.einsum("bhqk,bqhd->bkhd", probs_low, d_mixed, preferred_element_type=f32))
        return d_left, d_right, d_values

    (d_cq, d_ck, d_cv), out_grads = chain_step(
        lambda one, two: (
            through(matmul_right(one, w_cross_out), cross_q, cross_k, cross_p, cross_low, cross_v),
            from_y(two),
        ),
        d_cross_out,
        g_out,
    )
    d_ckv = jnp.concatenate([d_ck, d_cv], axis=1)
    t_cross = jnp.concatenate(
        [
            value.astype(bf16)
            for value in (matmul_left(b_all, d_cq), matmul_left(ctx_low, d_ckv), matmul_left(ctx_high, d_ckv))
        ],
        axis=1,
    )
    g_cross = sum_rows(t_cross)
    part = matmul_right(d_cq, w_cross_q)
    d_b = chain_step(scatter_rows, part)
    part_one, gain_grad_one = jax.vjp(normalize, h1, gains[1])[1](d_b)
    dh1 = dh2 + part_one
    d_self_out = chain_step(gather_rows, after(dh1.astype(bf16), t_cross, g_in))
    g_self_out = matmul_left(attended, d_self_out)
    t_outer = jnp.concatenate(
        [
            jnp.where(low_y, g_self_out, g_cross_out).astype(bf16),
            jnp.where(low_y, g_cross_out, g_self_out).astype(bf16),
        ],
        axis=0,
    )
    g_outer = sum_rows(after(t_outer, g_cross))
    d_mixed = matmul_right(after(d_self_out, t_outer), w_self_out)
    d_q, d_k, d_v = through(d_mixed, query, keys, probs, probs_low, values)
    d_qkv = jnp.concatenate([d_q, d_k, d_v], axis=1)
    t_qkv = matmul_left(a_all, d_qkv).astype(bf16)
    g_qkv = sum_rows(t_qkv)
    group_of = np.array([0, 0, 0, 0, 0, 0, 0, 0, 0, 0, 1, 1, 1, 1, 0, 0, 0, 0], np.int32)
    column_of = np.array([0, 0, 0, 0, 0, 1, 3, 2, 4, 0, 0, 1, 2, 3, 0, 0, 0, 0], np.int32)
    group_at = jnp.sum(jnp.where(holds, group_of, 0), axis=2)
    column_at = jnp.sum(jnp.where(holds, column_of, 0), axis=2)
    column_at = jnp.where(group_at == 1, (column_at + f) % 4, column_at)
    sent = pack_gradients(
        [after(g_cross, t_qkv), g_in], jnp.tile(group_at.reshape(-1), 2), jnp.tile(column_at.reshape(-1), 2), rows, block, cap
    )
    early_grads = lax.all_to_all(sent, PLANE, 0, 0, tiled=True).reshape(8 * cap, rows, block)

    def last_step(part, out_pair, gain_grad_one, gain_grad_two):
        part_zero, gain_grad_zero = jax.vjp(normalize, h0, gains[0])[1](scatter_rows(part))
        gain_grads = jnp.stack([gain_grad_zero, gain_grad_one, gain_grad_two])
        return part_zero, sum_everywhere(gain_grads), with_core(out_pair)

    part_zero, gain_total, out_grads = chain_step(
        last_step, matmul_right(after(d_qkv, sent), w_qkv), out_grads, gain_grad_one, gain_grad_two
    )
    grad_tokens = (dh1 + part_zero).astype(bf16)

    by_tile = jnp.swapaxes(after(g_qkv, out_grads).reshape(2, rows, 3, block), 1, 2)
    sent = jnp.broadcast_to(by_tile[:, None], (2, 4, 3, rows, block)).reshape(8, 3, rows, block)
    late_grads = lax.all_to_all(sent, PLANE, 0, 0, tiled=True).reshape(8 * 3, rows, block)
    back_swap = [(target, source) for source, target in pair_swap]
    place = np.arange(8)
    source_x, source_f = (place % 2)[None, :], ((place // 2)[None, :] - my_shift[:, None]) % 4
    slot = np.arange(cap, dtype=np.int32)
    column_place = (source_x * 4 + source_f) * cap + slot[:, None]
    other_row = ((z - my_shift) % 4) ^ f
    row_source = (other_row % 2) * 2 + other_row // 2
    late = (my_used == 1) & ((my_tile < 4) | (my_tile == 9))
    early_mode = jnp.where(my_used == 0, 1, jnp.where(late, 0, jnp.where(my_row == 1, 3, 2)))
    states = (master, moment_one, moment_two)

    def early_step(early_grads, out_grads, half):
        other_half = lax.ppermute(half, ALL_AXES, back_swap)
        in_order = jnp.where(odd == 0, jnp.stack([half, other_half]), jnp.stack([other_half, half]))
        in_order = in_order.reshape(rows, width)
        counts = jnp.where(f % 2 == z % 2, in_order, swap(in_order, "c"))
        early = None
        for first in (0, half_cap):
            chosen = slice(first, first + half_cap)
            early = adam_tiles(
                *states,
                [early_grads],
                [out_grads],
                slot[chosen],
                early_mode[chosen],
                column_place[chosen].reshape(-1),
                row_source[chosen],
                np.zeros(half_cap, np.int32),
                early,
            )
        return *early, from_y(counts)

    *early, outer_grads = chain_step(early_step, early_grads, out_grads, g_outer)

    n_late = 5
    order = jnp.sum(jnp.where(slot[None, :] < slot[:, None], late.astype(jnp.int32)[None, :], 0), axis=1)
    count_late = jnp.sum(late.astype(jnp.int32))
    step = np.arange(n_late)
    wanted = jnp.minimum(step, jnp.maximum(count_late - 1, 0))
    here = late[None, :] & (order[None, :] == wanted[:, None])

    def at_step(value):
        return jnp.sum(jnp.where(here, value.astype(jnp.int32)[None, :], 0), axis=1)

    hold = (step >= jnp.maximum(count_late, 1)).astype(jnp.int32)
    tile = at_step(my_tile)
    some = count_late > 0
    visit = jnp.where(some, at_step(slot), 0)
    first_mode = jnp.where(early_mode[0] == 3, 4, early_mode[0])
    late_mode = jnp.where(at_step(my_row) == 1, 5, 3)
    mode = jnp.where(hold == 1, 0, jnp.where(some, late_mode, first_mode))
    late_place = ((place % 2)[None, :] * 4 + (place // 2)[None, :]) * 3 + tile[:, None]
    late_place = jnp.where(some, late_place, column_place[:1])
    new_w, new_m, new_v = adam_tiles(
        *states,
        [early_grads, late_grads],
        [out_grads, outer_grads],
        visit,
        mode,
        late_place.reshape(-1),
        jnp.where(some, at_step(other_row // 2), row_source[0]),
        hold,
        early,
    )
    new_g, new_gm, new_gv = adam_update(gains, gain_one, gain_two, gain_total, rate_gain, 0.0)
    return (layer_out, grad_tokens, new_w, new_m, new_v, new_g, new_gm, new_gv)


def whole_body(
    tokens, cotangent, context, lengths, keep, owners, master, moment_one, moment_two, gains, gain_one, gain_two
):
    cap = master.shape[0]
    n_tiles = owners.shape[0]
    slot_of = owners * cap + ranks_of(owners)
    owner_rows = lax.all_gather(master.astype(bf16), "fsdp", axis=0, tiled=True)
    tiles = [
        lax.all_gather(
            lax.dynamic_index_in_dim(owner_rows, slot_of[tile], 0, keepdims=False), "dp", axis=0, tiled=True
        )
        for tile in range(n_tiles)
    ]
    w_in = jnp.concatenate(tiles[10:14], axis=1)
    w_out = jnp.concatenate(tiles[14:18], axis=0)
    count, width = tokens.shape
    head_dim = width // HEADS
    scale = head_dim ** (-0.5)
    seg = segments(lengths[0], count)
    live = keep == 1
    places = jnp.arange(count)

    def split(value):
        return value.astype(bf16).reshape(-1, HEADS, head_dim)

    def joined(value):
        return value.astype(bf16).reshape(-1, width)

    def probabilities(left, right, mask):
        scores = jnp.einsum("qhd,khd->hqk", left, right, preferred_element_type=f32) * scale
        scores = jnp.where(mask[None], scores, -1e30)
        expo = jnp.exp(scores - jnp.max(scores, axis=-1, keepdims=True))
        return expo / jnp.sum(expo, axis=-1, keepdims=True)

    def weighted(probs, right):
        return jnp.einsum("hqk,khd->qhd", probs, right, preferred_element_type=f32)

    def through(weights, d_out, left, right, probs, values):
        d_mixed = split(matmul_right(d_out, weights))
        d_probs = jnp.einsum("qhd,khd->hqk", d_mixed, values, preferred_element_type=f32)
        d_scores = (probs * (d_probs - jnp.sum(probs * d_probs, axis=-1, keepdims=True))).astype(bf16)
        d_left = joined(weighted(d_scores, right) * scale)
        d_right = joined(jnp.einsum("hqk,qhd->khd", d_scores, left, preferred_element_type=f32) * scale)
        d_values = joined(jnp.einsum("hqk,qhd->khd", probs.astype(bf16), d_mixed, preferred_element_type=f32))
        return d_left, d_right, d_values

    h0 = tokens.astype(f32)
    a_in = normalize(h0, gains[0]).astype(bf16)
    query, keys, values = (split(matmul(a_in, tiles[n])) for n in range(3))
    allowed = (seg[:, None] == seg[None, :]) & (live[None, :] | (places[:, None] == places[None, :]))
    probs = probabilities(query, keys, allowed)
    attended = joined(weighted(probs.astype(bf16), values))
    h1 = h0 + matmul(attended, tiles[3])
    b_in = normalize(h1, gains[1]).astype(bf16)
    slots, ctx_len, ctx_width = context.shape
    ctx = context.reshape(slots * ctx_len, ctx_width)
    ctx_low, ctx_high = ctx[:, :width], ctx[:, width:]
    cross_q = split(matmul(b_in, tiles[4]))
    cross_k = split(matmul(ctx_low, tiles[5]) + matmul(ctx_high, tiles[6]))
    cross_v = split(matmul(ctx_low, tiles[7]) + matmul(ctx_high, tiles[8]))
    item = jnp.arange(slots * ctx_len) // ctx_len
    cross_p = probabilities(cross_q, cross_k, seg[:, None] == item[None, :])
    cross_o = joined(weighted(cross_p.astype(bf16), cross_v))
    h2 = h1 + matmul(cross_o, tiles[9])
    c_in = normalize(h2, gains[2]).astype(bf16)
    hidden = matmul(c_in, w_in)
    activated = gelu_tanh(hidden).astype(bf16)
    layer_out = (h2 + matmul(activated, w_out)).astype(bf16)
    grad_out = cotangent.astype(f32) * live.astype(f32)[:, None]
    d_ff = grad_out.astype(bf16)
    d_hidden = jax.vjp(gelu_tanh, hidden)[1](matmul_right(d_ff, w_out))[0].astype(bf16)
    part_two, gain_grad_two = jax.vjp(normalize, h2, gains[2])[1](matmul_right(d_hidden, w_in))
    dh2 = grad_out + part_two
    d_cross_out = dh2.astype(bf16)
    d_cq, d_ck, d_cv = through(tiles[9], d_cross_out, cross_q, cross_k, cross_p, cross_v)
    part_one, gain_grad_one = jax.vjp(normalize, h1, gains[1])[1](matmul_right(d_cq, tiles[4]))
    dh1 = dh2 + part_one
    d_self_out = dh1.astype(bf16)
    d_q, d_k, d_v = through(tiles[3], d_self_out, query, keys, probs, values)
    d_a = matmul_right(d_q, tiles[0]) + matmul_right(d_k, tiles[1]) + matmul_right(d_v, tiles[2])
    part_zero, gain_grad_zero = jax.vjp(normalize, h0, gains[0])[1](d_a)
    grad_tokens = (dh1 + part_zero).astype(bf16)
    pairs = [
        (a_in, d_q),
        (a_in, d_k),
        (a_in, d_v),
        (attended, d_self_out),
        (b_in, d_cq),
        (ctx_low, d_ck),
        (ctx_high, d_ck),
        (ctx_low, d_cv),
        (ctx_high, d_cv),
        (cross_o, d_cross_out),
    ]
    for part in range(4):
        pairs.append((c_in, d_hidden[:, part * width : (part + 1) * width]))
    for part in range(4):
        pairs.append((activated[:, part * width : (part + 1) * width], d_ff))
    total_slots = lax.axis_size("fsdp") * cap
    placed = jnp.zeros((total_slots,) + master.shape[1:], bf16)
    for tile, (left, right) in enumerate(pairs):
        term = lax.psum_scatter(
            matmul_left(left, right).astype(bf16), "dp", scatter_dimension=0, tiled=True
        )
        placed = lax.dynamic_update_index_in_dim(placed, term, slot_of[tile], 0)
    owned = lax.psum_scatter(placed, "fsdp", scatter_dimension=0, tiled=True).astype(f32)
    my_slots = lax.axis_index("fsdp") * cap + jnp.arange(cap)
    used = jnp.any(slot_of[None, :] == my_slots[:, None], axis=1)[:, None, None]
    updated = adam_update(master, moment_one, moment_two, owned, rate_matrix, decay_rate)
    new_w, new_m, new_v = (jnp.where(used, value, 0.0) for value in updated)
    gain_grads = jnp.stack([gain_grad_zero, gain_grad_one, gain_grad_two])
    gain_total = lax.psum(gain_grads, ("dp", "fsdp"))
    new_g, new_gm, new_gv = adam_update(gains, gain_one, gain_two, gain_total, rate_gain, 0.0)
    return (layer_out, grad_tokens, new_w, new_m, new_v, new_g, new_gm, new_gv)


def solution(mesh):
    planes = mesh.shape["dp"] == 8 and mesh.shape["fsdp"] == 4
    if planes:
        used = Mesh(mesh.devices.reshape(4, 2, 2, 2), ALL_AXES)
        dp, fsdp, body = ("z", "x"), ("y", "c"), plane_body
    else:
        used, dp, fsdp, body = mesh, ("dp",), ("fsdp",), whole_body
    rows = P(dp + fsdp, None)
    tiles = P(fsdp, dp, None)
    return jax.shard_map(
        body,
        mesh=used,
        in_specs=(rows, rows, P(dp + fsdp, None, None), rows, P(dp + fsdp), P(), tiles, tiles, tiles, P(), P(), P()),
        out_specs=(rows, rows, tiles, tiles, tiles, P(), P(), P()),
        check_vma=False,
    )
```

```python
import jax
import jax.numpy as jnp
import numpy as np
from jax import lax
from jax.experimental import pallas as pl
from jax.experimental.layout import Layout, with_layout_constraint
from jax.experimental.pallas import tpu as pltpu
from jax.sharding import Mesh
from jax.sharding import PartitionSpec as P

HEADS = 16
STEP = 10

norm_eps = 1e-06
beta_one = 0.9
beta_two = 0.95
adam_eps = 1e-08
decay_rate = 0.1
rate_matrix = 0.1
rate_gain = 0.8

f32 = jnp.float32
bf16 = jnp.bfloat16

SHIFT = (0, 0, 0, 0, 2, 2, 2, 2, 2, 2, 0, 1, 2, 3, 0, 1, 2, 3)
ROW_TILES = (3, 9, 14, 15, 16, 17)
VMEM_LIMIT = 48 << 20


def normalize(h, gain):
    scale = lax.rsqrt(jnp.mean(h * h, axis=-1, keepdims=True) + norm_eps)
    return h * scale * gain


def gelu_tanh(u):
    return 0.5 * u * (1.0 + jnp.tanh(0.7978845608028654 * (u + 0.044715 * u * u * u)))


def matmul(left, right):
    return jnp.dot(left, right, preferred_element_type=f32)


def matmul_left(left, right):
    return lax.dot_general(left, right, (((0,), (0,)), ((), ())), preferred_element_type=f32)


def matmul_right(left, right):
    return lax.dot_general(left, right, (((1,), (1,)), ((), ())), preferred_element_type=f32)


def ranks_of(owners):
    order = jnp.arange(owners.shape[0])
    same = (owners[:, None] == owners[None, :]) & (order[None, :] < order[:, None])
    return jnp.sum(same.astype(jnp.int32), axis=1)


def segments(lengths, count):
    places = jnp.arange(count)
    end = jnp.zeros((), jnp.int32)
    seg = jnp.zeros((count,), jnp.int32)
    for item in range(lengths.shape[0]):
        end = end + lengths[item]
        seg = seg + (places >= end).astype(jnp.int32)
    return seg


def adam_update(weight, first, second, grad, rate, decay):
    first = beta_one * first + (1.0 - beta_one) * grad
    second = beta_two * second + (1.0 - beta_two) * grad * grad
    fix_one = 1.0 / (1.0 - beta_one**STEP)
    fix_two = 1.0 / (1.0 - beta_two**STEP)
    move = first * fix_one / (jnp.sqrt(second * fix_two) + adam_eps)
    return (weight - rate * (move + decay * weight), first, second)


def pack_columns(master, table, first_slot, slots):
    _, rows, columns = master.shape
    width = columns // 8

    def kernel(table_ref, in_ref, out_ref):
        slot = pl.program_id(0)
        for rank in range(8):
            start = pl.multiple_of(table_ref[slot * 8 + rank] * width, width)
            out_ref[rank, 0] = in_ref[0, :, pl.ds(start, width)].astype(bf16)

    return pl.pallas_call(
        kernel,
        out_shape=jax.ShapeDtypeStruct((8, slots, rows, width), bf16),
        grid_spec=pltpu.PrefetchScalarGridSpec(
            num_scalar_prefetch=1,
            grid=(slots,),
            in_specs=[pl.BlockSpec((1, rows, columns), lambda k, t: (first_slot + k, 0, 0))],
            out_specs=pl.BlockSpec((8, 1, rows, width), lambda k, t: (0, k, 0, 0)),
        ),
        compiler_params=pltpu.CompilerParams(vmem_limit_bytes=VMEM_LIMIT),
        name="pack_columns",
    )(table, master)


def pick_blocks(sources, which, index, count):
    _, rows, width = sources[0].shape
    n_src = len(sources)

    def kernel(which_ref, index_ref, *refs):
        place = pl.program_id(0) * 2 + pl.program_id(1)
        out_ref = refs[n_src]
        for number in range(n_src):

            @pl.when(which_ref[place] == number)
            def _():
                out_ref[...] = refs[number][0]

    def spec(number):
        def at(n, half, which, index):
            place = n * 2 + half
            return (jnp.where(which[place] == number, index[place], 0), 0, 0)

        return pl.BlockSpec((1, rows, width), at)

    return pl.pallas_call(
        kernel,
        out_shape=jax.ShapeDtypeStruct((2 * rows, count * width), bf16),
        grid_spec=pltpu.PrefetchScalarGridSpec(
            num_scalar_prefetch=2,
            grid=(count, 2),
            in_specs=[spec(number) for number in range(n_src)],
            out_specs=pl.BlockSpec((rows, width), lambda n, half, which, index: (half, n)),
        ),
        compiler_params=pltpu.CompilerParams(vmem_limit_bytes=VMEM_LIMIT),
        name="pick_blocks",
    )(which, index, *sources)


def pack_gradients(groups, which, column, rows, width, slots):
    n_src = len(groups)

    def kernel(which_ref, column_ref, *refs):
        rank = pl.program_id(0)
        out_ref = refs[n_src]
        for k in range(slots):
            start = pl.multiple_of(column_ref[rank * slots + k] * width, width)
            for number in range(n_src):

                @pl.when(which_ref[rank * slots + k] == number)
                def _():
                    out_ref[0, k] = refs[number][:, pl.ds(start, width)]

    return pl.pallas_call(
        kernel,
        out_shape=jax.ShapeDtypeStruct((8, slots, rows, width), bf16),
        grid_spec=pltpu.PrefetchScalarGridSpec(
            num_scalar_prefetch=2,
            grid=(8,),
            in_specs=[
                pl.BlockSpec((rows, group.shape[1]), lambda rank, which, column: (rank // 4, 0)) for group in groups
            ],
            out_specs=pl.BlockSpec((1, slots, rows, width), lambda rank, which, column: (rank, 0, 0, 0)),
        ),
        compiler_params=pltpu.CompilerParams(vmem_limit_bytes=VMEM_LIMIT),
        name="pack_gradients",
    )(which, column, *groups)


def adam_tiles(master, one, two, columns_from, rows_from, visit, mode, column_place, row_place, hold, previous=None):
    _, rows, columns = master.shape
    width = columns // 8
    n_visit = visit.shape[0]
    n_col, n_row = len(columns_from), len(rows_from)
    kept = () if previous is None else tuple(previous)

    def kernel(visit_ref, mode_ref, cp_ref, rp_ref, hold_ref, *refs):
        w_ref, m_ref, v_ref = refs[:3]
        grads = refs[3 : 3 + n_col + n_row]
        outs = refs[3 + n_col + n_row + len(kept) :]
        how = mode_ref[pl.program_id(0)]

        @pl.when(how == 1)
        def _():
            for ref in outs:
                ref[...] = jnp.zeros_like(ref)

        for number, grad_ref in enumerate(grads):

            @pl.when(how == number + 2)
            def _():
                grad = grad_ref[0].astype(f32)
                results = adam_update(w_ref[0], m_ref[0], v_ref[0], grad, rate_matrix, decay_rate)
                for ref, value in zip(outs, results, strict=True):
                    ref[0] = value

    def block_of(n, b, hold):
        return jnp.where(hold[n] == 1, 7, b)

    state = pl.BlockSpec((1, rows, width), lambda n, b, vi, mo, cp, rp, ho: (vi[n], 0, block_of(n, b, ho)))

    def column_spec(number):
        def at(n, b, vi, mo, cp, rp, ho):
            return (jnp.where(mo[n] == number + 2, cp[n * 8 + block_of(n, b, ho)], 0), 0, 0)

        return pl.BlockSpec((1, rows, width), at)

    def row_spec(number):
        def at(n, b, vi, mo, cp, rp, ho):
            taken = mo[n] == number + 2
            return (jnp.where(taken, rp[n], 0), 0, jnp.where(taken, block_of(n, b, ho), 0))

        return pl.BlockSpec((1, rows, width), at)

    shape = jax.ShapeDtypeStruct(master.shape, f32)
    n_before = 5 + 3 + n_col + n_row
    return pl.pallas_call(
        kernel,
        out_shape=(shape, shape, shape),
        grid_spec=pltpu.PrefetchScalarGridSpec(
            num_scalar_prefetch=5,
            grid=(n_visit, 8),
            in_specs=[
                state,
                state,
                state,
                *(column_spec(number) for number in range(n_col)),
                *(row_spec(n_col + number) for number in range(n_row)),
                *(pl.BlockSpec(memory_space=pl.ANY) for _ in kept),
            ],
            out_specs=(state, state, state),
        ),
        input_output_aliases={n_before + n: n for n in range(len(kept))},
        compiler_params=pltpu.CompilerParams(vmem_limit_bytes=VMEM_LIMIT),
        cost_estimate=pl.CostEstimate(
            flops=30 * n_visit * rows * columns, bytes_accessed=26 * n_visit * rows * columns, transcendentals=0
        ),
        name="adam_tiles",
    )(visit, mode, column_place, row_place, hold, master, one, two, *columns_from, *rows_from, *kept)


def after(value, *others):
    return lax.optimization_barrier((value, *others))[0]


def swap(value, axis):
    return lax.ppermute(value, axis, [(0, 1), (1, 0)])


def gather_rows(value):
    half = value.shape[0] // 2
    over_x = swap(value, "x")
    over_y = swap(value, "y")
    far_low = swap(over_y[:half], "x")
    far_high = swap(over_x[half:], "y")
    four = jnp.concatenate([value, over_y, over_x, far_low, far_high], axis=0)
    return jnp.concatenate([four, swap(four, "c")], axis=0)


def scatter_rows(part):
    rows, width = part.shape[0] // 8, part.shape[1]
    half = width // 2
    part = part.reshape(2, 2, 2, rows, width)
    chip = part[0] + swap(part[1], "c")
    low, high = chip[..., :half], chip[..., half:]
    low_two = low[:, 0] + swap(low[:, 1].astype(bf16), "y").astype(f32)
    high_two = high[0] + swap(high[1].astype(bf16), "x").astype(f32)
    low_one = low_two[0] + swap(low_two[1].astype(bf16), "x").astype(f32)
    high_one = high_two[0] + swap(high_two[1].astype(bf16), "y").astype(f32)
    return jnp.concatenate([low_one, high_one], axis=1)


def sum_everywhere(value):
    for axis in ("c", "y", "x"):
        value = value + swap(value, axis)
    for step in (1, 2):
        value = value + lax.ppermute(value, "z", [(z, z ^ step) for z in range(4)])
    return value


def flip_pairs(mask, keep=None):
    pairs = []
    for z in range(4):
        for place in range(8):
            target = place ^ mask
            if keep is None or keep(z, place, target):
                pairs.append((z * 8 + place, z * 8 + target))
    return pairs


ALL_AXES = ("z", "x", "y", "c")
PLANE = ("x", "y", "c")


def plane_body(
    tokens, cotangent, context, lengths, keep, owners, master, moment_one, moment_two, gains, gain_one, gain_two
):
    cap, rows, _ = master.shape
    count, width = tokens.shape
    heads_here = HEADS // 8
    head_dim = width // HEADS
    scale = head_dim ** (-0.5)
    block = width // 8
    z = lax.axis_index("z")
    x = lax.axis_index("x")
    f = lax.axis_index("y") * 2 + lax.axis_index("c")

    n_tiles = owners.shape[0]
    rank = ranks_of(owners)
    shift_of = np.array(SHIFT, np.int32)
    row_of = np.array([t in ROW_TILES for t in range(n_tiles)])
    all_slots = jnp.arange(4 * cap).reshape(4, cap)
    holds = (owners * cap + rank)[None, None, :] == all_slots[:, :, None]
    used_at = jnp.any(holds, axis=2)
    tile_at = jnp.sum(jnp.where(holds, np.arange(n_tiles, dtype=np.int32), 0), axis=2)
    shift_at = jnp.sum(jnp.where(holds, shift_of, 0), axis=2)
    row_at = jnp.any(holds & row_of, axis=2)
    mine = (jnp.arange(4) == f)[:, None]

    def my(value):
        return jnp.sum(jnp.where(mine, value.astype(jnp.int32), 0), axis=0)

    my_used, my_tile, my_shift, my_row = my(used_at), my(tile_at), my(shift_at), my(row_at)

    to_x = np.arange(8) // 4
    to_f = np.arange(8) % 4
    column_table = 2 * ((to_f[None, :] + my_shift[:, None]) % 4) + to_x[None, :]
    half_cap = cap // 2
    place = np.arange(4)

    def of_tiles(tiles, values):
        chosen = tiles[:, None] == np.arange(n_tiles)[None, :]
        return jnp.sum(jnp.where(chosen, values[None, :], 0), axis=1)

    column_tiles = jnp.concatenate([np.array([0, 1, 2, 4, 5, 7, 6, 8], np.int32), 10 + (place - f) % 4])
    column_part = jnp.repeat(of_tiles(column_tiles, rank // half_cap), 2)
    column_place = of_tiles(column_tiles, owners * half_cap + rank % half_cap)
    column_place = (column_place[:, None] + np.array([0, 4 * half_cap])[None, :]).reshape(-1)
    other_f = f ^ place
    outer_tiles = jnp.where(other_f == z, 3, 9)
    out_tiles = 14 + (z - other_f) % 4
    row_slots = of_tiles(jnp.concatenate([outer_tiles, out_tiles]), rank)
    row_owners = of_tiles(jnp.stack([outer_tiles[0], outer_tiles[2], out_tiles[0], out_tiles[2]]), owners)

    def pack_first(weights):
        return pack_columns(weights, column_table[:half_cap].reshape(-1), 0, half_cap)

    def pack_second(weights):
        return pack_columns(weights, column_table[half_cap:].reshape(-1), half_cap, half_cap)

    def my_block(slot):
        return lax.dynamic_index_in_dim(master, slot, 0, keepdims=False).astype(bf16)

    present = owners[0] >= 0

    def chain_step(move, *values):
        shapes = jax.eval_shape(move, *values)
        idle = jax.tree.map(lambda leaf: jnp.zeros(leaf.shape, leaf.dtype), shapes)
        return lax.cond(present, move, lambda *_: idle, *values)

    h0 = tokens.astype(f32)
    outer_blocks = [my_block(row_slots[mask]) for mask in range(4)]
    out_blocks = [my_block(row_slots[4 + mask]) for mask in range(4)]
    a_in = normalize(h0, gains[0]).astype(bf16)
    sent = pack_first(after(master, column_part, column_place, row_slots, row_owners))
    received = [lax.all_to_all(sent, PLANE, 0, 0, tiled=True).reshape(8 * half_cap, rows, block)]
    seg = segments(lengths[0], count)
    live = keep == 1
    code = seg * 2 + live.astype(jnp.int32)

    def spread_code(code):
        for axis in ("y", "x", "c"):
            code = jnp.concatenate([code, swap(code, axis)])
        return code

    code = chain_step(spread_code, after(code, a_in, *outer_blocks, *out_blocks))
    seg_all = (code // 2).reshape(8, count)
    live_all = (code % 2 == 1).reshape(8, count)
    grad_out = cotangent.astype(f32) * live.astype(f32)[:, None]
    received = [after(received[0], a_in, code, *outer_blocks, *out_blocks)]

    def columns_here(first, count, parts):
        chosen = slice(2 * first, 2 * (first + count))
        return pick_blocks(received[:parts], column_part[chosen], column_place[chosen], count)

    def gather_z(value):
        return lax.all_gather(value, "z", axis=0, tiled=True)

    local = columns_here(0, 3, 1)
    w_qkv = gather_z(local)
    a_all = gather_rows(after(a_in, local))
    d_ff = gather_rows(after(grad_out.astype(bf16), local))
    def meet_on_chip(kind, blocks):
        here, there = row_owners[2 * kind], row_owners[2 * kind + 1]
        core = f % 2
        from_core = swap(jnp.stack([blocks[1], blocks[3]]), "c")
        mine = jnp.where(here % 2 == core, blocks[0], from_core[0])
        return mine, jnp.where(there % 2 == core, blocks[2], from_core[1])

    def mine_or_over_y(kind, mine, over_y):
        return jnp.where(row_owners[2 * kind] // 2 == f // 2, mine, over_y)

    out_mine, out_across = meet_on_chip(1, [after(value, local) for value in out_blocks])
    sent = pack_second(after(master, a_all, d_ff, out_across))
    received.append(lax.all_to_all(sent, PLANE, 0, 0, tiled=True).reshape(8 * half_cap, rows, block))

    def needs_outer(zz, place, target):
        return target % 4 in (zz, (zz + 2) % 4)

    outer_mine, across = meet_on_chip(0, [after(value, local) for value in outer_blocks])
    outer = mine_or_over_y(0, outer_mine, lax.ppermute(across, ALL_AXES, flip_pairs(2, needs_outer)))
    half_rows = rows // 2
    odd = z % 2
    to_pair = lax.dynamic_slice_in_dim(after(outer, sent), (1 - odd) * half_rows, half_rows, 0)
    own_half = lax.dynamic_slice_in_dim(outer, odd * half_rows, half_rows, 0)
    pair_swap = [
        (zz * 8 + place, (zz ^ 1) * 8 + place)
        for zz in range(4)
        for place in range(8)
        if place % 4 in (zz, (zz + 2) % 4)
    ]
    from_pair = lax.ppermute(to_pair, ALL_AXES, pair_swap)
    has_outer = (f == z) | (f == (z + 2) % 4)
    outer_all = lax.all_gather(jnp.where(has_outer, own_half, from_pair), "z", axis=0, tiled=True)
    low_y = lax.axis_index("y") == 0
    w_self_out = jnp.where(low_y, outer_all[:rows], outer_all[rows:])
    w_cross_out = jnp.where(low_y, outer_all[rows:], outer_all[:rows])

    def split(value):
        return value.reshape(8, -1, heads_here, head_dim)

    qkv = matmul(a_all, w_qkv)
    qkv = qkv.astype(bf16)
    query, keys, values = (split(qkv[:, n * block : (n + 1) * block]) for n in range(3))
    places = jnp.arange(count)
    allowed = (seg_all[:, :, None] == seg_all[:, None, :]) & (
        live_all[:, None, :] | (places[:, None] == places[None, :])
    )

    def probabilities(left, right, mask):
        scores = jnp.einsum("bqhd,bkhd->bhqk", left, right, preferred_element_type=f32) * scale
        scores = jnp.where(mask[:, None], scores, -1e30)
        expo = jnp.exp(scores - jnp.max(scores, axis=-1, keepdims=True))
        return expo / jnp.sum(expo, axis=-1, keepdims=True)

    def weighted(probs, right):
        return jnp.einsum("bhqk,bkhd->bqhd", probs, right, preferred_element_type=f32)

    def joined(value):
        return value.astype(bf16).reshape(-1, block)

    probs = probabilities(query, keys, allowed)
    probs_low = probs.astype(bf16)
    mixed = weighted(probs_low, values).astype(bf16)
    attended = mixed.reshape(-1, block)
    received[1] = after(received[1], mixed)
    local_cross, local_in = columns_here(3, 5, 2), columns_here(8, 4, 2)
    w_cross = gather_z(local_cross)
    w_in = gather_z(local_in)

    slots, ctx_len, ctx_width = context.shape
    ctx = after(context.reshape(slots * ctx_len, ctx_width), local_cross, local_in)
    ctx_x, ctx_y = swap(ctx, "x"), swap(ctx, "y")
    h1 = h0 + chain_step(scatter_rows, matmul(after(attended, local_in), w_self_out))

    def second_step(one, own, over_x, over_y):
        half = over_x.shape[0] // 2
        far_low, far_high = swap(over_y[:half], "x"), swap(over_x[half:], "y")
        four = jnp.concatenate([own, over_y, over_x, far_low, far_high], axis=0)
        return gather_rows(one), four, swap(four, "c")

    b_all, ctx_here, ctx_there = chain_step(
        second_step, normalize(h1, gains[1]).astype(bf16), ctx, ctx_x, ctx_y
    )

    w_cross_q = w_cross[:, :block]

    def keys_step(here, there, weights, moved):
        w_low, w_high = weights[:, block : 3 * block], weights[:, 3 * block :]
        parts = [
            (matmul(part[:, :width], w_low) + matmul(part[:, width:], w_high)).astype(bf16) for part in (here, there)
        ]
        return jnp.concatenate(parts, axis=0), swap(moved, "y")

    ctx_kv, over_y = chain_step(keys_step, ctx_here, ctx_there, w_cross, out_across)
    w_out = gather_z(mine_or_over_y(1, out_mine, over_y))
    cross_q = matmul(b_all, w_cross_q)
    cross_q = split(cross_q.astype(bf16))
    cross_k, cross_v = split(ctx_kv[:, :block]), split(ctx_kv[:, block:])
    item = jnp.arange(slots * ctx_len) // ctx_len
    own_item = seg_all[:, :, None] == item[None, None, :]
    cross_p = probabilities(cross_q, cross_k, own_item)
    cross_low = cross_p.astype(bf16)
    cross_o = joined(weighted(cross_low, cross_v))
    h2, ctx_all = chain_step(
        lambda one, *pieces: (scatter_rows(one), jnp.concatenate(pieces, axis=0)),
        matmul(cross_o, w_cross_out),
        ctx_here,
        ctx_there,
    )
    ctx_low, ctx_high = ctx_all[:, :width], ctx_all[:, width:]
    h2 = h1 + h2
    c_all = chain_step(gather_rows, normalize(h2, gains[2]).astype(bf16))

    hidden = matmul(c_all, w_in)
    activated = gelu_tanh(hidden).astype(bf16)

    def sum_rows(value):
        value = with_layout_constraint(value, Layout(major_to_minor=(0, 1)))
        value = lax.psum_scatter(value, "z", scatter_dimension=0, tiled=True)
        return with_layout_constraint(value, Layout(major_to_minor=(0, 1)))

    def from_y(value, keep_pair=None):
        return jnp.stack([value, lax.ppermute(value, ALL_AXES, flip_pairs(2, keep_pair))])

    def with_core(pair):
        return jnp.concatenate([pair, swap(pair, "c")])

    t_out = matmul_left(activated, d_ff).astype(bf16)
    g_out = sum_rows(t_out)
    d_act = matmul_right(after(d_ff, t_out), w_out)
    d_hidden = jax.vjp(gelu_tanh, hidden)[1](d_act)[0].astype(bf16)
    t_in = matmul_left(c_all, d_hidden).astype(bf16)
    g_in = sum_rows(t_in)
    d_c, out_sum = chain_step(
        lambda one, two: (scatter_rows(one), scatter_rows(two)), matmul_right(d_hidden, w_in), matmul(activated, w_out)
    )
    layer_out = (h2 + out_sum).astype(bf16)
    part_two, gain_grad_two = jax.vjp(normalize, h2, gains[2])[1](d_c)
    dh2 = grad_out + part_two
    d_cross_out = chain_step(gather_rows, after(dh2.astype(bf16), t_in))
    g_cross_out = matmul_left(cross_o, d_cross_out)

    def through(d_mixed, left, right, probs, probs_low, values):
        d_mixed = split(d_mixed.astype(bf16))
        d_probs = jnp.einsum("bqhd,bkhd->bhqk", d_mixed, values, preferred_element_type=f32)
        d_scores = (probs * (d_probs - jnp.sum(probs * d_probs, axis=-1, keepdims=True))).astype(bf16)
        d_left = joined(weighted(d_scores, right) * scale)
        d_right = joined(jnp.einsum("bhqk,bqhd->bkhd", d_scores, left, preferred_element_type=f32) * scale)
        d_values = joined(jnp.einsum("bhqk,bqhd->bkhd", probs_low, d_mixed, preferred_element_type=f32))
        return d_left, d_right, d_values

    (d_cq, d_ck, d_cv), out_grads = chain_step(
        lambda one, two: (
            through(matmul_right(one, w_cross_out), cross_q, cross_k, cross_p, cross_low, cross_v),
            from_y(two),
        ),
        d_cross_out,
        g_out,
    )
    d_ckv = jnp.concatenate([d_ck, d_cv], axis=1)
    t_cross = jnp.concatenate(
        [
            value.astype(bf16)
            for value in (matmul_left(b_all, d_cq), matmul_left(ctx_low, d_ckv), matmul_left(ctx_high, d_ckv))
        ],
        axis=1,
    )
    g_cross = sum_rows(t_cross)
    part = matmul_right(d_cq, w_cross_q)
    d_b = chain_step(scatter_rows, part)
    part_one, gain_grad_one = jax.vjp(normalize, h1, gains[1])[1](d_b)
    dh1 = dh2 + part_one
    d_self_out = chain_step(gather_rows, after(dh1.astype(bf16), t_cross, g_in))
    g_self_out = matmul_left(attended, d_self_out)
    t_outer = jnp.concatenate(
        [
            jnp.where(low_y, g_self_out, g_cross_out).astype(bf16),
            jnp.where(low_y, g_cross_out, g_self_out).astype(bf16),
        ],
        axis=0,
    )
    g_outer = sum_rows(after(t_outer, g_cross))
    d_mixed = matmul_right(after(d_self_out, t_outer), w_self_out)
    d_q, d_k, d_v = through(d_mixed, query, keys, probs, probs_low, values)
    d_qkv = jnp.concatenate([d_q, d_k, d_v], axis=1)
    t_qkv = matmul_left(a_all, d_qkv).astype(bf16)
    g_qkv = sum_rows(t_qkv)
    group_of = np.array([0, 0, 0, 0, 0, 0, 0, 0, 0, 0, 1, 1, 1, 1, 0, 0, 0, 0], np.int32)
    column_of = np.array([0, 0, 0, 0, 0, 1, 3, 2, 4, 0, 0, 1, 2, 3, 0, 0, 0, 0], np.int32)
    group_at = jnp.sum(jnp.where(holds, group_of, 0), axis=2)
    column_at = jnp.sum(jnp.where(holds, column_of, 0), axis=2)
    column_at = jnp.where(group_at == 1, (column_at + f) % 4, column_at)
    sent = pack_gradients(
        [after(g_cross, t_qkv), g_in], jnp.tile(group_at.reshape(-1), 2), jnp.tile(column_at.reshape(-1), 2), rows, block, cap
    )
    early_grads = lax.all_to_all(sent, PLANE, 0, 0, tiled=True).reshape(8 * cap, rows, block)

    def last_step(part, out_pair, gain_grad_one, gain_grad_two):
        part_zero, gain_grad_zero = jax.vjp(normalize, h0, gains[0])[1](scatter_rows(part))
        gain_grads = jnp.stack([gain_grad_zero, gain_grad_one, gain_grad_two])
        return part_zero, gain_grads, with_core(out_pair)

    part_zero, gain_grads, out_grads = chain_step(
        last_step, matmul_right(after(d_qkv, sent), w_qkv), out_grads, gain_grad_one, gain_grad_two
    )
    grad_tokens = (dh1 + part_zero).astype(bf16)

    by_tile = jnp.swapaxes(after(g_qkv, out_grads).reshape(2, rows, 3, block), 1, 2)
    sent = jnp.broadcast_to(by_tile[:, None], (2, 4, 3, rows, block)).reshape(8, 3, rows, block)
    late_grads = lax.all_to_all(sent, PLANE, 0, 0, tiled=True).reshape(8 * 3, rows, block)
    back_swap = [(target, source) for source, target in pair_swap]
    place = np.arange(8)
    source_x, source_f = (place % 2)[None, :], ((place // 2)[None, :] - my_shift[:, None]) % 4
    slot = np.arange(cap, dtype=np.int32)
    column_place = (source_x * 4 + source_f) * cap + slot[:, None]
    other_row = ((z - my_shift) % 4) ^ f
    row_source = (other_row % 2) * 2 + other_row // 2
    late = (my_used == 1) & ((my_tile < 4) | (my_tile == 9))
    early_mode = jnp.where(my_used == 0, 1, jnp.where(late, 0, jnp.where(my_row == 1, 3, 2)))
    states = (master, moment_one, moment_two)

    def early_step(early_grads, out_grads, half, gain_grads):
        other_half = lax.ppermute(half, ALL_AXES, back_swap)
        in_order = jnp.where(odd == 0, jnp.stack([half, other_half]), jnp.stack([other_half, half]))
        in_order = in_order.reshape(rows, width)
        counts = jnp.where(f % 2 == z % 2, in_order, swap(in_order, "c"))
        early = None
        for first in (0, half_cap):
            chosen = slice(first, first + half_cap)
            early = adam_tiles(
                *states,
                [early_grads],
                [out_grads],
                slot[chosen],
                early_mode[chosen],
                column_place[chosen].reshape(-1),
                row_source[chosen],
                np.zeros(half_cap, np.int32),
                early,
            )
        return *early, from_y(counts), sum_everywhere(gain_grads)

    *early, outer_grads, gain_total = chain_step(early_step, early_grads, out_grads, g_outer, gain_grads)

    n_late = 5
    order = jnp.sum(jnp.where(slot[None, :] < slot[:, None], late.astype(jnp.int32)[None, :], 0), axis=1)
    count_late = jnp.sum(late.astype(jnp.int32))
    step = np.arange(n_late)
    wanted = jnp.minimum(step, jnp.maximum(count_late - 1, 0))
    here = late[None, :] & (order[None, :] == wanted[:, None])

    def at_step(value):
        return jnp.sum(jnp.where(here, value.astype(jnp.int32)[None, :], 0), axis=1)

    hold = (step >= jnp.maximum(count_late, 1)).astype(jnp.int32)
    tile = at_step(my_tile)
    some = count_late > 0
    visit = jnp.where(some, at_step(slot), 0)
    first_mode = jnp.where(early_mode[0] == 3, 4, early_mode[0])
    late_mode = jnp.where(at_step(my_row) == 1, 5, 3)
    mode = jnp.where(hold == 1, 0, jnp.where(some, late_mode, first_mode))
    late_place = ((place % 2)[None, :] * 4 + (place // 2)[None, :]) * 3 + tile[:, None]
    late_place = jnp.where(some, late_place, column_place[:1])
    new_w, new_m, new_v = adam_tiles(
        *states,
        [early_grads, late_grads],
        [out_grads, outer_grads],
        visit,
        mode,
        late_place.reshape(-1),
        jnp.where(some, at_step(other_row // 2), row_source[0]),
        hold,
        early,
    )
    new_g, new_gm, new_gv = adam_update(gains, gain_one, gain_two, gain_total, rate_gain, 0.0)
    return (layer_out, grad_tokens, new_w, new_m, new_v, new_g, new_gm, new_gv)


def whole_body(
    tokens, cotangent, context, lengths, keep, owners, master, moment_one, moment_two, gains, gain_one, gain_two
):
    cap = master.shape[0]
    n_tiles = owners.shape[0]
    slot_of = owners * cap + ranks_of(owners)
    owner_rows = lax.all_gather(master.astype(bf16), "fsdp", axis=0, tiled=True)
    tiles = [
        lax.all_gather(
            lax.dynamic_index_in_dim(owner_rows, slot_of[tile], 0, keepdims=False), "dp", axis=0, tiled=True
        )
        for tile in range(n_tiles)
    ]
    w_in = jnp.concatenate(tiles[10:14], axis=1)
    w_out = jnp.concatenate(tiles[14:18], axis=0)
    count, width = tokens.shape
    head_dim = width // HEADS
    scale = head_dim ** (-0.5)
    seg = segments(lengths[0], count)
    live = keep == 1
    places = jnp.arange(count)

    def split(value):
        return value.astype(bf16).reshape(-1, HEADS, head_dim)

    def joined(value):
        return value.astype(bf16).reshape(-1, width)

    def probabilities(left, right, mask):
        scores = jnp.einsum("qhd,khd->hqk", left, right, preferred_element_type=f32) * scale
        scores = jnp.where(mask[None], scores, -1e30)
        expo = jnp.exp(scores - jnp.max(scores, axis=-1, keepdims=True))
        return expo / jnp.sum(expo, axis=-1, keepdims=True)

    def weighted(probs, right):
        return jnp.einsum("hqk,khd->qhd", probs, right, preferred_element_type=f32)

    def through(weights, d_out, left, right, probs, values):
        d_mixed = split(matmul_right(d_out, weights))
        d_probs = jnp.einsum("qhd,khd->hqk", d_mixed, values, preferred_element_type=f32)
        d_scores = (probs * (d_probs - jnp.sum(probs * d_probs, axis=-1, keepdims=True))).astype(bf16)
        d_left = joined(weighted(d_scores, right) * scale)
        d_right = joined(jnp.einsum("hqk,qhd->khd", d_scores, left, preferred_element_type=f32) * scale)
        d_values = joined(jnp.einsum("hqk,qhd->khd", probs.astype(bf16), d_mixed, preferred_element_type=f32))
        return d_left, d_right, d_values

    h0 = tokens.astype(f32)
    a_in = normalize(h0, gains[0]).astype(bf16)
    query, keys, values = (split(matmul(a_in, tiles[n])) for n in range(3))
    allowed = (seg[:, None] == seg[None, :]) & (live[None, :] | (places[:, None] == places[None, :]))
    probs = probabilities(query, keys, allowed)
    attended = joined(weighted(probs.astype(bf16), values))
    h1 = h0 + matmul(attended, tiles[3])
    b_in = normalize(h1, gains[1]).astype(bf16)
    slots, ctx_len, ctx_width = context.shape
    ctx = context.reshape(slots * ctx_len, ctx_width)
    ctx_low, ctx_high = ctx[:, :width], ctx[:, width:]
    cross_q = split(matmul(b_in, tiles[4]))
    cross_k = split(matmul(ctx_low, tiles[5]) + matmul(ctx_high, tiles[6]))
    cross_v = split(matmul(ctx_low, tiles[7]) + matmul(ctx_high, tiles[8]))
    item = jnp.arange(slots * ctx_len) // ctx_len
    cross_p = probabilities(cross_q, cross_k, seg[:, None] == item[None, :])
    cross_o = joined(weighted(cross_p.astype(bf16), cross_v))
    h2 = h1 + matmul(cross_o, tiles[9])
    c_in = normalize(h2, gains[2]).astype(bf16)
    hidden = matmul(c_in, w_in)
    activated = gelu_tanh(hidden).astype(bf16)
    layer_out = (h2 + matmul(activated, w_out)).astype(bf16)
    grad_out = cotangent.astype(f32) * live.astype(f32)[:, None]
    d_ff = grad_out.astype(bf16)
    d_hidden = jax.vjp(gelu_tanh, hidden)[1](matmul_right(d_ff, w_out))[0].astype(bf16)
    part_two, gain_grad_two = jax.vjp(normalize, h2, gains[2])[1](matmul_right(d_hidden, w_in))
    dh2 = grad_out + part_two
    d_cross_out = dh2.astype(bf16)
    d_cq, d_ck, d_cv = through(tiles[9], d_cross_out, cross_q, cross_k, cross_p, cross_v)
    part_one, gain_grad_one = jax.vjp(normalize, h1, gains[1])[1](matmul_right(d_cq, tiles[4]))
    dh1 = dh2 + part_one
    d_self_out = dh1.astype(bf16)
    d_q, d_k, d_v = through(tiles[3], d_self_out, query, keys, probs, values)
    d_a = matmul_right(d_q, tiles[0]) + matmul_right(d_k, tiles[1]) + matmul_right(d_v, tiles[2])
    part_zero, gain_grad_zero = jax.vjp(normalize, h0, gains[0])[1](d_a)
    grad_tokens = (dh1 + part_zero).astype(bf16)
    pairs = [
        (a_in, d_q),
        (a_in, d_k),
        (a_in, d_v),
        (attended, d_self_out),
        (b_in, d_cq),
        (ctx_low, d_ck),
        (ctx_high, d_ck),
        (ctx_low, d_cv),
        (ctx_high, d_cv),
        (cross_o, d_cross_out),
    ]
    for part in range(4):
        pairs.append((c_in, d_hidden[:, part * width : (part + 1) * width]))
    for part in range(4):
        pairs.append((activated[:, part * width : (part + 1) * width], d_ff))
    total_slots = lax.axis_size("fsdp") * cap
    placed = jnp.zeros((total_slots,) + master.shape[1:], bf16)
    for tile, (left, right) in enumerate(pairs):
        term = lax.psum_scatter(
            matmul_left(left, right).astype(bf16), "dp", scatter_dimension=0, tiled=True
        )
        placed = lax.dynamic_update_index_in_dim(placed, term, slot_of[tile], 0)
    owned = lax.psum_scatter(placed, "fsdp", scatter_dimension=0, tiled=True).astype(f32)
    my_slots = lax.axis_index("fsdp") * cap + jnp.arange(cap)
    used = jnp.any(slot_of[None, :] == my_slots[:, None], axis=1)[:, None, None]
    updated = adam_update(master, moment_one, moment_two, owned, rate_matrix, decay_rate)
    new_w, new_m, new_v = (jnp.where(used, value, 0.0) for value in updated)
    gain_grads = jnp.stack([gain_grad_zero, gain_grad_one, gain_grad_two])
    gain_total = lax.psum(gain_grads, ("dp", "fsdp"))
    new_g, new_gm, new_gv = adam_update(gains, gain_one, gain_two, gain_total, rate_gain, 0.0)
    return (layer_out, grad_tokens, new_w, new_m, new_v, new_g, new_gm, new_gv)


def solution(mesh):
    planes = mesh.shape["dp"] == 8 and mesh.shape["fsdp"] == 4
    if planes:
        used = Mesh(mesh.devices.reshape(4, 2, 2, 2), ALL_AXES)
        dp, fsdp, body = ("z", "x"), ("y", "c"), plane_body
    else:
        used, dp, fsdp, body = mesh, ("dp",), ("fsdp",), whole_body
    rows = P(dp + fsdp, None)
    tiles = P(fsdp, dp, None)
    return jax.shard_map(
        body,
        mesh=used,
        in_specs=(rows, rows, P(dp + fsdp, None, None), rows, P(dp + fsdp), P(), tiles, tiles, tiles, P(), P(), P()),
        out_specs=(rows, rows, tiles, tiles, tiles, P(), P(), P()),
        check_vma=False,
    )
```
